32 devices in a mesh: dp: 8 (over z, y), row: 2 (over x), col: 2 (over core).
Axes of the slice: x: 2, y: 2, z: 4, core: 2. Of those that a mesh axis runs over, the one named last changes fastest.
Arguments:
- tokens: bfloat16 [32768, 768], P(('dp', 'col'), 'row'), may hold values from -6 to 6
- cotangent: bfloat16 [32768, 768], P(('dp', 'col'), 'row'), may hold values from -6 to 6
- seq_lengths: int32 [16], P('dp'), may hold values from 1024 to 2048, as said below
- w_query: bfloat16 [768, 384], P('row', 'col'), may hold values from -0.3125 to 0.3125
- w_key: bfloat16 [768, 384], P('row', 'col'), may hold values from -0.3125 to 0.3125
- w_value: bfloat16 [768, 384], P('row', 'col'), may hold values from -0.21875 to 0.21875
- w_convout: bfloat16 [768, 384], P('row', 'col'), may hold values from -0.21875 to 0.21875
- w_point: bfloat16 [768, 384], P('row', 'col'), may hold values from -0.21875 to 0.21875
- w_depth: bfloat16 [768, 9], replicated, may hold values from -2 to 2
- b_query: bfloat16 [384], replicated, may hold values from -1.5 to 1.5
- b_value: bfloat16 [384], replicated, may hold values from -1.5 to 1.5
- b_convout: bfloat16 [384], replicated, may hold values from -1.5 to 1.5
- b_point: bfloat16 [384], replicated, may hold values from -1.5 to 1.5
- w_kernel: bfloat16 [384, 54], replicated, may hold values from -0.3125 to 0.3125
- b_kernel: bfloat16 [54], replicated, may hold values from -1.5 to 1.5
- w_dense: bfloat16 [768, 768], P('col', 'row'), may hold values from -0.625 to 0.625
- b_dense: bfloat16 [768], replicated, may hold values from -1.5 to 1.5
- gain_one: bfloat16 [768], replicated, may hold values from 0.5 to 1.5
- bias_one: bfloat16 [768], replicated, may hold values from -1.5 to 1.5
- w_inter: bfloat16 [2, 384, 1536], P('row', None, 'col'), may hold values from -0.3125 to 0.3125
- b_inter: bfloat16 [3072], replicated, may hold values from -1.5 to 1.5
- w_output: bfloat16 [2, 1536, 384], P('row', 'col'), may hold values from -0.21875 to 0.21875
- b_output: bfloat16 [768], replicated, may hold values from -1.5 to 1.5
- gain_two: bfloat16 [768], replicated, may hold values from 0.5 to 1.5
- bias_two: bfloat16 [768], replicated, may hold values from -1.5 to 1.5
Outputs:
- hidden_out: bfloat16 [32768, 768], P(('dp', 'col'), 'row')
- grad_tokens: float32 [32768, 768], P(('dp', 'col'), 'row')
- grad_w_query: float32 [768, 384], P('row', 'col')
- grad_w_key: float32 [768, 384], P('row', 'col')
- grad_w_value: float32 [768, 384], P('row', 'col')
- grad_w_convout: float32 [768, 384], P('row', 'col')
- grad_w_point: float32 [768, 384], P('row', 'col')
- grad_w_depth: float32 [768, 9], replicated
- grad_b_query: float32 [384], replicated
- grad_b_value: float32 [384], replicated
- grad_b_convout: float32 [384], replicated
- grad_b_point: float32 [384], replicated
- grad_w_kernel: float32 [384, 54], replicated
- grad_b_kernel: float32 [54], replicated
- grad_w_dense: float32 [768, 768], P('col', 'row')
- grad_b_dense: float32 [768], replicated
- grad_gain_one: float32 [768], replicated
- grad_bias_one: float32 [768], replicated
- grad_w_inter: float32 [2, 384, 1536], P('row', None, 'col')
- grad_b_inter: float32 [3072], replicated
- grad_w_output: float32 [2, 1536, 384], P('row', 'col')
- grad_b_output: float32 [768], replicated
- grad_gain_two: float32 [768], replicated
- grad_bias_two: float32 [768], replicated
The draws below stay inside these ranges and needn't reach their ends.
Inputs may be any that keep to these rules, and one draw needn't show every extreme that they name: `seq_lengths`: valid tokens of each sequence are counted from the start of its 2048 slots; every draw holds a full sequence.
All inputs are finite; a program needn't handle non-finite values.
Results may differ from the reference program's by a relative error of at most 0.025.
Values may be sent and summed in bfloat16 or wider, within the bound.
A program may use at most 192 MiB of HBM per device.

```python
import jax
import jax.numpy as jnp
from jax import lax

D = 768
HD = 64
KW = 9
FF = 3072
GROUPS = 2
LMAX = 2048
HEADS = 6
NSEQ = 16
TOKENS = 32768


def draw_seq_lengths(key, part):
    key_one, key_two = jax.random.split(key)
    lengths_drawn = jax.random.randint(key_one, (NSEQ,), LMAX // 2, LMAX + 1)
    longest = jax.random.randint(key_two, (), 0, NSEQ)
    return jnp.where(jnp.arange(NSEQ) == longest, LMAX, lengths_drawn).astype(jnp.int32)


def levels(own_key, shape, cuts, low, top_value):
    gain = 1.0
    for dim, blocks in cuts:
        draws = jax.random.uniform(jax.random.fold_in(jax.random.fold_in(own_key, 6), dim), (blocks,), jnp.float32, low / len(cuts), top_value / len(cuts))
        gain = gain * jnp.repeat(jnp.exp(draws), shape[dim] // blocks).reshape((-1,) + (1,) * (len(shape) - 1 - dim))
    return gain


def bell_draw(rng, shape, width, reach, shards=(), dtype=jnp.bfloat16):
    values = width * jax.random.normal(rng, shape, jnp.float32)
    if shards:
        values = values * levels(rng, shape, shards, -0.22, 0.18)
    return jnp.clip(values, -reach, reach).astype(dtype)


def setup_inputs(seed: int = 0) -> dict:
    arg_keys = jax.random.split(jax.random.key(seed), 26)
    tokens = bell_draw(arg_keys[0], (TOKENS, D), 1.0, 6.0, ((0, 16), (1, 2)))
    cotangent = bell_draw(arg_keys[1], (TOKENS, D), 1.0, 6.0, ((0, 16), (1, 2)))
    seq_lengths = draw_seq_lengths(jax.random.fold_in(arg_keys[25], 71), 0)
    w_query = bell_draw(arg_keys[3], (D, D // 2), (D // 2) ** -0.5, 0.3125, ((0, 2), (1, 2)))
    w_key = bell_draw(arg_keys[4], (D, D // 2), (D // 2) ** -0.5, 0.3125, ((0, 2), (1, 2)))
    w_value = bell_draw(arg_keys[5], (D, D // 2), D ** -0.5, 0.21875, ((0, 2), (1, 2)))
    w_convout = bell_draw(arg_keys[6], (D, D // 2), D ** -0.5, 0.21875, ((0, 2), (1, 2)))
    w_point = bell_draw(arg_keys[7], (D, D // 2), D ** -0.5, 0.21875, ((0, 2), (1, 2)))
    w_depth = bell_draw(arg_keys[8], (D, KW), KW ** -0.5, 2.0)
    b_query = bell_draw(arg_keys[9], (D // 2,), 0.3, 1.5)
    b_value = bell_draw(arg_keys[10], (D // 2,), 0.3, 1.5)
    b_convout = bell_draw(arg_keys[11], (D // 2,), 0.3, 1.5)
    b_point = bell_draw(arg_keys[12], (D // 2,), 0.3, 1.5)
    w_kernel = bell_draw(arg_keys[13], (D // 2, HEADS * KW), (D // 2) ** -0.5, 0.3125)
    b_kernel = bell_draw(arg_keys[14], (HEADS * KW,), 0.3, 1.5)
    w_dense = bell_draw(arg_keys[15], (D, D), (D // 8) ** -0.5, 0.625, ((0, 2), (1, 2)))
    b_dense = bell_draw(arg_keys[16], (D,), 0.3, 1.5)
    gain_one = jnp.clip(1.0 + 0.1 * jax.random.normal(arg_keys[17], (D,), jnp.float32), 0.5, 1.5).astype(jnp.bfloat16)
    bias_one = bell_draw(arg_keys[18], (D,), 0.3, 1.5)
    w_inter = bell_draw(arg_keys[19], (GROUPS, D // GROUPS, FF // GROUPS), (D // GROUPS) ** -0.5, 0.3125, ((0, 2), (2, 2)))
    b_inter = bell_draw(arg_keys[20], (FF,), 0.3, 1.5)
    w_output = bell_draw(arg_keys[21], (GROUPS, FF // GROUPS, D // GROUPS), (FF // 4) ** -0.5, 0.21875, ((0, 2), (1, 2)))
    b_output = bell_draw(arg_keys[22], (D,), 0.3, 1.5)
    gain_two = jnp.clip(1.0 + 0.1 * jax.random.normal(arg_keys[23], (D,), jnp.float32), 0.5, 1.5).astype(jnp.bfloat16)
    bias_two = bell_draw(arg_keys[24], (D,), 0.3, 1.5)
    return dict(tokens=tokens, cotangent=cotangent, seq_lengths=seq_lengths, w_query=w_query, w_key=w_key, w_value=w_value, w_convout=w_convout, w_point=w_point, w_depth=w_depth, b_query=b_query, b_value=b_value, b_convout=b_convout, b_point=b_point, w_kernel=w_kernel, b_kernel=b_kernel, w_dense=w_dense, b_dense=b_dense, gain_one=gain_one, bias_one=bias_one, w_inter=w_inter, b_inter=b_inter, w_output=w_output, b_output=b_output, gain_two=gain_two, bias_two=bias_two)


@jax.custom_vjp
def low(v):
    return lax.optimization_barrier(v.astype(jnp.bfloat16)).astype(jnp.float32)

@jax.custom_vjp
def low_back(v):
    return v

def low_keep(v):
    return (low(v), None)

def low_pass(kept, grad):
    return (grad,)

def back_keep(v):
    return (v, None)

def back_low(kept, grad):
    return (low(grad),)
low.defvjp(low_keep, low_pass)
low_back.defvjp(back_keep, back_low)
EPS = 1e-12
HIGH = lax.Precision.HIGHEST

def both_ways(value):
    return low(low_back(value))

def matmul(left_op, right_op):
    return jnp.dot(left_op, right_op, precision=HIGH)

def layer_norm(value, gain_vec, bias_vec):
    center = lax.optimization_barrier(jnp.mean(value, axis=-1, keepdims=True))
    spread = lax.optimization_barrier(jnp.mean((value - center) ** 2, axis=-1, keepdims=True))
    return (value - center) * lax.rsqrt(spread + EPS) * gain_vec + bias_vec

def layer(tokens_in, params, mask_rows, seq_len):
    w_query, w_key, w_value, w_convout, w_point, w_depth, b_query, b_value, b_convout, b_point, w_kernel, b_kernel, w_dense, b_dense, gain_one, bias_one, w_inter, b_inter, w_output, b_output, gain_two, bias_two = params
    head_count = D // (2 * HD)
    half_kw = KW // 2
    masked = tokens_in * mask_rows[:, None]
    padded = jnp.pad(masked, ((half_kw, half_kw), (0, 0)))
    depth_mix = jnp.zeros_like(masked)
    for offset in range(KW):
        depth_mix = depth_mix + padded[offset:offset + LMAX] * w_depth[:, offset]
    depth_mix = low(depth_mix)
    query_rows = both_ways(matmul(masked, w_query) + b_query)
    key_rows = both_ways(matmul(masked, w_key))
    value_rows = both_ways(matmul(masked, w_value) + b_value)
    convout = mask_rows[:, None] * low_back(matmul(masked, w_convout) + b_convout)
    point_rows = low_back(matmul(depth_mix, w_point) + b_point)
    shaped_query = query_rows.reshape(LMAX, head_count, HD)
    shaped_key = key_rows.reshape(LMAX, head_count, HD)
    shaped_value = value_rows.reshape(LMAX, head_count, HD)
    scores = low_back(jnp.einsum('qhd,khd->hqk', shaped_query, shaped_key, precision=HIGH) * HD ** (-0.5))
    key_valid = jnp.arange(LMAX) < seq_len
    scores = jnp.where(key_valid[None, None, :], scores, -1e+30)
    attn_probs = low(jax.nn.softmax(scores, axis=-1))
    context = both_ways(jnp.einsum('hqk,khd->qhd', attn_probs, shaped_value, precision=HIGH).reshape(LMAX, D // 2))
    mixer_rows = low(point_rows * query_rows)
    logits = low_back(matmul(mixer_rows, w_kernel) + b_kernel)
    kernel_probs = jax.nn.softmax(logits.reshape(LMAX, head_count, KW), axis=-1)
    conv_pad = jnp.pad(convout.reshape(LMAX, head_count, HD), ((half_kw, half_kw), (0, 0), (0, 0)))
    conv_mix = jnp.zeros((LMAX, head_count, HD), jnp.float32)
    for offset in range(KW):
        conv_mix = conv_mix + kernel_probs[:, :, offset, None] * conv_pad[offset:offset + LMAX]
    conv_mix = low(conv_mix.reshape(LMAX, D // 2))
    mixed_rows = jnp.stack([context.reshape(LMAX, 2, D // 4), conv_mix.reshape(LMAX, 2, D // 4)], axis=2).reshape(LMAX, D)
    dense_out = low_back(matmul(mixed_rows, w_dense) + b_dense)
    first_norm = layer_norm(dense_out + masked, gain_one, bias_one)
    first_low = low(first_norm)
    inter_pre = low_back(jnp.einsum('lgi,gio->lgo', first_low.reshape(LMAX, GROUPS, D // GROUPS), w_inter, precision=HIGH).reshape(LMAX, FF) + b_inter)
    activated = low(jax.nn.gelu(inter_pre, approximate=False))
    output = low_back(jnp.einsum('lgi,gio->lgo', activated.reshape(LMAX, GROUPS, FF // GROUPS), w_output, precision=HIGH).reshape(LMAX, D) + b_output)
    return layer_norm(output + first_norm, gain_two, bias_two)

def reference(tokens, cotangent, seq_lengths, w_query, w_key, w_value, w_convout, w_point, w_depth, b_query, b_value, b_convout, b_point, w_kernel, b_kernel, w_dense, b_dense, gain_one, bias_one, w_inter, b_inter, w_output, b_output, gain_two, bias_two):
    params = tuple((weight_arg.astype(jnp.float32) for weight_arg in (w_query, w_key, w_value, w_convout, w_point, w_depth, b_query, b_value, b_convout, b_point, w_kernel, b_kernel, w_dense, b_dense, gain_one, bias_one, w_inter, b_inter, w_output, b_output, gain_two, bias_two)))
    seq_tokens = tokens.astype(jnp.float32).reshape(NSEQ, LMAX, D)
    seq_cot = cotangent.astype(jnp.float32).reshape(NSEQ, LMAX, D)

    def seq_step(running, pieces):
        tok_seq, cot_seq, seq_len = pieces
        mask_rows = (jnp.arange(LMAX) < seq_len).astype(jnp.float32)
        result, pullback = jax.vjp(lambda tok_in, par_in: layer(tok_in, par_in, mask_rows, seq_len), tok_seq, params)
        grad_tok, grad_par = pullback(cot_seq * mask_rows[:, None])
        running = jax.tree.map(lambda total_old, fresh: total_old + fresh, running, grad_par)
        return (running, (result.astype(jnp.bfloat16), grad_tok))
    zero_tree = jax.tree.map(jnp.zeros_like, params)
    totals, (hidden_all, grad_all) = lax.scan(seq_step, zero_tree, (seq_tokens, seq_cot, seq_lengths))
    return (hidden_all.reshape(TOKENS, D), grad_all.reshape(TOKENS, D), totals[0], totals[1], totals[2], totals[3], totals[4], totals[5], totals[6], totals[7], totals[8], totals[9], totals[10], totals[11], totals[12], totals[13], totals[14], totals[15], totals[16], totals[17], totals[18], totals[19], totals[20], totals[21])
```

```python
import functools

import jax
import jax.numpy as jnp
import numpy as np
from jax import lax
from jax.experimental import pallas as pl
from jax.experimental.pallas import tpu as pltpu
from jax.sharding import PartitionSpec as P

D = 768
HALF = 384
HD = 64
KW = 9
FF = 3072
GW = 1536
LMAX = 2048
ROWS = 1024
EPS = 1e-12
LOG2E = 1.4426950408889634
LN2 = 0.6931471805599453
BF = jnp.bfloat16
F32 = jnp.float32
VMEM_BYTES = 63 * 1024 * 1024


def nn(a, b):
    return lax.dot_general(a, b, (((1,), (0,)), ((), ())), preferred_element_type=F32)


def nt(a, b):
    return lax.dot_general(a, b, (((1,), (1,)), ((), ())), preferred_element_type=F32)


def col_sum(x):
    return jnp.sum(x, axis=0, keepdims=True)


def row_ids(start, rows):
    return start + lax.broadcasted_iota(jnp.int32, (rows, 1), 0)


def whole(shape):
    return pl.BlockSpec(shape, lambda i, info: (0,) * len(shape))


def params(name):
    return dict(
        name=name,
        compiler_params=pltpu.CompilerParams(vmem_limit_bytes=VMEM_BYTES),
    )


def kv_kernel(info, tok_ref, w_ref, bv_ref, kd_ref, kt_ref, vz_ref, first_key):
    i = pl.program_id(0)
    rows = tok_ref.shape[0]
    keep = row_ids(i * rows, rows) < info[0]
    h = jnp.where(keep, tok_ref[...].astype(F32), 0.0).astype(BF)
    k = nn(h, w_ref[0])
    v = nn(h, w_ref[1]) + bv_ref[...]

    @pl.when(i == 0)
    def _():
        first_key[...] = k[0:8]

    kd_ref[...] = jnp.where(keep, k, first_key[0:1]).astype(BF)
    kt_ref[...] = k.T.astype(BF)
    vz_ref[...] = jnp.where(keep, v, 0.0).astype(BF)


def keys_values(info, tok, w5, b_value):
    rows = 512
    return pl.pallas_call(
        kv_kernel,
        grid_spec=pltpu.PrefetchScalarGridSpec(
            num_scalar_prefetch=1,
            grid=(LMAX // rows,),
            in_specs=[
                pl.BlockSpec((rows, D), lambda i, info: (i, 0)),
                pl.BlockSpec((2, D, HALF), lambda i, info: (0, 0, 0)),
                whole((1, HALF)),
            ],
            out_specs=[
                pl.BlockSpec((rows, HALF), lambda i, info: (i, 0)),
                pl.BlockSpec((HALF, rows), lambda i, info: (0, i)),
                pl.BlockSpec((rows, HALF), lambda i, info: (i, 0)),
            ],
            scratch_shapes=[pltpu.VMEM((8, HALF), F32)],
        ),
        out_shape=[
            jax.ShapeDtypeStruct((LMAX, HALF), BF),
            jax.ShapeDtypeStruct((HALF, LMAX), BF),
            jax.ShapeDtypeStruct((LMAX, HALF), BF),
        ],
        **params("keys_values"),
    )(info, tok, w5, b_value)


def own_kernel(
    info, hx_ref, w_ref, wdep_ref, vec_ref, wk_ref, bk_ref, spread_ref,
    q_ref, qs_ref, pt_ref, kp_ref, conv_ref, mix_ref, dep_ref, hbuf, cbuf,
):
    i = pl.program_id(0)
    rows = q_ref.shape[0]
    wide = rows + 32
    base = pl.multiple_of(i * rows, 16)
    ids = row_ids(info[1] * ROWS + i * rows - 16, wide)
    keep = (ids >= 0) & (ids < info[0])
    hw = jnp.where(keep, hx_ref[pl.ds(base, wide), :].astype(F32), 0.0)
    hbuf[...] = hw
    depth = jnp.zeros((rows, D), F32)
    for j in range(KW):
        depth = depth + hbuf[12 + j : 12 + j + rows, :] * wdep_ref[j : j + 1, :]
    depth_low = depth.astype(BF)
    dep_ref[...] = depth_low
    hl = hw.astype(BF)
    conv = jnp.where(keep, nn(hl, w_ref[0]) + vec_ref[0:1, :], 0.0)
    cbuf[...] = conv
    conv_ref[pl.ds(base, wide), :] = conv.astype(BF)
    q = nn(hl[16 : 16 + rows], w_ref[1]) + vec_ref[1:2, :]
    q_low = q.astype(BF)
    q_ref[...] = q_low
    qs_ref[...] = (q * (0.125 * LOG2E)).astype(BF)
    pt = nn(depth_low, w_ref[2]) + vec_ref[2:3, :]
    pt_ref[...] = pt.astype(BF)
    mixer = (pt * q_low.astype(F32)).astype(BF)
    logits = (nt(wk_ref[...], mixer) + bk_ref[:, 0:1]).reshape(KW, 8, rows)
    peak = jnp.max(logits, axis=0, keepdims=True)
    raised = jnp.exp(logits - peak)
    kp = (raised / jnp.sum(raised, axis=0, keepdims=True)).reshape(KW * 8, rows)
    kp_ref[...] = kp
    kpt = kp.T.astype(BF)
    mix = jnp.zeros((rows, HALF), F32)
    for j in range(KW):
        mix = mix + nn(kpt, spread_ref[:, j * HALF : (j + 1) * HALF]) * cbuf[12 + j : 12 + j + rows, :]
    mix_ref[...] = mix.astype(BF)


def own_rows(info, hx, w5, wdep, vec, wk72, bk72, spread):
    rows = 256
    blk = pl.BlockSpec((rows, HALF), lambda i, info: (i, 0))
    half = jax.ShapeDtypeStruct((ROWS, HALF), BF)
    return pl.pallas_call(
        own_kernel,
        grid_spec=pltpu.PrefetchScalarGridSpec(
            num_scalar_prefetch=1,
            grid=(ROWS // rows,),
            in_specs=[
                whole((ROWS + 32, D)),
                whole((3, D, HALF)),
                whole((16, D)),
                whole((8, HALF)),
                whole((72, HALF)),
                whole((72, 128)),
                whole((72, KW * HALF)),
            ],
            out_specs=[
                blk,
                blk,
                blk,
                pl.BlockSpec((72, rows), lambda i, info: (0, i)),
                whole((ROWS + 32, HALF)),
                blk,
                pl.BlockSpec((rows, D), lambda i, info: (i, 0)),
            ],
            scratch_shapes=[pltpu.VMEM((rows + 32, D), F32), pltpu.VMEM((rows + 32, HALF), F32)],
        ),
        out_shape=[
            half,
            half,
            half,
            jax.ShapeDtypeStruct((72, ROWS), F32),
            jax.ShapeDtypeStruct((ROWS + 32, HALF), BF),
            half,
            jax.ShapeDtypeStruct((ROWS, D), BF),
        ],
        **params("own_rows"),
    )(info, hx, w5, wdep, vec, wk72, bk72, spread)


def attend_kernel(info, q_ref, k_ref, v_ref, ctx_ref, lse_ref):
    k = k_ref[...]
    ones = jnp.where(row_ids(0, LMAX) < info[0], 1.0, 0.0)
    ve = jnp.concatenate([v_ref[...], jnp.broadcast_to(ones, (LMAX, 128)).astype(BF)], axis=1)
    rows = 256
    lane = lax.broadcasted_iota(jnp.int32, (rows, 128), 1)
    for u in range(ROWS // rows):
        part = slice(u * rows, (u + 1) * rows)
        outs = []
        for hh in range(2):
            q = jnp.where((lane < HD) == (hh == 0), q_ref[part, :], jnp.zeros((), BF))
            s = nt(q, k)
            peak = jnp.max(s, axis=1, keepdims=True)
            p = jnp.exp2(s - peak).astype(BF)
            o = nn(p, ve)
            outs.append(o[:, :128] / o[:, 128:])
            lse_ref[0, hh : hh + 1, part] = (peak + jnp.log2(o[:, 128:129])).T
        ctx_ref[part, :] = jnp.where(lane < HD, outs[0], outs[1]).astype(BF)


def attend(info, qs, kd, vz):
    pair = lambda rows: pl.BlockSpec((rows, 128), lambda p, info: (0, p))
    return pl.pallas_call(
        attend_kernel,
        grid_spec=pltpu.PrefetchScalarGridSpec(
            num_scalar_prefetch=1,
            grid=(3,),
            in_specs=[pair(ROWS), pair(LMAX), pair(LMAX)],
            out_specs=[pair(ROWS), pl.BlockSpec((1, 8, ROWS), lambda p, info: (p, 0, 0))],
        ),
        out_shape=[
            jax.ShapeDtypeStruct((ROWS, HALF), BF),
            jax.ShapeDtypeStruct((3, 8, ROWS), F32),
        ],
        **params("attend"),
    )(info, qs, kd, vz)


def attend_back_kernel(info, q_ref, do_ref, k_ref, v_ref, kt_ref, lse_ref, del_ref, dq_ref, dk_ref, dv_ref, dka, dva):
    i = pl.program_id(1)
    k = k_ref[...]
    v = v_ref[...]
    rows = q_ref.shape[0]
    lane = lax.broadcasted_iota(jnp.int32, (rows, 128), 1)
    dk = dv = None
    for hh in range(2):
        mine = (lane < HD) == (hh == 0)
        q = jnp.where(mine, q_ref[...], jnp.zeros((), BF))
        do = jnp.where(mine, do_ref[...], jnp.zeros((), BF))
        p = jnp.exp2(nt(k, q) - lse_ref[0, hh : hh + 1, :])
        ds = (p * (nt(v, do) - del_ref[0, hh : hh + 1, :])).astype(BF)
        dv_one = nn(p.astype(BF), do)
        dk_one = nn(ds, q)
        dv = dv_one if dv is None else dv + dv_one
        dk = dk_one if dk is None else dk + dk_one
        dq_ref[hh * HD : (hh + 1) * HD, :] = (nn(kt_ref[hh * HD : (hh + 1) * HD, :], ds) * 0.125).astype(BF)

    @pl.when(i == 0)
    def _():
        dka[...] = dk
        dva[...] = dv

    @pl.when(i == pl.num_programs(1) - 1)
    def _():
        keep = row_ids(0, LMAX) < info[0]
        dk_ref[...] = jnp.where(keep, (dka[...] + dk) * LN2, 0.0).astype(BF)
        dv_ref[...] = jnp.where(keep, dva[...] + dv, 0.0).astype(BF)


def attend_back(info, qs, do, kd, vz, kt, lse, delta):
    rows = 512
    mine = pl.BlockSpec((rows, 128), lambda p, i, info: (i, p))
    pair = pl.BlockSpec((LMAX, 128), lambda p, i, info: (0, p))
    line = pl.BlockSpec((1, 8, rows), lambda p, i, info: (p, 0, i))
    return pl.pallas_call(
        attend_back_kernel,
        grid_spec=pltpu.PrefetchScalarGridSpec(
            num_scalar_prefetch=1,
            grid=(3, ROWS // rows),
            in_specs=[mine, mine, pair, pair, pl.BlockSpec((128, LMAX), lambda p, i, info: (p, 0)), line, line],
            out_specs=[pl.BlockSpec((128, rows), lambda p, i, info: (p, i)), pair, pair],
            scratch_shapes=[pltpu.VMEM((LMAX, 128), F32), pltpu.VMEM((LMAX, 128), F32)],
        ),
        out_shape=[
            jax.ShapeDtypeStruct((HALF, ROWS), BF),
            jax.ShapeDtypeStruct((LMAX, HALF), BF),
            jax.ShapeDtypeStruct((LMAX, HALF), BF),
        ],
        **params("attend_back"),
    )(info, qs, do, kd, vz, kt, lse, delta)


def norm_parts(x):
    xc = x - jnp.mean(x, axis=1, keepdims=True)
    inv = lax.rsqrt(jnp.mean(xc * xc, axis=1, keepdims=True) + EPS)
    return xc * inv, inv


def norm_back(up, normal, inv, gain):
    e = up * gain
    return inv * (e - jnp.mean(e, axis=1, keepdims=True) - normal * jnp.mean(e * normal, axis=1, keepdims=True))


def ffn_kernel(
    info, ctx_ref, mix_ref, tok_ref, cot_ref, wd_ref, wi_ref, wo_ref, vec_ref, bi_ref, ones_ref,
    hid_ref, gpre_ref, gctx_ref, gcv_ref, del_ref, gwd_ref, gwi_ref, gwo_ref, sm_ref, gbi_ref,
    act_s, gp_s, awd, awi, awo,
):
    i = pl.program_id(0)
    rows = ctx_ref.shape[0]
    keep = row_ids(info[1] * ROWS + i * rows, rows) < info[0]

    @pl.when(i == 0)
    def _():
        awd[...] = jnp.zeros_like(awd)
        awi[...] = jnp.zeros_like(awi)
        awo[...] = jnp.zeros_like(awo)
        sm_ref[...] = jnp.zeros_like(sm_ref)
        gbi_ref[...] = jnp.zeros_like(gbi_ref)

    vec = lambda k: vec_ref[k : k + 1, :]
    h = jnp.where(keep, tok_ref[...].astype(F32), 0.0)
    ctx = ctx_ref[...]
    mixed = jnp.concatenate([ctx, mix_ref[...]], axis=1)
    n1, inv1 = norm_parts(nn(mixed, wd_ref[...]) + vec(0) + h)
    f1 = n1 * vec(1) + vec(2)
    fl = f1.astype(BF)
    chunk = 512
    outs = []
    for g in range(2):
        fg = fl[:, g * HALF : (g + 1) * HALF]
        for ch in range(GW // chunk):
            cols = slice(ch * chunk, (ch + 1) * chunk)
            put = slice(g * GW + ch * chunk, g * GW + (ch + 1) * chunk)
            x = nn(fg, wi_ref[g, :, cols]) + bi_ref[0:1, put]
            phi = 0.5 + 0.5 * lax.erf(x * 0.7071067811865476)
            act_s[:, put] = (x * phi).astype(BF)
            gp_s[:, put] = phi + x * jnp.exp2(x * x * (-0.5 * LOG2E)) * 0.3989422804014327
        outs.append(nn(act_s[:, g * GW : (g + 1) * GW], wo_ref[g]))
    n2, inv2 = norm_parts(jnp.concatenate(outs, axis=1) + vec(3) + f1)
    hid_ref[...] = (n2 * vec(4) + vec(5)).astype(BF)
    u = jnp.where(keep, cot_ref[...].astype(F32), 0.0)
    gp2 = norm_back(u, n2, inv2, vec(4))
    go = gp2.astype(BF)
    got = go.T
    flt = fl.T
    gfs = []
    for g in range(2):
        sel = slice(g * HALF, (g + 1) * HALF)
        gf = gp2[:, sel]
        for ch in range(GW // chunk):
            cols = slice(ch * chunk, (ch + 1) * chunk)
            put = slice(g * GW + ch * chunk, g * GW + (ch + 1) * chunk)
            gi = (gp_s[:, put] * nt(go[:, sel], wo_ref[g, cols, :])).astype(BF)
            gbi_ref[0:1, put] += col_sum(gi.astype(F32))
            awo[g, :, cols] += nn(got[sel], act_s[:, put])
            awi[g, :, cols] += nn(flt[sel], gi)
            gf = gf + nt(gi, wi_ref[g, :, cols])
        gfs.append(gf)
    gf = jnp.concatenate(gfs, axis=1)
    gpre = norm_back(gf, n1, inv1, vec(1))
    gd = gpre.astype(BF)
    gpre_ref[...] = gd
    sm_ref[0:1, :] += col_sum(go.astype(F32))
    sm_ref[1:2, :] += col_sum(u * n2)
    sm_ref[2:3, :] += col_sum(u)
    sm_ref[3:4, :] += col_sum(gd.astype(F32))
    sm_ref[4:5, :] += col_sum(gf * n1)
    sm_ref[5:6, :] += col_sum(gf)
    awd[...] += nn(mixed.T, gd)
    gm = nt(gd, wd_ref[...])
    gctx = gm[:, :HALF].astype(BF)
    gctx_ref[...] = gctx
    gcv_ref[...] = gm[:, HALF:].astype(BF)
    prod = (gctx.astype(F32) * ctx.astype(F32)).astype(BF)
    del_ref[...] = nt(ones_ref[...], prod).reshape(3, 8, rows)

    @pl.when(i == pl.num_programs(0) - 1)
    def _():
        gwd_ref[...] = awd[...].astype(BF)
        gwi_ref[...] = awi[...].astype(BF)
        for g in range(2):
            gwo_ref[g] = awo[g].T.astype(BF)


def ffn(info, ctx, mix, tok, cot, wd, wi, wo, vec, bi, ones24):
    rows = 256
    blk = lambda w: pl.BlockSpec((rows, w), lambda i, info: (i, 0))
    return pl.pallas_call(
        ffn_kernel,
        grid_spec=pltpu.PrefetchScalarGridSpec(
            num_scalar_prefetch=1,
            grid=(ROWS // rows,),
            in_specs=[
                blk(HALF),
                blk(HALF),
                pl.BlockSpec((rows, D), lambda i, info: (info[1] * (ROWS // rows) + i, 0)),
                blk(D),
                whole((D, D)),
                whole((2, HALF, GW)),
                whole((2, GW, HALF)),
                whole((8, D)),
                whole((1, FF)),
                whole((24, HALF)),
            ],
            out_specs=[
                blk(D),
                blk(D),
                blk(HALF),
                blk(HALF),
                pl.BlockSpec((3, 8, rows), lambda i, info: (0, 0, i)),
                whole((D, D)),
                whole((2, HALF, GW)),
                whole((2, GW, HALF)),
                whole((8, D)),
                whole((1, FF)),
            ],
            scratch_shapes=[
                pltpu.VMEM((rows, FF), BF),
                pltpu.VMEM((rows, FF), F32),
                pltpu.VMEM((D, D), F32),
                pltpu.VMEM((2, HALF, GW), F32),
                pltpu.VMEM((2, HALF, GW), F32),
            ],
        ),
        out_shape=[
            jax.ShapeDtypeStruct((ROWS, D), BF),
            jax.ShapeDtypeStruct((ROWS, D), BF),
            jax.ShapeDtypeStruct((ROWS, HALF), BF),
            jax.ShapeDtypeStruct((ROWS, HALF), BF),
            jax.ShapeDtypeStruct((3, 8, ROWS), F32),
            jax.ShapeDtypeStruct((D, D), BF),
            jax.ShapeDtypeStruct((2, HALF, GW), BF),
            jax.ShapeDtypeStruct((2, GW, HALF), BF),
            jax.ShapeDtypeStruct((8, D), F32),
            jax.ShapeDtypeStruct((1, FF), F32),
        ],
        **params("ffn"),
    )(info, ctx, mix, tok, cot, wd, wi, wo, vec, bi, ones24)


def conv_back_kernel(
    info, gcv_ref, conv_ref, kp_ref, q_ref, pt_ref, wk_ref, spread_ref, ones_ref,
    gqm_ref, gpt_ref, gco_ref, gwk_ref, gbk_ref, acc, wbuf, tbuf,
):
    i = pl.program_id(0)
    rows = gcv_ref.shape[0]
    wide = rows + 32

    @pl.when(i == 0)
    def _():
        acc[...] = jnp.zeros_like(acc)
        tbuf[...] = jnp.zeros_like(tbuf)
        gwk_ref[...] = jnp.zeros_like(gwk_ref)
        gbk_ref[...] = jnp.zeros_like(gbk_ref)

    gcv = gcv_ref[...].astype(F32)
    wbuf[...] = conv_ref[pl.ds(pl.multiple_of(i * rows, 16), wide), :].astype(F32)
    kp = kp_ref[...]
    kpt = kp.T.astype(BF)
    gkps = []
    total = jnp.zeros((wide, HALF), F32)
    for j in range(KW):
        prod = (gcv * wbuf[12 + j : 12 + j + rows, :]).astype(BF)
        gkps.append(nt(ones_ref[...], prod))
        tbuf[24 : 24 + rows, :] = nn(kpt, spread_ref[:, j * HALF : (j + 1) * HALF]) * gcv
        total = total + tbuf[12 - j : 12 - j + wide, :]
    acc[pl.ds(pl.multiple_of(info[1] * ROWS + i * rows, 16), wide), :] += total
    gkp = jnp.concatenate(gkps, axis=0).reshape(KW, 8, rows)
    kp3 = kp.reshape(KW, 8, rows)
    inner = jnp.sum(kp3 * gkp, axis=0, keepdims=True)
    gl = (kp3 * (gkp - inner)).reshape(KW * 8, rows)
    gll = gl.astype(BF)
    gbk_ref[...] += jnp.broadcast_to(jnp.sum(gll.astype(F32), axis=1, keepdims=True), gbk_ref.shape)
    q = q_ref[...].astype(F32)
    pt = pt_ref[...].astype(F32)
    gwk_ref[...] += nn(gll, (pt * q).astype(BF))
    gmix = nn(gl.T.astype(BF), wk_ref[...])
    gqm_ref[...] = (gmix * pt).astype(BF)
    gpt_ref[...] = (gmix * q).astype(BF)

    @pl.when(i == pl.num_programs(0) - 1)
    def _():
        keep = row_ids(0, LMAX) < info[0]
        gco_ref[...] = jnp.where(keep, acc[16 : 16 + LMAX, :], 0.0).astype(BF)


def conv_back(info, gcv, conv, kp, q, pt, wk72, spread, ones8):
    rows = 256
    blk = pl.BlockSpec((rows, HALF), lambda i, info: (i, 0))
    return pl.pallas_call(
        conv_back_kernel,
        grid_spec=pltpu.PrefetchScalarGridSpec(
            num_scalar_prefetch=1,
            grid=(ROWS // rows,),
            in_specs=[
                blk,
                whole((ROWS + 32, HALF)),
                pl.BlockSpec((72, rows), lambda i, info: (0, i)),
                blk,
                blk,
                whole((72, HALF)),
                whole((72, KW * HALF)),
                whole((8, HALF)),
            ],
            out_specs=[blk, blk, whole((LMAX, HALF)), whole((72, HALF)), whole((72, 128))],
            scratch_shapes=[
                pltpu.VMEM((LMAX + 32, HALF), F32),
                pltpu.VMEM((rows + 32, HALF), F32),
                pltpu.VMEM((rows + 48, HALF), F32),
            ],
        ),
        out_shape=[
            jax.ShapeDtypeStruct((ROWS, HALF), BF),
            jax.ShapeDtypeStruct((ROWS, HALF), BF),
            jax.ShapeDtypeStruct((LMAX, HALF), BF),
            jax.ShapeDtypeStruct((72, HALF), F32),
            jax.ShapeDtypeStruct((72, 128), F32),
        ],
        **params("conv_back"),
    )(info, gcv, conv, kp, q, pt, wk72, spread, ones8)


def final_kernel(
    info, tok_ref, dk_ref, dv_ref, gco_ref, dq_ref, gqm_ref, gpt_ref, gpre_ref, dep_ref, w_ref, wdep_ref,
    gh_ref, gw_ref, sm_ref, gdep_ref, hbuf, gacc, agw, wbuf, dbuf,
):
    i = pl.program_id(0)
    rows = dk_ref.shape[0]
    wide = rows + 32
    b = lax.rem(info[1] * 2 + i, 4)
    n = info[0]

    @pl.when(i == 0)
    def _():
        hbuf[0:16, :] = jnp.zeros((16, D), F32)
        hbuf[16 + LMAX :, :] = jnp.zeros((16, D), F32)
        for k in range(4):
            keep = row_ids(k * rows, rows) < n
            hbuf[16 + k * rows : 16 + (k + 1) * rows, :] = jnp.where(
                keep, tok_ref[k * rows : (k + 1) * rows, :].astype(F32), 0.0
            )
        gacc[...] = jnp.zeros_like(gacc)
        agw[...] = jnp.zeros_like(agw)
        dbuf[...] = jnp.zeros_like(dbuf)
        sm_ref[...] = jnp.zeros_like(sm_ref)
        gdep_ref[...] = jnp.zeros_like(gdep_ref)

    start = pl.multiple_of(b * rows, 16)
    here = pl.ds(pl.multiple_of(b * rows + 16, 16), rows)
    ht = hbuf[here, :].T.astype(BF)
    dk, dv, gco = dk_ref[...], dv_ref[...], gco_ref[...]
    gacc[here, :] += nt(dk, w_ref[0]) + nt(dv, w_ref[1]) + nt(gco, w_ref[2])
    agw[0] += nn(ht, dk)
    agw[1] += nn(ht, dv)
    agw[2] += nn(ht, gco)
    sm_ref[1:2, :] += col_sum(dv.astype(F32))
    sm_ref[2:3, :] += col_sum(gco.astype(F32))

    @pl.when(i < 2)
    def _():
        gq = (dq_ref[...].astype(F32).T + gqm_ref[...].astype(F32)).astype(BF)
        gpt = gpt_ref[...]
        sm_ref[0:1, :] += col_sum(gq.astype(F32))
        sm_ref[3:4, :] += col_sum(gpt.astype(F32))
        agw[3] += nn(ht, gq)
        agw[4] += nn(dep_ref[...].T, gpt)
        gacc[here, :] += nt(gq, w_ref[3]) + gpre_ref[...].astype(F32)
        gdep = nt(gpt, w_ref[4])
        wbuf[...] = hbuf[pl.ds(start, wide), :]
        dbuf[24 : 24 + rows, :] = gdep
        total = jnp.zeros((wide, D), F32)
        for j in range(KW):
            gdep_ref[j : j + 1, :] += col_sum(gdep * wbuf[12 + j : 12 + j + rows, :])
            total = total + dbuf[12 - j : 12 - j + wide, :] * wdep_ref[j : j + 1, :]
        gacc[pl.ds(start, wide), :] += total

    @pl.when(i == pl.num_programs(0) - 1)
    def _():
        keep = row_ids(0, LMAX) < n
        gh_ref[...] = jnp.where(keep, gacc[16 : 16 + LMAX, :], 0.0).astype(BF)
        gw_ref[...] = agw[...].astype(BF)


def final(info, tok, dk, dv, gco, dq, gqm, gpt, gpre, dep, w5, wdep):
    rows = 512
    seq = pl.BlockSpec((rows, HALF), lambda i, info: (lax.rem(info[1] * 2 + i, 4), 0))
    own = lambda w: pl.BlockSpec((rows, w), lambda i, info: (jnp.minimum(i, 1), 0))
    return pl.pallas_call(
        final_kernel,
        grid_spec=pltpu.PrefetchScalarGridSpec(
            num_scalar_prefetch=1,
            grid=(LMAX // rows,),
            in_specs=[
                whole((LMAX, D)),
                seq,
                seq,
                seq,
                pl.BlockSpec((HALF, rows), lambda i, info: (0, jnp.minimum(i, 1))),
                own(HALF),
                own(HALF),
                own(D),
                own(D),
                whole((5, D, HALF)),
                whole((16, D)),
            ],
            out_specs=[whole((LMAX, D)), whole((5, D, HALF)), whole((8, HALF)), whole((16, D))],
            scratch_shapes=[
                pltpu.VMEM((LMAX + 32, D), F32),
                pltpu.VMEM((LMAX + 32, D), F32),
                pltpu.VMEM((5, D, HALF), F32),
                pltpu.VMEM((rows + 32, D), F32),
                pltpu.VMEM((rows + 48, D), F32),
            ],
        ),
        out_shape=[
            jax.ShapeDtypeStruct((LMAX, D), BF),
            jax.ShapeDtypeStruct((5, D, HALF), BF),
            jax.ShapeDtypeStruct((8, HALF), F32),
            jax.ShapeDtypeStruct((16, D), F32),
        ],
        **params("final"),
    )(info, tok, dk, dv, gco, dq, gqm, gpt, gpre, dep, w5, wdep)


DIAG = [(0, 0), (1, 2), (2, 1), (3, 3)]
SWAP = [(0, 1), (1, 0)]


def to_sequence(x):
    return lax.ppermute(x, ("row", "col"), DIAG)


def constants():
    spread = np.zeros((72, KW * HALF), np.float32)
    ones8 = np.zeros((8, HALF), np.float32)
    ones24 = np.zeros((24, HALF), np.float32)
    for head in range(6):
        cols = slice(head * HD, (head + 1) * HD)
        ones8[head, cols] = 1
        ones24[head // 2 * 8 + head % 2, cols] = 1
        for j in range(KW):
            spread[j * 8 + head, j * HALF + head * HD : j * HALF + (head + 1) * HD] = 1
    return jnp.asarray(spread, BF), jnp.asarray(ones8, BF), jnp.asarray(ones24, BF)


def gather_four(x):
    return lax.all_gather(lax.all_gather(x, "row", axis=0), "col", axis=1)


def per_device(
    tokens, cotangent, seq_lengths, w_query, w_key, w_value, w_convout, w_point, w_depth,
    b_query, b_value, b_convout, b_point, w_kernel, b_kernel, w_dense, b_dense, gain_one, bias_one,
    w_inter, b_inter, w_output, b_output, gain_two, bias_two,
):
    r = lax.axis_index("row")
    c = lax.axis_index("col")
    info = jnp.stack([lax.dynamic_index_in_dim(seq_lengths, r, 0, False), c]).astype(jnp.int32)
    spread, ones8, ones24 = constants()

    tok = lax.all_gather(to_sequence(tokens), "col", axis=1, tiled=True)
    cot_cols = to_sequence(cotangent).reshape(2, ROWS, HALF)
    cot_mine = lax.dynamic_index_in_dim(cot_cols, c, 0, False)
    cot_there = lax.ppermute(lax.dynamic_index_in_dim(cot_cols, 1 - c, 0, False), "col", SWAP)
    cot = jnp.where(
        c == 0,
        jnp.concatenate([cot_mine, cot_there], axis=1),
        jnp.concatenate([cot_there, cot_mine], axis=1),
    )
    proj = gather_four(jnp.stack([w_key, w_value, w_convout, w_query, w_point]))
    w5 = proj.transpose(2, 0, 3, 1, 4).reshape(5, D, HALF)
    wd = gather_four(w_dense).reshape(2, 2, 2, 192, HALF).transpose(2, 1, 3, 0, 4).reshape(D, D)
    wi = gather_four(w_inter[0]).transpose(0, 2, 1, 3).reshape(2, HALF, GW)
    wo = gather_four(w_output[0]).reshape(2, GW, HALF)

    hx = lax.dynamic_slice_in_dim(jnp.pad(tok, ((16, 16), (0, 0))), c * ROWS, ROWS + 32, 0)
    wdep = jnp.pad(w_depth.astype(F32).T, ((0, 7), (0, 0)))
    vec3 = jnp.pad(jnp.stack([b_convout, b_query, b_point]).astype(F32), ((0, 5), (0, 0)))
    wk72 = jnp.pad(w_kernel.T.reshape(6, KW, HALF).transpose(1, 0, 2), ((0, 0), (0, 2), (0, 0))).reshape(72, HALF)
    bk72 = jnp.pad(b_kernel.astype(F32).reshape(6, KW).T, ((0, 0), (0, 2))).reshape(72, 1)
    bk72 = jnp.broadcast_to(bk72, (72, 128))
    vec6 = jnp.pad(
        jnp.stack([b_dense, gain_one, bias_one, b_output, gain_two, bias_two]).astype(F32), ((0, 2), (0, 0))
    )
    bi = b_inter.astype(F32).reshape(1, FF)

    kd, kt, vz = keys_values(info, tok, w5[0:2], b_value.astype(F32).reshape(1, HALF))
    q, qs, pt, kp, conv, mix, dep = own_rows(info, hx, w5[2:5], wdep, vec3, wk72, bk72, spread)
    ctx, lse = attend(info, qs, kd, vz)
    hid, gpre, gctx, gcv, delta, gwd, gwi, gwo, sm_ffn, gbi = ffn(
        info, ctx, mix, tok, cot, wd, wi, wo, vec6, bi, ones24
    )
    hid3 = hid.reshape(ROWS, 2, HALF)
    hid_mine = lax.dynamic_index_in_dim(hid3, c, 1, False)
    hid_there = lax.ppermute(lax.dynamic_index_in_dim(hid3, 1 - c, 1, False), "col", SWAP)
    hid_cols = jnp.where(
        c == 0,
        jnp.concatenate([hid_mine, hid_there], axis=0),
        jnp.concatenate([hid_there, hid_mine], axis=0),
    )
    hidden_out = to_sequence(hid_cols)

    def reduce_blocks(x):
        x = lax.psum_scatter(x, "col", scatter_dimension=1, tiled=True)
        x = lax.psum_scatter(x, "row", scatter_dimension=0, tiled=True)
        return lax.psum(x, "dp").astype(F32)[0, 0]

    g_out = reduce_blocks(gwo.reshape(2, 2, D, HALF))
    g_inter = reduce_blocks(gwi.reshape(2, HALF, 2, D).transpose(0, 2, 1, 3))
    g_dense = reduce_blocks(gwd.reshape(2, 2, 192, 2, HALF).transpose(3, 1, 0, 2, 4).reshape(2, 2, HALF, HALF))

    gqm, gpt, gco, gwk, gbk = conv_back(info, gcv, conv, kp, q, pt, wk72, spread, ones8)
    dq, dk, dv = attend_back(info, qs, gctx, kd, vz, kt, lse, delta)
    gh, gw5, sm_fin, gdep = final(info, tok, dk, dv, gco, dq, gqm, gpt, gpre, dep, w5, wdep)

    gh3 = gh.reshape(LMAX, 2, HALF)
    gh_mine = lax.dynamic_index_in_dim(gh3, c, 1, False)
    gh_there = lax.ppermute(lax.dynamic_index_in_dim(gh3, 1 - c, 1, False), "col", SWAP)
    grad_tokens = to_sequence((gh_mine.astype(F32) + gh_there.astype(F32)).astype(BF)).astype(F32)

    g5 = reduce_blocks(gw5.reshape(5, 2, HALF, 2, 192).transpose(1, 3, 0, 2, 4).reshape(2, 2, 5 * HALF, 192))
    g5 = g5.reshape(5, HALF, 192)
    parts = [sm_ffn[0:6].reshape(-1), gbi.reshape(-1), sm_fin[0:4].reshape(-1), gdep[0:KW].reshape(-1), gwk.reshape(-1), gbk[:, 0]]
    flat = lax.psum(jnp.concatenate(parts), ("dp", "row", "col"))
    sizes = [6 * D, FF, 4 * HALF, KW * D, 72 * HALF, 72]
    cuts = np.cumsum([0] + sizes)
    sf, si, sp, sd, sk, sb = [flat[cuts[k] : cuts[k + 1]] for k in range(6)]
    sf = sf.reshape(6, D)
    sp = sp.reshape(4, HALF)
    g_wk = sk.reshape(KW, 8, HALF)[:, :6].transpose(2, 1, 0).reshape(HALF, 54)
    g_bk = sb.reshape(KW, 8)[:, :6].T.reshape(54)
    return (
        hidden_out,
        grad_tokens,
        g5[3],
        g5[0],
        g5[1],
        g5[2],
        g5[4],
        sd.reshape(KW, D).T,
        sp[0],
        sp[1],
        sp[2],
        sp[3],
        g_wk,
        g_bk,
        g_dense,
        sf[3],
        sf[4],
        sf[5],
        g_inter[None],
        si,
        g_out[None],
        sf[0],
        sf[1],
        sf[2],
    )


def solution(mesh):
    act = P(("dp", "col"), "row")
    rep = P()
    proj = P("row", "col")
    in_specs = (
        act, act, P("dp"), proj, proj, proj, proj, proj, rep, rep, rep, rep, rep, rep, rep, P("col", "row"),
        rep, rep, rep, P("row", None, "col"), rep, P("row", "col", None), rep, rep, rep,
    )
    out_specs = (
        act, act, proj, proj, proj, proj, proj, rep, rep, rep, rep, rep, rep, rep, P("col", "row"),
        rep, rep, rep, P("row", None, "col"), rep, P("row", "col", None), rep, rep, rep,
    )
    return jax.shard_map(per_device, mesh=mesh, in_specs=in_specs, out_specs=out_specs, check_vma=False)
```

```python
import functools

import jax
import jax.numpy as jnp
import numpy as np
from jax import lax
from jax.experimental import pallas as pl
from jax.experimental.pallas import tpu as pltpu
from jax.sharding import PartitionSpec as P

D = 768
HALF = 384
HD = 64
KW = 9
FF = 3072
GW = 1536
LMAX = 2048
ROWS = 1024
EPS = 1e-12
LOG2E = 1.4426950408889634
LN2 = 0.6931471805599453
BF = jnp.bfloat16
F32 = jnp.float32
VMEM_BYTES = 63 * 1024 * 1024
PAD = 16
FFN_ROWS = 1920
PROJ_ROWS = 1024
MESH = pl.DeviceIdType.MESH
HBM = pl.BlockSpec(memory_space=pl.ANY)
VMEM = pl.BlockSpec(memory_space=pltpu.VMEM)


def nn(a, b):
    return lax.dot_general(a, b, (((1,), (0,)), ((), ())), preferred_element_type=F32)


def nt(a, b):
    return lax.dot_general(a, b, (((1,), (1,)), ((), ())), preferred_element_type=F32)


def col_sum(x):
    return jnp.sum(x, axis=0, keepdims=True)


def row_ids(start, rows):
    return start + lax.broadcasted_iota(jnp.int32, (rows, 1), 0)


def whole(shape):
    return pl.BlockSpec(shape, lambda i, info: (0,) * len(shape))


def params(name):
    return dict(
        name=name,
        compiler_params=pltpu.CompilerParams(vmem_limit_bytes=VMEM_BYTES),
    )


def lanes(k, width=HALF):
    return pl.ds(pl.multiple_of(k * width, 128), width)


def rows_at(start, count, step=16):
    return pl.ds(pl.multiple_of(start, step), count)


def send(src, dst, send_sem, recv_sem, device):
    return pltpu.make_async_remote_copy(
        src_ref=src, dst_ref=dst, send_sem=send_sem, recv_sem=recv_sem, device_id=device, device_id_type=MESH
    )


class Place:
    def __init__(self):
        self.d = lax.axis_index("dp")
        self.r = lax.axis_index("row")
        self.c = lax.axis_index("col")
        self.k = lax.rem(self.d, 8)
        self.base = self.d - self.k
        self.y = lax.rem(self.k, 2)
        self.z = lax.div(self.k, 2)
        self.across = {"row": 1 - self.r}
        self.core = {"col": 1 - self.c}
        self.diagonal = {"row": 1 - self.r, "col": 1 - self.c}

    def eight(self, offset):
        other = lax.rem(self.k + offset, 8)
        return other, {"dp": self.base + other}

    def four(self, offset):
        other = lax.rem(self.z + offset, 4)
        return other, {"dp": self.base + other * 2 + self.y}


def meet(devices):
    barrier = pltpu.get_barrier_semaphore()
    for device in devices:
        pl.semaphore_signal(barrier, inc=1, device_id=device, device_id_type=MESH)
    pl.semaphore_wait(barrier, len(devices))


def comm_params(name, number):
    return dict(
        name=name,
        compiler_params=pltpu.CompilerParams(
            vmem_limit_bytes=VMEM_BYTES, collective_id=number, has_side_effects=True
        ),
    )


class Gather:
    def __init__(self, place, own, full, part, block, send_sem, recv_sem, first):
        self.p, self.own, self.full, self.part, self.block = place, own, full, part, block
        self.s, self.v, self.f = send_sem, recv_sem, first

    def _move(self, src, dst, n, device):
        return send(src, dst, self.s.at[self.f + n], self.v.at[self.f + n], device)

    def _cross(self, r):
        p = self.p
        return self._move(self.part(self.own, p.z), self.block(self.full, r, p.c, p.z), 0, p.across)

    def _near(self, c):
        p = self.p
        return self._move(self.block(self.full, p.r, c, None), self.block(self.full, p.r, c, None), 1, p.core)

    def _pass(self, offset, z):
        p = self.p
        _, device = p.four(offset)
        here = self.block(self.full, 1 - p.r, p.c, z)
        return self._move(here, here, 1 + offset, device)

    def _last(self, c):
        p = self.p
        here = self.block(self.full, 1 - p.r, c, None)
        return self._move(here, here, 5, p.core)

    def relay(self):
        p = self.p
        self._cross(1 - p.r).wait_recv()
        for offset in (1, 2, 3):
            self._pass(offset, p.z).start()

    def share(self):
        p = self.p
        for offset in (1, 2, 3):
            back = lax.rem(p.z + 4 - offset, 4)
            self._pass(offset, back).wait_recv()
        self._last(p.c).start()

    def finish(self):
        p = self.p
        self._last(1 - p.c).wait_recv()
        self._near(1 - p.c).wait_recv()
        self._cross(p.r).wait_send()
        self._near(p.c).wait_send()
        for offset in (1, 2, 3):
            self._pass(offset, p.z).wait_send()
        self._last(p.c).wait_send()


def proj_part(ref, z):
    return ref.at[:, rows_at(z * 48, 48), :]


def proj_block(ref, r, c, z):
    if z is None:
        return ref.at[:, rows_at(c * 192, 192), lanes(r)]
    return ref.at[:, rows_at(c * 192 + z * 48, 48), lanes(r)]


def inter_part(ref, z):
    return ref.at[rows_at(z * 96, 96), :]


def inter_block(ref, r, c, z):
    if z is None:
        return ref.at[r, :, lanes(c, 768)]
    return ref.at[r, rows_at(z * 96, 96), lanes(c, 768)]


def output_part(ref, z):
    return ref.at[rows_at(z * 192, 192), :]


def output_block(ref, r, c, z):
    if z is None:
        return ref.at[r, rows_at(c * 768, 768), :]
    return ref.at[r, rows_at(c * 768 + z * 192, 192), :]


def dense_part(ref, z):
    return ref.at[lax.div(z, 2), rows_at(lax.rem(z, 2) * 96, 96), :]


def dense_block(ref, r, c, z):
    if z is None:
        return ref.at[:, rows_at(c * 192, 192), lanes(r)]
    return ref.at[lax.div(z, 2), rows_at(c * 192 + lax.rem(z, 2) * 96, 96), lanes(r)]


def start_kernel(tok_ref, wk_ref, wv_ref, wc_ref, wq_ref, wp_ref, seq_ref, w5_ref, own, stage, lsem, ts, tr, gs, gr):
    p = Place()
    r, c = p.r, p.c
    for j, ref in enumerate((wk_ref, wv_ref, wc_ref, wq_ref, wp_ref)):
        own[j] = ref[...].astype(F32).T.astype(BF)
    keep = pltpu.make_async_copy(own, proj_block(w5_ref, r, c, None), lsem.at[0])
    keep.start()
    load = pltpu.make_async_copy(tok_ref, stage, lsem.at[1])
    store = pltpu.make_async_copy(stage, seq_ref.at[PAD : PAD + LMAX, lanes(r)], lsem.at[2])
    load.start()
    meet([p.across, p.core, p.diagonal] + [p.four(o)[1] for o in (1, 2, 3)])
    gather = Gather(p, own, w5_ref, proj_part, proj_block, gs, gr, 0)

    def chunk(m, k):
        return seq_ref.at[PAD + m * 512 : PAD + (m + 1) * 512, lanes(k)]

    def cross(m, k):
        return send(tok_ref.at[m * 512 : (m + 1) * 512, :], chunk(m, k), ts.at[m], tr.at[m], {"row": 1 - r, "col": m // 2})

    def near(k):
        return send(tok_ref, seq_ref.at[PAD : PAD + LMAX, lanes(k)], ts.at[4], tr.at[4], p.core)

    def forward(m):
        return send(chunk(m, 1 - r), chunk(m, 1 - r), ts.at[5 + m], tr.at[5 + m], p.core)

    gather._cross(r).start()

    @pl.when(r != c)
    def _():
        for m in (0, 2, 1, 3):
            cross(m, r).start()

    load.wait()

    @pl.when(r == c)
    def _():
        near(r).start()
        store.start()

    keep.wait()
    gather._near(c).start()
    gather.relay()
    for q in range(2):

        @pl.when(c == q)
        def _():
            for m in (2 * q, 2 * q + 1):
                cross(m, 1 - r).wait_recv()
                forward(m).start()

    gather.share()
    for q in range(2):

        @pl.when(c == q)
        def _():
            for m in (2 - 2 * q, 3 - 2 * q):
                forward(m).wait_recv()
            for m in (2 * q, 2 * q + 1):
                forward(m).wait_send()

    @pl.when(r != c)
    def _():
        for m in range(4):
            cross(m, r).wait_send()
        near(r).wait_recv()

    @pl.when(r == c)
    def _():
        near(r).wait_send()
        store.wait()

    gather.finish()


def start(tokens, weights):
    return pl.pallas_call(
        start_kernel,
        in_specs=[HBM] + [VMEM] * 5,
        out_specs=[HBM, HBM],
        out_shape=[jax.ShapeDtypeStruct((LMAX + 2 * PAD, D), BF), jax.ShapeDtypeStruct((5, HALF, D), BF)],
        scratch_shapes=[
            pltpu.VMEM((5, 192, HALF), BF),
            pltpu.VMEM((LMAX, HALF), BF),
            pltpu.SemaphoreType.DMA((3,)),
            pltpu.SemaphoreType.DMA((9,)),
            pltpu.SemaphoreType.DMA((9,)),
            pltpu.SemaphoreType.DMA((6,)),
            pltpu.SemaphoreType.DMA((6,)),
        ],
        **comm_params("start", 1),
    )(tokens, *weights)


class ToRows:
    def __init__(self, place, src, dst, local_sem, send_sem, recv_sem):
        self.p, self.src, self.dst = place, src, dst
        self.l, self.s, self.v = local_sem, send_sem, recv_sem

    def _cross(self, q, k):
        half = self.src.at[q * ROWS : (q + 1) * ROWS, :]
        return send(half, self.dst.at[:, lanes(k)], self.s.at[q], self.v.at[0], {"row": 1 - self.p.r, "col": q})

    def _near(self):
        p = self.p
        half = self.src.at[rows_at((1 - p.c) * ROWS, ROWS), :]
        return send(half, self.dst.at[:, lanes(p.r)], self.s.at[2], self.v.at[1], p.core)

    def _local(self):
        p = self.p
        half = self.src.at[rows_at(p.c * ROWS, ROWS), :]
        return pltpu.make_async_copy(half, self.dst.at[:, lanes(p.r)], self.l)

    def start(self):
        p = self.p

        @pl.when(p.r != p.c)
        def _():
            self._cross(0, p.r).start()
            self._cross(1, p.r).start()

        @pl.when(p.r == p.c)
        def _():
            self._near().start()
            self._local().start()

    def finish(self):
        p = self.p
        self._cross(0, 1 - p.r).wait_recv()

        @pl.when(p.r != p.c)
        def _():
            self._cross(0, p.r).wait_send()
            self._cross(1, p.r).wait_send()
            self._near().wait_recv()

        @pl.when(p.r == p.c)
        def _():
            self._near().wait_send()
            self._local().wait()


class FromRows:
    def __init__(self, place, src, dst, local_sem, send_sem, recv_sem):
        self.p, self.src, self.dst = place, src, dst
        self.l, self.s, self.v = local_sem, send_sem, recv_sem

    def _cross(self, q):
        p = self.p
        place = self.dst.at[rows_at(q * ROWS, ROWS), :]
        return send(self.src.at[:, lanes(1 - p.r)], place, self.s.at[0], self.v.at[q], {"row": 1 - p.r, "col": p.r})

    def _near(self, q):
        p = self.p
        place = self.dst.at[rows_at(q * ROWS, ROWS), :]
        return send(self.src.at[:, lanes(p.r)], place, self.s.at[1], self.v.at[2], p.core)

    def _local(self):
        p = self.p
        place = self.dst.at[rows_at(p.c * ROWS, ROWS), :]
        return pltpu.make_async_copy(self.src.at[:, lanes(p.r)], place, self.l)

    def start(self):
        p = self.p
        self._cross(p.c).start()

        @pl.when(p.r != p.c)
        def _():
            self._near(p.c).start()

        @pl.when(p.r == p.c)
        def _():
            self._local().start()

    def finish(self):
        p = self.p
        self._cross(p.c).wait_send()

        @pl.when(p.r != p.c)
        def _():
            self._near(p.c).wait_send()
            self._cross(0).wait_recv()
            self._cross(1).wait_recv()

        @pl.when(p.r == p.c)
        def _():
            self._near(1 - p.c).wait_recv()
            self._local().wait()


def middle_kernel(wi_own, wo_own, wd_own, cot_ref, wi_ref, wo_ref, wd_ref, rows_ref, lsem, gs, gr, cs, cr):
    p = Place()
    r, c = p.r, p.c
    keeps = [
        pltpu.make_async_copy(wi_own, inter_block(wi_ref, r, c, None), lsem.at[0]),
        pltpu.make_async_copy(wo_own, output_block(wo_ref, r, c, None), lsem.at[1]),
        pltpu.make_async_copy(wd_own, dense_block(wd_ref, r, c, None), lsem.at[2]),
    ]
    for keep in keeps:
        keep.start()
    meet([p.across, p.core, p.diagonal] + [p.four(o)[1] for o in (1, 2, 3)])
    gathers = [
        Gather(p, wi_own, wi_ref, inter_part, inter_block, gs, gr, 0),
        Gather(p, wo_own, wo_ref, output_part, output_block, gs, gr, 6),
        Gather(p, wd_own, wd_ref, dense_part, dense_block, gs, gr, 12),
    ]
    for gather in gathers:
        gather._cross(r).start()
    rows = ToRows(p, cot_ref, rows_ref, lsem.at[3], cs, cr)
    rows.start()
    for keep, gather in zip(keeps, gathers):
        keep.wait()
        gather._near(c).start()
    for gather in gathers:
        gather.relay()
    for gather in gathers:
        gather.share()
    rows.finish()
    for gather in gathers:
        gather.finish()


def middle(w_inter, w_output, w_dense, cotangent):
    return pl.pallas_call(
        middle_kernel,
        in_specs=[VMEM, VMEM, VMEM, VMEM],
        out_specs=[HBM] * 4,
        out_shape=[
            jax.ShapeDtypeStruct((2, HALF, GW), BF),
            jax.ShapeDtypeStruct((2, GW, HALF), BF),
            jax.ShapeDtypeStruct((2, HALF, D), BF),
            jax.ShapeDtypeStruct((ROWS, D), BF),
        ],
        scratch_shapes=[
            pltpu.SemaphoreType.DMA((4,)),
            pltpu.SemaphoreType.DMA((18,)),
            pltpu.SemaphoreType.DMA((18,)),
            pltpu.SemaphoreType.DMA((3,)),
            pltpu.SemaphoreType.DMA((2,)),
        ],
        **comm_params("middle", 2),
    )(w_inter, w_output, w_dense, cotangent)


class Reduce:
    def __init__(self, place, pay, near, far, eighth, total, chunks, s, v):
        self.p, self.pay, self.near, self.far, self.eighth, self.total = place, pay, near, far, eighth, total
        self.chunks, self.s, self.v = chunks, s, v
        self.rows = total.shape[0] // chunks
        self.piece = self.rows // 8
        self.stride = 18

    def _slice(self, ch):
        return slice(ch * self.rows, (ch + 1) * self.rows)

    def _near(self, rr, n, ch):
        p = self.p
        part = self._slice(ch)
        i = ch * self.stride + n
        return send(self.pay.at[rr, 1 - p.c, part, :], self.near.at[rr, part, :], self.s.at[i], self.v.at[i], p.core)

    def _far(self, ch):
        p = self.p
        part = self._slice(ch)
        i = ch * self.stride + 2
        return send(self.near.at[1 - p.r, part, :], self.far.at[part, :], self.s.at[i], self.v.at[i], p.across)

    def _scatter(self, ch, offset):
        other, device = self.p.eight(offset)
        i = ch * self.stride + 2 + offset
        src = self.far.at[rows_at(ch * self.rows + other * self.piece, self.piece), :]
        return send(src, self.eighth.at[ch, offset], self.s.at[i], self.v.at[i], device)

    def _spread(self, ch, offset, k):
        _, device = self.p.eight(offset)
        i = ch * self.stride + 9 + offset
        here = self.total.at[rows_at(ch * self.rows + k * self.piece, self.piece), :]
        return send(here, here, self.s.at[i], self.v.at[i], device)

    def start(self):
        for n in range(2):
            for ch in range(self.chunks):
                self._near(1 - self.p.r if n == 0 else self.p.r, n, ch).start()

    def cross(self, ch):
        p = self.p
        part = self._slice(ch)
        self._near(1 - p.r, 0, ch).wait_recv()
        both = self.near[1 - p.r, part, :].astype(F32) + self.pay[1 - p.r, p.c, part, :].astype(F32)
        self.near[1 - p.r, part, :] = both.astype(BF)
        self._far(ch).start()

    def scatter(self, ch):
        p = self.p
        part = self._slice(ch)
        self._near(p.r, 1, ch).wait_recv()
        self._far(ch).wait_recv()
        both = self.near[p.r, part, :].astype(F32) + self.pay[p.r, p.c, part, :].astype(F32)
        self.far[part, :] = (both + self.far[part, :].astype(F32)).astype(BF)
        for offset in range(1, 8):
            self._scatter(ch, offset).start()

    def spread(self, ch):
        p = self.p
        mine = rows_at(ch * self.rows + p.k * self.piece, self.piece)
        both = self.far[mine, :].astype(F32)
        for offset in range(1, 8):
            self._scatter(ch, offset).wait_recv()
            both = both + self.eighth[ch, offset].astype(F32)
        self.total[mine, :] = both.astype(BF)
        for offset in range(1, 8):
            self._spread(ch, offset, p.k).start()

    def finish(self, ch):
        p = self.p
        for offset in range(1, 8):
            self._spread(ch, offset, lax.rem(p.k + 8 - offset, 8)).wait_recv()
        self._near(1 - p.r, 0, ch).wait_send()
        self._near(p.r, 1, ch).wait_send()
        self._far(ch).wait_send()
        for offset in range(1, 8):
            self._scatter(ch, offset).wait_send()
            self._spread(ch, offset, p.k).wait_send()

    @staticmethod
    def scratch(rows, chunks):
        return [
            pltpu.VMEM((2, rows, HALF), BF),
            pltpu.VMEM((rows, HALF), BF),
            pltpu.VMEM((chunks, 8, rows // chunks // 8, HALF), BF),
            pltpu.VMEM((rows, HALF), BF),
            pltpu.SemaphoreType.DMA((18 * chunks,)),
            pltpu.SemaphoreType.DMA((18 * chunks,)),
        ]


def ffn_sum_kernel(pay, hid_ref, gi_ref, go_ref, gd_ref, out_ref, near, far, eighth, total, s, v, ls, hs, hr):
    p = Place()
    meet([p.across, p.core, p.diagonal] + [p.eight(o)[1] for o in range(1, 8)])
    red = Reduce(p, pay, near, far, eighth, total, 3, s, v)
    back = FromRows(p, hid_ref, out_ref, ls, hs, hr)
    red.start()
    for ch in range(3):
        red.cross(ch)
    back.start()
    for ch in range(3):
        red.scatter(ch)
    for ch in range(3):
        red.spread(ch)
    for ch in range(3):
        red.finish(ch)
    back.finish()
    gi_ref[:, 0:HALF] = total[0:HALF, :].astype(F32)
    gi_ref[:, HALF:D] = total[HALF:D, :].astype(F32)
    go_ref[...] = total[D : 2 * D, :].astype(F32)
    gd_ref[...] = total[2 * D :, :].astype(F32)


def ffn_sum(pay, hid):
    return pl.pallas_call(
        ffn_sum_kernel,
        in_specs=[VMEM, VMEM],
        out_specs=[VMEM, VMEM, VMEM, HBM],
        out_shape=[
            jax.ShapeDtypeStruct((HALF, D), F32),
            jax.ShapeDtypeStruct((D, HALF), F32),
            jax.ShapeDtypeStruct((HALF, HALF), F32),
            jax.ShapeDtypeStruct((LMAX, HALF), BF),
        ],
        scratch_shapes=Reduce.scratch(FFN_ROWS, 3)
        + [pltpu.SemaphoreType.DMA, pltpu.SemaphoreType.DMA((2,)), pltpu.SemaphoreType.DMA((3,))],
        **comm_params("ffn_sum", 3),
    )(pay, hid)


def end_kernel(
    pay, gh_ref, perm_ref,
    gt_ref, gk_ref, gv_ref, gc_ref, gq_ref, gp_ref, gdep_ref, gbq_ref, gbv_ref, gbc_ref, gbp_ref, gwk_ref, gbk_ref,
    gbd_ref, gg1_ref, gb1_ref, gbi_ref, gbo_ref, gg2_ref, gb2_ref,
    near, far, eighth, total, s, v, small, ghn, gho, ght, es, er, ls, hs, hr,
):
    p = Place()
    r, c = p.r, p.c
    meet([p.across, p.core, p.diagonal] + [p.eight(o)[1] for o in range(1, 8)])
    red = Reduce(p, pay, near, far, eighth, total, 2, s, v)
    red.start()
    theirs = gh_ref.at[rows_at((1 - c) * ROWS, ROWS), :]
    part = send(theirs, ghn, es.at[0], er.at[0], p.core)
    part.start()
    back = FromRows(p, gho, ght, ls, hs, hr)
    for ch in range(2):
        red.cross(ch)
    part.wait_recv()
    gho[...] = (gh_ref[rows_at(c * ROWS, ROWS), :].astype(F32) + ghn[...].astype(F32)).astype(BF)
    back.start()
    for ch in range(2):
        red.scatter(ch)
    for ch in range(2):
        red.spread(ch)
    for ch in range(2):
        red.finish(ch)
    own = total.at[960:PROJ_ROWS, :]
    mine = small.at[r * 2 + c]
    moves = []
    for n, device in enumerate((p.across, p.core, p.diagonal)):
        moves.append(send(own, mine, es.at[1 + n], er.at[1 + n], device))
    for move in moves:
        move.start()
    small[r * 2 + c] = total[960:PROJ_ROWS, :]
    for j, ref in enumerate((gk_ref, gv_ref, gc_ref, gq_ref, gp_ref)):
        ref[...] = total[j * 192 : (j + 1) * 192, :].astype(F32).T
    for n, (rr, cc) in enumerate(((1 - r, c), (r, 1 - c), (1 - r, 1 - c))):
        send(own, small.at[rr * 2 + cc], es.at[1 + n], er.at[1 + n], p.core).wait_recv()
    head = small[0]
    tail = small[1].astype(F32)
    norms = small[2].astype(F32)
    depth = small[3].astype(F32)
    kernel_grad = jnp.concatenate([head, small[1][0:8]], axis=0)
    gwk_ref[...] = nn(kernel_grad.astype(F32).T.astype(BF), perm_ref[...])
    gbk_ref[...] = nn(small[1][16:24, 0:128], perm_full(perm_ref))[0:1, :]
    for k, ref in enumerate((gbq_ref, gbv_ref, gbc_ref, gbp_ref)):
        ref[...] = tail[8 + k : 9 + k, :]
    for k, ref in enumerate((gbo_ref, gg2_ref, gb2_ref, gbd_ref, gg1_ref, gb1_ref)):
        ref[:, 0:HALF] = norms[k : k + 1, :]
        ref[:, HALF:D] = norms[8 + k : 9 + k, :]
    for k in range(8):
        gbi_ref[:, k * HALF : (k + 1) * HALF] = norms[16 + k : 17 + k, :]
    gdep_ref[0:HALF, :] = depth[0:16, :].T[:, 0:KW]
    gdep_ref[HALF:D, :] = depth[16:32, :].T[:, 0:KW]
    for move in moves:
        move.wait_send()
    part.wait_send()
    back.finish()
    gt_ref[...] = ght[...].astype(F32)


def perm_full(perm_ref):
    return jnp.concatenate([perm_ref[...], jnp.zeros((56, 54), BF)], axis=0)


def end(pay, gh, perm):
    line = lambda n: jax.ShapeDtypeStruct((1, n), F32)
    block = jax.ShapeDtypeStruct((HALF, 192), F32)
    shapes = [jax.ShapeDtypeStruct((LMAX, HALF), F32)] + [block] * 5
    shapes += [jax.ShapeDtypeStruct((D, KW), F32)] + [line(HALF)] * 4
    shapes += [jax.ShapeDtypeStruct((HALF, 54), F32), line(54)]
    shapes += [line(D)] * 3 + [line(FF)] + [line(D)] * 3
    return pl.pallas_call(
        end_kernel,
        in_specs=[VMEM, VMEM, VMEM],
        out_specs=[VMEM] * len(shapes),
        out_shape=shapes,
        scratch_shapes=Reduce.scratch(PROJ_ROWS, 2)
        + [
            pltpu.VMEM((4, 64, HALF), BF),
            pltpu.VMEM((ROWS, D), BF),
            pltpu.VMEM((ROWS, D), BF),
            pltpu.VMEM((LMAX, HALF), BF),
            pltpu.SemaphoreType.DMA((4,)),
            pltpu.SemaphoreType.DMA((4,)),
            pltpu.SemaphoreType.DMA,
            pltpu.SemaphoreType.DMA((2,)),
            pltpu.SemaphoreType.DMA((3,)),
        ],
        **comm_params("end", 4),
    )(pay, gh, perm)


def kv_kernel(info, seq_ref, w_ref, bv_ref, kd_ref, kt_ref, vz_ref, first_key):
    i = pl.program_id(0)
    rows = kd_ref.shape[0]
    keep = row_ids(i * rows, rows) < info[0]
    tok = seq_ref[rows_at(PAD + i * rows, rows), :]
    h = jnp.where(keep, tok.astype(F32), 0.0).astype(BF)
    k = nt(h, w_ref[0])
    v = nt(h, w_ref[1]) + bv_ref[...]

    @pl.when(i == 0)
    def _():
        first_key[...] = k[0:8]

    kd_ref[...] = jnp.where(keep, k, first_key[0:1]).astype(BF)
    kt_ref[...] = k.T.astype(BF)
    vz_ref[...] = jnp.where(keep, v, 0.0).astype(BF)


def keys_values(info, seq, w5, b_value):
    rows = 512
    return pl.pallas_call(
        kv_kernel,
        grid_spec=pltpu.PrefetchScalarGridSpec(
            num_scalar_prefetch=1,
            grid=(LMAX // rows,),
            in_specs=[whole((LMAX + 2 * PAD, D)), whole((2, HALF, D)), whole((1, HALF))],
            out_specs=[
                pl.BlockSpec((rows, HALF), lambda i, info: (i, 0)),
                pl.BlockSpec((HALF, rows), lambda i, info: (0, i)),
                pl.BlockSpec((rows, HALF), lambda i, info: (i, 0)),
            ],
            scratch_shapes=[pltpu.VMEM((8, HALF), F32)],
        ),
        out_shape=[
            jax.ShapeDtypeStruct((LMAX, HALF), BF),
            jax.ShapeDtypeStruct((HALF, LMAX), BF),
            jax.ShapeDtypeStruct((LMAX, HALF), BF),
        ],
        **params("keys_values"),
    )(info, seq, w5, b_value)


def own_kernel(
    info, seq_ref, w_ref, wdep_ref, vec_ref, wk_ref, bk_ref, spread_ref,
    q_ref, qs_ref, pt_ref, kp_ref, conv_ref, mix_ref, dep_ref, h_ref, hbuf, cbuf,
):
    i = pl.program_id(0)
    rows = q_ref.shape[0]
    wide = rows + 32
    base = pl.multiple_of(i * rows, 16)
    start = pl.multiple_of(info[1] * ROWS + i * rows, 16)
    ids = row_ids(start - 16, wide)
    keep = (ids >= 0) & (ids < info[0])
    hw = jnp.where(keep, seq_ref[pl.ds(start, wide), :].astype(F32), 0.0)
    hbuf[...] = hw
    depth = jnp.zeros((rows, D), F32)
    for j in range(KW):
        depth = depth + hbuf[12 + j : 12 + j + rows, :] * wdep_ref[j : j + 1, :]
    depth_low = depth.astype(BF)
    dep_ref[...] = depth_low
    hl = hw.astype(BF)
    h_ref[...] = hl[16 : 16 + rows]
    conv = jnp.where(keep, nt(hl, w_ref[2]) + vec_ref[0:1, :], 0.0)
    cbuf[...] = conv
    conv_ref[pl.ds(base, wide), :] = conv.astype(BF)
    q = nt(hl[16 : 16 + rows], w_ref[3]) + vec_ref[1:2, :]
    q_low = q.astype(BF)
    q_ref[...] = q_low
    qs_ref[...] = (q * (0.125 * LOG2E)).astype(BF)
    pt = nt(depth_low, w_ref[4]) + vec_ref[2:3, :]
    pt_ref[...] = pt.astype(BF)
    mixer = (pt * q_low.astype(F32)).astype(BF)
    logits = (nt(wk_ref[...], mixer) + bk_ref[:, 0:1]).reshape(KW, 8, rows)
    peak = jnp.max(logits, axis=0, keepdims=True)
    raised = jnp.exp(logits - peak)
    kp = (raised / jnp.sum(raised, axis=0, keepdims=True)).reshape(KW * 8, rows)
    kp_ref[...] = kp
    kpt = kp.T.astype(BF)
    mix = jnp.zeros((rows, HALF), F32)
    for j in range(KW):
        mix = mix + nn(kpt, spread_ref[:, j * HALF : (j + 1) * HALF]) * cbuf[12 + j : 12 + j + rows, :]
    mix_ref[...] = mix.astype(BF)


def own_rows(info, seq, w5, wdep, vec, wk72, bk72, spread):
    rows = 256
    blk = pl.BlockSpec((rows, HALF), lambda i, info: (i, 0))
    full = pl.BlockSpec((rows, D), lambda i, info: (i, 0))
    half = jax.ShapeDtypeStruct((ROWS, HALF), BF)
    return pl.pallas_call(
        own_kernel,
        grid_spec=pltpu.PrefetchScalarGridSpec(
            num_scalar_prefetch=1,
            grid=(ROWS // rows,),
            in_specs=[
                whole((LMAX + 2 * PAD, D)),
                whole((5, HALF, D)),
                whole((16, D)),
                whole((8, HALF)),
                whole((72, HALF)),
                whole((72, 128)),
                whole((72, KW * HALF)),
            ],
            out_specs=[
                blk,
                blk,
                blk,
                pl.BlockSpec((72, rows), lambda i, info: (0, i)),
                whole((ROWS + 32, HALF)),
                blk,
                full,
                full,
            ],
            scratch_shapes=[pltpu.VMEM((rows + 32, D), F32), pltpu.VMEM((rows + 32, HALF), F32)],
        ),
        out_shape=[
            half,
            half,
            half,
            jax.ShapeDtypeStruct((72, ROWS), F32),
            jax.ShapeDtypeStruct((ROWS + 32, HALF), BF),
            half,
            jax.ShapeDtypeStruct((ROWS, D), BF),
            jax.ShapeDtypeStruct((ROWS, D), BF),
        ],
        **params("own_rows"),
    )(info, seq, w5, wdep, vec, wk72, bk72, spread)


def attend_kernel(info, q_ref, k_ref, v_ref, ctx_ref, lse_ref):
    k = k_ref[...]
    ones = jnp.where(row_ids(0, LMAX) < info[0], 1.0, 0.0)
    ve = jnp.concatenate([v_ref[...], jnp.broadcast_to(ones, (LMAX, 128)).astype(BF)], axis=1)
    rows = 256
    lane = lax.broadcasted_iota(jnp.int32, (rows, 128), 1)
    for u in range(ROWS // rows):
        part = slice(u * rows, (u + 1) * rows)
        outs = []
        for hh in range(2):
            q = jnp.where((lane < HD) == (hh == 0), q_ref[part, :], jnp.zeros((), BF))
            s = nt(q, k)
            peak = jnp.max(s, axis=1, keepdims=True)
            p = jnp.exp2(s - peak).astype(BF)
            o = nn(p, ve)
            outs.append(o[:, :128] / o[:, 128:])
            lse_ref[0, hh : hh + 1, part] = (peak + jnp.log2(o[:, 128:129])).T
        ctx_ref[part, :] = jnp.where(lane < HD, outs[0], outs[1]).astype(BF)


def attend(info, qs, kd, vz):
    pair = lambda rows: pl.BlockSpec((rows, 128), lambda p, info: (0, p))
    return pl.pallas_call(
        attend_kernel,
        grid_spec=pltpu.PrefetchScalarGridSpec(
            num_scalar_prefetch=1,
            grid=(3,),
            in_specs=[pair(ROWS), pair(LMAX), pair(LMAX)],
            out_specs=[pair(ROWS), pl.BlockSpec((1, 8, ROWS), lambda p, info: (p, 0, 0))],
        ),
        out_shape=[
            jax.ShapeDtypeStruct((ROWS, HALF), BF),
            jax.ShapeDtypeStruct((3, 8, ROWS), F32),
        ],
        **params("attend"),
    )(info, qs, kd, vz)


def attend_back_kernel(info, q_ref, do_ref, k_ref, v_ref, kt_ref, lse_ref, del_ref, dq_ref, dk_ref, dv_ref, dka, dva):
    i = pl.program_id(1)
    k = k_ref[...]
    v = v_ref[...]
    rows = q_ref.shape[0]
    lane = lax.broadcasted_iota(jnp.int32, (rows, 128), 1)
    dk = dv = None
    for hh in range(2):
        mine = (lane < HD) == (hh == 0)
        q = jnp.where(mine, q_ref[...], jnp.zeros((), BF))
        do = jnp.where(mine, do_ref[...], jnp.zeros((), BF))
        p = jnp.exp2(nt(k, q) - lse_ref[0, hh : hh + 1, :])
        ds = (p * (nt(v, do) - del_ref[0, hh : hh + 1, :])).astype(BF)
        dv_one = nn(p.astype(BF), do)
        dk_one = nn(ds, q)
        dv = dv_one if dv is None else dv + dv_one
        dk = dk_one if dk is None else dk + dk_one
        dq_ref[hh * HD : (hh + 1) * HD, :] = (nn(kt_ref[hh * HD : (hh + 1) * HD, :], ds) * 0.125).astype(BF)

    @pl.when(i == 0)
    def _():
        dka[...] = dk
        dva[...] = dv

    @pl.when(i == pl.num_programs(1) - 1)
    def _():
        keep = row_ids(0, LMAX) < info[0]
        dk_ref[...] = jnp.where(keep, (dka[...] + dk) * LN2, 0.0).astype(BF)
        dv_ref[...] = jnp.where(keep, dva[...] + dv, 0.0).astype(BF)


def attend_back(info, qs, do, kd, vz, kt, lse, delta):
    rows = 512
    mine = pl.BlockSpec((rows, 128), lambda p, i, info: (i, p))
    pair = pl.BlockSpec((LMAX, 128), lambda p, i, info: (0, p))
    line = pl.BlockSpec((1, 8, rows), lambda p, i, info: (p, 0, i))
    return pl.pallas_call(
        attend_back_kernel,
        grid_spec=pltpu.PrefetchScalarGridSpec(
            num_scalar_prefetch=1,
            grid=(3, ROWS // rows),
            in_specs=[mine, mine, pair, pair, pl.BlockSpec((128, LMAX), lambda p, i, info: (p, 0)), line, line],
            out_specs=[pl.BlockSpec((128, rows), lambda p, i, info: (p, i)), pair, pair],
            scratch_shapes=[pltpu.VMEM((LMAX, 128), F32), pltpu.VMEM((LMAX, 128), F32)],
        ),
        out_shape=[
            jax.ShapeDtypeStruct((HALF, ROWS), BF),
            jax.ShapeDtypeStruct((LMAX, HALF), BF),
            jax.ShapeDtypeStruct((LMAX, HALF), BF),
        ],
        **params("attend_back"),
    )(info, qs, do, kd, vz, kt, lse, delta)


def norm_parts(x):
    xc = x - jnp.mean(x, axis=1, keepdims=True)
    inv = lax.rsqrt(jnp.mean(xc * xc, axis=1, keepdims=True) + EPS)
    return xc * inv, inv


def norm_back(up, normal, inv, gain):
    e = up * gain
    return inv * (e - jnp.mean(e, axis=1, keepdims=True) - normal * jnp.mean(e * normal, axis=1, keepdims=True))


def ffn_kernel(
    info, ctx_ref, mix_ref, tok_ref, cot_ref, wd_ref, wi_ref, wo_ref, vec_ref, bi_ref, ones_ref,
    hid_ref, gpre_ref, gctx_ref, gcv_ref, del_ref, pay_ref, sm_ref, gbi_ref,
    act_s, gp_s, awd, awi, awo,
):
    i = pl.program_id(0)
    rows = ctx_ref.shape[0]
    keep = row_ids(info[1] * ROWS + i * rows, rows) < info[0]

    @pl.when(i == 0)
    def _():
        awd[...] = jnp.zeros_like(awd)
        awi[...] = jnp.zeros_like(awi)
        awo[...] = jnp.zeros_like(awo)
        sm_ref[...] = jnp.zeros_like(sm_ref)
        gbi_ref[...] = jnp.zeros_like(gbi_ref)

    vec = lambda k: vec_ref[k : k + 1, :]
    h = tok_ref[...].astype(F32)
    ctx = ctx_ref[...]
    mixed = jnp.concatenate([ctx, mix_ref[...]], axis=1)
    n1, inv1 = norm_parts(nn(mixed, wd_ref[...]) + vec(0) + h)
    f1 = n1 * vec(1) + vec(2)
    fl = f1.astype(BF)
    chunk = 512
    outs = []
    for g in range(2):
        fg = fl[:, g * HALF : (g + 1) * HALF]
        for ch in range(GW // chunk):
            cols = slice(ch * chunk, (ch + 1) * chunk)
            put = slice(g * GW + ch * chunk, g * GW + (ch + 1) * chunk)
            x = nn(fg, wi_ref[g, :, cols]) + bi_ref[0:1, put]
            phi = 0.5 + 0.5 * lax.erf(x * 0.7071067811865476)
            act_s[:, put] = (x * phi).astype(BF)
            gp_s[:, put] = phi + x * jnp.exp2(x * x * (-0.5 * LOG2E)) * 0.3989422804014327
        outs.append(nn(act_s[:, g * GW : (g + 1) * GW], wo_ref[g]))
    n2, inv2 = norm_parts(jnp.concatenate(outs, axis=1) + vec(3) + f1)
    hid_ref[...] = (n2 * vec(4) + vec(5)).astype(BF)
    u = jnp.where(keep, cot_ref[...].astype(F32), 0.0)
    gp2 = norm_back(u, n2, inv2, vec(4))
    go = gp2.astype(BF)
    got = go.T
    flt = fl.T
    gfs = []
    for g in range(2):
        sel = slice(g * HALF, (g + 1) * HALF)
        gf = gp2[:, sel]
        for ch in range(GW // chunk):
            cols = slice(ch * chunk, (ch + 1) * chunk)
            put = slice(g * GW + ch * chunk, g * GW + (ch + 1) * chunk)
            gi = (gp_s[:, put] * nt(go[:, sel], wo_ref[g, cols, :])).astype(BF)
            gbi_ref[0:1, put] += col_sum(gi.astype(F32))
            awo[g, :, cols] += nn(got[sel], act_s[:, put])
            awi[g, :, cols] += nn(flt[sel], gi)
            gf = gf + nt(gi, wi_ref[g, :, cols])
        gfs.append(gf)
    gf = jnp.concatenate(gfs, axis=1)
    gpre = norm_back(gf, n1, inv1, vec(1))
    gd = gpre.astype(BF)
    gpre_ref[...] = gd
    sm_ref[0:1, :] += col_sum(go.astype(F32))
    sm_ref[1:2, :] += col_sum(u * n2)
    sm_ref[2:3, :] += col_sum(u)
    sm_ref[3:4, :] += col_sum(gd.astype(F32))
    sm_ref[4:5, :] += col_sum(gf * n1)
    sm_ref[5:6, :] += col_sum(gf)
    awd[...] += nn(mixed.T, gd)
    gm = nt(gd, wd_ref[...])
    gctx = gm[:, :HALF].astype(BF)
    gctx_ref[...] = gctx
    gcv_ref[...] = gm[:, HALF:].astype(BF)
    prod = (gctx.astype(F32) * ctx.astype(F32)).astype(BF)
    del_ref[...] = nt(ones_ref[...], prod).reshape(3, 8, rows)

    @pl.when(i == pl.num_programs(0) - 1)
    def _():
        for r in range(2):
            for c in range(2):
                pay_ref[r, c, 0:HALF, :] = awi[r, :, c * D : c * D + HALF].astype(BF)
                pay_ref[r, c, HALF:D, :] = awi[r, :, c * D + HALF : (c + 1) * D].astype(BF)
                pay_ref[r, c, D : 2 * D, :] = awo[r, :, c * D : (c + 1) * D].T.astype(BF)
                for part in range(2):
                    piece = awd[part * HALF + c * 192 : part * HALF + (c + 1) * 192, r * HALF : (r + 1) * HALF]
                    pay_ref[r, c, 2 * D + part * 192 : 2 * D + (part + 1) * 192, :] = piece.astype(BF)


def ffn(info, ctx, mix, tok, cot, wd, wi, wo, vec, bi, ones24):
    rows = 256
    blk = lambda w: pl.BlockSpec((rows, w), lambda i, info: (i, 0))
    return pl.pallas_call(
        ffn_kernel,
        grid_spec=pltpu.PrefetchScalarGridSpec(
            num_scalar_prefetch=1,
            grid=(ROWS // rows,),
            in_specs=[
                blk(HALF),
                blk(HALF),
                blk(D),
                blk(D),
                whole((D, D)),
                whole((2, HALF, GW)),
                whole((2, GW, HALF)),
                whole((8, D)),
                whole((1, FF)),
                whole((24, HALF)),
            ],
            out_specs=[
                blk(D),
                blk(D),
                blk(HALF),
                blk(HALF),
                pl.BlockSpec((3, 8, rows), lambda i, info: (0, 0, i)),
                whole((2, 2, FFN_ROWS, HALF)),
                whole((8, D)),
                whole((1, FF)),
            ],
            scratch_shapes=[
                pltpu.VMEM((rows, FF), BF),
                pltpu.VMEM((rows, FF), F32),
                pltpu.VMEM((D, D), F32),
                pltpu.VMEM((2, HALF, GW), F32),
                pltpu.VMEM((2, HALF, GW), F32),
            ],
        ),
        out_shape=[
            jax.ShapeDtypeStruct((ROWS, D), BF),
            jax.ShapeDtypeStruct((ROWS, D), BF),
            jax.ShapeDtypeStruct((ROWS, HALF), BF),
            jax.ShapeDtypeStruct((ROWS, HALF), BF),
            jax.ShapeDtypeStruct((3, 8, ROWS), F32),
            jax.ShapeDtypeStruct((2, 2, FFN_ROWS, HALF), BF),
            jax.ShapeDtypeStruct((8, D), F32),
            jax.ShapeDtypeStruct((1, FF), F32),
        ],
        **params("ffn"),
    )(info, ctx, mix, tok, cot, wd, wi, wo, vec, bi, ones24)


def conv_back_kernel(
    info, gcv_ref, conv_ref, kp_ref, q_ref, pt_ref, wk_ref, spread_ref, ones_ref,
    gqm_ref, gpt_ref, gco_ref, gwk_ref, gbk_ref, acc, wbuf, tbuf,
):
    i = pl.program_id(0)
    rows = gcv_ref.shape[0]
    wide = rows + 32

    @pl.when(i == 0)
    def _():
        acc[...] = jnp.zeros_like(acc)
        tbuf[...] = jnp.zeros_like(tbuf)
        gwk_ref[...] = jnp.zeros_like(gwk_ref)
        gbk_ref[...] = jnp.zeros_like(gbk_ref)

    gcv = gcv_ref[...].astype(F32)
    wbuf[...] = conv_ref[pl.ds(pl.multiple_of(i * rows, 16), wide), :].astype(F32)
    kp = kp_ref[...]
    kpt = kp.T.astype(BF)
    gkps = []
    total = jnp.zeros((wide, HALF), F32)
    for j in range(KW):
        prod = (gcv * wbuf[12 + j : 12 + j + rows, :]).astype(BF)
        gkps.append(nt(ones_ref[...], prod))
        tbuf[24 : 24 + rows, :] = nn(kpt, spread_ref[:, j * HALF : (j + 1) * HALF]) * gcv
        total = total + tbuf[12 - j : 12 - j + wide, :]
    acc[pl.ds(pl.multiple_of(info[1] * ROWS + i * rows, 16), wide), :] += total
    gkp = jnp.concatenate(gkps, axis=0).reshape(KW, 8, rows)
    kp3 = kp.reshape(KW, 8, rows)
    inner = jnp.sum(kp3 * gkp, axis=0, keepdims=True)
    gl = (kp3 * (gkp - inner)).reshape(KW * 8, rows)
    gll = gl.astype(BF)
    glt = gl.T.astype(BF)
    gbk_ref[0:1, 0:72] += col_sum(glt.astype(F32))
    q = q_ref[...].astype(F32)
    pt = pt_ref[...].astype(F32)
    gwk_ref[...] += nn(gll, (pt * q).astype(BF))
    gmix = nn(glt, wk_ref[...])
    gqm_ref[...] = (gmix * pt).astype(BF)
    gpt_ref[...] = (gmix * q).astype(BF)

    @pl.when(i == pl.num_programs(0) - 1)
    def _():
        keep = row_ids(0, LMAX) < info[0]
        gco_ref[...] = jnp.where(keep, acc[16 : 16 + LMAX, :], 0.0).astype(BF)


def conv_back(info, gcv, conv, kp, q, pt, wk72, spread, ones8):
    rows = 256
    blk = pl.BlockSpec((rows, HALF), lambda i, info: (i, 0))
    return pl.pallas_call(
        conv_back_kernel,
        grid_spec=pltpu.PrefetchScalarGridSpec(
            num_scalar_prefetch=1,
            grid=(ROWS // rows,),
            in_specs=[
                blk,
                whole((ROWS + 32, HALF)),
                pl.BlockSpec((72, rows), lambda i, info: (0, i)),
                blk,
                blk,
                whole((72, HALF)),
                whole((72, KW * HALF)),
                whole((8, HALF)),
            ],
            out_specs=[blk, blk, whole((LMAX, HALF)), whole((72, HALF)), whole((8, 128))],
            scratch_shapes=[
                pltpu.VMEM((LMAX + 32, HALF), F32),
                pltpu.VMEM((rows + 32, HALF), F32),
                pltpu.VMEM((rows + 48, HALF), F32),
            ],
        ),
        out_shape=[
            jax.ShapeDtypeStruct((ROWS, HALF), BF),
            jax.ShapeDtypeStruct((ROWS, HALF), BF),
            jax.ShapeDtypeStruct((LMAX, HALF), BF),
            jax.ShapeDtypeStruct((72, HALF), F32),
            jax.ShapeDtypeStruct((8, 128), F32),
        ],
        **params("conv_back"),
    )(info, gcv, conv, kp, q, pt, wk72, spread, ones8)


def final_kernel(
    info, seq_ref, dk_ref, dv_ref, gco_ref, dq_ref, gqm_ref, gpt_ref, gpre_ref, dep_ref, w_ref, wdep_ref,
    smf_ref, gbi_ref, gwk_ref, gbk_ref,
    gh_ref, pay_ref, hbuf, gacc, agw, wbuf, dbuf, sm, gdp,
):
    i = pl.program_id(0)
    rows = dk_ref.shape[0]
    wide = rows + 32
    b = lax.rem(info[1] * 2 + i, 4)
    n = info[0]

    @pl.when(i == 0)
    def _():
        hbuf[0:16, :] = jnp.zeros((16, D), F32)
        hbuf[16 + LMAX :, :] = jnp.zeros((16, D), F32)
        for k in range(4):
            keep = row_ids(k * rows, rows) < n
            hbuf[16 + k * rows : 16 + (k + 1) * rows, :] = jnp.where(
                keep, seq_ref[PAD + k * rows : PAD + (k + 1) * rows, :].astype(F32), 0.0
            )
        gacc[...] = jnp.zeros_like(gacc)
        agw[...] = jnp.zeros_like(agw)
        dbuf[...] = jnp.zeros_like(dbuf)
        sm[...] = jnp.zeros_like(sm)
        gdp[...] = jnp.zeros_like(gdp)

    start = pl.multiple_of(b * rows, 16)
    here = pl.ds(pl.multiple_of(b * rows + 16, 16), rows)
    h = hbuf[here, :].astype(BF)
    dk, dv, gco = dk_ref[...], dv_ref[...], gco_ref[...]
    gacc[here, :] += nn(dk, w_ref[0]) + nn(dv, w_ref[1]) + nn(gco, w_ref[2])
    agw[0] += nn(dk.T, h)
    agw[1] += nn(dv.T, h)
    agw[2] += nn(gco.T, h)
    sm[1:2, :] += col_sum(dv.astype(F32))
    sm[2:3, :] += col_sum(gco.astype(F32))

    @pl.when(i < 2)
    def _():
        gqt = dq_ref[...].astype(F32) + gqm_ref[...].astype(F32).T
        gqt = gqt.astype(BF)
        gq = gqt.T
        gpt = gpt_ref[...]
        sm[0:1, :] += col_sum(gq.astype(F32))
        sm[3:4, :] += col_sum(gpt.astype(F32))
        agw[3] += nn(gqt, h)
        agw[4] += nn(gpt.T, dep_ref[...])
        gacc[here, :] += nn(gq, w_ref[3]) + gpre_ref[...].astype(F32)
        gdep = nn(gpt, w_ref[4])
        wbuf[...] = hbuf[pl.ds(start, wide), :]
        dbuf[24 : 24 + rows, :] = gdep
        total = jnp.zeros((wide, D), F32)
        for j in range(KW):
            gdp[j : j + 1, :] += col_sum(gdep * wbuf[12 + j : 12 + j + rows, :])
            total = total + dbuf[12 - j : 12 - j + wide, :] * wdep_ref[j : j + 1, :]
        gacc[pl.ds(start, wide), :] += total

    @pl.when(i == pl.num_programs(0) - 1)
    def _():
        keep = row_ids(0, LMAX) < n
        gh_ref[...] = jnp.where(keep, gacc[16 : 16 + LMAX, :], 0.0).astype(BF)
        for r in range(2):
            for c in range(2):
                for j in range(5):
                    piece = agw[j, c * 192 : (c + 1) * 192, r * HALF : (r + 1) * HALF]
                    pay_ref[r, c, j * 192 : (j + 1) * 192, :] = piece.astype(BF)
        zeros = lambda k: jnp.zeros((k, HALF), F32)
        pay_ref[0, 0, 960:, :] = gwk_ref[0:64, :].astype(BF)
        bias = jnp.concatenate([gbk_ref[...], jnp.zeros((8, 256), F32)], axis=1)
        pay_ref[0, 1, 960:, :] = jnp.concatenate([gwk_ref[64:72, :], sm[...], bias, zeros(40)], axis=0).astype(BF)
        inter = jnp.concatenate([gbi_ref[:, k * HALF : (k + 1) * HALF] for k in range(8)], axis=0)
        pay_ref[1, 0, 960:, :] = jnp.concatenate(
            [smf_ref[:, 0:HALF], smf_ref[:, HALF:D], inter, zeros(40)], axis=0
        ).astype(BF)
        pay_ref[1, 1, 960:, :] = jnp.concatenate([gdp[:, 0:HALF], gdp[:, HALF:D], zeros(32)], axis=0).astype(BF)


def final(info, seq_tok, dk, dv, gco, dq, gqm, gpt, gpre, dep, w5, wdep, smf, gbi, gwk, gbk):
    rows = 512
    seq = pl.BlockSpec((rows, HALF), lambda i, info: (lax.rem(info[1] * 2 + i, 4), 0))
    own = lambda w: pl.BlockSpec((rows, w), lambda i, info: (jnp.minimum(i, 1), 0))
    return pl.pallas_call(
        final_kernel,
        grid_spec=pltpu.PrefetchScalarGridSpec(
            num_scalar_prefetch=1,
            grid=(LMAX // rows,),
            in_specs=[
                whole((LMAX + 2 * PAD, D)),
                seq,
                seq,
                seq,
                pl.BlockSpec((HALF, rows), lambda i, info: (0, jnp.minimum(i, 1))),
                own(HALF),
                own(HALF),
                own(D),
                own(D),
                whole((5, HALF, D)),
                whole((16, D)),
                whole((8, D)),
                whole((1, FF)),
                whole((72, HALF)),
                whole((8, 128)),
            ],
            out_specs=[whole((LMAX, D)), whole((2, 2, PROJ_ROWS, HALF))],
            scratch_shapes=[
                pltpu.VMEM((LMAX + 32, D), F32),
                pltpu.VMEM((LMAX + 32, D), F32),
                pltpu.VMEM((5, HALF, D), F32),
                pltpu.VMEM((rows + 32, D), F32),
                pltpu.VMEM((rows + 48, D), F32),
                pltpu.VMEM((8, HALF), F32),
                pltpu.VMEM((16, D), F32),
            ],
        ),
        out_shape=[
            jax.ShapeDtypeStruct((LMAX, D), BF),
            jax.ShapeDtypeStruct((2, 2, PROJ_ROWS, HALF), BF),
        ],
        **params("final"),
    )(info, seq_tok, dk, dv, gco, dq, gqm, gpt, gpre, dep, w5, wdep, smf, gbi, gwk, gbk)


def constants():
    spread = np.zeros((72, KW * HALF), np.float32)
    ones8 = np.zeros((8, HALF), np.float32)
    ones24 = np.zeros((24, HALF), np.float32)
    perm = np.zeros((72, 54), np.float32)
    for head in range(6):
        cols = slice(head * HD, (head + 1) * HD)
        ones8[head, cols] = 1
        ones24[head // 2 * 8 + head % 2, cols] = 1
        for j in range(KW):
            spread[j * 8 + head, j * HALF + head * HD : j * HALF + (head + 1) * HD] = 1
            perm[j * 8 + head, head * KW + j] = 1
    return [jnp.asarray(a, BF) for a in (spread, ones8, ones24, perm)]


def per_device(
    groups, tokens, cotangent, seq_lengths, w_query, w_key, w_value, w_convout, w_point, w_depth,
    b_query, b_value, b_convout, b_point, w_kernel, b_kernel, w_dense, b_dense, gain_one, bias_one,
    w_inter, b_inter, w_output, b_output, gain_two, bias_two,
):
    r = lax.axis_index("row")
    c = lax.axis_index("col")
    info = jnp.stack([lax.dynamic_index_in_dim(seq_lengths, r, 0, False), c]).astype(jnp.int32)
    spread, ones8, ones24, perm = constants()

    seq, w5 = start(tokens, (w_key, w_value, w_convout, w_query, w_point))
    wi, wo, wd, cot = middle(w_inter[0], w_output[0], w_dense.reshape(2, 192, HALF), cotangent)
    wd = wd.reshape(D, D)

    wdep = jnp.pad(w_depth.astype(F32).T, ((0, 7), (0, 0)))
    vec3 = jnp.pad(jnp.stack([b_convout, b_query, b_point]).astype(F32), ((0, 5), (0, 0)))
    wk72 = jnp.pad(w_kernel.T.reshape(6, KW, HALF).transpose(1, 0, 2), ((0, 0), (0, 2), (0, 0))).reshape(72, HALF)
    bk72 = jnp.pad(b_kernel.astype(F32).reshape(6, KW).T, ((0, 0), (0, 2))).reshape(72, 1)
    bk72 = jnp.broadcast_to(bk72, (72, 128))
    vec6 = jnp.pad(
        jnp.stack([b_dense, gain_one, bias_one, b_output, gain_two, bias_two]).astype(F32), ((0, 2), (0, 0))
    )
    bi = b_inter.astype(F32).reshape(1, FF)

    kd, kt, vz = keys_values(info, seq, w5, b_value.astype(F32).reshape(1, HALF))
    q, qs, pt, kp, conv, mix, dep, hown = own_rows(info, seq, w5, wdep, vec3, wk72, bk72, spread)
    ctx, lse = attend(info, qs, kd, vz)
    hid, gpre, gctx, gcv, delta, payf, smf, gbi = ffn(info, ctx, mix, hown, cot, wd, wi, wo, vec6, bi, ones24)
    g_inter, g_out, g_dense, hidden_out = ffn_sum(payf, hid)
    gqm, gpt, gco, gwk, gbk = conv_back(info, gcv, conv, kp, q, pt, wk72, spread, ones8)
    dq, dk, dv = attend_back(info, qs, gctx, kd, vz, kt, lse, delta)
    gh, pay5 = final(info, seq, dk, dv, gco, dq, gqm, gpt, gpre, dep, w5, wdep, smf, gbi, gwk, gbk)
    (gt, gk, gv, gc, gq, gp, gdep, gbq, gbv, gbc, gbp, gwk, gbk, gbd, gg1, gb1, gbi, gbo, gg2, gb2) = end(pay5, gh, perm)
    if groups > 8:
        mine = (gk, gv, gc, gq, gp, gdep, gbq, gbv, gbc, gbp, gwk, gbk, gbd, gg1, gb1, gbi, gbo, gg2, gb2, g_inter, g_out, g_dense)
        mine = lax.psum(tuple(x * 0.125 for x in mine), "dp")
        (gk, gv, gc, gq, gp, gdep, gbq, gbv, gbc, gbp, gwk, gbk, gbd, gg1, gb1, gbi, gbo, gg2, gb2, g_inter, g_out, g_dense) = mine
    return (
        hidden_out, gt, gq, gk, gv, gc, gp, gdep, gbq[0], gbv[0], gbc[0], gbp[0], gwk, gbk[0], g_dense, gbd[0], gg1[0],
        gb1[0], g_inter[None], gbi[0], g_out[None], gbo[0], gg2[0], gb2[0],
    )


def solution(mesh):
    act = P(("dp", "col"), "row")
    rep = P()
    proj = P("row", "col")
    in_specs = (
        act, act, P("dp"), proj, proj, proj, proj, proj, rep, rep, rep, rep, rep, rep, rep, P("col", "row"),
        rep, rep, rep, P("row", None, "col"), rep, P("row", "col", None), rep, rep, rep,
    )
    out_specs = (
        act, act, proj, proj, proj, proj, proj, rep, rep, rep, rep, rep, rep, rep, P("col", "row"),
        rep, rep, rep, P("row", None, "col"), rep, P("row", "col", None), rep, rep, rep,
    )
    return jax.shard_map(
        functools.partial(per_device, mesh.shape["dp"]), mesh=mesh, in_specs=in_specs, out_specs=out_specs, check_vma=False)
```

```python
import functools

import jax
import jax.numpy as jnp
import numpy as np
from jax import lax
from jax.experimental import pallas as pl
from jax.experimental.pallas import tpu as pltpu
from jax.sharding import PartitionSpec as P

D = 768
HALF = 384
HD = 64
KW = 9
FF = 3072
GW = 1536
LMAX = 2048
ROWS = 1024
EPS = 1e-12
LOG2E = 1.4426950408889634
LN2 = 0.6931471805599453
BF = jnp.bfloat16
F32 = jnp.float32
VMEM_BYTES = 63 * 1024 * 1024
PAD = 16
FFN_ROWS = 1920
FFN_CHUNK = 640
PROJ_ROWS = 1024
MESH = pl.DeviceIdType.MESH
HBM = pl.BlockSpec(memory_space=pl.ANY)
VMEM = pl.BlockSpec(memory_space=pltpu.VMEM)


def nn(a, b):
    return lax.dot_general(a, b, (((1,), (0,)), ((), ())), preferred_element_type=F32)


def nt(a, b):
    return lax.dot_general(a, b, (((1,), (1,)), ((), ())), preferred_element_type=F32)


def col_sum(x):
    return jnp.sum(x, axis=0, keepdims=True)


def row_ids(start, rows):
    return start + lax.broadcasted_iota(jnp.int32, (rows, 1), 0)


def whole(shape):
    return pl.BlockSpec(shape, lambda *_: (0,) * len(shape))


def once(shape):
    return pl.BlockSpec(shape, lambda *_: (0,) * len(shape), pipeline_mode=pl.Buffered(1))


def half_index():
    return lax.axis_index("col")


def length(lens):
    return lens[lax.axis_index("row")]


def line(ref):
    return ref[...].astype(F32).reshape(1, ref.shape[0])


def params(name):
    return dict(
        name=name,
        compiler_params=pltpu.CompilerParams(vmem_limit_bytes=VMEM_BYTES),
    )


def lanes(k, width=HALF):
    return pl.ds(pl.multiple_of(k * width, 128), width)


def rows_at(start, count, step=16):
    return pl.ds(pl.multiple_of(start, step), count)


def send(src, dst, send_sem, recv_sem, device):
    return pltpu.make_async_remote_copy(
        src_ref=src, dst_ref=dst, send_sem=send_sem, recv_sem=recv_sem, device_id=device, device_id_type=MESH
    )


class Place:
    def __init__(self):
        self.d = lax.axis_index("dp")
        self.r = lax.axis_index("row")
        self.c = lax.axis_index("col")
        self.k = lax.rem(self.d, 8)
        self.base = self.d - self.k
        self.y = lax.rem(self.k, 2)
        self.z = lax.div(self.k, 2)
        self.across = {"row": 1 - self.r}
        self.core = {"col": 1 - self.c}
        self.diagonal = {"row": 1 - self.r, "col": 1 - self.c}

    def eight(self, offset):
        other = lax.rem(self.k + offset, 8)
        return other, {"dp": self.base + other}

    def four(self, offset):
        other = lax.rem(self.z + offset, 4)
        return other, {"dp": self.base + other * 2 + self.y}


def meet(devices):
    barrier = pltpu.get_barrier_semaphore()
    for device in devices:
        pl.semaphore_signal(barrier, inc=1, device_id=device, device_id_type=MESH)
    pl.semaphore_wait(barrier, len(devices))


def comm_params(name, number):
    return dict(
        name=name,
        compiler_params=pltpu.CompilerParams(
            vmem_limit_bytes=VMEM_BYTES, collective_id=number, has_side_effects=True
        ),
    )


class Gather:
    def __init__(self, place, own, full, part, block, send_sem, recv_sem, first):
        self.p, self.own, self.full, self.part, self.block = place, own, full, part, block
        self.s, self.v, self.f = send_sem, recv_sem, first

    def _move(self, src, dst, n, device):
        return send(src, dst, self.s.at[self.f + n], self.v.at[self.f + n], device)

    def _cross(self, r):
        p = self.p
        return self._move(self.part(self.own, p.z), self.block(self.full, r, p.c, p.z), 0, p.across)

    def _near(self, c):
        p = self.p
        return self._move(self.block(self.full, p.r, c, None), self.block(self.full, p.r, c, None), 1, p.core)

    def _pass(self, offset, z):
        p = self.p
        _, device = p.four(offset)
        here = self.block(self.full, 1 - p.r, p.c, z)
        return self._move(here, here, 1 + offset, device)

    def _last(self, c):
        p = self.p
        here = self.block(self.full, 1 - p.r, c, None)
        return self._move(here, here, 5, p.core)

    def relay(self):
        p = self.p
        self._cross(1 - p.r).wait_recv()
        for offset in (1, 2, 3):
            self._pass(offset, p.z).start()

    def share(self):
        p = self.p
        for offset in (1, 2, 3):
            back = lax.rem(p.z + 4 - offset, 4)
            self._pass(offset, back).wait_recv()
        self._last(p.c).start()

    def finish(self):
        p = self.p
        self._last(1 - p.c).wait_recv()
        self._near(1 - p.c).wait_recv()
        self._cross(p.r).wait_send()
        self._near(p.c).wait_send()
        for offset in (1, 2, 3):
            self._pass(offset, p.z).wait_send()
        self._last(p.c).wait_send()


def proj_part(ref, z):
    return ref.at[:, rows_at(z * 48, 48), :]


def proj_block(ref, r, c, z):
    if z is None:
        return ref.at[:, rows_at(c * 192, 192), lanes(r)]
    return ref.at[:, rows_at(c * 192 + z * 48, 48), lanes(r)]


def inter_part(ref, z):
    return ref.at[rows_at(z * 96, 96), :]


def inter_block(ref, r, c, z):
    if z is None:
        return ref.at[r, :, lanes(c, 768)]
    return ref.at[r, rows_at(z * 96, 96), lanes(c, 768)]


def output_part(ref, z):
    return ref.at[rows_at(z * 192, 192), :]


def output_block(ref, r, c, z):
    if z is None:
        return ref.at[r, rows_at(c * 768, 768), :]
    return ref.at[r, rows_at(c * 768 + z * 192, 192), :]


def dense_part(ref, z):
    return ref.at[lax.div(z, 2), rows_at(lax.rem(z, 2) * 96, 96), :]


def dense_block(ref, r, c, z):
    if z is None:
        return ref.at[:, rows_at(c * 192, 192), lanes(r)]
    return ref.at[lax.div(z, 2), rows_at(c * 192 + lax.rem(z, 2) * 96, 96), lanes(r)]


def start_kernel(
    tok_ref, wk_ref, wv_ref, wc_ref, wq_ref, wp_ref, kern_ref, kb_ref, perm_ref,
    seq_ref, w5_ref, k72_ref, b72_ref, own, stage, lsem, ts, tr, gs, gr,
):
    p = Place()
    r, c = p.r, p.c
    for j, ref in enumerate((wk_ref, wv_ref, wc_ref, wq_ref, wp_ref)):
        own[j] = ref[...]
    keep = pltpu.make_async_copy(own, proj_block(w5_ref, r, c, None), lsem.at[0])
    keep.start()
    load = pltpu.make_async_copy(tok_ref, stage, lsem.at[1])
    store = pltpu.make_async_copy(stage, seq_ref.at[PAD : PAD + LMAX, lanes(r)], lsem.at[2])
    load.start()
    meet([p.across, p.core, p.diagonal] + [p.four(o)[1] for o in (1, 2, 3)])
    gather = Gather(p, own, w5_ref, proj_part, proj_block, gs, gr, 0)

    def chunk(m, k):
        return seq_ref.at[PAD + m * 512 : PAD + (m + 1) * 512, lanes(k)]

    def cross(m, k):
        return send(tok_ref.at[m * 512 : (m + 1) * 512, :], chunk(m, k), ts.at[m], tr.at[m], {"row": 1 - r, "col": m // 2})

    def near(k):
        return send(tok_ref, seq_ref.at[PAD : PAD + LMAX, lanes(k)], ts.at[4], tr.at[4], p.core)

    def forward(m):
        return send(chunk(m, 1 - r), chunk(m, 1 - r), ts.at[5 + m], tr.at[5 + m], p.core)

    gather._cross(r).start()

    @pl.when(r != c)
    def _():
        for m in (0, 2, 1, 3):
            cross(m, r).start()

    load.wait()

    @pl.when(r == c)
    def _():
        near(r).start()
        store.start()

    k72_ref[...] = nn(perm_ref[...], kern_ref[...]).astype(BF)
    bias = jnp.broadcast_to(line(kb_ref), (128, 54)).astype(BF)
    b72_ref[...] = nt(perm_ref[...], bias)
    keep.wait()
    gather._near(c).start()
    gather.relay()
    for q in range(2):

        @pl.when(c == q)
        def _():
            for m in (2 * q, 2 * q + 1):
                cross(m, 1 - r).wait_recv()
                forward(m).start()

    gather.share()
    for q in range(2):

        @pl.when(c == q)
        def _():
            for m in (2 - 2 * q, 3 - 2 * q):
                forward(m).wait_recv()
            for m in (2 * q, 2 * q + 1):
                forward(m).wait_send()

    @pl.when(r != c)
    def _():
        for m in range(4):
            cross(m, r).wait_send()
        near(r).wait_recv()

    @pl.when(r == c)
    def _():
        near(r).wait_send()
        store.wait()

    gather.finish()


def start(tokens, weights, w_kernel, b_kernel, perm):
    return pl.pallas_call(
        start_kernel,
        in_specs=[HBM] + [VMEM] * 8,
        out_specs=[HBM, HBM, VMEM, VMEM],
        out_shape=[
            jax.ShapeDtypeStruct((LMAX + 2 * PAD, D), BF),
            jax.ShapeDtypeStruct((5, HALF, D), BF),
            jax.ShapeDtypeStruct((72, HALF), BF),
            jax.ShapeDtypeStruct((72, 128), F32),
        ],
        scratch_shapes=[
            pltpu.VMEM((5, 192, HALF), BF),
            pltpu.VMEM((LMAX, HALF), BF),
            pltpu.SemaphoreType.DMA((3,)),
            pltpu.SemaphoreType.DMA((9,)),
            pltpu.SemaphoreType.DMA((9,)),
            pltpu.SemaphoreType.DMA((6,)),
            pltpu.SemaphoreType.DMA((6,)),
        ],
        **comm_params("start", 1),
    )(tokens, *weights, w_kernel, b_kernel, perm)


class ToRows:
    def __init__(self, place, src, dst, local_sem, send_sem, recv_sem):
        self.p, self.src, self.dst = place, src, dst
        self.l, self.s, self.v = local_sem, send_sem, recv_sem

    def _cross(self, q, k):
        half = self.src.at[q * ROWS : (q + 1) * ROWS, :]
        return send(half, self.dst.at[:, lanes(k)], self.s.at[q], self.v.at[0], {"row": 1 - self.p.r, "col": q})

    def _near(self):
        p = self.p
        half = self.src.at[rows_at((1 - p.c) * ROWS, ROWS), :]
        return send(half, self.dst.at[:, lanes(p.r)], self.s.at[2], self.v.at[1], p.core)

    def _local(self):
        p = self.p
        half = self.src.at[rows_at(p.c * ROWS, ROWS), :]
        return pltpu.make_async_copy(half, self.dst.at[:, lanes(p.r)], self.l)

    def start(self):
        p = self.p

        @pl.when(p.r != p.c)
        def _():
            self._cross(0, p.r).start()
            self._cross(1, p.r).start()

        @pl.when(p.r == p.c)
        def _():
            self._near().start()
            self._local().start()

    def finish(self):
        p = self.p
        self._cross(0, 1 - p.r).wait_recv()

        @pl.when(p.r != p.c)
        def _():
            self._cross(0, p.r).wait_send()
            self._cross(1, p.r).wait_send()
            self._near().wait_recv()

        @pl.when(p.r == p.c)
        def _():
            self._near().wait_send()
            self._local().wait()


class FromRows:
    def __init__(self, place, src, dst, local_sem, send_sem, recv_sem):
        self.p, self.src, self.dst = place, src, dst
        self.l, self.s, self.v = local_sem, send_sem, recv_sem

    def _cross(self, q):
        p = self.p
        place = self.dst.at[rows_at(q * ROWS, ROWS), :]
        return send(self.src.at[:, lanes(1 - p.r)], place, self.s.at[0], self.v.at[q], {"row": 1 - p.r, "col": p.r})

    def _near(self, q):
        p = self.p
        place = self.dst.at[rows_at(q * ROWS, ROWS), :]
        return send(self.src.at[:, lanes(p.r)], place, self.s.at[1], self.v.at[2], p.core)

    def _local(self):
        p = self.p
        place = self.dst.at[rows_at(p.c * ROWS, ROWS), :]
        return pltpu.make_async_copy(self.src.at[:, lanes(p.r)], place, self.l)

    def start(self):
        p = self.p
        self._cross(p.c).start()

        @pl.when(p.r != p.c)
        def _():
            self._near(p.c).start()

        @pl.when(p.r == p.c)
        def _():
            self._local().start()

    def finish(self):
        p = self.p
        self._cross(p.c).wait_send()

        @pl.when(p.r != p.c)
        def _():
            self._near(p.c).wait_send()
            self._cross(0).wait_recv()
            self._cross(1).wait_recv()

        @pl.when(p.r == p.c)
        def _():
            self._near(1 - p.c).wait_recv()
            self._local().wait()


class Sum:
    def __init__(self, place, far, mid, ybuf, zbuf, total, rows, s, v, first=0):
        self.p, self.far, self.mid, self.ybuf, self.zbuf, self.total = place, far, mid, ybuf, zbuf, total
        self.rows, self.s, self.v, self.first = rows, s, v, first

    def _sems(self, ch, n):
        i = self.first + ch * 8 + n
        return self.s.at[i], self.v.at[i]

    def _beside(self):
        p = self.p
        return {"dp": p.base + p.z * 2 + 1 - p.y}

    def _halves(self, ch, y):
        return rows_at(ch * self.rows + y * (self.rows // 2), self.rows // 2)

    def _piece(self, ch, z):
        return rows_at(ch * self.rows + self.p.y * (self.rows // 2) + z * (self.rows // 8), self.rows // 8)

    def _half(self, ch):
        return send(self.far.at[self._halves(ch, 1 - self.p.y), :], self.ybuf.at[ch], *self._sems(ch, 0), self._beside())

    def _quarter(self, ch, offset):
        other, device = self.p.four(offset)
        src = self.mid.at[ch, rows_at(other * (self.rows // 8), self.rows // 8), :]
        return send(src, self.zbuf.at[ch, offset - 1], *self._sems(ch, offset), device)

    def _along(self, ch, offset, z):
        _, device = self.p.four(offset)
        here = self.total.at[self._piece(ch, z), :]
        return send(here, here, *self._sems(ch, 3 + offset), device)

    def _back(self, ch, y):
        here = self.total.at[self._halves(ch, y), :]
        return send(here, here, *self._sems(ch, 7), self._beside())

    def half(self, ch):
        self._half(ch).start()

    def quarter(self, ch):
        self._half(ch).wait_recv()
        both = self.far[self._halves(ch, self.p.y), :].astype(F32) + self.ybuf[ch].astype(F32)
        self.mid[ch] = both.astype(BF)
        for offset in (1, 2, 3):
            self._quarter(ch, offset).start()

    def collect(self, ch):
        both = self.mid[ch, rows_at(self.p.z * (self.rows // 8), self.rows // 8), :].astype(F32)
        for offset in (1, 2, 3):
            self._quarter(ch, offset).wait_recv()
            both = both + self.zbuf[ch, offset - 1].astype(F32)
        return both.astype(BF)

    def along(self, ch, piece):
        self.total[self._piece(ch, self.p.z), :] = piece
        for offset in (1, 2, 3):
            self._along(ch, offset, self.p.z).start()

    def back(self, ch):
        for offset in (1, 2, 3):
            self._along(ch, offset, lax.rem(self.p.z + 4 - offset, 4)).wait_recv()
        self._back(ch, self.p.y).start()

    def finish_sum(self, ch):
        self._half(ch).wait_send()
        for offset in (1, 2, 3):
            self._quarter(ch, offset).wait_send()

    def finish_spread(self, ch):
        self._back(ch, 1 - self.p.y).wait_recv()
        for offset in (1, 2, 3):
            self._along(ch, offset, self.p.z).wait_send()
        self._back(ch, self.p.y).wait_send()

    @staticmethod
    def scratch(rows, chunks):
        return [
            pltpu.VMEM((chunks, rows // 2, HALF), BF),
            pltpu.VMEM((chunks, rows // 2, HALF), BF),
            pltpu.VMEM((chunks, 3, rows // 8, HALF), BF),
            pltpu.SemaphoreType.DMA((8 * chunks,)),
            pltpu.SemaphoreType.DMA((8 * chunks,)),
        ]


class Near:
    def __init__(self, place, pay, near, s, v):
        self.p, self.pay, self.near, self.s, self.v = place, pay, near, s, v

    def _move(self, n):
        p = self.p
        rr = 1 - p.r if n == 0 else p.r
        return send(self.pay.at[rr, 1 - p.c], self.near.at[rr], self.s.at[n], self.v.at[n], p.core)

    def start(self):
        for n in range(2):
            self._move(n).start()

    def finish(self):
        for n in range(2):
            self._move(n).wait()


def everyone(p):
    return [p.across, p.core, p.diagonal, {"dp": p.base + p.z * 2 + 1 - p.y}] + [p.four(o)[1] for o in (1, 2, 3)]


def front_kernel(
    lens, seq_ref, w_ref, wdep_ref, bv_ref, bc_ref, bq_ref, bp_ref, wk_ref, bk_ref, spread_ref, wi_own, wd_own, cot_own,
    kd_ref, kt_ref, vz_ref, q_ref, qs_ref, pt_ref, kp_ref, conv_ref, mix_ref, dep_ref, h_ref, wi_ref, wd_ref, cot_ref,
    first_key, hbuf, cbuf, lsem, gs, gr, cs, cr,
):
    i = pl.program_id(0)
    p = Place()
    n = lens[p.r]
    keeps = [
        pltpu.make_async_copy(wi_own, inter_block(wi_ref, p.r, p.c, None), lsem.at[0]),
        pltpu.make_async_copy(wd_own, dense_block(wd_ref, p.r, p.c, None), lsem.at[1]),
    ]
    gathers = [
        Gather(p, wi_own, wi_ref, inter_part, inter_block, gs, gr, 0),
        Gather(p, wd_own, wd_ref, dense_part, dense_block, gs, gr, 6),
    ]
    cot_rows = ToRows(p, cot_own, cot_ref, lsem.at[2], cs, cr)

    @pl.when(i == 0)
    def _():
        meet([p.across, p.core, p.diagonal] + [p.four(o)[1] for o in (1, 2, 3)])
        for keep, gather in zip(keeps, gathers):
            gather._cross(p.r).start()
            keep.start()

    @pl.when(i == 1)
    def _():
        for keep, gather in zip(keeps, gathers):
            keep.wait()
            gather._near(p.c).start()
            gather.relay()
        cot_rows.start()

    krows = kd_ref.shape[0]
    keep_key = row_ids(i * krows, krows) < n
    tok = seq_ref[rows_at(PAD + i * krows, krows), :]
    h = jnp.where(keep_key, tok.astype(F32), 0.0).astype(BF)
    k = nt(h, w_ref[0])
    v = nt(h, w_ref[1]) + line(bv_ref)

    @pl.when(i == 0)
    def _():
        first_key[...] = k[0:8]

    kd_ref[...] = jnp.where(keep_key, k, first_key[0:1]).astype(BF)
    kt_ref[...] = k.T.astype(BF)
    vz_ref[...] = jnp.where(keep_key, v, 0.0).astype(BF)

    rows = q_ref.shape[0]
    wide = rows + 32
    base = pl.multiple_of(i * rows, 16)
    start = pl.multiple_of(p.c * ROWS + i * rows, 16)
    ids = row_ids(start - 16, wide)
    keep = (ids >= 0) & (ids < n)
    hw = jnp.where(keep, seq_ref[pl.ds(start, wide), :].astype(F32), 0.0)
    hbuf[...] = hw
    depth = jnp.zeros((rows, D), F32)
    wdep = wdep_ref[...].astype(F32)
    for j in range(KW):
        depth = depth + hbuf[12 + j : 12 + j + rows, :] * wdep[j : j + 1, :]
    depth_low = depth.astype(BF)
    dep_ref[...] = depth_low
    hl = hw.astype(BF)
    h_ref[...] = hl[16 : 16 + rows]
    conv = jnp.where(keep, nt(hl, w_ref[2]) + line(bc_ref), 0.0)
    cbuf[...] = conv
    conv_ref[pl.ds(base, wide), :] = conv.astype(BF)
    q = nt(hl[16 : 16 + rows], w_ref[3]) + line(bq_ref)
    q_low = q.astype(BF)
    q_ref[...] = q_low
    qs_ref[...] = (q * (0.125 * LOG2E)).astype(BF)
    pt = nt(depth_low, w_ref[4]) + line(bp_ref)
    pt_ref[...] = pt.astype(BF)
    mixer = (pt * q_low.astype(F32)).astype(BF)
    logits = (nt(wk_ref[...], mixer) + bk_ref[:, 0:1]).reshape(KW, 8, rows)
    peak = jnp.max(logits, axis=0, keepdims=True)
    raised = jnp.exp(logits - peak)
    kp = (raised / jnp.sum(raised, axis=0, keepdims=True)).reshape(KW * 8, rows)
    kp_ref[...] = kp
    kpt = kp.T.astype(BF)
    mix = jnp.zeros((rows, HALF), F32)
    for j in range(KW):
        mix = mix + nn(kpt, spread_ref[:, j * HALF : (j + 1) * HALF]) * cbuf[12 + j : 12 + j + rows, :]
    mix_ref[...] = mix.astype(BF)

    @pl.when(i == pl.num_programs(0) - 1)
    def _():
        for gather in gathers:
            gather.share()
        cot_rows.finish()
        for gather in gathers:
            gather.finish()


def front(lens, seq, w5, wdep, bv, bc, bq, bp, wk72, bk72, spread, w_inter, w_dense, cotangent):
    rows = 256
    keys = 512
    blk = pl.BlockSpec((rows, HALF), lambda i, lens: (i, 0))
    full = pl.BlockSpec((rows, D), lambda i, lens: (i, 0))
    half = jax.ShapeDtypeStruct((ROWS, HALF), BF)
    return pl.pallas_call(
        front_kernel,
        grid_spec=pltpu.PrefetchScalarGridSpec(
            num_scalar_prefetch=1,
            grid=(ROWS // rows,),
            in_specs=[once((LMAX + 2 * PAD, D)), once((5, HALF, D)), whole((KW, D))]
            + [whole((HALF,))] * 4
            + [whole((72, HALF)), whole((72, 128)), once((72, KW * HALF))]
            + [once((HALF, D)), once((2, 192, HALF)), once((LMAX, HALF))],
            out_specs=[
                pl.BlockSpec((keys, HALF), lambda i, lens: (i, 0)),
                pl.BlockSpec((HALF, keys), lambda i, lens: (0, i)),
                pl.BlockSpec((keys, HALF), lambda i, lens: (i, 0)),
                blk,
                blk,
                blk,
                pl.BlockSpec((72, rows), lambda i, lens: (0, i)),
                whole((ROWS + 32, HALF)),
                blk,
                full,
                full,
                HBM,
                HBM,
                HBM,
            ],
            scratch_shapes=[
                pltpu.VMEM((8, HALF), F32),
                pltpu.VMEM((rows + 32, D), F32),
                pltpu.VMEM((rows + 32, HALF), F32),
                pltpu.SemaphoreType.DMA((3,)),
                pltpu.SemaphoreType.DMA((12,)),
                pltpu.SemaphoreType.DMA((12,)),
                pltpu.SemaphoreType.DMA((3,)),
                pltpu.SemaphoreType.DMA((2,)),
            ],
        ),
        out_shape=[
            jax.ShapeDtypeStruct((LMAX, HALF), BF),
            jax.ShapeDtypeStruct((HALF, LMAX), BF),
            jax.ShapeDtypeStruct((LMAX, HALF), BF),
            half,
            half,
            half,
            jax.ShapeDtypeStruct((72, ROWS), F32),
            jax.ShapeDtypeStruct((ROWS + 32, HALF), BF),
            half,
            jax.ShapeDtypeStruct((ROWS, D), BF),
            jax.ShapeDtypeStruct((ROWS, D), BF),
            jax.ShapeDtypeStruct((2, HALF, GW), BF),
            jax.ShapeDtypeStruct((2, HALF, D), BF),
            jax.ShapeDtypeStruct((ROWS, D), BF),
        ],
        **comm_params("front", 2),
    )(lens, seq, w5, wdep, bv, bc, bq, bp, wk72, bk72, spread, w_inter, w_dense, cotangent)


def attend_kernel(lens, q_ref, k_ref, v_ref, wo_own, ctx_ref, lse_ref, wo_ref, lsem, gs, gr):
    i = pl.program_id(0)
    p = Place()
    keep = pltpu.make_async_copy(wo_own, output_block(wo_ref, p.r, p.c, None), lsem)
    gather = Gather(p, wo_own, wo_ref, output_part, output_block, gs, gr, 0)

    @pl.when(i == 0)
    def _():
        meet([p.across, p.core] + [p.four(o)[1] for o in (1, 2, 3)])
        gather._cross(p.r).start()
        keep.start()

    @pl.when(i == 1)
    def _():
        keep.wait()
        gather._near(p.c).start()
        gather.relay()

    k = k_ref[...]
    ones = jnp.where(row_ids(0, LMAX) < lens[p.r], 1.0, 0.0)
    ve = jnp.concatenate([v_ref[...], jnp.broadcast_to(ones, (LMAX, 128)).astype(BF)], axis=1)
    rows = 256
    lane = lax.broadcasted_iota(jnp.int32, (rows, 128), 1)
    for u in range(ROWS // rows):
        part = slice(u * rows, (u + 1) * rows)
        outs = []
        for hh in range(2):
            q = jnp.where((lane < HD) == (hh == 0), q_ref[part, :], jnp.zeros((), BF))
            s = nt(q, k)
            peak = jnp.max(s, axis=1, keepdims=True)
            prob = jnp.exp2(s - peak).astype(BF)
            o = nn(prob, ve)
            outs.append(o[:, :128] / o[:, 128:])
            lse_ref[0, hh : hh + 1, part] = (peak + jnp.log2(o[:, 128:129])).T
        ctx_ref[part, :] = jnp.where(lane < HD, outs[0], outs[1]).astype(BF)

    @pl.when(i == pl.num_programs(0) - 1)
    def _():
        gather.share()
        gather.finish()


def attend(lens, qs, kd, vz, w_output):
    pair = lambda rows: pl.BlockSpec((rows, 128), lambda p, lens: (0, p))
    return pl.pallas_call(
        attend_kernel,
        grid_spec=pltpu.PrefetchScalarGridSpec(
            num_scalar_prefetch=1,
            grid=(3,),
            in_specs=[pair(ROWS), pair(LMAX), pair(LMAX), once((D, HALF))],
            out_specs=[pair(ROWS), pl.BlockSpec((1, 8, ROWS), lambda p, lens: (p, 0, 0)), HBM],
            scratch_shapes=[
                pltpu.SemaphoreType.DMA,
                pltpu.SemaphoreType.DMA((6,)),
                pltpu.SemaphoreType.DMA((6,)),
            ],
        ),
        out_shape=[
            jax.ShapeDtypeStruct((ROWS, HALF), BF),
            jax.ShapeDtypeStruct((3, 8, ROWS), F32),
            jax.ShapeDtypeStruct((2, GW, HALF), BF),
        ],
        **comm_params("attend", 3),
    )(lens, qs, kd, vz, w_output)


def attend_back_kernel(
    lens, q_ref, do_ref, k_ref, v_ref, kt_ref, lse_ref, del_ref, pay_ref, near_ref,
    dq_ref, dk_ref, dv_ref, far_ref, tot_ref, dka, dva, far, out, cs, cr, mid, ybuf, zbuf, s, v_sem,
):
    i = pl.program_id(1)
    step = pl.program_id(0) * 2 + i
    place = Place()
    summed = Sum(place, far, mid, ybuf, zbuf, None, FFN_CHUNK, s, v_sem)

    def chunk(ch):
        return slice(ch * FFN_CHUNK, (ch + 1) * FFN_CHUNK)

    def cross(ch):
        return send(out.at[chunk(ch), :], far.at[chunk(ch), :], cs.at[ch], cr.at[ch], place.across)

    def arrive(ch):
        cross(ch).wait_recv()
        both = near_ref[place.r, chunk(ch), :].astype(F32) + pay_ref[place.r, 0, chunk(ch), :].astype(F32)
        far[chunk(ch), :] = (both + far[chunk(ch), :].astype(F32)).astype(BF)

    @pl.when(step == 0)
    def _():
        meet(everyone(place))
        for ch in range(3):
            there = 1 - place.r
            both = near_ref[there, chunk(ch), :].astype(F32) + pay_ref[there, 0, chunk(ch), :].astype(F32)
            out[chunk(ch), :] = both.astype(BF)
            cross(ch).start()

    @pl.when(step == 2)
    def _():
        arrive(0)
        summed.half(0)

    @pl.when(step == 3)
    def _():
        summed.quarter(0)

    @pl.when(step == 4)
    def _():
        arrive(1)
        summed.half(1)
        tot_ref[0] = summed.collect(0)

    @pl.when(step == 5)
    def _():
        summed.quarter(1)

    k = k_ref[...]
    v = v_ref[...]
    rows = q_ref.shape[0]
    lane = lax.broadcasted_iota(jnp.int32, (rows, 128), 1)
    dk = dv = None
    for hh in range(2):
        mine = (lane < HD) == (hh == 0)
        q = jnp.where(mine, q_ref[...], jnp.zeros((), BF))
        do = jnp.where(mine, do_ref[...], jnp.zeros((), BF))
        p = jnp.exp2(nt(k, q) - lse_ref[0, hh : hh + 1, :])
        ds = (p * (nt(v, do) - del_ref[0, hh : hh + 1, :])).astype(BF)
        dv_one = nn(p.astype(BF), do)
        dk_one = nn(ds, q)
        dv = dv_one if dv is None else dv + dv_one
        dk = dk_one if dk is None else dk + dk_one
        dq_ref[hh * HD : (hh + 1) * HD, :] = (nn(kt_ref[hh * HD : (hh + 1) * HD, :], ds) * 0.125).astype(BF)

    @pl.when(i == 0)
    def _():
        dka[...] = dk
        dva[...] = dv

    @pl.when(step == 5)
    def _():
        arrive(2)
        far_ref[chunk(2), :] = far[chunk(2), :]
        tot_ref[1] = summed.collect(1)
        for ch in range(3):
            cross(ch).wait_send()
        for ch in range(2):
            summed.finish_sum(ch)

    @pl.when(i == pl.num_programs(1) - 1)
    def _():
        keep = row_ids(0, LMAX) < lens[place.r]
        dk_ref[...] = jnp.where(keep, (dka[...] + dk) * LN2, 0.0).astype(BF)
        dv_ref[...] = jnp.where(keep, dva[...] + dv, 0.0).astype(BF)


def attend_back(lens, qs, do, kd, vz, kt, lse, delta, pay, near):
    rows = 512
    mine = pl.BlockSpec((rows, 128), lambda p, i, lens: (i, p))
    pair = pl.BlockSpec((LMAX, 128), lambda p, i, lens: (0, p))
    stats = pl.BlockSpec((1, 8, rows), lambda p, i, lens: (p, 0, i))
    mine_pay = pl.BlockSpec(
        (2, 1, FFN_ROWS, HALF), lambda p, i, lens: (0, half_index(), 0, 0), pipeline_mode=pl.Buffered(1)
    )
    return pl.pallas_call(
        attend_back_kernel,
        grid_spec=pltpu.PrefetchScalarGridSpec(
            num_scalar_prefetch=1,
            grid=(3, ROWS // rows),
            in_specs=[mine, mine, pair, pair, pl.BlockSpec((128, LMAX), lambda p, i, lens: (p, 0)), stats, stats]
            + [mine_pay, once((2, FFN_ROWS, HALF))],
            out_specs=[pl.BlockSpec((128, rows), lambda p, i, lens: (p, i)), pair, pair]
            + [once((FFN_ROWS, HALF)), whole((2, FFN_CHUNK // 8, HALF))],
            scratch_shapes=[
                pltpu.VMEM((LMAX, 128), F32),
                pltpu.VMEM((LMAX, 128), F32),
                pltpu.VMEM((FFN_ROWS, HALF), BF),
                pltpu.VMEM((FFN_ROWS, HALF), BF),
                pltpu.SemaphoreType.DMA((3,)),
                pltpu.SemaphoreType.DMA((3,)),
            ]
            + Sum.scratch(FFN_CHUNK, 2),
        ),
        out_shape=[
            jax.ShapeDtypeStruct((HALF, ROWS), BF),
            jax.ShapeDtypeStruct((LMAX, HALF), BF),
            jax.ShapeDtypeStruct((LMAX, HALF), BF),
            jax.ShapeDtypeStruct((FFN_ROWS, HALF), BF),
            jax.ShapeDtypeStruct((2, FFN_CHUNK // 8, HALF), BF),
        ],
        **comm_params("attend_back", 5),
    )(lens, qs, do, kd, vz, kt, lse, delta, pay, near)


def norm_parts(x):
    xc = x - jnp.mean(x, axis=1, keepdims=True)
    inv = lax.rsqrt(jnp.mean(xc * xc, axis=1, keepdims=True) + EPS)
    return xc * inv, inv


def norm_back(up, normal, inv, gain):
    e = up * gain
    return inv * (e - jnp.mean(e, axis=1, keepdims=True) - normal * jnp.mean(e * normal, axis=1, keepdims=True))


def ffn_kernel(
    lens, ctx_ref, mix_ref, tok_ref, cot_ref, wd_ref, wi_ref, wo_ref, v0, v1, v2, v3, v4, v5, bi_ref, ones_ref,
    hid_ref, gpre_ref, gctx_ref, gcv_ref, del_ref, pay_ref, sm_ref, gbi_ref,
    act_s, gp_s, awd, awi, awo,
):
    i = pl.program_id(0)
    rows = ctx_ref.shape[0]
    keep = row_ids(half_index() * ROWS + i * rows, rows) < length(lens)

    @pl.when(i == 0)
    def _():
        awd[...] = jnp.zeros_like(awd)
        awi[...] = jnp.zeros_like(awi)
        awo[...] = jnp.zeros_like(awo)
        sm_ref[...] = jnp.zeros_like(sm_ref)
        gbi_ref[...] = jnp.zeros_like(gbi_ref)

    vectors = [line(ref) for ref in (v0, v1, v2, v3, v4, v5)]
    vec = lambda k: vectors[k]
    inter_bias = line(bi_ref)
    h = tok_ref[...].astype(F32)
    ctx = ctx_ref[...]
    mixed = jnp.concatenate([ctx, mix_ref[...]], axis=1)
    n1, inv1 = norm_parts(nn(mixed, wd_ref[...]) + vec(0) + h)
    f1 = n1 * vec(1) + vec(2)
    fl = f1.astype(BF)
    chunk = 512
    outs = []
    for g in range(2):
        fg = fl[:, g * HALF : (g + 1) * HALF]
        for ch in range(GW // chunk):
            cols = slice(ch * chunk, (ch + 1) * chunk)
            put = slice(g * GW + ch * chunk, g * GW + (ch + 1) * chunk)
            x = nn(fg, wi_ref[g, :, cols]) + inter_bias[:, put]
            phi = 0.5 + 0.5 * lax.erf(x * 0.7071067811865476)
            act_s[:, put] = (x * phi).astype(BF)
            gp_s[:, put] = phi + x * jnp.exp2(x * x * (-0.5 * LOG2E)) * 0.3989422804014327
        outs.append(nn(act_s[:, g * GW : (g + 1) * GW], wo_ref[g]))
    n2, inv2 = norm_parts(jnp.concatenate(outs, axis=1) + vec(3) + f1)
    hid_ref[...] = (n2 * vec(4) + vec(5)).astype(BF)
    u = jnp.where(keep, cot_ref[...].astype(F32), 0.0)
    gp2 = norm_back(u, n2, inv2, vec(4))
    go = gp2.astype(BF)
    got = go.T
    flt = fl.T
    gfs = []
    for g in range(2):
        sel = slice(g * HALF, (g + 1) * HALF)
        gf = gp2[:, sel]
        for ch in range(GW // chunk):
            cols = slice(ch * chunk, (ch + 1) * chunk)
            put = slice(g * GW + ch * chunk, g * GW + (ch + 1) * chunk)
            gi = (gp_s[:, put] * nt(go[:, sel], wo_ref[g, cols, :])).astype(BF)
            gbi_ref[0:1, put] += col_sum(gi.astype(F32))
            awo[g, :, cols] += nn(got[sel], act_s[:, put])
            awi[g, :, cols] += nn(flt[sel], gi)
            gf = gf + nt(gi, wi_ref[g, :, cols])
        gfs.append(gf)
    gf = jnp.concatenate(gfs, axis=1)
    gpre = norm_back(gf, n1, inv1, vec(1))
    gd = gpre.astype(BF)
    gpre_ref[...] = gd
    sm_ref[0:1, :] += col_sum(go.astype(F32))
    sm_ref[1:2, :] += col_sum(u * n2)
    sm_ref[2:3, :] += col_sum(u)
    sm_ref[3:4, :] += col_sum(gd.astype(F32))
    sm_ref[4:5, :] += col_sum(gf * n1)
    sm_ref[5:6, :] += col_sum(gf)
    awd[...] += nn(mixed.T, gd)
    gm = nt(gd, wd_ref[...])
    gctx = gm[:, :HALF].astype(BF)
    gctx_ref[...] = gctx
    gcv_ref[...] = gm[:, HALF:].astype(BF)
    prod = (gctx.astype(F32) * ctx.astype(F32)).astype(BF)
    del_ref[...] = nt(ones_ref[...], prod).reshape(3, 8, rows)

    @pl.when(i == pl.num_programs(0) - 1)
    def _():
        for r in range(2):
            for c in range(2):
                pay_ref[r, c, 0:HALF, :] = awi[r, :, c * D : c * D + HALF].astype(BF)
                pay_ref[r, c, HALF:D, :] = awi[r, :, c * D + HALF : (c + 1) * D].astype(BF)
                pay_ref[r, c, D : 2 * D, :] = awo[r, :, c * D : (c + 1) * D].T.astype(BF)
                for part in range(2):
                    piece = awd[part * HALF + c * 192 : part * HALF + (c + 1) * 192, r * HALF : (r + 1) * HALF]
                    pay_ref[r, c, 2 * D + part * 192 : 2 * D + (part + 1) * 192, :] = piece.astype(BF)


def ffn(lens, ctx, mix, tok, cot, wd, wi, wo, vectors, bi, ones24):
    rows = 256
    blk = lambda w: pl.BlockSpec((rows, w), lambda i, lens: (i, 0))
    return pl.pallas_call(
        ffn_kernel,
        grid_spec=pltpu.PrefetchScalarGridSpec(
            num_scalar_prefetch=1,
            grid=(ROWS // rows,),
            in_specs=[
                blk(HALF),
                blk(HALF),
                blk(D),
                blk(D),
                whole((D, D)),
                whole((2, HALF, GW)),
                whole((2, GW, HALF)),
                *[whole((D,))] * 6,
                whole((FF,)),
                whole((24, HALF)),
            ],
            out_specs=[
                blk(D),
                blk(D),
                blk(HALF),
                blk(HALF),
                pl.BlockSpec((3, 8, rows), lambda i, lens: (0, 0, i)),
                whole((2, 2, FFN_ROWS, HALF)),
                whole((8, D)),
                whole((1, FF)),
            ],
            scratch_shapes=[
                pltpu.VMEM((rows, FF), BF),
                pltpu.VMEM((rows, FF), F32),
                pltpu.VMEM((D, D), F32),
                pltpu.VMEM((2, HALF, GW), F32),
                pltpu.VMEM((2, HALF, GW), F32),
            ],
        ),
        out_shape=[
            jax.ShapeDtypeStruct((ROWS, D), BF),
            jax.ShapeDtypeStruct((ROWS, D), BF),
            jax.ShapeDtypeStruct((ROWS, HALF), BF),
            jax.ShapeDtypeStruct((ROWS, HALF), BF),
            jax.ShapeDtypeStruct((3, 8, ROWS), F32),
            jax.ShapeDtypeStruct((2, 2, FFN_ROWS, HALF), BF),
            jax.ShapeDtypeStruct((8, D), F32),
            jax.ShapeDtypeStruct((1, FF), F32),
        ],
        **params("ffn"),
    )(lens, ctx, mix, tok, cot, wd, wi, wo, *vectors, bi, ones24)


def conv_back_kernel(
    lens, gcv_ref, conv_ref, kp_ref, q_ref, pt_ref, wk_ref, spread_ref, ones_ref, pay_ref,
    gqm_ref, gpt_ref, gco_ref, gwk_ref, gbk_ref, near_ref, acc, wbuf, tbuf, ns, nr,
):
    i = pl.program_id(0)
    rows = gcv_ref.shape[0]
    wide = rows + 32
    p = Place()
    near = Near(p, pay_ref, near_ref, ns, nr)

    @pl.when(i == 0)
    def _():
        meet([p.core])
        near.start()
        acc[...] = jnp.zeros_like(acc)
        tbuf[...] = jnp.zeros_like(tbuf)
        gwk_ref[...] = jnp.zeros_like(gwk_ref)
        gbk_ref[...] = jnp.zeros_like(gbk_ref)

    gcv = gcv_ref[...].astype(F32)
    wbuf[...] = conv_ref[pl.ds(pl.multiple_of(i * rows, 16), wide), :].astype(F32)
    kp = kp_ref[...]
    kpt = kp.T.astype(BF)
    gkps = []
    total = jnp.zeros((wide, HALF), F32)
    for j in range(KW):
        prod = (gcv * wbuf[12 + j : 12 + j + rows, :]).astype(BF)
        gkps.append(nt(ones_ref[...], prod))
        tbuf[24 : 24 + rows, :] = nn(kpt, spread_ref[:, j * HALF : (j + 1) * HALF]) * gcv
        total = total + tbuf[12 - j : 12 - j + wide, :]
    acc[pl.ds(pl.multiple_of(p.c * ROWS + i * rows, 16), wide), :] += total
    gkp = jnp.concatenate(gkps, axis=0).reshape(KW, 8, rows)
    kp3 = kp.reshape(KW, 8, rows)
    inner = jnp.sum(kp3 * gkp, axis=0, keepdims=True)
    gl = (kp3 * (gkp - inner)).reshape(KW * 8, rows)
    gll = gl.astype(BF)
    glt = gl.T.astype(BF)
    gbk_ref[0:1, 0:72] += col_sum(glt.astype(F32))
    q = q_ref[...].astype(F32)
    pt = pt_ref[...].astype(F32)
    gwk_ref[...] += nn(gll, (pt * q).astype(BF))
    gmix = nn(glt, wk_ref[...])
    gqm_ref[...] = (gmix * pt).astype(BF)
    gpt_ref[...] = (gmix * q).astype(BF)

    @pl.when(i == pl.num_programs(0) - 1)
    def _():
        near.finish()
        keep = row_ids(0, LMAX) < lens[p.r]
        gco_ref[...] = jnp.where(keep, acc[16 : 16 + LMAX, :], 0.0).astype(BF)


def conv_back(lens, gcv, conv, kp, q, pt, wk72, spread, ones8, pay):
    rows = 256
    blk = pl.BlockSpec((rows, HALF), lambda i, lens: (i, 0))
    return pl.pallas_call(
        conv_back_kernel,
        grid_spec=pltpu.PrefetchScalarGridSpec(
            num_scalar_prefetch=1,
            grid=(ROWS // rows,),
            in_specs=[
                blk,
                whole((ROWS + 32, HALF)),
                pl.BlockSpec((72, rows), lambda i, lens: (0, i)),
                blk,
                blk,
                whole((72, HALF)),
                whole((72, KW * HALF)),
                whole((8, HALF)),
                HBM,
            ],
            out_specs=[blk, blk, whole((LMAX, HALF)), whole((72, HALF)), whole((8, 128)), HBM],
            scratch_shapes=[
                pltpu.VMEM((LMAX + 32, HALF), F32),
                pltpu.VMEM((rows + 32, HALF), F32),
                pltpu.VMEM((rows + 48, HALF), F32),
                pltpu.SemaphoreType.DMA((2,)),
                pltpu.SemaphoreType.DMA((2,)),
            ],
        ),
        out_shape=[
            jax.ShapeDtypeStruct((ROWS, HALF), BF),
            jax.ShapeDtypeStruct((ROWS, HALF), BF),
            jax.ShapeDtypeStruct((LMAX, HALF), BF),
            jax.ShapeDtypeStruct((72, HALF), F32),
            jax.ShapeDtypeStruct((8, 128), F32),
            jax.ShapeDtypeStruct((2, FFN_ROWS, HALF), BF),
        ],
        **comm_params("conv_back", 4),
    )(lens, gcv, conv, kp, q, pt, wk72, spread, ones8, pay)


def final_kernel(
    lens, seq_ref, dk_ref, dv_ref, gco_ref, dq_ref, gqm_ref, gpt_ref, gpre_ref, dep_ref, w_ref, wdep_ref,
    smf_ref, gbi_ref, gwk_ref, gbk_ref, far_ref, tot_ref, hid_ref,
    gh_ref, pay_ref, sum_ref, out_ref, hbuf, gacc, agw, wbuf, dbuf, sm, gdp, total_sum, mid, ybuf, zbuf, s, v, ls, hs, hr,
):
    i = pl.program_id(0)
    rows = dk_ref.shape[0]
    wide = rows + 32
    p = Place()
    b = lax.rem(p.c * 2 + i, 4)
    n = lens[p.r]
    summed = Sum(p, far_ref, mid, ybuf, zbuf, total_sum, FFN_CHUNK, s, v)
    place = FromRows(p, hid_ref, out_ref, ls, hs, hr)

    @pl.when(i == 0)
    def _():
        meet(everyone(p))
        summed.half(2)
        place.start()
        for ch in range(2):
            summed.along(ch, tot_ref[ch])

    @pl.when(i == 1)
    def _():
        summed.quarter(2)
        for ch in range(2):
            summed.back(ch)

    @pl.when(i == 2)
    def _():
        summed.along(2, summed.collect(2))

    @pl.when(i == 3)
    def _():
        summed.back(2)

    @pl.when(i == 0)
    def _():
        hbuf[0:16, :] = jnp.zeros((16, D), F32)
        hbuf[16 + LMAX :, :] = jnp.zeros((16, D), F32)
        for k in range(4):
            keep = row_ids(k * rows, rows) < n
            hbuf[16 + k * rows : 16 + (k + 1) * rows, :] = jnp.where(
                keep, seq_ref[PAD + k * rows : PAD + (k + 1) * rows, :].astype(F32), 0.0
            )
        gacc[...] = jnp.zeros_like(gacc)
        agw[...] = jnp.zeros_like(agw)
        dbuf[...] = jnp.zeros_like(dbuf)
        sm[...] = jnp.zeros_like(sm)
        gdp[...] = jnp.zeros_like(gdp)

    start = pl.multiple_of(b * rows, 16)
    here = pl.ds(pl.multiple_of(b * rows + 16, 16), rows)
    h = hbuf[here, :].astype(BF)
    dk, dv, gco = dk_ref[...], dv_ref[...], gco_ref[...]
    gacc[here, :] += nn(dk, w_ref[0]) + nn(dv, w_ref[1]) + nn(gco, w_ref[2])
    agw[0] += nn(dk.T, h)
    agw[1] += nn(dv.T, h)
    agw[2] += nn(gco.T, h)
    sm[1:2, :] += col_sum(dv.astype(F32))
    sm[2:3, :] += col_sum(gco.astype(F32))

    @pl.when(i < 2)
    def _():
        gqt = dq_ref[...].astype(F32) + gqm_ref[...].astype(F32).T
        gqt = gqt.astype(BF)
        gq = gqt.T
        gpt = gpt_ref[...]
        sm[0:1, :] += col_sum(gq.astype(F32))
        sm[3:4, :] += col_sum(gpt.astype(F32))
        agw[3] += nn(gqt, h)
        agw[4] += nn(gpt.T, dep_ref[...])
        gacc[here, :] += nn(gq, w_ref[3]) + gpre_ref[...].astype(F32)
        gdep = nn(gpt, w_ref[4])
        wbuf[...] = hbuf[pl.ds(start, wide), :]
        dbuf[24 : 24 + rows, :] = gdep
        total = jnp.zeros((wide, D), F32)
        wdep = wdep_ref[...].astype(F32)
        for j in range(KW):
            gdp[j : j + 1, :] += col_sum(gdep * wbuf[12 + j : 12 + j + rows, :])
            total = total + dbuf[12 - j : 12 - j + wide, :] * wdep[j : j + 1, :]
        gacc[pl.ds(start, wide), :] += total

    @pl.when(i == pl.num_programs(0) - 1)
    def _():
        keep = row_ids(0, LMAX) < n
        gh_ref[...] = jnp.where(keep, gacc[16 : 16 + LMAX, :], 0.0).astype(BF)
        for r in range(2):
            for c in range(2):
                for j in range(5):
                    piece = agw[j, c * 192 : (c + 1) * 192, r * HALF : (r + 1) * HALF]
                    pay_ref[r, c, j * 192 : (j + 1) * 192, :] = piece.astype(BF)
        zeros = lambda k: jnp.zeros((k, HALF), F32)
        pay_ref[0, 0, 960:, :] = gwk_ref[0:64, :].astype(BF)
        bias = jnp.concatenate([gbk_ref[...], jnp.zeros((8, 256), F32)], axis=1)
        pay_ref[0, 1, 960:, :] = jnp.concatenate([gwk_ref[64:72, :], sm[...], bias, zeros(40)], axis=0).astype(BF)
        inter = jnp.concatenate([gbi_ref[:, k * HALF : (k + 1) * HALF] for k in range(8)], axis=0)
        pay_ref[1, 0, 960:, :] = jnp.concatenate(
            [smf_ref[:, 0:HALF], smf_ref[:, HALF:D], inter, zeros(40)], axis=0
        ).astype(BF)
        pay_ref[1, 1, 960:, :] = jnp.concatenate([gdp[:, 0:HALF], gdp[:, HALF:D], zeros(32)], axis=0).astype(BF)
        summed.finish_sum(2)
        for ch in range(3):
            summed.finish_spread(ch)
        sum_ref[...] = total_sum[...]
        place.finish()


def final(lens, seq_tok, dk, dv, gco, dq, gqm, gpt, gpre, dep, w5, wdep, smf, gbi, gwk, gbk, far, tot, hid):
    rows = 512
    seq = pl.BlockSpec((rows, HALF), lambda i, lens: (lax.rem(half_index() * 2 + i, 4), 0))
    own = lambda w: pl.BlockSpec((rows, w), lambda i, lens: (jnp.minimum(i, 1), 0))
    return pl.pallas_call(
        final_kernel,
        grid_spec=pltpu.PrefetchScalarGridSpec(
            num_scalar_prefetch=1,
            grid=(LMAX // rows,),
            in_specs=[
                once((LMAX + 2 * PAD, D)),
                seq,
                seq,
                seq,
                pl.BlockSpec((HALF, rows), lambda i, lens: (0, jnp.minimum(i, 1))),
                own(HALF),
                own(HALF),
                own(D),
                own(D),
                once((5, HALF, D)),
                whole((KW, D)),
                whole((8, D)),
                whole((1, FF)),
                whole((72, HALF)),
                whole((8, 128)),
                once((FFN_ROWS, HALF)),
                whole((2, FFN_CHUNK // 8, HALF)),
                once((ROWS, D)),
            ],
            out_specs=[once((LMAX, D)), once((2, 2, PROJ_ROWS, HALF)), once((FFN_ROWS, HALF)), HBM],
            scratch_shapes=[
                pltpu.VMEM((LMAX + 32, D), F32),
                pltpu.VMEM((LMAX + 32, D), F32),
                pltpu.VMEM((5, HALF, D), F32),
                pltpu.VMEM((rows + 32, D), F32),
                pltpu.VMEM((rows + 48, D), F32),
                pltpu.VMEM((8, HALF), F32),
                pltpu.VMEM((16, D), F32),
                pltpu.VMEM((FFN_ROWS, HALF), BF),
                *Sum.scratch(FFN_CHUNK, 3),
                pltpu.SemaphoreType.DMA,
                pltpu.SemaphoreType.DMA((2,)),
                pltpu.SemaphoreType.DMA((3,)),
            ],
        ),
        out_shape=[
            jax.ShapeDtypeStruct((LMAX, D), BF),
            jax.ShapeDtypeStruct((2, 2, PROJ_ROWS, HALF), BF),
            jax.ShapeDtypeStruct((FFN_ROWS, HALF), BF),
            jax.ShapeDtypeStruct((LMAX, HALF), BF),
        ],
        **comm_params("final", 6),
    )(lens, seq_tok, dk, dv, gco, dq, gqm, gpt, gpre, dep, w5, wdep, smf, gbi, gwk, gbk, far, tot, hid)


def end_kernel(
    pay, gh_ref, ght, sum_ref, small_ref, small, total_sum, near, far, out, mid, ybuf, zbuf, s, v, ns, nr, cs, cr, ghn, gho, es, er, ls, hs, hr
):
    p = Place()
    r, c = p.r, p.c
    meet(everyone(p))
    rows = PROJ_ROWS // 2
    summed = Sum(p, far, mid, ybuf, zbuf, total_sum, rows, s, v)

    def part(ch):
        return slice(ch * rows, (ch + 1) * rows)

    def beside(n, ch):
        rr = 1 - r if n == 0 else r
        k = n * 2 + ch
        return send(pay.at[rr, 1 - c, part(ch), :], near.at[rr, part(ch), :], ns.at[k], nr.at[k], p.core)

    def cross(ch):
        return send(out.at[part(ch), :], far.at[part(ch), :], cs.at[ch], cr.at[ch], p.across)

    for n in range(2):
        for ch in range(2):
            beside(n, ch).start()
    theirs = send(gh_ref.at[rows_at((1 - c) * ROWS, ROWS), :], ghn, es.at[0], er.at[0], p.core)
    theirs.start()
    back = FromRows(p, gho, ght, ls, hs, hr)
    for ch in range(2):
        beside(0, ch).wait_recv()
        both = near[1 - r, part(ch), :].astype(F32) + pay[1 - r, c, part(ch), :].astype(F32)
        out[part(ch), :] = both.astype(BF)
        cross(ch).start()
    theirs.wait_recv()
    gho[...] = (gh_ref[rows_at(c * ROWS, ROWS), :].astype(F32) + ghn[...].astype(F32)).astype(BF)
    back.start()
    for ch in range(2):
        beside(1, ch).wait_recv()
        cross(ch).wait_recv()
        both = near[r, part(ch), :].astype(F32) + pay[r, c, part(ch), :].astype(F32)
        far[part(ch), :] = (both + far[part(ch), :].astype(F32)).astype(BF)
        summed.half(ch)
    for ch in range(2):
        summed.quarter(ch)
    for ch in range(2):
        summed.along(ch, summed.collect(ch))
    for ch in range(2):
        summed.back(ch)
    for ch in range(2):
        summed.finish_spread(ch)
    own = total_sum.at[960:PROJ_ROWS, :]
    moves = [
        send(own, small.at[r * 2 + c], es.at[1 + n], er.at[1 + n], device)
        for n, device in enumerate((p.across, p.core, p.diagonal))
    ]
    for move in moves:
        move.start()
    small[r * 2 + c] = total_sum[960:PROJ_ROWS, :]
    sum_ref[...] = total_sum[...]
    for ch in range(2):
        summed.finish_sum(ch)
        cross(ch).wait_send()
        for n in range(2):
            beside(n, ch).wait_send()
    for n, (rr, cc) in enumerate(((1 - r, c), (r, 1 - c), (1 - r, 1 - c))):
        send(own, small.at[rr * 2 + cc], es.at[1 + n], er.at[1 + n], p.core).wait_recv()
    for move in moves:
        move.wait_send()
    theirs.wait_send()
    small_ref[...] = small[...]
    back.finish()


def end(pay, gh):
    return pl.pallas_call(
        end_kernel,
        in_specs=[VMEM, VMEM],
        out_specs=[HBM, VMEM, VMEM],
        out_shape=[
            jax.ShapeDtypeStruct((LMAX, HALF), BF),
            jax.ShapeDtypeStruct((PROJ_ROWS, HALF), BF),
            jax.ShapeDtypeStruct((4, 64, HALF), BF),
        ],
        scratch_shapes=[
            pltpu.VMEM((4, 64, HALF), BF),
            pltpu.VMEM((PROJ_ROWS, HALF), BF),
            pltpu.VMEM((2, PROJ_ROWS, HALF), BF),
            pltpu.VMEM((PROJ_ROWS, HALF), BF),
            pltpu.VMEM((PROJ_ROWS, HALF), BF),
            *Sum.scratch(PROJ_ROWS // 2, 2),
            pltpu.SemaphoreType.DMA((4,)),
            pltpu.SemaphoreType.DMA((4,)),
            pltpu.SemaphoreType.DMA((2,)),
            pltpu.SemaphoreType.DMA((2,)),
            pltpu.VMEM((ROWS, D), BF),
            pltpu.VMEM((ROWS, D), BF),
            pltpu.SemaphoreType.DMA((4,)),
            pltpu.SemaphoreType.DMA((4,)),
            pltpu.SemaphoreType.DMA,
            pltpu.SemaphoreType.DMA((2,)),
            pltpu.SemaphoreType.DMA((3,)),
        ],
        **comm_params("end", 7),
    )(pay, gh)


def outputs_kernel(
    ght, hid, total, big, small, perm_ref,
    hid_ref, gt_ref, gq_ref, gk_ref, gv_ref, gc_ref, gp_ref, gdep_ref, gbq_ref, gbv_ref, gbc_ref, gbp_ref, gwk_ref, gbk_ref,
    gd_ref, gbd_ref, gg1_ref, gb1_ref, gi_ref, gbi_ref, go_ref, gbo_ref, gg2_ref, gb2_ref,
):
    hid_ref[...] = hid[...]
    gt_ref[...] = ght[...].astype(F32)

    @pl.when(pl.program_id(0) == 0)
    def _():
        for j, ref in enumerate((gk_ref, gv_ref, gc_ref, gq_ref, gp_ref)):
            ref[...] = total[j * 192 : (j + 1) * 192, :].astype(F32)
        gi_ref[:, 0:HALF] = big[0:HALF, :].astype(F32)
        gi_ref[:, HALF:D] = big[HALF:D, :].astype(F32)
        go_ref[...] = big[D : 2 * D, :].astype(F32)
        gd_ref[...] = big[2 * D :, :].astype(F32)
        tail = small[1].astype(F32)
        norms = small[2].astype(F32)
        depth = small[3].astype(F32)
        kernel_grad = jnp.concatenate([small[0].astype(F32), tail[0:8]], axis=0).astype(BF)
        gwk_ref[...] = nn(perm_ref[...], kernel_grad)
        bias = nt(tail[16:24, 0:72].astype(BF), perm_ref[...])
        gbk_ref[...] = bias[0:1, :].reshape(54)
        for k, ref in enumerate((gbq_ref, gbv_ref, gbc_ref, gbp_ref)):
            ref[...] = tail[8 + k : 9 + k, :].reshape(HALF)
        for k, ref in enumerate((gbo_ref, gg2_ref, gb2_ref, gbd_ref, gg1_ref, gb1_ref)):
            ref[...] = jnp.concatenate([norms[k : k + 1, :], norms[8 + k : 9 + k, :]], axis=1).reshape(D)
        gbi_ref[...] = jnp.concatenate([norms[16 + k : 17 + k, :] for k in range(8)], axis=1).reshape(FF)
        gdep_ref[:, 0:HALF] = depth[0:KW, :]
        gdep_ref[:, HALF:D] = depth[16 : 16 + KW, :]


def outputs(ght, hid, total, big, small, perm):
    rows = 512
    blk = pl.BlockSpec((rows, HALF), lambda i: (i, 0))
    shapes = [(192, HALF)] * 5 + [(KW, D)] + [(HALF,)] * 4 + [(54, HALF), (54,), (HALF, HALF)] + [(D,)] * 3
    shapes += [(HALF, D), (FF,), (D, HALF)] + [(D,)] * 3
    return pl.pallas_call(
        outputs_kernel,
        grid=(LMAX // rows,),
        in_specs=[
            blk,
            blk,
            whole((PROJ_ROWS, HALF)),
            whole((FFN_ROWS, HALF)),
            whole((4, 64, HALF)),
            whole((54, 72)),
        ],
        out_specs=[blk, blk] + [whole(shape) for shape in shapes],
        out_shape=[jax.ShapeDtypeStruct((LMAX, HALF), BF), jax.ShapeDtypeStruct((LMAX, HALF), F32)]
        + [jax.ShapeDtypeStruct(shape, F32) for shape in shapes],
        **params("outputs"),
    )(ght, hid, total, big, small, perm)


def constants():
    spread = np.zeros((72, KW * HALF), np.float32)
    ones8 = np.zeros((8, HALF), np.float32)
    ones24 = np.zeros((24, HALF), np.float32)
    perm = np.zeros((72, 54), np.float32)
    for head in range(6):
        cols = slice(head * HD, (head + 1) * HD)
        ones8[head, cols] = 1
        ones24[head // 2 * 8 + head % 2, cols] = 1
        for j in range(KW):
            spread[j * 8 + head, j * HALF + head * HD : j * HALF + (head + 1) * HD] = 1
            perm[j * 8 + head, head * KW + j] = 1
    return [jnp.asarray(a, BF) for a in (spread, ones8, ones24, perm)]


def per_device(
    groups, tokens, cotangent, seq_lengths, w_query, w_key, w_value, w_convout, w_point, w_depth,
    b_query, b_value, b_convout, b_point, w_kernel, b_kernel, w_dense, b_dense, gain_one, bias_one,
    w_inter, b_inter, w_output, b_output, gain_two, bias_two,
):
    lens = seq_lengths
    spread, ones8, ones24, perm = constants()
    wdep = w_depth.T

    seq, w5, wk72, bk72 = start(
        tokens, (w_key.T, w_value.T, w_convout.T, w_query.T, w_point.T), w_kernel.T, b_kernel, perm
    )
    kd, kt, vz, q, qs, pt, kp, conv, mix, dep, hown, wi, wd, cot = front(
        lens, seq, w5, wdep, b_value, b_convout, b_query, b_point, wk72, bk72, spread,
        w_inter[0], w_dense.reshape(2, 192, HALF), cotangent,
    )
    ctx, lse, wo = attend(lens, qs, kd, vz, w_output[0])
    vectors = (b_dense, gain_one, bias_one, b_output, gain_two, bias_two)
    hid, gpre, gctx, gcv, delta, payf, smf, gbi = ffn(
        lens, ctx, mix, hown, cot, wd.reshape(D, D), wi, wo, vectors, b_inter, ones24
    )
    gqm, gpt, gco, gwk, gbk, near = conv_back(lens, gcv, conv, kp, q, pt, wk72, spread, ones8, payf)
    dq, dk, dv, far, tot = attend_back(lens, qs, gctx, kd, vz, kt, lse, delta, payf, near)
    gh, pay5, big, hid = final(
        lens, seq, dk, dv, gco, dq, gqm, gpt, gpre, dep, w5, wdep, smf, gbi, gwk, gbk, far, tot, hid
    )
    ght, total, small = end(pay5, gh)
    if groups > 8:
        total, big, small = lax.psum(tuple(x.astype(F32) * 0.125 for x in (total, big, small)), "dp")
        total, big, small = total.astype(BF), big.astype(BF), small.astype(BF)
    (
        hidden_out, gt, gq, gk, gv, gc, gp, gdep, gbq, gbv, gbc, gbp, gwk, gbk, gd, gbd, gg1, gb1, gi, gbi, go, gbo, gg2, gb2,
    ) = outputs(ght, hid, total, big, small, perm.T)
    return (
        hidden_out, gt, gq.T, gk.T, gv.T, gc.T, gp.T, gdep.T, gbq, gbv, gbc, gbp, gwk.T, gbk, gd, gbd, gg1, gb1,
        gi[None], gbi, go[None], gbo, gg2, gb2,
    )


def solution(mesh):
    act = P(("dp", "col"), "row")
    rep = P()
    proj = P("row", "col")
    in_specs = (
        act, act, P("dp"), proj, proj, proj, proj, proj, rep, rep, rep, rep, rep, rep, rep, P("col", "row"),
        rep, rep, rep, P("row", None, "col"), rep, P("row", "col", None), rep, rep, rep,
    )
    out_specs = (
        act, act, proj, proj, proj, proj, proj, rep, rep, rep, rep, rep, rep, rep, P("col", "row"),
        rep, rep, rep, P("row", None, "col"), rep, P("row", "col", None), rep, rep, rep,
    )
    return jax.shard_map(
        functools.partial(per_device, mesh.shape["dp"]), mesh=mesh, in_specs=in_specs, out_specs=out_specs, check_vma=False)
```

```python
import functools

import jax
import jax.numpy as jnp
import numpy as np
from jax import lax
from jax.experimental import pallas as pl
from jax.experimental.pallas import tpu as pltpu
from jax.sharding import PartitionSpec as P

D = 768
HALF = 384
HD = 64
KW = 9
FF = 3072
GW = 1536
LMAX = 2048
ROWS = 1024
EPS = 1e-12
LOG2E = 1.4426950408889634
LN2 = 0.6931471805599453
BF = jnp.bfloat16
F32 = jnp.float32
VMEM_BYTES = 63 * 1024 * 1024
PAD = 16
FFN_ROWS = 1920
FFN_CHUNK = 640
PROJ_ROWS = 1024
MESH = pl.DeviceIdType.MESH
HBM = pl.BlockSpec(memory_space=pl.ANY)
VMEM = pl.BlockSpec(memory_space=pltpu.VMEM)


def nn(a, b):
    return lax.dot_general(a, b, (((1,), (0,)), ((), ())), preferred_element_type=F32)


def nt(a, b):
    return lax.dot_general(a, b, (((1,), (1,)), ((), ())), preferred_element_type=F32)


def col_sum(x):
    return jnp.sum(x, axis=0, keepdims=True)


def row_ids(start, rows):
    return start + lax.broadcasted_iota(jnp.int32, (rows, 1), 0)


def whole(shape):
    return pl.BlockSpec(shape, lambda *_: (0,) * len(shape))


def once(shape):
    return pl.BlockSpec(shape, lambda *_: (0,) * len(shape), pipeline_mode=pl.Buffered(1))


def half_index():
    return lax.axis_index("col")


def length(lens):
    return lens[lax.axis_index("row")]


def line(ref):
    return ref[...].astype(F32).reshape(1, ref.shape[0])


def params(name):
    return dict(
        name=name,
        compiler_params=pltpu.CompilerParams(vmem_limit_bytes=VMEM_BYTES),
    )


def lanes(k, width=HALF):
    return pl.ds(pl.multiple_of(k * width, 128), width)


def rows_at(start, count, step=16):
    return pl.ds(pl.multiple_of(start, step), count)


def send(src, dst, send_sem, recv_sem, device):
    return pltpu.make_async_remote_copy(
        src_ref=src, dst_ref=dst, send_sem=send_sem, recv_sem=recv_sem, device_id=device, device_id_type=MESH
    )


class Place:
    def __init__(self):
        self.d = lax.axis_index("dp")
        self.r = lax.axis_index("row")
        self.c = lax.axis_index("col")
        self.k = lax.rem(self.d, 8)
        self.base = self.d - self.k
        self.y = lax.rem(self.k, 2)
        self.z = lax.div(self.k, 2)
        self.beside = {"dp": self.base + self.z * 2 + 1 - self.y}
        self.across = {"row": 1 - self.r}
        self.core = {"col": 1 - self.c}
        self.diagonal = {"row": 1 - self.r, "col": 1 - self.c}

    def eight(self, offset):
        other = lax.rem(self.k + offset, 8)
        return other, {"dp": self.base + other}

    def four(self, offset):
        other = lax.rem(self.z + offset, 4)
        return other, {"dp": self.base + other * 2 + self.y}


def meet(devices):
    barrier = pltpu.get_barrier_semaphore()
    for device in devices:
        pl.semaphore_signal(barrier, inc=1, device_id=device, device_id_type=MESH)
    pl.semaphore_wait(barrier, len(devices))


def comm_params(name, number):
    return dict(
        name=name,
        compiler_params=pltpu.CompilerParams(
            vmem_limit_bytes=VMEM_BYTES, collective_id=number, has_side_effects=True
        ),
    )


class Gather:
    def __init__(self, place, own, full, part, block, send_sem, recv_sem, first):
        self.p, self.own, self.full, self.part, self.block = place, own, full, part, block
        self.s, self.v, self.f = send_sem, recv_sem, first

    def _move(self, src, dst, n, device):
        return send(src, dst, self.s.at[self.f + n], self.v.at[self.f + n], device)

    def _cross(self, r):
        p = self.p
        return self._move(self.part(self.own, p.z), self.block(self.full, r, p.c, p.z), 0, p.across)

    def _near(self, c):
        p = self.p
        return self._move(self.own, self.block(self.full, p.r, c, None), 1, p.core)

    def _pass(self, offset, z):
        p = self.p
        _, device = p.four(offset)
        here = self.block(self.full, 1 - p.r, p.c, z)
        return self._move(here, here, 1 + offset, device)

    def _last(self, c):
        p = self.p
        here = self.block(self.full, 1 - p.r, c, None)
        return self._move(here, here, 5, p.core)

    def relay(self):
        p = self.p
        self._cross(1 - p.r).wait_recv()
        for offset in (1, 2, 3):
            self._pass(offset, p.z).start()

    def share(self):
        p = self.p
        for offset in (1, 2, 3):
            back = lax.rem(p.z + 4 - offset, 4)
            self._pass(offset, back).wait_recv()
        self._last(p.c).start()

    def finish(self):
        p = self.p
        self._last(1 - p.c).wait_recv()
        self._near(1 - p.c).wait_recv()
        self._cross(p.r).wait_send()
        self._near(p.c).wait_send()
        for offset in (1, 2, 3):
            self._pass(offset, p.z).wait_send()
        self._last(p.c).wait_send()


def proj_part(ref, z):
    return ref.at[:, rows_at(z * 48, 48), :]


def proj_block(ref, r, c, z):
    if z is None:
        return ref.at[:, rows_at(c * 192, 192), lanes(r)]
    return ref.at[:, rows_at(c * 192 + z * 48, 48), lanes(r)]


def inter_part(ref, z):
    return ref.at[rows_at(z * 96, 96), :]


def inter_block(ref, r, c, z):
    if z is None:
        return ref.at[r, :, lanes(c, 768)]
    return ref.at[r, rows_at(z * 96, 96), lanes(c, 768)]


def output_part(ref, z):
    return ref.at[rows_at(z * 192, 192), :]


def output_block(ref, r, c, z):
    if z is None:
        return ref.at[r, rows_at(c * 768, 768), :]
    return ref.at[r, rows_at(c * 768 + z * 192, 192), :]


def dense_part(ref, z):
    return ref.at[lax.div(z, 2), rows_at(lax.rem(z, 2) * 96, 96), :]


def dense_block(ref, r, c, z):
    if z is None:
        return ref.at[:, rows_at(c * 192, 192), lanes(r)]
    return ref.at[lax.div(z, 2), rows_at(c * 192 + lax.rem(z, 2) * 96, 96), lanes(r)]


def start_kernel(
    tok_ref, wk_ref, wv_ref, wc_ref, wq_ref, wp_ref, kern_ref, kb_ref, perm_ref,
    seq_ref, w5_ref, k72_ref, b72_ref, own, stage, lsem, ts, tr, gs, gr,
):
    p = Place()
    r, c = p.r, p.c
    for j, ref in enumerate((wk_ref, wv_ref, wc_ref, wq_ref, wp_ref)):
        own[j] = ref[...]
    keep = pltpu.make_async_copy(own, proj_block(w5_ref, r, c, None), lsem.at[0])
    keep.start()
    load = pltpu.make_async_copy(tok_ref, stage, lsem.at[1])
    store = pltpu.make_async_copy(stage, seq_ref.at[PAD : PAD + LMAX, lanes(r)], lsem.at[2])
    load.start()
    meet([p.across, p.core, p.diagonal] + [p.four(o)[1] for o in (1, 2, 3)])
    gather = Gather(p, own, w5_ref, proj_part, proj_block, gs, gr, 0)

    def chunk(m, k):
        return seq_ref.at[PAD + m * 512 : PAD + (m + 1) * 512, lanes(k)]

    def cross(m, k):
        return send(tok_ref.at[m * 512 : (m + 1) * 512, :], chunk(m, k), ts.at[m], tr.at[m], {"row": 1 - r, "col": m // 2})

    def near(k):
        return send(tok_ref, seq_ref.at[PAD : PAD + LMAX, lanes(k)], ts.at[4], tr.at[4], p.core)

    def forward(m):
        return send(chunk(m, 1 - r), chunk(m, 1 - r), ts.at[5 + m], tr.at[5 + m], p.core)

    gather._cross(r).start()
    gather._near(c).start()

    @pl.when(r != c)
    def _():
        for m in (0, 2, 1, 3):
            cross(m, r).start()

    load.wait()

    @pl.when(r == c)
    def _():
        near(r).start()
        store.start()

    k72_ref[...] = nn(perm_ref[...], kern_ref[...]).astype(BF)
    bias = jnp.broadcast_to(line(kb_ref), (128, 54)).astype(BF)
    b72_ref[...] = nt(perm_ref[...], bias)
    gather.relay()
    for q in range(2):

        @pl.when(c == q)
        def _():
            for m in (2 * q, 2 * q + 1):
                cross(m, 1 - r).wait_recv()
                forward(m).start()

    gather.share()
    for q in range(2):

        @pl.when(c == q)
        def _():
            for m in (2 - 2 * q, 3 - 2 * q):
                forward(m).wait_recv()
            for m in (2 * q, 2 * q + 1):
                forward(m).wait_send()

    @pl.when(r != c)
    def _():
        for m in range(4):
            cross(m, r).wait_send()
        near(r).wait_recv()

    @pl.when(r == c)
    def _():
        near(r).wait_send()
        store.wait()

    keep.wait()
    gather.finish()


def start(tokens, weights, w_kernel, b_kernel, perm):
    return pl.pallas_call(
        start_kernel,
        in_specs=[HBM] + [VMEM] * 8,
        out_specs=[HBM, HBM, VMEM, VMEM],
        out_shape=[
            jax.ShapeDtypeStruct((LMAX + 2 * PAD, D), BF),
            jax.ShapeDtypeStruct((5, HALF, D), BF),
            jax.ShapeDtypeStruct((72, HALF), BF),
            jax.ShapeDtypeStruct((72, 128), F32),
        ],
        scratch_shapes=[
            pltpu.VMEM((5, 192, HALF), BF),
            pltpu.VMEM((LMAX, HALF), BF),
            pltpu.SemaphoreType.DMA((3,)),
            pltpu.SemaphoreType.DMA((9,)),
            pltpu.SemaphoreType.DMA((9,)),
            pltpu.SemaphoreType.DMA((6,)),
            pltpu.SemaphoreType.DMA((6,)),
        ],
        **comm_params("start", 1),
    )(tokens, *weights, w_kernel, b_kernel, perm)


class ToRows:
    def __init__(self, place, src, dst, local_sem, send_sem, recv_sem):
        self.p, self.src, self.dst = place, src, dst
        self.l, self.s, self.v = local_sem, send_sem, recv_sem

    def _cross(self, q, k):
        half = self.src.at[q * ROWS : (q + 1) * ROWS, :]
        return send(half, self.dst.at[:, lanes(k)], self.s.at[q], self.v.at[0], {"row": 1 - self.p.r, "col": q})

    def _near(self):
        p = self.p
        half = self.src.at[rows_at((1 - p.c) * ROWS, ROWS), :]
        return send(half, self.dst.at[:, lanes(p.r)], self.s.at[2], self.v.at[1], p.core)

    def _local(self):
        p = self.p
        half = self.src.at[rows_at(p.c * ROWS, ROWS), :]
        return pltpu.make_async_copy(half, self.dst.at[:, lanes(p.r)], self.l)

    def start(self):
        p = self.p

        @pl.when(p.r != p.c)
        def _():
            self._cross(0, p.r).start()
            self._cross(1, p.r).start()

        @pl.when(p.r == p.c)
        def _():
            self._near().start()
            self._local().start()

    def finish(self):
        p = self.p
        self._cross(0, 1 - p.r).wait_recv()

        @pl.when(p.r != p.c)
        def _():
            self._cross(0, p.r).wait_send()
            self._cross(1, p.r).wait_send()
            self._near().wait_recv()

        @pl.when(p.r == p.c)
        def _():
            self._near().wait_send()
            self._local().wait()


class FromRows:
    def __init__(self, place, src, dst, local_sem, send_sem, recv_sem):
        self.p, self.src, self.dst = place, src, dst
        self.l, self.s, self.v = local_sem, send_sem, recv_sem

    def _cross(self, q):
        p = self.p
        place = self.dst.at[q]
        return send(self.src.at[:, lanes(1 - p.r)], place, self.s.at[0], self.v.at[q], {"row": 1 - p.r, "col": p.r})

    def _near(self, q):
        p = self.p
        place = self.dst.at[q]
        return send(self.src.at[:, lanes(p.r)], place, self.s.at[1], self.v.at[2], p.core)

    def _local(self):
        p = self.p
        place = self.dst.at[p.c]
        return pltpu.make_async_copy(self.src.at[:, lanes(p.r)], place, self.l)

    def start(self):
        p = self.p
        self._cross(p.c).start()

        @pl.when(p.r != p.c)
        def _():
            self._near(p.c).start()

        @pl.when(p.r == p.c)
        def _():
            self._local().start()

    def finish(self):
        p = self.p
        self._cross(p.c).wait_send()

        @pl.when(p.r != p.c)
        def _():
            self._near(p.c).wait_send()
            self._cross(0).wait_recv()
            self._cross(1).wait_recv()

        @pl.when(p.r == p.c)
        def _():
            self._near(1 - p.c).wait_recv()
            self._local().wait()


class Sum:
    def __init__(self, place, far, mid, ybuf, zbuf, total, rows, s, v, first=0):
        self.p, self.far, self.mid, self.ybuf, self.zbuf, self.total = place, far, mid, ybuf, zbuf, total
        self.rows, self.s, self.v, self.first = rows, s, v, first

    def _sems(self, ch, n):
        i = self.first + ch * 8 + n
        return self.s.at[i], self.v.at[i]

    def _beside(self):
        return self.p.beside

    def _halves(self, ch, y):
        return rows_at(ch * self.rows + y * (self.rows // 2), self.rows // 2)

    def _piece(self, ch, z):
        return rows_at(ch * self.rows + self.p.y * (self.rows // 2) + z * (self.rows // 8), self.rows // 8)

    def _half(self, ch):
        return send(self.far.at[self._halves(ch, 1 - self.p.y), :], self.ybuf.at[ch], *self._sems(ch, 0), self._beside())

    def _quarter(self, ch, offset):
        other, device = self.p.four(offset)
        src = self.mid.at[ch, rows_at(other * (self.rows // 8), self.rows // 8), :]
        return send(src, self.zbuf.at[ch, offset - 1], *self._sems(ch, offset), device)

    def _along(self, ch, offset, z):
        _, device = self.p.four(offset)
        here = self.total.at[self._piece(ch, z), :]
        return send(here, here, *self._sems(ch, 3 + offset), device)

    def _back(self, ch, y):
        here = self.total.at[self._halves(ch, y), :]
        return send(here, here, *self._sems(ch, 7), self._beside())

    def half(self, ch):
        self._half(ch).start()

    def quarter(self, ch):
        self._half(ch).wait_recv()
        both = self.far[self._halves(ch, self.p.y), :].astype(F32) + self.ybuf[ch].astype(F32)
        self.mid[ch] = both.astype(BF)
        for offset in (1, 2, 3):
            self._quarter(ch, offset).start()

    def collect(self, ch):
        both = self.mid[ch, rows_at(self.p.z * (self.rows // 8), self.rows // 8), :].astype(F32)
        for offset in (1, 2, 3):
            self._quarter(ch, offset).wait_recv()
            both = both + self.zbuf[ch, offset - 1].astype(F32)
        return both.astype(BF)

    def along(self, ch, piece):
        self.total[self._piece(ch, self.p.z), :] = piece
        for offset in (1, 2, 3):
            self._along(ch, offset, self.p.z).start()

    def back(self, ch):
        for offset in (1, 2, 3):
            self._along(ch, offset, lax.rem(self.p.z + 4 - offset, 4)).wait_recv()
        self._back(ch, self.p.y).start()

    def finish_sum(self, ch):
        self._half(ch).wait_send()
        for offset in (1, 2, 3):
            self._quarter(ch, offset).wait_send()

    def finish_spread(self, ch):
        self._back(ch, 1 - self.p.y).wait_recv()
        for offset in (1, 2, 3):
            self._along(ch, offset, self.p.z).wait_send()
        self._back(ch, self.p.y).wait_send()

    @staticmethod
    def scratch(rows, chunks):
        return [
            pltpu.VMEM((chunks, rows // 2, HALF), BF),
            pltpu.VMEM((chunks, rows // 2, HALF), BF),
            pltpu.VMEM((chunks, 3, rows // 8, HALF), BF),
            pltpu.SemaphoreType.DMA((8 * chunks,)),
            pltpu.SemaphoreType.DMA((8 * chunks,)),
        ]


class Groups:
    def __init__(self, place, s, v):
        self.p, self.s, self.v = place, s, v

    def half(self, n, mine, ybuf):
        return send(mine.at[1 - self.p.y], ybuf, self.s.at[n], self.v.at[n], self.p.beside)

    def quarter(self, n, mid, zbuf, offset):
        other, device = self.p.four(offset)
        n = n + offset - 1
        return send(mid.at[other], zbuf.at[offset - 1], self.s.at[n], self.v.at[n], device)

    def cross(self, n, both, xbuf):
        return send(both.at[1 - self.p.r], xbuf, self.s.at[n], self.v.at[n], self.p.across)

    def along(self, n, half, offset, z):
        n = n + offset - 1
        return send(half.at[z], half.at[z], self.s.at[n], self.v.at[n], self.p.four(offset)[1])

    def back(self, n, half, other):
        return send(half, other, self.s.at[n], self.v.at[n], self.p.beside)

    def start_quarters(self, n, mid, zbuf):
        for offset in (1, 2, 3):
            self.quarter(n, mid, zbuf, offset).start()

    def collect(self, n, mid, zbuf, both):
        total = mid[self.p.z].astype(F32)
        for offset in (1, 2, 3):
            self.quarter(n, mid, zbuf, offset).wait_recv()
            total = total + zbuf[offset - 1].astype(F32)
        both[...] = total.astype(BF)

    def start_along(self, n, half, piece):
        half[self.p.z] = piece
        for offset in (1, 2, 3):
            self.along(n, half, offset, self.p.z).start()

    def await_along(self, n, half):
        for offset in (1, 2, 3):
            self.along(n, half, offset, lax.rem(self.p.z + 4 - offset, 4)).wait_recv()

    def sent(self, n, ref, kind):
        for offset in (1, 2, 3):
            kind(n, *ref, offset).wait_send()


def everyone(p):
    return [p.across, p.core, p.diagonal, p.beside] + [p.four(o)[1] for o in (1, 2, 3)]


def front_kernel(
    lens, seq_ref, w_ref, wdep_ref, bv_ref, bc_ref, bq_ref, bp_ref, wk_ref, bk_ref, spread_ref, wi_own, wd_own, wo_own, cot_own,
    kd_ref, kt_ref, vz_ref, q_ref, qs_ref, pt_ref, kp_ref, conv_ref, mix_ref, dep_ref, h_ref, wi_ref, wd_ref, cot_ref, woq_ref,
    first_key, hbuf, cbuf, lsem, gs, gr, cs, cr,
):
    i = pl.program_id(0)
    p = Place()
    n = lens[p.r]
    keeps = [
        pltpu.make_async_copy(wi_own, inter_block(wi_ref, p.r, p.c, None), lsem.at[0]),
        pltpu.make_async_copy(wd_own, dense_block(wd_ref, p.r, p.c, None), lsem.at[1]),
    ]
    gathers = [
        Gather(p, wi_own, wi_ref, inter_part, inter_block, gs, gr, 0),
        Gather(p, wd_own, wd_ref, dense_part, dense_block, gs, gr, 6),
    ]
    cot_rows = ToRows(p, cot_own, cot_ref, lsem.at[2], cs, cr)
    part_output = send(output_part(wo_own, p.z), woq_ref, gs.at[12], gr.at[12], p.across)

    @pl.when(i == 0)
    def _():
        meet([p.across, p.core, p.diagonal] + [p.four(o)[1] for o in (1, 2, 3)])
        for keep, gather in zip(keeps, gathers):
            gather._cross(p.r).start()
            gather._near(p.c).start()
            keep.start()

    krows = kd_ref.shape[0]
    keep_key = row_ids(i * krows, krows) < n
    tok = seq_ref[rows_at(PAD + i * krows, krows), :]
    h = jnp.where(keep_key, tok.astype(F32), 0.0).astype(BF)
    k = nt(h, w_ref[0])
    v = nt(h, w_ref[1]) + line(bv_ref)

    @pl.when(i == 0)
    def _():
        first_key[...] = k[0:8]

    kd_ref[...] = jnp.where(keep_key, k, first_key[0:1]).astype(BF)
    kt_ref[...] = k.T.astype(BF)
    vz_ref[...] = jnp.where(keep_key, v, 0.0).astype(BF)

    @pl.when(i == 0)
    def _():
        for gather in gathers:
            gather.relay()
        part_output.start()
        cot_rows.start()

    rows = q_ref.shape[0]
    wide = rows + 32
    base = pl.multiple_of(i * rows, 16)
    start = pl.multiple_of(p.c * ROWS + i * rows, 16)
    ids = row_ids(start - 16, wide)
    keep = (ids >= 0) & (ids < n)
    hw = jnp.where(keep, seq_ref[pl.ds(start, wide), :].astype(F32), 0.0)
    hbuf[...] = hw
    depth = jnp.zeros((rows, D), F32)
    wdep = wdep_ref[...].astype(F32)
    for j in range(KW):
        depth = depth + hbuf[12 + j : 12 + j + rows, :] * wdep[j : j + 1, :]
    depth_low = depth.astype(BF)
    dep_ref[...] = depth_low
    hl = hw.astype(BF)
    h_ref[...] = hl[16 : 16 + rows]
    conv = jnp.where(keep, nt(hl, w_ref[2]) + line(bc_ref), 0.0)
    cbuf[...] = conv
    conv_ref[pl.ds(base, wide), :] = conv.astype(BF)
    q = nt(hl[16 : 16 + rows], w_ref[3]) + line(bq_ref)
    q_low = q.astype(BF)
    q_ref[...] = q_low
    qs_ref[...] = (q * (0.125 * LOG2E)).astype(BF)
    pt = nt(depth_low, w_ref[4]) + line(bp_ref)
    pt_ref[...] = pt.astype(BF)
    mixer = (pt * q_low.astype(F32)).astype(BF)
    logits = (nt(wk_ref[...], mixer) + bk_ref[:, 0:1]).reshape(KW, 8, rows)
    peak = jnp.max(logits, axis=0, keepdims=True)
    raised = jnp.exp(logits - peak)
    kp = (raised / jnp.sum(raised, axis=0, keepdims=True)).reshape(KW * 8, rows)
    kp_ref[...] = kp
    kpt = kp.T.astype(BF)
    mix = jnp.zeros((rows, HALF), F32)
    for j in range(KW):
        mix = mix + nn(kpt, spread_ref[:, j * HALF : (j + 1) * HALF]) * cbuf[12 + j : 12 + j + rows, :]
    mix_ref[...] = mix.astype(BF)

    @pl.when(i == pl.num_programs(0) - 1)
    def _():
        for gather in gathers:
            gather.share()
        cot_rows.finish()
        part_output.wait()
        for keep, gather in zip(keeps, gathers):
            keep.wait()
            gather.finish()


def front(lens, seq, w5, wdep, bv, bc, bq, bp, wk72, bk72, spread, w_inter, w_dense, w_output, cotangent):
    rows = 256
    keys = 512
    blk = pl.BlockSpec((rows, HALF), lambda i, lens: (i, 0))
    full = pl.BlockSpec((rows, D), lambda i, lens: (i, 0))
    half = jax.ShapeDtypeStruct((ROWS, HALF), BF)
    return pl.pallas_call(
        front_kernel,
        grid_spec=pltpu.PrefetchScalarGridSpec(
            num_scalar_prefetch=1,
            grid=(ROWS // rows,),
            in_specs=[once((LMAX + 2 * PAD, D)), once((5, HALF, D)), whole((KW, D))]
            + [whole((HALF,))] * 4
            + [whole((72, HALF)), whole((72, 128)), once((72, KW * HALF))]
            + [once((HALF, D)), once((2, 192, HALF)), once((D, HALF)), once((LMAX, HALF))],
            out_specs=[
                pl.BlockSpec((keys, HALF), lambda i, lens: (i, 0)),
                pl.BlockSpec((HALF, keys), lambda i, lens: (0, i)),
                pl.BlockSpec((keys, HALF), lambda i, lens: (i, 0)),
                blk,
                blk,
                blk,
                pl.BlockSpec((72, rows), lambda i, lens: (0, i)),
                whole((ROWS + 32, HALF)),
                blk,
                full,
                full,
                HBM,
                HBM,
                HBM,
                HBM,
            ],
            scratch_shapes=[
                pltpu.VMEM((8, HALF), F32),
                pltpu.VMEM((rows + 32, D), F32),
                pltpu.VMEM((rows + 32, HALF), F32),
                pltpu.SemaphoreType.DMA((3,)),
                pltpu.SemaphoreType.DMA((13,)),
                pltpu.SemaphoreType.DMA((13,)),
                pltpu.SemaphoreType.DMA((3,)),
                pltpu.SemaphoreType.DMA((2,)),
            ],
        ),
        out_shape=[
            jax.ShapeDtypeStruct((LMAX, HALF), BF),
            jax.ShapeDtypeStruct((HALF, LMAX), BF),
            jax.ShapeDtypeStruct((LMAX, HALF), BF),
            half,
            half,
            half,
            jax.ShapeDtypeStruct((72, ROWS), F32),
            jax.ShapeDtypeStruct((ROWS + 32, HALF), BF),
            half,
            jax.ShapeDtypeStruct((ROWS, D), BF),
            jax.ShapeDtypeStruct((ROWS, D), BF),
            jax.ShapeDtypeStruct((2, HALF, GW), BF),
            jax.ShapeDtypeStruct((2, HALF, D), BF),
            jax.ShapeDtypeStruct((ROWS, D), BF),
            jax.ShapeDtypeStruct((192, HALF), BF),
        ],
        **comm_params("front", 2),
    )(lens, seq, w5, wdep, bv, bc, bq, bp, wk72, bk72, spread, w_inter, w_dense, w_output, cotangent)


def attend_kernel(lens, q_ref, k_ref, v_ref, wo_own, woq, ctx_ref, lse_ref, wo_ref, lsem, gs, gr):
    i = pl.program_id(0)
    p = Place()
    there = 1 - p.r
    keep = pltpu.make_async_copy(wo_own, output_block(wo_ref, p.r, p.c, None), lsem.at[0])
    keep_part = pltpu.make_async_copy(woq, output_block(wo_ref, there, p.c, p.z), lsem.at[1])

    def near(c):
        return send(wo_own, output_block(wo_ref, p.r, c, None), gs.at[0], gr.at[0], p.core)

    def pass_on(offset, z):
        return send(woq, output_block(wo_ref, there, p.c, z), gs.at[offset], gr.at[offset], p.four(offset)[1])

    def last(c):
        here = output_block(wo_ref, there, c, None)
        return send(here, here, gs.at[4], gr.at[4], p.core)

    @pl.when(i == 0)
    def _():
        meet([p.core] + [p.four(o)[1] for o in (1, 2, 3)])
        for offset in (1, 2, 3):
            pass_on(offset, p.z).start()
        near(p.c).start()
        keep.start()
        keep_part.start()

    @pl.when(i == pl.num_programs(0) - 1)
    def _():
        keep_part.wait()
        for offset in (1, 2, 3):
            pass_on(offset, lax.rem(p.z + 4 - offset, 4)).wait_recv()
        last(p.c).start()

    k = k_ref[...]
    ones = jnp.where(row_ids(0, LMAX) < lens[p.r], 1.0, 0.0)
    ve = jnp.concatenate([v_ref[...], jnp.broadcast_to(ones, (LMAX, 128)).astype(BF)], axis=1)
    rows = 256
    lane = lax.broadcasted_iota(jnp.int32, (rows, 128), 1)
    for u in range(ROWS // rows):
        part = slice(u * rows, (u + 1) * rows)
        outs = []
        for hh in range(2):
            q = jnp.where((lane < HD) == (hh == 0), q_ref[part, :], jnp.zeros((), BF))
            s = nt(q, k)
            peak = jnp.max(s, axis=1, keepdims=True)
            prob = jnp.exp2(s - peak).astype(BF)
            o = nn(prob, ve)
            outs.append(o[:, :128] / o[:, 128:])
            lse_ref[0, hh : hh + 1, part] = (peak + jnp.log2(o[:, 128:129])).T
        ctx_ref[part, :] = jnp.where(lane < HD, outs[0], outs[1]).astype(BF)

    @pl.when(i == pl.num_programs(0) - 1)
    def _():
        last(1 - p.c).wait_recv()
        near(1 - p.c).wait_recv()
        keep.wait()
        near(p.c).wait_send()
        last(p.c).wait_send()
        for offset in (1, 2, 3):
            pass_on(offset, p.z).wait_send()


def attend(lens, qs, kd, vz, w_output, part):
    pair = lambda rows: pl.BlockSpec((rows, 128), lambda p, lens: (0, p))
    return pl.pallas_call(
        attend_kernel,
        grid_spec=pltpu.PrefetchScalarGridSpec(
            num_scalar_prefetch=1,
            grid=(3,),
            in_specs=[pair(ROWS), pair(LMAX), pair(LMAX), once((D, HALF)), once((192, HALF))],
            out_specs=[pair(ROWS), pl.BlockSpec((1, 8, ROWS), lambda p, lens: (p, 0, 0)), HBM],
            scratch_shapes=[
                pltpu.SemaphoreType.DMA((2,)),
                pltpu.SemaphoreType.DMA((5,)),
                pltpu.SemaphoreType.DMA((5,)),
            ],
        ),
        out_shape=[
            jax.ShapeDtypeStruct((ROWS, HALF), BF),
            jax.ShapeDtypeStruct((3, 8, ROWS), F32),
            jax.ShapeDtypeStruct((2, GW, HALF), BF),
        ],
        **comm_params("attend", 3),
    )(lens, qs, kd, vz, w_output, part)


def back_kernel(
    lens, gcv_ref, conv_ref, kp_ref, q_ref, pt_ref, wk_ref, spread_ref, ones_ref,
    qs_ref, do_ref, k_ref, v_ref, kt_ref, lse_ref, del_ref, pay_all, pay_ref, hid_ref,
    gqm_ref, gpt_ref, gco_ref, gwk_ref, gbk_ref, dq_ref, dk_ref, dv_ref, half_ref, piece_ref, mid_ref, out_ref,
    acc, wbuf, tbuf, dka, dva, near, mine, ybuf, mid, zbuf, both, xbuf, half, ns, nr, s, v_sem, ls, hs, hr,
):
    step = pl.program_id(0)
    place = Place()
    groups = Groups(place, s, v_sem)
    hidden = FromRows(place, hid_ref, out_ref, ls, hs, hr)

    def near_copy(n):
        rr = 1 - place.r if n == 0 else place.r
        return send(pay_all.at[rr, 1 - place.c], near.at[rr], ns.at[n], nr.at[n], place.core)

    @pl.when(step == 0)
    def _():
        meet(everyone(place))
        near_copy(0).start()
        near_copy(1).start()
        hidden.start()
        acc[...] = jnp.zeros_like(acc)
        tbuf[...] = jnp.zeros_like(tbuf)
        gwk_ref[...] = jnp.zeros_like(gwk_ref)
        gbk_ref[...] = jnp.zeros_like(gbk_ref)

    @pl.when(step == 2)
    def _():
        near_copy(0).wait()
        near_copy(1).wait()
        for ch in range(3):
            for rr in range(2):
                total = near[rr, ch].astype(F32) + pay_ref[rr, 0, ch].astype(F32)
                mine[ch, :, :, rr] = total.astype(BF)
            groups.half(ch, mine.at[ch], ybuf.at[ch]).start()

    def settle(ch):
        groups.half(ch, mine.at[ch], ybuf.at[ch]).wait_recv()
        mid[ch] = (mine[ch, place.y].astype(F32) + ybuf[ch].astype(F32)).astype(BF)

    @pl.when(step == 5)
    def _():
        settle(0)
        groups.start_quarters(3, mid.at[0], zbuf.at[0])

    @pl.when(step == 7)
    def _():
        settle(1)
        groups.start_quarters(6, mid.at[1], zbuf.at[1])
        groups.collect(3, mid.at[0], zbuf.at[0], both.at[0])
        groups.cross(9, both.at[0], xbuf.at[0]).start()

    def merge(ch):
        groups.cross(9 + ch, both.at[ch], xbuf.at[ch]).wait_recv()
        return (both[ch, place.r].astype(F32) + xbuf[ch].astype(F32)).astype(BF)

    @pl.when(step == 8)
    def _():
        groups.start_along(11, half, merge(0))

    @pl.when(step == 9)
    def _():
        groups.collect(6, mid.at[1], zbuf.at[1], both.at[1])
        groups.cross(10, both.at[1], xbuf.at[1]).start()
        settle(2)
        mid_ref[...] = mid[2]

    @pl.when(step < 4)
    def _():
        rows = gcv_ref.shape[0]
        wide = rows + 32
        gcv = gcv_ref[...].astype(F32)
        wbuf[...] = conv_ref[pl.ds(pl.multiple_of(step * rows, 16), wide), :].astype(F32)
        kp = kp_ref[...]
        kpt = kp.T.astype(BF)
        gkps = []
        total = jnp.zeros((wide, HALF), F32)
        for j in range(KW):
            prod = (gcv * wbuf[12 + j : 12 + j + rows, :]).astype(BF)
            gkps.append(nt(ones_ref[...], prod))
            tbuf[24 : 24 + rows, :] = nn(kpt, spread_ref[:, j * HALF : (j + 1) * HALF]) * gcv
            total = total + tbuf[12 - j : 12 - j + wide, :]
        acc[pl.ds(pl.multiple_of(place.c * ROWS + step * rows, 16), wide), :] += total
        gkp = jnp.concatenate(gkps, axis=0).reshape(KW, 8, rows)
        kp3 = kp.reshape(KW, 8, rows)
        inner = jnp.sum(kp3 * gkp, axis=0, keepdims=True)
        gl = (kp3 * (gkp - inner)).reshape(KW * 8, rows)
        glt = gl.T.astype(BF)
        gbk_ref[0:1, 0:72] += col_sum(glt.astype(F32))
        q = q_ref[...].astype(F32)
        pt = pt_ref[...].astype(F32)
        gwk_ref[...] += nn(gl.astype(BF), (pt * q).astype(BF))
        gmix = nn(glt, wk_ref[...])
        gqm_ref[...] = (gmix * pt).astype(BF)
        gpt_ref[...] = (gmix * q).astype(BF)

    @pl.when(step == 3)
    def _():
        keep = row_ids(0, LMAX) < lens[place.r]
        gco_ref[...] = jnp.where(keep, acc[16 : 16 + LMAX, :], 0.0).astype(BF)

    @pl.when(step >= 4)
    def _():
        i = lax.rem(step, 2)
        k = k_ref[...]
        v = v_ref[...]
        rows = qs_ref.shape[0]
        lane = lax.broadcasted_iota(jnp.int32, (rows, 128), 1)
        dk = dv = None
        for hh in range(2):
            head = (lane < HD) == (hh == 0)
            q = jnp.where(head, qs_ref[...], jnp.zeros((), BF))
            do = jnp.where(head, do_ref[...], jnp.zeros((), BF))
            p = jnp.exp2(nt(k, q) - lse_ref[0, hh : hh + 1, :])
            ds = (p * (nt(v, do) - del_ref[0, hh : hh + 1, :])).astype(BF)
            dv_one = nn(p.astype(BF), do)
            dk_one = nn(ds, q)
            dv = dv_one if dv is None else dv + dv_one
            dk = dk_one if dk is None else dk + dk_one
            dq_ref[hh * HD : (hh + 1) * HD, :] = (nn(kt_ref[hh * HD : (hh + 1) * HD, :], ds) * 0.125).astype(BF)

        @pl.when(i == 0)
        def _():
            dka[...] = dk
            dva[...] = dv

        @pl.when(i == 1)
        def _():
            keep = row_ids(0, LMAX) < lens[place.r]
            dk_ref[...] = jnp.where(keep, (dka[...] + dk) * LN2, 0.0).astype(BF)
            dv_ref[...] = jnp.where(keep, dva[...] + dv, 0.0).astype(BF)

    @pl.when(step == 9)
    def _():
        piece_ref[...] = merge(1)
        groups.await_along(11, half)
        half_ref[...] = half[...]
        for ch in range(3):
            groups.half(ch, mine.at[ch], ybuf.at[ch]).wait_send()
        for ch in range(2):
            groups.cross(9 + ch, both.at[ch], xbuf.at[ch]).wait_send()
            for offset in (1, 2, 3):
                groups.quarter(3 + 3 * ch, mid.at[ch], zbuf.at[ch], offset).wait_send()
        for offset in (1, 2, 3):
            groups.along(11, half, offset, place.z).wait_send()
        hidden.finish()


def back(lens, gcv, conv, kp, q, pt, wk72, spread, ones8, qs, do, kd, vz, kt, lse, delta, pay, hid):
    crows = 256
    rows = 512
    early = lambda s: jnp.minimum(s, 3)
    late = lambda s: jnp.maximum(s - 4, 0)
    which = lambda s: lax.div(late(s), 2)
    part = lambda s: lax.rem(late(s), 2)
    cblk = pl.BlockSpec((crows, HALF), lambda s, lens: (early(s), 0))
    mine = pl.BlockSpec((rows, 128), lambda s, lens: (part(s), which(s)))
    pair = pl.BlockSpec((LMAX, 128), lambda s, lens: (0, which(s)))
    stats = pl.BlockSpec((1, 8, rows), lambda s, lens: (which(s), 0, part(s)))
    block = (3, 2, 4, 80, HALF)
    pay = pay.reshape((2, 2) + block)
    mine_pay = pl.BlockSpec(
        (2, 1) + block, lambda s, lens: (0, half_index(), 0, 0, 0, 0, 0), pipeline_mode=pl.Buffered(1)
    )
    return pl.pallas_call(
        back_kernel,
        grid_spec=pltpu.PrefetchScalarGridSpec(
            num_scalar_prefetch=1,
            grid=(10,),
            in_specs=[
                cblk,
                once((ROWS + 32, HALF)),
                pl.BlockSpec((72, crows), lambda s, lens: (0, early(s))),
                cblk,
                cblk,
                whole((72, HALF)),
                once((72, KW * HALF)),
                whole((8, HALF)),
                mine,
                mine,
                pair,
                pair,
                pl.BlockSpec((128, LMAX), lambda s, lens: (which(s), 0)),
                stats,
                stats,
                HBM,
                mine_pay,
                once((ROWS, D)),
            ],
            out_specs=[
                cblk,
                cblk,
                once((LMAX, HALF)),
                whole((72, HALF)),
                whole((8, 128)),
                pl.BlockSpec((128, rows), lambda s, lens: (which(s), part(s))),
                pair,
                pair,
                whole((4, 80, HALF)),
                whole((80, HALF)),
                whole((4, 2, 80, HALF)),
                HBM,
            ],
            scratch_shapes=[
                pltpu.VMEM((LMAX + 32, HALF), F32),
                pltpu.VMEM((crows + 32, HALF), F32),
                pltpu.VMEM((crows + 48, HALF), F32),
                pltpu.VMEM((LMAX, 128), F32),
                pltpu.VMEM((LMAX, 128), F32),
                pltpu.VMEM((2,) + block, BF),
                pltpu.VMEM((3, 2, 4, 2, 80, HALF), BF),
                pltpu.VMEM((3, 4, 2, 80, HALF), BF),
                pltpu.VMEM((3, 4, 2, 80, HALF), BF),
                pltpu.VMEM((2, 3, 2, 80, HALF), BF),
                pltpu.VMEM((2, 2, 80, HALF), BF),
                pltpu.VMEM((2, 80, HALF), BF),
                pltpu.VMEM((4, 80, HALF), BF),
                pltpu.SemaphoreType.DMA((2,)),
                pltpu.SemaphoreType.DMA((2,)),
                pltpu.SemaphoreType.DMA((14,)),
                pltpu.SemaphoreType.DMA((14,)),
                pltpu.SemaphoreType.DMA,
                pltpu.SemaphoreType.DMA((2,)),
                pltpu.SemaphoreType.DMA((3,)),
            ],
        ),
        out_shape=[
            jax.ShapeDtypeStruct((ROWS, HALF), BF),
            jax.ShapeDtypeStruct((ROWS, HALF), BF),
            jax.ShapeDtypeStruct((LMAX, HALF), BF),
            jax.ShapeDtypeStruct((72, HALF), F32),
            jax.ShapeDtypeStruct((8, 128), F32),
            jax.ShapeDtypeStruct((HALF, ROWS), BF),
            jax.ShapeDtypeStruct((LMAX, HALF), BF),
            jax.ShapeDtypeStruct((LMAX, HALF), BF),
            jax.ShapeDtypeStruct((4, 80, HALF), BF),
            jax.ShapeDtypeStruct((80, HALF), BF),
            jax.ShapeDtypeStruct((4, 2, 80, HALF), BF),
            jax.ShapeDtypeStruct((2, ROWS, HALF), BF),
        ],
        **comm_params("back", 4),
    )(lens, gcv, conv, kp, q, pt, wk72, spread, ones8, qs, do, kd, vz, kt, lse, delta, pay, pay, hid)


def norm_parts(x):
    xc = x - jnp.mean(x, axis=1, keepdims=True)
    inv = lax.rsqrt(jnp.mean(xc * xc, axis=1, keepdims=True) + EPS)
    return xc * inv, inv


def norm_back(up, normal, inv, gain):
    e = up * gain
    return inv * (e - jnp.mean(e, axis=1, keepdims=True) - normal * jnp.mean(e * normal, axis=1, keepdims=True))


def ffn_kernel(
    lens, ctx_ref, mix_ref, tok_ref, cot_ref, wd_ref, wi_ref, wo_ref, v0, v1, v2, v3, v4, v5, bi_ref, ones_ref,
    hid_ref, gpre_ref, gctx_ref, gcv_ref, del_ref, pay_ref, sm_ref, gbi_ref,
    act_s, gp_s, awd, awi, awo,
):
    i = pl.program_id(0)
    rows = ctx_ref.shape[0]
    keep = row_ids(half_index() * ROWS + i * rows, rows) < length(lens)

    @pl.when(i == 0)
    def _():
        awd[...] = jnp.zeros_like(awd)
        awi[...] = jnp.zeros_like(awi)
        awo[...] = jnp.zeros_like(awo)
        sm_ref[...] = jnp.zeros_like(sm_ref)
        gbi_ref[...] = jnp.zeros_like(gbi_ref)

    vectors = [line(ref) for ref in (v0, v1, v2, v3, v4, v5)]
    vec = lambda k: vectors[k]
    inter_bias = line(bi_ref)
    h = tok_ref[...].astype(F32)
    ctx = ctx_ref[...]
    mixed = jnp.concatenate([ctx, mix_ref[...]], axis=1)
    n1, inv1 = norm_parts(nn(mixed, wd_ref[...]) + vec(0) + h)
    f1 = n1 * vec(1) + vec(2)
    fl = f1.astype(BF)
    chunk = 512
    outs = []
    for g in range(2):
        fg = fl[:, g * HALF : (g + 1) * HALF]
        for ch in range(GW // chunk):
            cols = slice(ch * chunk, (ch + 1) * chunk)
            put = slice(g * GW + ch * chunk, g * GW + (ch + 1) * chunk)
            x = nn(fg, wi_ref[g, :, cols]) + inter_bias[:, put]
            phi = 0.5 + 0.5 * lax.erf(x * 0.7071067811865476)
            act_s[:, put] = (x * phi).astype(BF)
            gp_s[:, put] = phi + x * jnp.exp2(x * x * (-0.5 * LOG2E)) * 0.3989422804014327
        outs.append(nn(act_s[:, g * GW : (g + 1) * GW], wo_ref[g]))
    n2, inv2 = norm_parts(jnp.concatenate(outs, axis=1) + vec(3) + f1)
    hid_ref[...] = (n2 * vec(4) + vec(5)).astype(BF)
    u = jnp.where(keep, cot_ref[...].astype(F32), 0.0)
    gp2 = norm_back(u, n2, inv2, vec(4))
    go = gp2.astype(BF)
    got = go.T
    flt = fl.T
    gfs = []
    for g in range(2):
        sel = slice(g * HALF, (g + 1) * HALF)
        gf = gp2[:, sel]
        for ch in range(GW // chunk):
            cols = slice(ch * chunk, (ch + 1) * chunk)
            put = slice(g * GW + ch * chunk, g * GW + (ch + 1) * chunk)
            gi = (gp_s[:, put] * nt(go[:, sel], wo_ref[g, cols, :])).astype(BF)
            gbi_ref[0:1, put] += col_sum(gi.astype(F32))
            awo[g, :, cols] += nn(got[sel], act_s[:, put])
            awi[g, :, cols] += nn(flt[sel], gi)
            gf = gf + nt(gi, wi_ref[g, :, cols])
        gfs.append(gf)
    gf = jnp.concatenate(gfs, axis=1)
    gpre = norm_back(gf, n1, inv1, vec(1))
    gd = gpre.astype(BF)
    gpre_ref[...] = gd
    sm_ref[0:1, :] += col_sum(go.astype(F32))
    sm_ref[1:2, :] += col_sum(u * n2)
    sm_ref[2:3, :] += col_sum(u)
    sm_ref[3:4, :] += col_sum(gd.astype(F32))
    sm_ref[4:5, :] += col_sum(gf * n1)
    sm_ref[5:6, :] += col_sum(gf)
    awd[...] += nn(mixed.T, gd)
    gm = nt(gd, wd_ref[...])
    gctx = gm[:, :HALF].astype(BF)
    gctx_ref[...] = gctx
    gcv_ref[...] = gm[:, HALF:].astype(BF)
    prod = (gctx.astype(F32) * ctx.astype(F32)).astype(BF)
    del_ref[...] = nt(ones_ref[...], prod).reshape(3, 8, rows)

    @pl.when(i == pl.num_programs(0) - 1)
    def _():
        for r in range(2):
            for c in range(2):
                pay_ref[r, c, 0:HALF, :] = awi[r, :, c * D : c * D + HALF].astype(BF)
                pay_ref[r, c, HALF:D, :] = awi[r, :, c * D + HALF : (c + 1) * D].astype(BF)
                pay_ref[r, c, D : 2 * D, :] = awo[r, :, c * D : (c + 1) * D].T.astype(BF)
                for part in range(2):
                    piece = awd[part * HALF + c * 192 : part * HALF + (c + 1) * 192, r * HALF : (r + 1) * HALF]
                    pay_ref[r, c, 2 * D + part * 192 : 2 * D + (part + 1) * 192, :] = piece.astype(BF)


def ffn(lens, ctx, mix, tok, cot, wd, wi, wo, vectors, bi, ones24):
    rows = 256
    blk = lambda w: pl.BlockSpec((rows, w), lambda i, lens: (i, 0))
    return pl.pallas_call(
        ffn_kernel,
        grid_spec=pltpu.PrefetchScalarGridSpec(
            num_scalar_prefetch=1,
            grid=(ROWS // rows,),
            in_specs=[
                blk(HALF),
                blk(HALF),
                blk(D),
                blk(D),
                whole((D, D)),
                whole((2, HALF, GW)),
                whole((2, GW, HALF)),
                *[whole((D,))] * 6,
                whole((FF,)),
                whole((24, HALF)),
            ],
            out_specs=[
                blk(D),
                blk(D),
                blk(HALF),
                blk(HALF),
                pl.BlockSpec((3, 8, rows), lambda i, lens: (0, 0, i)),
                whole((2, 2, FFN_ROWS, HALF)),
                whole((8, D)),
                whole((1, FF)),
            ],
            scratch_shapes=[
                pltpu.VMEM((rows, FF), BF),
                pltpu.VMEM((rows, FF), F32),
                pltpu.VMEM((D, D), F32),
                pltpu.VMEM((2, HALF, GW), F32),
                pltpu.VMEM((2, HALF, GW), F32),
            ],
        ),
        out_shape=[
            jax.ShapeDtypeStruct((ROWS, D), BF),
            jax.ShapeDtypeStruct((ROWS, D), BF),
            jax.ShapeDtypeStruct((ROWS, HALF), BF),
            jax.ShapeDtypeStruct((ROWS, HALF), BF),
            jax.ShapeDtypeStruct((3, 8, ROWS), F32),
            jax.ShapeDtypeStruct((2, 2, FFN_ROWS, HALF), BF),
            jax.ShapeDtypeStruct((8, D), F32),
            jax.ShapeDtypeStruct((1, FF), F32),
        ],
        **params("ffn"),
    )(lens, ctx, mix, tok, cot, wd, wi, wo, *vectors, bi, ones24)


def final_kernel(
    lens, seq_ref, dk_ref, dv_ref, gco_ref, dq_ref, gqm_ref, gpt_ref, gpre_ref, dep_ref, w_ref, wdep_ref,
    smf_ref, gbi_ref, gwk_ref, gbk_ref, half0, piece1, mid2,
    pay_ref, own_ref, oth_ref, ght_ref, rest_ref,
    agw, wbuf, dbuf, accb, gpad, sbuf, strip, sm, gdp, tsend, trecv, gho, halves, other, zbuf, both, xbuf,
    s, v, es, er, ls, hs, hr,
):
    i = pl.program_id(0)
    p = Place()
    rows = dk_ref.shape[0]
    wide = rows + 32
    b = lax.rem((1 - p.c) * 2 + i, 4)
    n = lens[p.r]
    groups = Groups(p, s, v)
    place = FromRows(p, gho, ght_ref, ls, hs, hr)
    wdep = wdep_ref[...].astype(F32)

    def theirs(k):
        return send(tsend.at[k], trecv.at[k], es.at[k], er.at[k], p.core)

    @pl.when(i == 0)
    def _():
        meet(everyone(p))
        groups.start_quarters(0, mid2, zbuf)
        groups.start_along(4, halves.at[0], piece1[...])
        groups.back(10, half0, other.at[0]).start()
        agw[...] = jnp.zeros_like(agw)
        sm[...] = jnp.zeros_like(sm)
        gdp[...] = jnp.zeros_like(gdp)
        gpad[0:32, :] = jnp.zeros((32, HALF), BF)
        gpad[32 + ROWS :, :] = jnp.zeros((32, HALF), BF)
        gpad[32 : 32 + ROWS, :] = gpt_ref[...]
        edge = pl.multiple_of((1 - p.c) * (ROWS + 16), 16)
        sbuf[...] = nn(gpad[pl.ds(edge, 48), :], w_ref[4])
        total = jnp.zeros((16, D), F32)
        for j in range(KW):
            total = total + sbuf[20 - j : 36 - j, :] * wdep[j : j + 1, :]
        strip[...] = total

    @pl.when(i == 2)
    def _():
        groups.collect(0, mid2, zbuf, both)
        groups.cross(3, both, xbuf).start()

    @pl.when(i == 3)
    def _():
        groups.cross(3, both, xbuf).wait_recv()
        groups.start_along(7, halves.at[1], (both[p.r].astype(F32) + xbuf[...].astype(F32)).astype(BF))
        groups.await_along(4, halves.at[0])
        groups.back(11, halves.at[0], other.at[1]).start()

    keep = row_ids(b * rows, rows) < n
    tok = seq_ref[rows_at(PAD + b * rows, rows), :]
    h = jnp.where(keep, tok.astype(F32), 0.0).astype(BF)
    dk, dv, gco = dk_ref[...], dv_ref[...], gco_ref[...]
    accb[...] = nn(dk, w_ref[0]) + nn(dv, w_ref[1]) + nn(gco, w_ref[2])
    agw[0] += nn(dk.T, h)
    agw[1] += nn(dv.T, h)
    agw[2] += nn(gco.T, h)
    sm[1:2, :] += col_sum(dv.astype(F32))
    sm[2:3, :] += col_sum(gco.astype(F32))

    for k in range(2):

        @pl.when((i == k) & (p.c == k))
        def _():
            edge = slice(0, 16) if k == 0 else slice(rows - 16, rows)
            accb[edge, :] += strip[...]

        @pl.when(i == k)
        def _():
            tsend[k] = jnp.where(keep, accb[...], 0.0).astype(BF)
            theirs(k).start()

    @pl.when(i >= 2)
    def _():
        gqt = dq_ref[...].astype(F32) + gqm_ref[...].astype(F32).T
        gqt = gqt.astype(BF)
        gq = gqt.T
        at = pl.multiple_of((i - 2) * rows + 16, 16)
        win = gpad[pl.ds(at, wide), :]
        gpt = win[16 : 16 + rows]
        sm[0:1, :] += col_sum(gq.astype(F32))
        sm[3:4, :] += col_sum(gpt.astype(F32))
        agw[3] += nn(gqt, h)
        agw[4] += nn(gpt.T, dep_ref[...])
        dbuf[...] = nn(win, w_ref[4])
        ids = row_ids(b * rows - 16, wide)
        inside = (ids >= 0) & (ids < n)
        wbuf[...] = jnp.where(inside, seq_ref[rows_at(b * rows, wide), :].astype(F32), 0.0)
        total = accb[...] + nn(gq, w_ref[3]) + gpre_ref[...].astype(F32)
        gdep = dbuf[16 : 16 + rows, :]
        for j in range(KW):
            gdp[j : j + 1, :] += col_sum(gdep * wbuf[12 + j : 12 + j + rows, :])
            total = total + dbuf[20 - j : 20 - j + rows, :] * wdep[j : j + 1, :]
        accb[...] = total

    for k in range(2):

        @pl.when(i == 2 + k)
        def _():
            theirs(k).wait_recv()
            total = jnp.where(keep, accb[...] + trecv[k].astype(F32), 0.0).astype(BF)
            if k == 0:
                gho[...] = total
                place.start()
            else:
                rest_ref[...] = total

    @pl.when(i == pl.num_programs(0) - 1)
    def _():
        for r in range(2):
            for c in range(2):
                for j in range(5):
                    piece = agw[j, c * 192 : (c + 1) * 192, r * HALF : (r + 1) * HALF]
                    pay_ref[r, c, j * 192 : (j + 1) * 192, :] = piece.astype(BF)
        zeros = lambda k: jnp.zeros((k, HALF), F32)
        pay_ref[0, 0, 960:, :] = gwk_ref[0:64, :].astype(BF)
        bias = jnp.concatenate([gbk_ref[...], jnp.zeros((8, 256), F32)], axis=1)
        pay_ref[0, 1, 960:, :] = jnp.concatenate([gwk_ref[64:72, :], sm[...], bias, zeros(40)], axis=0).astype(BF)
        inter = jnp.concatenate([gbi_ref[:, k * HALF : (k + 1) * HALF] for k in range(8)], axis=0)
        pay_ref[1, 0, 960:, :] = jnp.concatenate(
            [smf_ref[:, 0:HALF], smf_ref[:, HALF:D], inter, zeros(40)], axis=0
        ).astype(BF)
        pay_ref[1, 1, 960:, :] = jnp.concatenate([gdp[:, 0:HALF], gdp[:, HALF:D], zeros(32)], axis=0).astype(BF)
        groups.await_along(7, halves.at[1])
        own_ref[0] = half0[...]
        own_ref[1] = halves[0]
        own_ref[2] = halves[1]
        groups.back(10, half0, other.at[0]).wait()
        groups.back(11, halves.at[0], other.at[1]).wait()
        oth_ref[...] = other[...]
        for offset in (1, 2, 3):
            groups.quarter(0, mid2, zbuf, offset).wait_send()
            groups.along(4, halves.at[0], offset, p.z).wait_send()
            groups.along(7, halves.at[1], offset, p.z).wait_send()
        groups.cross(3, both, xbuf).wait_send()
        theirs(0).wait_send()
        theirs(1).wait_send()
        place.finish()


def final(lens, seq_tok, dk, dv, gco, dq, gqm, gpt, gpre, dep, w5, wdep, smf, gbi, gwk, gbk, half0, piece1, mid2):
    rows = 512
    seq = pl.BlockSpec((rows, HALF), lambda i, lens: (lax.rem((1 - half_index()) * 2 + i, 4), 0))
    own = lambda w: pl.BlockSpec((rows, w), lambda i, lens: (jnp.maximum(i - 2, 0), 0))
    return pl.pallas_call(
        final_kernel,
        grid_spec=pltpu.PrefetchScalarGridSpec(
            num_scalar_prefetch=1,
            grid=(LMAX // rows,),
            in_specs=[
                once((LMAX + 2 * PAD, D)),
                seq,
                seq,
                seq,
                pl.BlockSpec((HALF, rows), lambda i, lens: (0, jnp.maximum(i - 2, 0))),
                own(HALF),
                once((ROWS, HALF)),
                own(D),
                own(D),
                once((5, HALF, D)),
                whole((KW, D)),
                whole((8, D)),
                whole((1, FF)),
                whole((72, HALF)),
                whole((8, 128)),
                once((4, 80, HALF)),
                whole((80, HALF)),
                once((4, 2, 80, HALF)),
            ],
            out_specs=[
                once((2, 2, PROJ_ROWS, HALF)),
                once((3, 4, 80, HALF)),
                once((2, 4, 80, HALF)),
                HBM,
                once((rows, D)),
            ],
            scratch_shapes=[
                pltpu.VMEM((5, HALF, D), F32),
                pltpu.VMEM((rows + 32, D), F32),
                pltpu.VMEM((rows + 32, D), F32),
                pltpu.VMEM((rows, D), F32),
                pltpu.VMEM((ROWS + 64, HALF), BF),
                pltpu.VMEM((48, D), F32),
                pltpu.VMEM((16, D), F32),
                pltpu.VMEM((8, HALF), F32),
                pltpu.VMEM((16, D), F32),
                pltpu.VMEM((2, rows, D), BF),
                pltpu.VMEM((2, rows, D), BF),
                pltpu.VMEM((rows, D), BF),
                pltpu.VMEM((2, 4, 80, HALF), BF),
                pltpu.VMEM((2, 4, 80, HALF), BF),
                pltpu.VMEM((3, 2, 80, HALF), BF),
                pltpu.VMEM((2, 80, HALF), BF),
                pltpu.VMEM((80, HALF), BF),
                pltpu.SemaphoreType.DMA((12,)),
                pltpu.SemaphoreType.DMA((12,)),
                pltpu.SemaphoreType.DMA((2,)),
                pltpu.SemaphoreType.DMA((2,)),
                pltpu.SemaphoreType.DMA,
                pltpu.SemaphoreType.DMA((2,)),
                pltpu.SemaphoreType.DMA((3,)),
            ],
        ),
        out_shape=[
            jax.ShapeDtypeStruct((2, 2, PROJ_ROWS, HALF), BF),
            jax.ShapeDtypeStruct((3, 4, 80, HALF), BF),
            jax.ShapeDtypeStruct((2, 4, 80, HALF), BF),
            jax.ShapeDtypeStruct((2, rows, HALF), BF),
            jax.ShapeDtypeStruct((rows, D), BF),
        ],
        **comm_params("final", 6),
    )(lens, seq_tok, dk, dv, gco, dq, gqm, gpt, gpre, dep, w5, wdep, smf, gbi, gwk, gbk, half0, piece1, mid2)


def end_kernel(
    pay, rest_ref, own_half, oth_half, ght, sum_ref, small_ref, big_ref,
    small, total_sum, near, far, out, mid, ybuf, zbuf, s, v, ns, nr, cs, cr, last, es, er, ls, hs, hr,
):
    p = Place()
    r, c = p.r, p.c
    meet(everyone(p))
    rows = PROJ_ROWS // 2
    summed = Sum(p, far, mid, ybuf, zbuf, total_sum, rows, s, v)

    def part(ch):
        return slice(ch * rows, (ch + 1) * rows)

    def beside(n, ch):
        rr = 1 - r if n == 0 else r
        k = n * 2 + ch
        return send(pay.at[rr, 1 - c, part(ch), :], near.at[rr, part(ch), :], ns.at[k], nr.at[k], p.core)

    def cross(ch):
        return send(out.at[part(ch), :], far.at[part(ch), :], cs.at[ch], cr.at[ch], p.across)

    for n in range(2):
        for ch in range(2):
            beside(n, ch).start()
    back_half = send(own_half.at[2], last, es.at[0], er.at[0], p.beside)
    back_half.start()
    back = FromRows(p, rest_ref, ght, ls, hs, hr)
    for ch in range(2):
        beside(0, ch).wait_recv()
        both = near[1 - r, part(ch), :].astype(F32) + pay[1 - r, c, part(ch), :].astype(F32)
        out[part(ch), :] = both.astype(BF)
        cross(ch).start()
    back.start()
    for ch in range(2):
        big_ref[ch, p.y] = own_half[ch]
        big_ref[ch, 1 - p.y] = oth_half[ch]
    big_ref[2, p.y] = own_half[2]
    for ch in range(2):
        beside(1, ch).wait_recv()
        cross(ch).wait_recv()
        both = near[r, part(ch), :].astype(F32) + pay[r, c, part(ch), :].astype(F32)
        far[part(ch), :] = (both + far[part(ch), :].astype(F32)).astype(BF)
        summed.half(ch)
    for ch in range(2):
        summed.quarter(ch)
    for ch in range(2):
        summed.along(ch, summed.collect(ch))
    for ch in range(2):
        summed.back(ch)
    for ch in range(2):
        summed.finish_spread(ch)
    own = total_sum.at[960:PROJ_ROWS, :]
    moves = [
        send(own, small.at[r * 2 + c], es.at[1 + n], er.at[1 + n], device)
        for n, device in enumerate((p.across, p.core, p.diagonal))
    ]
    for move in moves:
        move.start()
    small[r * 2 + c] = total_sum[960:PROJ_ROWS, :]
    sum_ref[...] = total_sum[...]
    for ch in range(2):
        summed.finish_sum(ch)
        cross(ch).wait_send()
        for n in range(2):
            beside(n, ch).wait_send()
    for n, (rr, cc) in enumerate(((1 - r, c), (r, 1 - c), (1 - r, 1 - c))):
        send(own, small.at[rr * 2 + cc], es.at[1 + n], er.at[1 + n], p.core).wait_recv()
    for move in moves:
        move.wait_send()
    back_half.wait()
    big_ref[2, 1 - p.y] = last[...]
    small_ref[...] = small[...]
    back.finish()


def end(pay, rest, own_half, oth_half):
    return pl.pallas_call(
        end_kernel,
        in_specs=[VMEM] * 4,
        out_specs=[HBM, VMEM, VMEM, VMEM],
        out_shape=[
            jax.ShapeDtypeStruct((2, ROWS // 2, HALF), BF),
            jax.ShapeDtypeStruct((PROJ_ROWS, HALF), BF),
            jax.ShapeDtypeStruct((4, 64, HALF), BF),
            jax.ShapeDtypeStruct((3, 2, 4, 80, HALF), BF),
        ],
        scratch_shapes=[
            pltpu.VMEM((4, 64, HALF), BF),
            pltpu.VMEM((PROJ_ROWS, HALF), BF),
            pltpu.VMEM((2, PROJ_ROWS, HALF), BF),
            pltpu.VMEM((PROJ_ROWS, HALF), BF),
            pltpu.VMEM((PROJ_ROWS, HALF), BF),
            *Sum.scratch(PROJ_ROWS // 2, 2),
            pltpu.SemaphoreType.DMA((4,)),
            pltpu.SemaphoreType.DMA((4,)),
            pltpu.SemaphoreType.DMA((2,)),
            pltpu.SemaphoreType.DMA((2,)),
            pltpu.VMEM((4, 80, HALF), BF),
            pltpu.SemaphoreType.DMA((4,)),
            pltpu.SemaphoreType.DMA((4,)),
            pltpu.SemaphoreType.DMA,
            pltpu.SemaphoreType.DMA((2,)),
            pltpu.SemaphoreType.DMA((3,)),
        ],
        **comm_params("end", 7),
    )(pay, rest, own_half, oth_half)


def outputs_kernel(
    ght0, ght1, hid, t0, t1, t2, t3, t4, big_i0, big_i1, big_o, big_d, small, perm_ref,
    hid_ref, gt_ref, gk_ref, gv_ref, gc_ref, gq_ref, gp_ref, gi_ref, go_ref, gd_ref,
    gdep_ref, gbq_ref, gbv_ref, gbc_ref, gbp_ref, gwk_ref, gbk_ref,
    gbd_ref, gg1_ref, gb1_ref, gbi_ref, gbo_ref, gg2_ref, gb2_ref,
):
    i = pl.program_id(0)
    hid_ref[...] = hid[...]

    @pl.when(lax.rem(i, 2) == 0)
    def _():
        gt_ref[...] = ght0[0].astype(F32)

    @pl.when(lax.rem(i, 2) == 1)
    def _():
        gt_ref[...] = ght1[0].astype(F32)

    for src, ref in ((t0, gk_ref), (t1, gv_ref), (t2, gc_ref), (t3, gq_ref), (t4, gp_ref), (big_o, go_ref), (big_d, gd_ref)):
        ref[...] = src[...].astype(F32)
    gi_ref[:, 0:HALF] = big_i0[...].astype(F32)
    gi_ref[:, HALF:D] = big_i1[...].astype(F32)

    @pl.when(i == 0)
    def _():
        tail = small[1].astype(F32)
        norms = small[2].astype(F32)
        depth = small[3].astype(F32)
        kernel_grad = jnp.concatenate([small[0].astype(F32), tail[0:8]], axis=0).astype(BF)
        gwk_ref[...] = nn(perm_ref[...], kernel_grad)
        bias = nt(tail[16:24, 0:72].astype(BF), perm_ref[...])
        gbk_ref[...] = bias[0:1, :].reshape(54)
        for k, ref in enumerate((gbq_ref, gbv_ref, gbc_ref, gbp_ref)):
            ref[...] = tail[8 + k : 9 + k, :].reshape(HALF)
        for k, ref in enumerate((gbo_ref, gg2_ref, gb2_ref, gbd_ref, gg1_ref, gb1_ref)):
            ref[...] = jnp.concatenate([norms[k : k + 1, :], norms[8 + k : 9 + k, :]], axis=1).reshape(D)
        gbi_ref[...] = jnp.concatenate([norms[16 + k : 17 + k, :] for k in range(8)], axis=1).reshape(FF)
        gdep_ref[:, 0:HALF] = depth[0:KW, :]
        gdep_ref[:, HALF:D] = depth[16 : 16 + KW, :]


def outputs(ght0, ght1, hid, total, big, small, perm):
    rows = 512
    at = lambda n, first: pl.BlockSpec((n, HALF), lambda i: (first + i, 0))
    blk = at(rows, 0)
    chunk = pl.BlockSpec((1, rows, HALF), lambda i: (lax.div(i, 2), 0, 0))
    shapes = [(KW, D)] + [(HALF,)] * 4 + [(54, HALF), (54,)] + [(D,)] * 3 + [(FF,)] + [(D,)] * 3
    main = [(192, HALF)] * 5 + [(HALF, D), (D, HALF), (HALF, HALF)]
    return pl.pallas_call(
        outputs_kernel,
        grid=(4,),
        in_specs=[chunk, chunk, blk]
        + [at(48, 4 * j) for j in range(5)]
        + [at(96, 0), at(96, 4), at(192, 4), at(96, 16), whole((4, 64, HALF)), whole((54, 72))],
        out_specs=[blk, blk]
        + [at(48, 0)] * 5
        + [pl.BlockSpec((96, D), lambda i: (i, 0)), at(192, 0), at(96, 0)]
        + [whole(shape) for shape in shapes],
        out_shape=[jax.ShapeDtypeStruct((LMAX, HALF), BF), jax.ShapeDtypeStruct((LMAX, HALF), F32)]
        + [jax.ShapeDtypeStruct(shape, F32) for shape in main + shapes],
        **params("outputs"),
    )(ght0, ght1, hid, total, total, total, total, total, big, big, big, big, small, perm)


def constants():
    spread = np.zeros((72, KW * HALF), np.float32)
    ones8 = np.zeros((8, HALF), np.float32)
    ones24 = np.zeros((24, HALF), np.float32)
    perm = np.zeros((72, 54), np.float32)
    for head in range(6):
        cols = slice(head * HD, (head + 1) * HD)
        ones8[head, cols] = 1
        ones24[head // 2 * 8 + head % 2, cols] = 1
        for j in range(KW):
            spread[j * 8 + head, j * HALF + head * HD : j * HALF + (head + 1) * HD] = 1
            perm[j * 8 + head, head * KW + j] = 1
    return [jnp.asarray(a, BF) for a in (spread, ones8, ones24, perm)]


def per_device(
    groups, tokens, cotangent, seq_lengths, w_query, w_key, w_value, w_convout, w_point, w_depth,
    b_query, b_value, b_convout, b_point, w_kernel, b_kernel, w_dense, b_dense, gain_one, bias_one,
    w_inter, b_inter, w_output, b_output, gain_two, bias_two,
):
    lens = seq_lengths
    spread, ones8, ones24, perm = constants()
    wdep = w_depth.T

    seq, w5, wk72, bk72 = start(
        tokens, (w_key.T, w_value.T, w_convout.T, w_query.T, w_point.T), w_kernel.T, b_kernel, perm
    )
    kd, kt, vz, q, qs, pt, kp, conv, mix, dep, hown, wi, wd, cot, woq = front(
        lens, seq, w5, wdep, b_value, b_convout, b_query, b_point, wk72, bk72, spread,
        w_inter[0], w_dense.reshape(2, 192, HALF), w_output[0], cotangent,
    )
    ctx, lse, wo = attend(lens, qs, kd, vz, w_output[0], woq)
    vectors = (b_dense, gain_one, bias_one, b_output, gain_two, bias_two)
    hid, gpre, gctx, gcv, delta, payf, smf, gbi = ffn(
        lens, ctx, mix, hown, cot, wd.reshape(D, D), wi, wo, vectors, b_inter, ones24
    )
    gqm, gpt, gco, gwk, gbk, dq, dk, dv, half0, piece1, mid2, hid = back(
        lens, gcv, conv, kp, q, pt, wk72, spread, ones8, qs, gctx, kd, vz, kt, lse, delta, payf, hid
    )
    pay5, own_half, oth_half, ght0, rest = final(
        lens, seq, dk, dv, gco, dq, gqm, gpt, gpre, dep, w5, wdep, smf, gbi, gwk, gbk, half0, piece1, mid2
    )
    ght1, total, small, big = end(pay5, rest, own_half, oth_half)
    big = big.reshape(FFN_ROWS, HALF)
    if groups > 8:
        total, big, small = lax.psum(tuple(x.astype(F32) * 0.125 for x in (total, big, small)), "dp")
        total, big, small = total.astype(BF), big.astype(BF), small.astype(BF)
    (
        hidden_out, gt, gk, gv, gc, gq, gp, gi, go, gd, gdep, gbq, gbv, gbc, gbp, gwk, gbk, gbd, gg1, gb1, gbi, gbo, gg2, gb2,
    ) = outputs(ght0, ght1, hid.reshape(LMAX, HALF), total, big, small, perm.T)
    return (
        hidden_out, gt, gq.T, gk.T, gv.T, gc.T, gp.T, gdep.T, gbq, gbv, gbc, gbp, gwk.T, gbk, gd, gbd, gg1, gb1,
        gi[None], gbi, go[None], gbo, gg2, gb2,
    )


def solution(mesh):
    act = P(("dp", "col"), "row")
    rep = P()
    proj = P("row", "col")
    in_specs = (
        act, act, P("dp"), proj, proj, proj, proj, proj, rep, rep, rep, rep, rep, rep, rep, P("col", "row"),
        rep, rep, rep, P("row", None, "col"), rep, P("row", "col", None), rep, rep, rep,
    )
    out_specs = (
        act, act, proj, proj, proj, proj, proj, rep, rep, rep, rep, rep, rep, rep, P("col", "row"),
        rep, rep, rep, P("row", None, "col"), rep, P("row", "col", None), rep, rep, rep,
    )
    return jax.shard_map(
        functools.partial(per_device, mesh.shape["dp"]), mesh=mesh, in_specs=in_specs, out_specs=out_specs, check_vma=False)
```

```python
import functools

import jax
import jax.numpy as jnp
import numpy as np
from jax import lax
from jax.experimental import pallas as pl
from jax.experimental.pallas import tpu as pltpu
from jax.sharding import PartitionSpec as P

D = 768
HALF = 384
HD = 64
KW = 9
FF = 3072
GW = 1536
LMAX = 2048
ROWS = 1024
EPS = 1e-12
LOG2E = 1.4426950408889634
LN2 = 0.6931471805599453
BF = jnp.bfloat16
F32 = jnp.float32
VMEM_BYTES = 63 * 1024 * 1024
PAD = 16
FFN_ROWS = 1920
FFN_CHUNK = 640
PROJ_ROWS = 1024
MESH = pl.DeviceIdType.MESH
HBM = pl.BlockSpec(memory_space=pl.ANY)
VMEM = pl.BlockSpec(memory_space=pltpu.VMEM)


def nn(a, b):
    return lax.dot_general(a, b, (((1,), (0,)), ((), ())), preferred_element_type=F32)


def nt(a, b):
    return lax.dot_general(a, b, (((1,), (1,)), ((), ())), preferred_element_type=F32)


def col_sum(x):
    return jnp.sum(x, axis=0, keepdims=True)


def row_ids(start, rows):
    return start + lax.broadcasted_iota(jnp.int32, (rows, 1), 0)


def whole(shape):
    return pl.BlockSpec(shape, lambda *_: (0,) * len(shape))


def once(shape):
    return pl.BlockSpec(shape, lambda *_: (0,) * len(shape), pipeline_mode=pl.Buffered(1))


def half_index():
    return lax.axis_index("col")


def length(lens):
    return lens[lax.axis_index("row")]


def line(ref):
    return ref[...].astype(F32).reshape(1, ref.shape[0])


def params(name):
    return dict(
        name=name,
        compiler_params=pltpu.CompilerParams(vmem_limit_bytes=VMEM_BYTES),
    )


def lanes(k, width=HALF):
    return pl.ds(pl.multiple_of(k * width, 128), width)


def rows_at(start, count, step=16):
    return pl.ds(pl.multiple_of(start, step), count)


def send(src, dst, send_sem, recv_sem, device):
    return pltpu.make_async_remote_copy(
        src_ref=src, dst_ref=dst, send_sem=send_sem, recv_sem=recv_sem, device_id=device, device_id_type=MESH
    )


class Place:
    def __init__(self):
        self.d = lax.axis_index("dp")
        self.r = lax.axis_index("row")
        self.c = lax.axis_index("col")
        self.k = lax.rem(self.d, 8)
        self.base = self.d - self.k
        self.y = lax.rem(self.k, 2)
        self.z = lax.div(self.k, 2)
        self.beside = {"dp": self.base + self.z * 2 + 1 - self.y}
        self.across = {"row": 1 - self.r}
        self.core = {"col": 1 - self.c}
        self.diagonal = {"row": 1 - self.r, "col": 1 - self.c}

    def eight(self, offset):
        other = lax.rem(self.k + offset, 8)
        return other, {"dp": self.base + other}

    def four(self, offset):
        other = lax.rem(self.z + offset, 4)
        return other, {"dp": self.base + other * 2 + self.y}


def meet(devices):
    barrier = pltpu.get_barrier_semaphore()
    for device in devices:
        pl.semaphore_signal(barrier, inc=1, device_id=device, device_id_type=MESH)
    pl.semaphore_wait(barrier, len(devices))


def comm_params(name, number):
    return dict(
        name=name,
        compiler_params=pltpu.CompilerParams(
            vmem_limit_bytes=VMEM_BYTES, collective_id=number, has_side_effects=True
        ),
    )


class Gather:
    def __init__(self, place, own, full, part, block, step, send_sem, recv_sem, first):
        self.p, self.own, self.full, self.part, self.block, self.h = place, own, full, part, block, step
        self.s, self.v, self.f = send_sem, recv_sem, first

    def _move(self, src, dst, n, device):
        return send(src, dst, self.s.at[self.f + n], self.v.at[self.f + n], device)

    def _cross(self, r):
        p = self.p
        at = (p.y * 4 + p.z) * self.h
        return self._move(self.part(self.own, at, self.h), self.block(self.full, r, p.c, at, self.h), 0, p.across)

    def _near(self, c):
        p = self.p
        return self._move(self.own, self.block(self.full, p.r, c, 0, 8 * self.h), 1, p.core)

    def _pass(self, offset, z):
        p = self.p
        here = self.block(self.full, 1 - p.r, p.c, (p.y * 4 + z) * self.h, self.h)
        return self._move(here, here, 1 + offset, p.four(offset)[1])

    def _turn(self, y):
        p = self.p
        here = self.block(self.full, 1 - p.r, p.c, y * 4 * self.h, 4 * self.h)
        return self._move(here, here, 5, p.beside)

    def _last(self, c):
        p = self.p
        here = self.block(self.full, 1 - p.r, c, 0, 8 * self.h)
        return self._move(here, here, 6, p.core)

    def start(self):
        self._cross(self.p.r).start()
        self._near(self.p.c).start()

    def relay(self):
        p = self.p
        self._cross(1 - p.r).wait_recv()
        for offset in (1, 2, 3):
            self._pass(offset, p.z).start()

    def turn(self):
        p = self.p
        for offset in (1, 2, 3):
            self._pass(offset, lax.rem(p.z + 4 - offset, 4)).wait_recv()
        self._turn(p.y).start()

    def share(self):
        p = self.p
        self._turn(1 - p.y).wait_recv()
        self._last(p.c).start()

    def finish(self):
        p = self.p
        self._last(1 - p.c).wait_recv()
        self._near(1 - p.c).wait_recv()
        self._cross(p.r).wait_send()
        self._near(p.c).wait_send()
        for offset in (1, 2, 3):
            self._pass(offset, p.z).wait_send()
        self._turn(p.y).wait_send()
        self._last(p.c).wait_send()


def middle_part(ref, first, rows):
    return ref.at[:, rows_at(first, rows, 8), :]


def middle_block(ref, r, c, first, rows):
    return ref.at[:, rows_at(c * 192 + first, rows, 8), lanes(r)]


def rows_part(ref, first, rows):
    return ref.at[rows_at(first, rows), :]


def inter_block(ref, r, c, first, rows):
    return ref.at[r, rows_at(first, rows), lanes(c, 768)]


def output_block(ref, r, c, first, rows):
    return ref.at[r, rows_at(c * 768 + first, rows), :]


class ToRows:
    def __init__(self, place, src, dst, stage, local_sem, send_sem, recv_sem):
        self.p, self.src, self.dst, self.stage = place, src, dst, stage
        self.l, self.s, self.v = local_sem, send_sem, recv_sem

    def _cross(self, q, k):
        half = self.src.at[q * ROWS : (q + 1) * ROWS, :]
        return send(half, self.dst.at[:, lanes(k)], self.s.at[q], self.v.at[0], {"row": 1 - self.p.r, "col": q})

    def _near(self):
        p = self.p
        half = self.src.at[rows_at((1 - p.c) * ROWS, ROWS), :]
        return send(half, self.dst.at[:, lanes(p.r)], self.s.at[2], self.v.at[1], p.core)

    def _load(self):
        return pltpu.make_async_copy(self.src.at[rows_at(self.p.c * ROWS, ROWS), :], self.stage, self.l.at[0])

    def _store(self):
        return pltpu.make_async_copy(self.stage, self.dst.at[:, lanes(self.p.r)], self.l.at[1])

    def start(self):
        p = self.p

        @pl.when(p.r != p.c)
        def _():
            self._cross(0, p.r).start()
            self._cross(1, p.r).start()

        @pl.when(p.r == p.c)
        def _():
            self._near().start()
            self._load().start()

    def store(self):
        @pl.when(self.p.r == self.p.c)
        def _():
            self._load().wait()
            self._store().start()

    def finish(self):
        p = self.p
        self._cross(0, 1 - p.r).wait_recv()

        @pl.when(p.r != p.c)
        def _():
            self._cross(0, p.r).wait_send()
            self._cross(1, p.r).wait_send()
            self._near().wait_recv()

        @pl.when(p.r == p.c)
        def _():
            self._near().wait_send()
            self._store().wait()


class FromRows:
    def __init__(self, place, src, dst, local_sem, send_sem, recv_sem):
        self.p, self.src, self.dst = place, src, dst
        self.l, self.s, self.v = local_sem, send_sem, recv_sem

    def _cross(self, q):
        p = self.p
        place = self.dst.at[q]
        return send(self.src.at[:, lanes(1 - p.r)], place, self.s.at[0], self.v.at[q], {"row": 1 - p.r, "col": p.r})

    def _near(self, q):
        p = self.p
        place = self.dst.at[q]
        return send(self.src.at[:, lanes(p.r)], place, self.s.at[1], self.v.at[2], p.core)

    def _local(self):
        p = self.p
        place = self.dst.at[p.c]
        return pltpu.make_async_copy(self.src.at[:, lanes(p.r)], place, self.l)

    def start(self):
        p = self.p
        self._cross(p.c).start()

        @pl.when(p.r != p.c)
        def _():
            self._near(p.c).start()

        @pl.when(p.r == p.c)
        def _():
            self._local().start()

    def finish(self):
        p = self.p
        self._cross(p.c).wait_send()

        @pl.when(p.r != p.c)
        def _():
            self._near(p.c).wait_send()
            self._cross(0).wait_recv()
            self._cross(1).wait_recv()

        @pl.when(p.r == p.c)
        def _():
            self._near(1 - p.c).wait_recv()
            self._local().wait()


class Sum:
    def __init__(self, place, far, mid, ybuf, zbuf, total, rows, s, v, first=0):
        self.p, self.far, self.mid, self.ybuf, self.zbuf, self.total = place, far, mid, ybuf, zbuf, total
        self.rows, self.s, self.v, self.first = rows, s, v, first

    def _sems(self, ch, n):
        i = self.first + ch * 8 + n
        return self.s.at[i], self.v.at[i]

    def _beside(self):
        return self.p.beside

    def _halves(self, ch, y):
        return rows_at(ch * self.rows + y * (self.rows // 2), self.rows // 2)

    def _piece(self, ch, z):
        return rows_at(ch * self.rows + self.p.y * (self.rows // 2) + z * (self.rows // 8), self.rows // 8)

    def _half(self, ch):
        return send(self.far.at[self._halves(ch, 1 - self.p.y), :], self.ybuf.at[ch], *self._sems(ch, 0), self._beside())

    def _quarter(self, ch, offset):
        other, device = self.p.four(offset)
        src = self.mid.at[ch, rows_at(other * (self.rows // 8), self.rows // 8), :]
        return send(src, self.zbuf.at[ch, offset - 1], *self._sems(ch, offset), device)

    def _along(self, ch, offset, z):
        _, device = self.p.four(offset)
        here = self.total.at[self._piece(ch, z), :]
        return send(here, here, *self._sems(ch, 3 + offset), device)

    def _back(self, ch, y):
        here = self.total.at[self._halves(ch, y), :]
        return send(here, here, *self._sems(ch, 7), self._beside())

    def half(self, ch):
        self._half(ch).start()

    def quarter(self, ch):
        self._half(ch).wait_recv()
        both = self.far[self._halves(ch, self.p.y), :].astype(F32) + self.ybuf[ch].astype(F32)
        self.mid[ch] = both.astype(BF)
        for offset in (1, 2, 3):
            self._quarter(ch, offset).start()

    def collect(self, ch):
        both = self.mid[ch, rows_at(self.p.z * (self.rows // 8), self.rows // 8), :].astype(F32)
        for offset in (1, 2, 3):
            self._quarter(ch, offset).wait_recv()
            both = both + self.zbuf[ch, offset - 1].astype(F32)
        return both.astype(BF)

    def along(self, ch, piece):
        self.total[self._piece(ch, self.p.z), :] = piece
        for offset in (1, 2, 3):
            self._along(ch, offset, self.p.z).start()

    def back(self, ch):
        for offset in (1, 2, 3):
            self._along(ch, offset, lax.rem(self.p.z + 4 - offset, 4)).wait_recv()
        self._back(ch, self.p.y).start()

    def finish_sum(self, ch):
        self._half(ch).wait_send()
        for offset in (1, 2, 3):
            self._quarter(ch, offset).wait_send()

    def finish_spread(self, ch):
        self._back(ch, 1 - self.p.y).wait_recv()
        for offset in (1, 2, 3):
            self._along(ch, offset, self.p.z).wait_send()
        self._back(ch, self.p.y).wait_send()

    @staticmethod
    def scratch(rows, chunks):
        return [
            pltpu.VMEM((chunks, rows // 2, HALF), BF),
            pltpu.VMEM((chunks, rows // 2, HALF), BF),
            pltpu.VMEM((chunks, 3, rows // 8, HALF), BF),
            pltpu.SemaphoreType.DMA((8 * chunks,)),
            pltpu.SemaphoreType.DMA((8 * chunks,)),
        ]


class Groups:
    def __init__(self, place, s, v):
        self.p, self.s, self.v = place, s, v

    def half(self, n, mine, ybuf):
        return send(mine.at[1 - self.p.y], ybuf, self.s.at[n], self.v.at[n], self.p.beside)

    def quarter(self, n, mid, zbuf, offset):
        other, device = self.p.four(offset)
        n = n + offset - 1
        return send(mid.at[other], zbuf.at[offset - 1], self.s.at[n], self.v.at[n], device)

    def cross(self, n, both, xbuf):
        return send(both.at[1 - self.p.r], xbuf, self.s.at[n], self.v.at[n], self.p.across)

    def along(self, n, half, offset, z):
        n = n + offset - 1
        return send(half.at[z], half.at[z], self.s.at[n], self.v.at[n], self.p.four(offset)[1])

    def back(self, n, half, other):
        return send(half, other, self.s.at[n], self.v.at[n], self.p.beside)

    def start_quarters(self, n, mid, zbuf):
        for offset in (1, 2, 3):
            self.quarter(n, mid, zbuf, offset).start()

    def collect(self, n, mid, zbuf, both):
        total = mid[self.p.z].astype(F32)
        for offset in (1, 2, 3):
            self.quarter(n, mid, zbuf, offset).wait_recv()
            total = total + zbuf[offset - 1].astype(F32)
        both[...] = total.astype(BF)

    def start_along(self, n, half, piece):
        half[self.p.z] = piece
        for offset in (1, 2, 3):
            self.along(n, half, offset, self.p.z).start()

    def await_along(self, n, half):
        for offset in (1, 2, 3):
            self.along(n, half, offset, lax.rem(self.p.z + 4 - offset, 4)).wait_recv()

    def sent(self, n, ref, kind):
        for offset in (1, 2, 3):
            kind(n, *ref, offset).wait_send()


def everyone(p):
    return [p.across, p.core, p.diagonal, p.beside] + [p.four(o)[1] for o in (1, 2, 3)]


def front_kernel(
    lens, tok_ref, wk_own, wv_own, wc_own, wq_own, wp_own, kern_ref, kb_ref, perm_ref,
    wdep_ref, bv_ref, bc_ref, bq_ref, bp_ref, spread_ref, wi_own, wd_own, wo_own, cot_own,
    kd_ref, kt_ref, vz_ref, q_ref, qs_ref, pt_ref, kp_ref, conv_ref, mix_ref, dep_ref, h_ref, wk_ref, bk_ref,
    seq_out, w5_out, wi_ref, wd_ref, cot_ref, wop_ref,
    own, seq_ref, w_ref, stage, first_key, hbuf, cbuf, lsem, ts, tr, gs, gr, cs, cr,
):
    i = pl.program_id(0)
    p = Place()
    r, c = p.r, p.c
    n = lens[r]
    proj = Gather(p, own, w_ref, middle_part, middle_block, 24, gs, gr, 0)
    inter = Gather(p, wi_own, wi_ref, rows_part, inter_block, 48, gs, gr, 7)
    dense = Gather(p, wd_own, wd_ref, middle_part, middle_block, 24, gs, gr, 14)
    cot_rows = ToRows(p, cot_own, cot_ref, stage, lsem, cs, cr)
    part_output = send(rows_part(wo_own, (p.y * 4 + p.z) * 96, 96), wop_ref, gs.at[21], gr.at[21], p.across)
    keep_inter = pltpu.make_async_copy(wi_own, inter_block(wi_ref, r, c, 0, HALF), lsem.at[2])
    keep_dense = pltpu.make_async_copy(wd_own, middle_block(wd_ref, r, c, 0, 192), lsem.at[3])
    keep_own = pltpu.make_async_copy(tok_ref, seq_ref.at[PAD : PAD + LMAX, lanes(r)], lsem.at[4])
    keep_seq = pltpu.make_async_copy(seq_ref, seq_out, lsem.at[5])
    keep_w = pltpu.make_async_copy(w_ref, w5_out, lsem.at[6])

    def chunk(m, k):
        return seq_ref.at[PAD + m * 512 : PAD + (m + 1) * 512, lanes(k)]

    def cross(m, k):
        return send(tok_ref.at[m * 512 : (m + 1) * 512, :], chunk(m, k), ts.at[m], tr.at[m], {"row": 1 - r, "col": m // 2})

    def near(k):
        return send(tok_ref, seq_ref.at[PAD : PAD + LMAX, lanes(k)], ts.at[4], tr.at[4], p.core)

    def forward(m):
        return send(chunk(m, 1 - r), chunk(m, 1 - r), ts.at[5 + m], tr.at[5 + m], p.core)

    @pl.when(i == 0)
    def _():
        for j, ref in enumerate((wk_own, wv_own, wc_own, wq_own, wp_own)):
            own[j] = ref[...]
        seq_ref[0:PAD, :] = jnp.zeros((PAD, D), BF)
        seq_ref[PAD + LMAX :, :] = jnp.zeros((PAD, D), BF)
        meet(everyone(p))
        proj.start()
        inter._cross(r).start()
        dense._cross(r).start()
        part_output.start()

        @pl.when(r != c)
        def _():
            for m in (0, 2, 1, 3):
                cross(m, r).start()

        @pl.when(r == c)
        def _():
            near(r).start()
            keep_own.start()

        cot_rows.start()
        inter._near(c).start()
        dense._near(c).start()
        keep_inter.start()
        keep_dense.start()
        middle_block(w_ref, r, c, 0, 192)[...] = own[...]
        wk_ref[...] = nn(perm_ref[...], kern_ref[...]).astype(BF)
        bk_ref[...] = nt(perm_ref[...], jnp.broadcast_to(line(kb_ref), (128, 54)).astype(BF))
        proj.relay()
        inter.relay()
        dense.relay()
        proj.turn()
        for q in range(2):

            @pl.when(c == q)
            def _():
                for m in (2 * q, 2 * q + 1):
                    cross(m, 1 - r).wait_recv()
                    forward(m).start()

        proj.share()
        for q in range(2):

            @pl.when(c == q)
            def _():
                for m in (2 - 2 * q, 3 - 2 * q):
                    forward(m).wait_recv()
                for m in (2 * q, 2 * q + 1):
                    forward(m).wait_send()

        @pl.when(r != c)
        def _():
            for m in range(4):
                cross(m, r).wait_send()
            near(r).wait_recv()

        @pl.when(r == c)
        def _():
            near(r).wait_send()
            keep_own.wait()

        proj.finish()
        keep_seq.start()
        keep_w.start()

    @pl.when(i == 1)
    def _():
        inter.turn()
        dense.turn()
        cot_rows.store()

    @pl.when(i == 3)
    def _():
        inter.share()
        dense.share()

    krows = kd_ref.shape[0]
    keep_key = row_ids(i * krows, krows) < n
    tok = seq_ref[rows_at(PAD + i * krows, krows), :]
    h = jnp.where(keep_key, tok.astype(F32), 0.0).astype(BF)
    k = nt(h, w_ref[0])
    v = nt(h, w_ref[1]) + line(bv_ref)

    @pl.when(i == 0)
    def _():
        first_key[...] = k[0:8]

    kd_ref[...] = jnp.where(keep_key, k, first_key[0:1]).astype(BF)
    kt_ref[...] = k.T.astype(BF)
    vz_ref[...] = jnp.where(keep_key, v, 0.0).astype(BF)

    rows = q_ref.shape[0]
    wide = rows + 32
    base = pl.multiple_of(i * rows, 16)
    start = pl.multiple_of(p.c * ROWS + i * rows, 16)
    ids = row_ids(start - 16, wide)
    keep = (ids >= 0) & (ids < n)
    hw = jnp.where(keep, seq_ref[pl.ds(start, wide), :].astype(F32), 0.0)
    hbuf[...] = hw
    depth = jnp.zeros((rows, D), F32)
    wdep = wdep_ref[...].astype(F32)
    for j in range(KW):
        depth = depth + hbuf[12 + j : 12 + j + rows, :] * wdep[j : j + 1, :]
    depth_low = depth.astype(BF)
    dep_ref[...] = depth_low
    hl = hw.astype(BF)
    h_ref[...] = hl[16 : 16 + rows]
    conv = jnp.where(keep, nt(hl, w_ref[2]) + line(bc_ref), 0.0)
    cbuf[...] = conv
    conv_ref[pl.ds(base, wide), :] = conv.astype(BF)
    q = nt(hl[16 : 16 + rows], w_ref[3]) + line(bq_ref)
    q_low = q.astype(BF)
    q_ref[...] = q_low
    qs_ref[...] = (q * (0.125 * LOG2E)).astype(BF)
    pt = nt(depth_low, w_ref[4]) + line(bp_ref)
    pt_ref[...] = pt.astype(BF)
    mixer = (pt * q_low.astype(F32)).astype(BF)
    logits = (nt(wk_ref[...], mixer) + bk_ref[:, 0:1]).reshape(KW, 8, rows)
    peak = jnp.max(logits, axis=0, keepdims=True)
    raised = jnp.exp(logits - peak)
    kp = (raised / jnp.sum(raised, axis=0, keepdims=True)).reshape(KW * 8, rows)
    kp_ref[...] = kp
    kpt = kp.T.astype(BF)
    mix = jnp.zeros((rows, HALF), F32)
    for j in range(KW):
        mix = mix + nn(kpt, spread_ref[:, j * HALF : (j + 1) * HALF]) * cbuf[12 + j : 12 + j + rows, :]
    mix_ref[...] = mix.astype(BF)

    @pl.when(i == pl.num_programs(0) - 1)
    def _():
        inter.finish()
        dense.finish()
        cot_rows.finish()
        part_output.wait()
        keep_inter.wait()
        keep_dense.wait()
        keep_seq.wait()
        keep_w.wait()


def front(lens, tokens, weights, w_kernel, b_kernel, perm, wdep, bv, bc, bq, bp, spread, w_inter, w_dense, w_output, cotangent):
    rows = 256
    keys = 512
    blk = pl.BlockSpec((rows, HALF), lambda i, lens: (i, 0))
    full = pl.BlockSpec((rows, D), lambda i, lens: (i, 0))
    half = jax.ShapeDtypeStruct((ROWS, HALF), BF)
    return pl.pallas_call(
        front_kernel,
        grid_spec=pltpu.PrefetchScalarGridSpec(
            num_scalar_prefetch=1,
            grid=(ROWS // rows,),
            in_specs=[HBM]
            + [once((192, HALF))] * 5
            + [once((54, HALF)), whole((54,)), once((72, 54)), once((KW, D))]
            + [whole((HALF,))] * 4
            + [once((72, KW * HALF)), once((HALF, D)), once((2, 192, HALF)), once((D, HALF)), HBM],
            out_specs=[
                pl.BlockSpec((keys, HALF), lambda i, lens: (i, 0)),
                pl.BlockSpec((HALF, keys), lambda i, lens: (0, i)),
                pl.BlockSpec((keys, HALF), lambda i, lens: (i, 0)),
                blk,
                blk,
                blk,
                pl.BlockSpec((72, rows), lambda i, lens: (0, i)),
                whole((ROWS + 32, HALF)),
                blk,
                full,
                full,
                whole((72, HALF)),
                whole((72, 128)),
            ]
            + [HBM] * 6,
            scratch_shapes=[
                pltpu.VMEM((5, 192, HALF), BF),
                pltpu.VMEM((LMAX + 2 * PAD, D), BF),
                pltpu.VMEM((5, HALF, D), BF),
                pltpu.VMEM((ROWS, HALF), BF),
                pltpu.VMEM((8, HALF), F32),
                pltpu.VMEM((rows + 32, D), F32),
                pltpu.VMEM((rows + 32, HALF), F32),
                pltpu.SemaphoreType.DMA((7,)),
                pltpu.SemaphoreType.DMA((9,)),
                pltpu.SemaphoreType.DMA((9,)),
                pltpu.SemaphoreType.DMA((22,)),
                pltpu.SemaphoreType.DMA((22,)),
                pltpu.SemaphoreType.DMA((3,)),
                pltpu.SemaphoreType.DMA((2,)),
            ],
        ),
        out_shape=[
            jax.ShapeDtypeStruct((LMAX, HALF), BF),
            jax.ShapeDtypeStruct((HALF, LMAX), BF),
            jax.ShapeDtypeStruct((LMAX, HALF), BF),
            half,
            half,
            half,
            jax.ShapeDtypeStruct((72, ROWS), F32),
            jax.ShapeDtypeStruct((ROWS + 32, HALF), BF),
            half,
            jax.ShapeDtypeStruct((ROWS, D), BF),
            jax.ShapeDtypeStruct((ROWS, D), BF),
            jax.ShapeDtypeStruct((72, HALF), BF),
            jax.ShapeDtypeStruct((72, 128), F32),
            jax.ShapeDtypeStruct((LMAX + 2 * PAD, D), BF),
            jax.ShapeDtypeStruct((5, HALF, D), BF),
            jax.ShapeDtypeStruct((2, HALF, GW), BF),
            jax.ShapeDtypeStruct((2, HALF, D), BF),
            jax.ShapeDtypeStruct((ROWS, D), BF),
            jax.ShapeDtypeStruct((96, HALF), BF),
        ],
        **comm_params("front", 2),
    )(
        lens, tokens, *weights, w_kernel, b_kernel, perm, wdep, bv, bc, bq, bp, spread, w_inter, w_dense, w_output, cotangent
    )


def attend_kernel(lens, q_ref, k_ref, v_ref, wo_own, woq, ctx_ref, lse_ref, wo_ref, lsem, gs, gr):
    i = pl.program_id(0)
    p = Place()
    there = 1 - p.r
    keep = pltpu.make_async_copy(wo_own, output_block(wo_ref, p.r, p.c, 0, D), lsem.at[0])
    at = lambda z: (p.y * 4 + z) * 96
    keep_part = pltpu.make_async_copy(woq, output_block(wo_ref, there, p.c, at(p.z), 96), lsem.at[1])

    def near(c):
        return send(wo_own, output_block(wo_ref, p.r, c, 0, D), gs.at[0], gr.at[0], p.core)

    def pass_on(offset, z):
        return send(woq, output_block(wo_ref, there, p.c, at(z), 96), gs.at[offset], gr.at[offset], p.four(offset)[1])

    def turn(y):
        here = output_block(wo_ref, there, p.c, y * HALF, HALF)
        return send(here, here, gs.at[4], gr.at[4], p.beside)

    def last(c):
        here = output_block(wo_ref, there, c, 0, D)
        return send(here, here, gs.at[5], gr.at[5], p.core)

    @pl.when(i == 0)
    def _():
        meet([p.core, p.beside] + [p.four(o)[1] for o in (1, 2, 3)])
        for offset in (1, 2, 3):
            pass_on(offset, p.z).start()
        near(p.c).start()
        keep.start()
        keep_part.start()

    @pl.when(i == 1)
    def _():
        keep_part.wait()
        for offset in (1, 2, 3):
            pass_on(offset, lax.rem(p.z + 4 - offset, 4)).wait_recv()
        turn(p.y).start()

    @pl.when(i == 2)
    def _():
        turn(1 - p.y).wait_recv()
        last(p.c).start()

    k = k_ref[...]
    ones = jnp.where(row_ids(0, LMAX) < lens[p.r], 1.0, 0.0)
    ve = jnp.concatenate([v_ref[...], jnp.broadcast_to(ones, (LMAX, 128)).astype(BF)], axis=1)
    rows = 256
    lane = lax.broadcasted_iota(jnp.int32, (rows, 128), 1)
    for u in range(ROWS // rows):
        part = slice(u * rows, (u + 1) * rows)
        outs = []
        for hh in range(2):
            q = jnp.where((lane < HD) == (hh == 0), q_ref[part, :], jnp.zeros((), BF))
            s = nt(q, k)
            peak = jnp.max(s, axis=1, keepdims=True)
            prob = jnp.exp2(s - peak).astype(BF)
            o = nn(prob, ve)
            outs.append(o[:, :128] / o[:, 128:])
            lse_ref[0, hh : hh + 1, part] = (peak + jnp.log2(o[:, 128:129])).T
        ctx_ref[part, :] = jnp.where(lane < HD, outs[0], outs[1]).astype(BF)

    @pl.when(i == pl.num_programs(0) - 1)
    def _():
        last(1 - p.c).wait_recv()
        near(1 - p.c).wait_recv()
        keep.wait()
        near(p.c).wait_send()
        last(p.c).wait_send()
        turn(p.y).wait_send()
        for offset in (1, 2, 3):
            pass_on(offset, p.z).wait_send()


def attend(lens, qs, kd, vz, w_output, part):
    pair = lambda rows: pl.BlockSpec((rows, 128), lambda p, lens: (0, p))
    return pl.pallas_call(
        attend_kernel,
        grid_spec=pltpu.PrefetchScalarGridSpec(
            num_scalar_prefetch=1,
            grid=(3,),
            in_specs=[pair(ROWS), pair(LMAX), pair(LMAX), once((D, HALF)), once((96, HALF))],
            out_specs=[pair(ROWS), pl.BlockSpec((1, 8, ROWS), lambda p, lens: (p, 0, 0)), HBM],
            scratch_shapes=[
                pltpu.SemaphoreType.DMA((2,)),
                pltpu.SemaphoreType.DMA((6,)),
                pltpu.SemaphoreType.DMA((6,)),
            ],
        ),
        out_shape=[
            jax.ShapeDtypeStruct((ROWS, HALF), BF),
            jax.ShapeDtypeStruct((3, 8, ROWS), F32),
            jax.ShapeDtypeStruct((2, GW, HALF), BF),
        ],
        **comm_params("attend", 3),
    )(lens, qs, kd, vz, w_output, part)


def back_kernel(
    lens, gcv_ref, conv_ref, kp_ref, q_ref, pt_ref, wk_ref, spread_ref, ones_ref,
    qs_ref, do_ref, k_ref, v_ref, kt_ref, lse_ref, del_ref, pay_all, pay_ref, hid_ref,
    gqm_ref, gpt_ref, gco_ref, gwk_ref, gbk_ref, dq_ref, dk_ref, dv_ref, half_ref, piece_ref, mid_ref, out_ref,
    acc, wbuf, tbuf, dka, dva, near, mine, ybuf, mid, zbuf, both, xbuf, half, ns, nr, s, v_sem, ls, hs, hr,
):
    step = pl.program_id(0)
    place = Place()
    groups = Groups(place, s, v_sem)
    hidden = FromRows(place, hid_ref, out_ref, ls, hs, hr)

    def near_copy(n):
        rr = 1 - place.r if n == 0 else place.r
        return send(pay_all.at[rr, 1 - place.c], near.at[rr], ns.at[n], nr.at[n], place.core)

    @pl.when(step == 0)
    def _():
        meet(everyone(place))
        near_copy(0).start()
        near_copy(1).start()
        hidden.start()
        acc[...] = jnp.zeros_like(acc)
        tbuf[...] = jnp.zeros_like(tbuf)
        gwk_ref[...] = jnp.zeros_like(gwk_ref)
        gbk_ref[...] = jnp.zeros_like(gbk_ref)

    @pl.when(step == 2)
    def _():
        near_copy(0).wait()
        near_copy(1).wait()
        for ch in range(3):
            for rr in range(2):
                total = near[rr, ch].astype(F32) + pay_ref[rr, 0, ch].astype(F32)
                mine[ch, :, :, rr] = total.astype(BF)
            groups.half(ch, mine.at[ch], ybuf.at[ch]).start()

    def settle(ch):
        groups.half(ch, mine.at[ch], ybuf.at[ch]).wait_recv()
        mid[ch] = (mine[ch, place.y].astype(F32) + ybuf[ch].astype(F32)).astype(BF)

    @pl.when(step == 5)
    def _():
        settle(0)
        groups.start_quarters(3, mid.at[0], zbuf.at[0])

    @pl.when(step == 7)
    def _():
        settle(1)
        groups.start_quarters(6, mid.at[1], zbuf.at[1])
        groups.collect(3, mid.at[0], zbuf.at[0], both.at[0])
        groups.cross(9, both.at[0], xbuf.at[0]).start()

    def merge(ch):
        groups.cross(9 + ch, both.at[ch], xbuf.at[ch]).wait_recv()
        return (both[ch, place.r].astype(F32) + xbuf[ch].astype(F32)).astype(BF)

    @pl.when(step == 8)
    def _():
        groups.start_along(11, half, merge(0))

    @pl.when(step == 9)
    def _():
        groups.collect(6, mid.at[1], zbuf.at[1], both.at[1])
        groups.cross(10, both.at[1], xbuf.at[1]).start()
        settle(2)
        mid_ref[...] = mid[2]

    @pl.when(step < 4)
    def _():
        rows = gcv_ref.shape[0]
        wide = rows + 32
        gcv = gcv_ref[...].astype(F32)
        wbuf[...] = conv_ref[pl.ds(pl.multiple_of(step * rows, 16), wide), :].astype(F32)
        kp = kp_ref[...]
        kpt = kp.T.astype(BF)
        gkps = []
        total = jnp.zeros((wide, HALF), F32)
        for j in range(KW):
            prod = (gcv * wbuf[12 + j : 12 + j + rows, :]).astype(BF)
            gkps.append(nt(ones_ref[...], prod))
            tbuf[24 : 24 + rows, :] = nn(kpt, spread_ref[:, j * HALF : (j + 1) * HALF]) * gcv
            total = total + tbuf[12 - j : 12 - j + wide, :]
        acc[pl.ds(pl.multiple_of(place.c * ROWS + step * rows, 16), wide), :] += total
        gkp = jnp.concatenate(gkps, axis=0).reshape(KW, 8, rows)
        kp3 = kp.reshape(KW, 8, rows)
        inner = jnp.sum(kp3 * gkp, axis=0, keepdims=True)
        gl = (kp3 * (gkp - inner)).reshape(KW * 8, rows)
        glt = gl.T.astype(BF)
        gbk_ref[0:1, 0:72] += col_sum(glt.astype(F32))
        q = q_ref[...].astype(F32)
        pt = pt_ref[...].astype(F32)
        gwk_ref[...] += nn(gl.astype(BF), (pt * q).astype(BF))
        gmix = nn(glt, wk_ref[...])
        gqm_ref[...] = (gmix * pt).astype(BF)
        gpt_ref[...] = (gmix * q).astype(BF)

    @pl.when(step == 3)
    def _():
        keep = row_ids(0, LMAX) < lens[place.r]
        gco_ref[...] = jnp.where(keep, acc[16 : 16 + LMAX, :], 0.0).astype(BF)

    @pl.when(step >= 4)
    def _():
        i = lax.rem(step, 2)
        k = k_ref[...]
        v = v_ref[...]
        rows = qs_ref.shape[0]
        lane = lax.broadcasted_iota(jnp.int32, (rows, 128), 1)
        dk = dv = None
        for hh in range(2):
            head = (lane < HD) == (hh == 0)
            q = jnp.where(head, qs_ref[...], jnp.zeros((), BF))
            do = jnp.where(head, do_ref[...], jnp.zeros((), BF))
            p = jnp.exp2(nt(k, q) - lse_ref[0, hh : hh + 1, :])
            ds = (p * (nt(v, do) - del_ref[0, hh : hh + 1, :])).astype(BF)
            dv_one = nn(p.astype(BF), do)
            dk_one = nn(ds, q)
            dv = dv_one if dv is None else dv + dv_one
            dk = dk_one if dk is None else dk + dk_one
            dq_ref[hh * HD : (hh + 1) * HD, :] = (nn(kt_ref[hh * HD : (hh + 1) * HD, :], ds) * 0.125).astype(BF)

        @pl.when(i == 0)
        def _():
            dka[...] = dk
            dva[...] = dv

        @pl.when(i == 1)
        def _():
            keep = row_ids(0, LMAX) < lens[place.r]
            dk_ref[...] = jnp.where(keep, (dka[...] + dk) * LN2, 0.0).astype(BF)
            dv_ref[...] = jnp.where(keep, dva[...] + dv, 0.0).astype(BF)

    @pl.when(step == 9)
    def _():
        piece_ref[...] = merge(1)
        groups.await_along(11, half)
        half_ref[...] = half[...]
        for ch in range(3):
            groups.half(ch, mine.at[ch], ybuf.at[ch]).wait_send()
        for ch in range(2):
            groups.cross(9 + ch, both.at[ch], xbuf.at[ch]).wait_send()
            for offset in (1, 2, 3):
                groups.quarter(3 + 3 * ch, mid.at[ch], zbuf.at[ch], offset).wait_send()
        for offset in (1, 2, 3):
            groups.along(11, half, offset, place.z).wait_send()
        hidden.finish()


def back(lens, gcv, conv, kp, q, pt, wk72, spread, ones8, qs, do, kd, vz, kt, lse, delta, pay, hid):
    crows = 256
    rows = 512
    early = lambda s: jnp.minimum(s, 3)
    late = lambda s: jnp.maximum(s - 4, 0)
    which = lambda s: lax.div(late(s), 2)
    part = lambda s: lax.rem(late(s), 2)
    cblk = pl.BlockSpec((crows, HALF), lambda s, lens: (early(s), 0))
    mine = pl.BlockSpec((rows, 128), lambda s, lens: (part(s), which(s)))
    pair = pl.BlockSpec((LMAX, 128), lambda s, lens: (0, which(s)))
    stats = pl.BlockSpec((1, 8, rows), lambda s, lens: (which(s), 0, part(s)))
    block = (3, 2, 4, 80, HALF)
    pay = pay.reshape((2, 2) + block)
    mine_pay = pl.BlockSpec(
        (2, 1) + block, lambda s, lens: (0, half_index(), 0, 0, 0, 0, 0), pipeline_mode=pl.Buffered(1)
    )
    return pl.pallas_call(
        back_kernel,
        grid_spec=pltpu.PrefetchScalarGridSpec(
            num_scalar_prefetch=1,
            grid=(10,),
            in_specs=[
                cblk,
                once((ROWS + 32, HALF)),
                pl.BlockSpec((72, crows), lambda s, lens: (0, early(s))),
                cblk,
                cblk,
                whole((72, HALF)),
                once((72, KW * HALF)),
                whole((8, HALF)),
                mine,
                mine,
                pair,
                pair,
                pl.BlockSpec((128, LMAX), lambda s, lens: (which(s), 0)),
                stats,
                stats,
                HBM,
                mine_pay,
                once((ROWS, D)),
            ],
            out_specs=[
                cblk,
                cblk,
                once((LMAX, HALF)),
                whole((72, HALF)),
                whole((8, 128)),
                pl.BlockSpec((128, rows), lambda s, lens: (which(s), part(s))),
                pair,
                pair,
                whole((4, 80, HALF)),
                whole((80, HALF)),
                whole((4, 2, 80, HALF)),
                HBM,
            ],
            scratch_shapes=[
                pltpu.VMEM((LMAX + 32, HALF), F32),
                pltpu.VMEM((crows + 32, HALF), F32),
                pltpu.VMEM((crows + 48, HALF), F32),
                pltpu.VMEM((LMAX, 128), F32),
                pltpu.VMEM((LMAX, 128), F32),
                pltpu.VMEM((2,) + block, BF),
                pltpu.VMEM((3, 2, 4, 2, 80, HALF), BF),
                pltpu.VMEM((3, 4, 2, 80, HALF), BF),
                pltpu.VMEM((3, 4, 2, 80, HALF), BF),
                pltpu.VMEM((2, 3, 2, 80, HALF), BF),
                pltpu.VMEM((2, 2, 80, HALF), BF),
                pltpu.VMEM((2, 80, HALF), BF),
                pltpu.VMEM((4, 80, HALF), BF),
                pltpu.SemaphoreType.DMA((2,)),
                pltpu.SemaphoreType.DMA((2,)),
                pltpu.SemaphoreType.DMA((14,)),
                pltpu.SemaphoreType.DMA((14,)),
                pltpu.SemaphoreType.DMA,
                pltpu.SemaphoreType.DMA((2,)),
                pltpu.SemaphoreType.DMA((3,)),
            ],
        ),
        out_shape=[
            jax.ShapeDtypeStruct((ROWS, HALF), BF),
            jax.ShapeDtypeStruct((ROWS, HALF), BF),
            jax.ShapeDtypeStruct((LMAX, HALF), BF),
            jax.ShapeDtypeStruct((72, HALF), F32),
            jax.ShapeDtypeStruct((8, 128), F32),
            jax.ShapeDtypeStruct((HALF, ROWS), BF),
            jax.ShapeDtypeStruct((LMAX, HALF), BF),
            jax.ShapeDtypeStruct((LMAX, HALF), BF),
            jax.ShapeDtypeStruct((4, 80, HALF), BF),
            jax.ShapeDtypeStruct((80, HALF), BF),
            jax.ShapeDtypeStruct((4, 2, 80, HALF), BF),
            jax.ShapeDtypeStruct((2, ROWS, HALF), BF),
        ],
        **comm_params("back", 4),
    )(lens, gcv, conv, kp, q, pt, wk72, spread, ones8, qs, do, kd, vz, kt, lse, delta, pay, pay, hid)


def norm_parts(x):
    xc = x - jnp.mean(x, axis=1, keepdims=True)
    inv = lax.rsqrt(jnp.mean(xc * xc, axis=1, keepdims=True) + EPS)
    return xc * inv, inv


def norm_back(up, normal, inv, gain):
    e = up * gain
    return inv * (e - jnp.mean(e, axis=1, keepdims=True) - normal * jnp.mean(e * normal, axis=1, keepdims=True))


def ffn_kernel(
    lens, ctx_ref, mix_ref, tok_ref, cot_ref, wd_ref, wi_ref, wo_ref, v0, v1, v2, v3, v4, v5, bi_ref, ones_ref,
    hid_ref, gpre_ref, gctx_ref, gcv_ref, del_ref, pay_ref, sm_ref, gbi_ref,
    act_s, gp_s, awd, awi, awo,
):
    i = pl.program_id(0)
    rows = ctx_ref.shape[0]
    keep = row_ids(half_index() * ROWS + i * rows, rows) < length(lens)

    @pl.when(i == 0)
    def _():
        awd[...] = jnp.zeros_like(awd)
        awi[...] = jnp.zeros_like(awi)
        awo[...] = jnp.zeros_like(awo)
        sm_ref[...] = jnp.zeros_like(sm_ref)
        gbi_ref[...] = jnp.zeros_like(gbi_ref)

    vectors = [line(ref) for ref in (v0, v1, v2, v3, v4, v5)]
    vec = lambda k: vectors[k]
    inter_bias = line(bi_ref)
    h = tok_ref[...].astype(F32)
    ctx = ctx_ref[...]
    mixed = jnp.concatenate([ctx, mix_ref[...]], axis=1)
    n1, inv1 = norm_parts(nn(mixed, wd_ref[...]) + vec(0) + h)
    f1 = n1 * vec(1) + vec(2)
    fl = f1.astype(BF)
    chunk = 512
    outs = []
    for g in range(2):
        fg = fl[:, g * HALF : (g + 1) * HALF]
        for ch in range(GW // chunk):
            cols = slice(ch * chunk, (ch + 1) * chunk)
            put = slice(g * GW + ch * chunk, g * GW + (ch + 1) * chunk)
            x = nn(fg, wi_ref[g, :, cols]) + inter_bias[:, put]
            phi = 0.5 + 0.5 * lax.erf(x * 0.7071067811865476)
            act_s[:, put] = (x * phi).astype(BF)
            gp_s[:, put] = phi + x * jnp.exp2(x * x * (-0.5 * LOG2E)) * 0.3989422804014327
        outs.append(nn(act_s[:, g * GW : (g + 1) * GW], wo_ref[g]))
    n2, inv2 = norm_parts(jnp.concatenate(outs, axis=1) + vec(3) + f1)
    hid_ref[...] = (n2 * vec(4) + vec(5)).astype(BF)
    u = jnp.where(keep, cot_ref[...].astype(F32), 0.0)
    gp2 = norm_back(u, n2, inv2, vec(4))
    go = gp2.astype(BF)
    got = go.T
    flt = fl.T
    gfs = []
    for g in range(2):
        sel = slice(g * HALF, (g + 1) * HALF)
        gf = gp2[:, sel]
        for ch in range(GW // chunk):
            cols = slice(ch * chunk, (ch + 1) * chunk)
            put = slice(g * GW + ch * chunk, g * GW + (ch + 1) * chunk)
            gi = (gp_s[:, put] * nt(go[:, sel], wo_ref[g, cols, :])).astype(BF)
            gbi_ref[0:1, put] += col_sum(gi.astype(F32))
            awo[g, :, cols] += nn(got[sel], act_s[:, put])
            awi[g, :, cols] += nn(flt[sel], gi)
            gf = gf + nt(gi, wi_ref[g, :, cols])
        gfs.append(gf)
    gf = jnp.concatenate(gfs, axis=1)
    gpre = norm_back(gf, n1, inv1, vec(1))
    gd = gpre.astype(BF)
    gpre_ref[...] = gd
    sm_ref[0:1, :] += col_sum(go.astype(F32))
    sm_ref[1:2, :] += col_sum(u * n2)
    sm_ref[2:3, :] += col_sum(u)
    sm_ref[3:4, :] += col_sum(gd.astype(F32))
    sm_ref[4:5, :] += col_sum(gf * n1)
    sm_ref[5:6, :] += col_sum(gf)
    awd[...] += nn(mixed.T, gd)
    gm = nt(gd, wd_ref[...])
    gctx = gm[:, :HALF].astype(BF)
    gctx_ref[...] = gctx
    gcv_ref[...] = gm[:, HALF:].astype(BF)
    prod = (gctx.astype(F32) * ctx.astype(F32)).astype(BF)
    del_ref[...] = nt(ones_ref[...], prod).reshape(3, 8, rows)

    @pl.when(i == pl.num_programs(0) - 1)
    def _():
        for r in range(2):
            for c in range(2):
                pay_ref[r, c, 0:HALF, :] = awi[r, :, c * D : c * D + HALF].astype(BF)
                pay_ref[r, c, HALF:D, :] = awi[r, :, c * D + HALF : (c + 1) * D].astype(BF)
                pay_ref[r, c, D : 2 * D, :] = awo[r, :, c * D : (c + 1) * D].T.astype(BF)
                for part in range(2):
                    piece = awd[part * HALF + c * 192 : part * HALF + (c + 1) * 192, r * HALF : (r + 1) * HALF]
                    pay_ref[r, c, 2 * D + part * 192 : 2 * D + (part + 1) * 192, :] = piece.astype(BF)


def ffn(lens, ctx, mix, tok, cot, wd, wi, wo, vectors, bi, ones24):
    rows = 256
    blk = lambda w: pl.BlockSpec((rows, w), lambda i, lens: (i, 0))
    return pl.pallas_call(
        ffn_kernel,
        grid_spec=pltpu.PrefetchScalarGridSpec(
            num_scalar_prefetch=1,
            grid=(ROWS // rows,),
            in_specs=[
                blk(HALF),
                blk(HALF),
                blk(D),
                blk(D),
                whole((D, D)),
                whole((2, HALF, GW)),
                whole((2, GW, HALF)),
                *[whole((D,))] * 6,
                whole((FF,)),
                whole((24, HALF)),
            ],
            out_specs=[
                blk(D),
                blk(D),
                blk(HALF),
                blk(HALF),
                pl.BlockSpec((3, 8, rows), lambda i, lens: (0, 0, i)),
                whole((2, 2, FFN_ROWS, HALF)),
                whole((8, D)),
                whole((1, FF)),
            ],
            scratch_shapes=[
                pltpu.VMEM((rows, FF), BF),
                pltpu.VMEM((rows, FF), F32),
                pltpu.VMEM((D, D), F32),
                pltpu.VMEM((2, HALF, GW), F32),
                pltpu.VMEM((2, HALF, GW), F32),
            ],
        ),
        out_shape=[
            jax.ShapeDtypeStruct((ROWS, D), BF),
            jax.ShapeDtypeStruct((ROWS, D), BF),
            jax.ShapeDtypeStruct((ROWS, HALF), BF),
            jax.ShapeDtypeStruct((ROWS, HALF), BF),
            jax.ShapeDtypeStruct((3, 8, ROWS), F32),
            jax.ShapeDtypeStruct((2, 2, FFN_ROWS, HALF), BF),
            jax.ShapeDtypeStruct((8, D), F32),
            jax.ShapeDtypeStruct((1, FF), F32),
        ],
        **params("ffn"),
    )(lens, ctx, mix, tok, cot, wd, wi, wo, *vectors, bi, ones24)


def final_kernel(
    lens, seq_ref, dk_ref, dv_ref, gco_ref, dq_ref, gqm_ref, gpt_ref, gpre_ref, dep_ref, w_ref, wdep_ref,
    smf_ref, gbi_ref, gwk_ref, gbk_ref, half0, piece1, mid2,
    pay_ref, own_ref, oth_ref, ght_ref, rest_ref,
    agw, wbuf, dbuf, accb, gpad, sbuf, strip, sm, gdp, tsend, trecv, gho, halves, other, zbuf, both, xbuf,
    s, v, es, er, ls, hs, hr,
):
    i = pl.program_id(0)
    p = Place()
    rows = dk_ref.shape[0]
    wide = rows + 32
    b = lax.rem((1 - p.c) * 2 + i, 4)
    n = lens[p.r]
    groups = Groups(p, s, v)
    place = FromRows(p, gho, ght_ref, ls, hs, hr)
    wdep = wdep_ref[...].astype(F32)

    def theirs(k):
        return send(tsend.at[k], trecv.at[k], es.at[k], er.at[k], p.core)

    @pl.when(i == 0)
    def _():
        meet(everyone(p))
        groups.start_quarters(0, mid2, zbuf)
        groups.start_along(4, halves.at[0], piece1[...])
        groups.back(10, half0, other.at[0]).start()
        agw[...] = jnp.zeros_like(agw)
        sm[...] = jnp.zeros_like(sm)
        gdp[...] = jnp.zeros_like(gdp)
        gpad[0:32, :] = jnp.zeros((32, HALF), BF)
        gpad[32 + ROWS :, :] = jnp.zeros((32, HALF), BF)
        gpad[32 : 32 + ROWS, :] = gpt_ref[...]
        edge = pl.multiple_of((1 - p.c) * (ROWS + 16), 16)
        sbuf[...] = nn(gpad[pl.ds(edge, 48), :], w_ref[4])
        total = jnp.zeros((16, D), F32)
        for j in range(KW):
            total = total + sbuf[20 - j : 36 - j, :] * wdep[j : j + 1, :]
        strip[...] = total

    @pl.when(i == 2)
    def _():
        groups.collect(0, mid2, zbuf, both)
        groups.cross(3, both, xbuf).start()

    @pl.when(i == 3)
    def _():
        groups.cross(3, both, xbuf).wait_recv()
        groups.start_along(7, halves.at[1], (both[p.r].astype(F32) + xbuf[...].astype(F32)).astype(BF))
        groups.await_along(4, halves.at[0])
        groups.back(11, halves.at[0], other.at[1]).start()

    keep = row_ids(b * rows, rows) < n
    tok = seq_ref[rows_at(PAD + b * rows, rows), :]
    h = jnp.where(keep, tok.astype(F32), 0.0).astype(BF)
    dk, dv, gco = dk_ref[...], dv_ref[...], gco_ref[...]
    accb[...] = nn(dk, w_ref[0]) + nn(dv, w_ref[1]) + nn(gco, w_ref[2])
    agw[0] += nn(dk.T, h)
    agw[1] += nn(dv.T, h)
    agw[2] += nn(gco.T, h)
    sm[1:2, :] += col_sum(dv.astype(F32))
    sm[2:3, :] += col_sum(gco.astype(F32))

    for k in range(2):

        @pl.when((i == k) & (p.c == k))
        def _():
            edge = slice(0, 16) if k == 0 else slice(rows - 16, rows)
            accb[edge, :] += strip[...]

        @pl.when(i == k)
        def _():
            tsend[k] = jnp.where(keep, accb[...], 0.0).astype(BF)
            theirs(k).start()

    @pl.when(i >= 2)
    def _():
        gqt = dq_ref[...].astype(F32) + gqm_ref[...].astype(F32).T
        gqt = gqt.astype(BF)
        gq = gqt.T
        at = pl.multiple_of((i - 2) * rows + 16, 16)
        win = gpad[pl.ds(at, wide), :]
        gpt = win[16 : 16 + rows]
        sm[0:1, :] += col_sum(gq.astype(F32))
        sm[3:4, :] += col_sum(gpt.astype(F32))
        agw[3] += nn(gqt, h)
        agw[4] += nn(gpt.T, dep_ref[...])
        dbuf[...] = nn(win, w_ref[4])
        ids = row_ids(b * rows - 16, wide)
        inside = (ids >= 0) & (ids < n)
        wbuf[...] = jnp.where(inside, seq_ref[rows_at(b * rows, wide), :].astype(F32), 0.0)
        total = accb[...] + nn(gq, w_ref[3]) + gpre_ref[...].astype(F32)
        gdep = dbuf[16 : 16 + rows, :]
        for j in range(KW):
            gdp[j : j + 1, :] += col_sum(gdep * wbuf[12 + j : 12 + j + rows, :])
            total = total + dbuf[20 - j : 20 - j + rows, :] * wdep[j : j + 1, :]
        accb[...] = total

    for k in range(2):

        @pl.when(i == 2 + k)
        def _():
            theirs(k).wait_recv()
            total = jnp.where(keep, accb[...] + trecv[k].astype(F32), 0.0).astype(BF)
            if k == 0:
                gho[...] = total
                place.start()
            else:
                rest_ref[...] = total

    @pl.when(i == pl.num_programs(0) - 1)
    def _():
        for r in range(2):
            for c in range(2):
                for j in range(5):
                    piece = agw[j, c * 192 : (c + 1) * 192, r * HALF : (r + 1) * HALF]
                    pay_ref[r, c, j * 192 : (j + 1) * 192, :] = piece.astype(BF)
        zeros = lambda k: jnp.zeros((k, HALF), F32)
        pay_ref[0, 0, 960:, :] = gwk_ref[0:64, :].astype(BF)
        bias = jnp.concatenate([gbk_ref[...], jnp.zeros((8, 256), F32)], axis=1)
        pay_ref[0, 1, 960:, :] = jnp.concatenate([gwk_ref[64:72, :], sm[...], bias, zeros(40)], axis=0).astype(BF)
        inter = jnp.concatenate([gbi_ref[:, k * HALF : (k + 1) * HALF] for k in range(8)], axis=0)
        pay_ref[1, 0, 960:, :] = jnp.concatenate(
            [smf_ref[:, 0:HALF], smf_ref[:, HALF:D], inter, zeros(40)], axis=0
        ).astype(BF)
        pay_ref[1, 1, 960:, :] = jnp.concatenate([gdp[:, 0:HALF], gdp[:, HALF:D], zeros(32)], axis=0).astype(BF)
        groups.await_along(7, halves.at[1])
        own_ref[0] = half0[...]
        own_ref[1] = halves[0]
        own_ref[2] = halves[1]
        groups.back(10, half0, other.at[0]).wait()
        groups.back(11, halves.at[0], other.at[1]).wait()
        oth_ref[...] = other[...]
        for offset in (1, 2, 3):
            groups.quarter(0, mid2, zbuf, offset).wait_send()
            groups.along(4, halves.at[0], offset, p.z).wait_send()
            groups.along(7, halves.at[1], offset, p.z).wait_send()
        groups.cross(3, both, xbuf).wait_send()
        theirs(0).wait_send()
        theirs(1).wait_send()
        place.finish()


def final(lens, seq_tok, dk, dv, gco, dq, gqm, gpt, gpre, dep, w5, wdep, smf, gbi, gwk, gbk, half0, piece1, mid2):
    rows = 512
    seq = pl.BlockSpec((rows, HALF), lambda i, lens: (lax.rem((1 - half_index()) * 2 + i, 4), 0))
    own = lambda w: pl.BlockSpec((rows, w), lambda i, lens: (jnp.maximum(i - 2, 0), 0))
    return pl.pallas_call(
        final_kernel,
        grid_spec=pltpu.PrefetchScalarGridSpec(
            num_scalar_prefetch=1,
            grid=(LMAX // rows,),
            in_specs=[
                once((LMAX + 2 * PAD, D)),
                seq,
                seq,
                seq,
                pl.BlockSpec((HALF, rows), lambda i, lens: (0, jnp.maximum(i - 2, 0))),
                own(HALF),
                once((ROWS, HALF)),
                own(D),
                own(D),
                once((5, HALF, D)),
                whole((KW, D)),
                whole((8, D)),
                whole((1, FF)),
                whole((72, HALF)),
                whole((8, 128)),
                once((4, 80, HALF)),
                whole((80, HALF)),
                once((4, 2, 80, HALF)),
            ],
            out_specs=[
                once((2, 2, PROJ_ROWS, HALF)),
                once((3, 4, 80, HALF)),
                once((2, 4, 80, HALF)),
                HBM,
                once((rows, D)),
            ],
            scratch_shapes=[
                pltpu.VMEM((5, HALF, D), F32),
                pltpu.VMEM((rows + 32, D), F32),
                pltpu.VMEM((rows + 32, D), F32),
                pltpu.VMEM((rows, D), F32),
                pltpu.VMEM((ROWS + 64, HALF), BF),
                pltpu.VMEM((48, D), F32),
                pltpu.VMEM((16, D), F32),
                pltpu.VMEM((8, HALF), F32),
                pltpu.VMEM((16, D), F32),
                pltpu.VMEM((2, rows, D), BF),
                pltpu.VMEM((2, rows, D), BF),
                pltpu.VMEM((rows, D), BF),
                pltpu.VMEM((2, 4, 80, HALF), BF),
                pltpu.VMEM((2, 4, 80, HALF), BF),
                pltpu.VMEM((3, 2, 80, HALF), BF),
                pltpu.VMEM((2, 80, HALF), BF),
                pltpu.VMEM((80, HALF), BF),
                pltpu.SemaphoreType.DMA((12,)),
                pltpu.SemaphoreType.DMA((12,)),
                pltpu.SemaphoreType.DMA((2,)),
                pltpu.SemaphoreType.DMA((2,)),
                pltpu.SemaphoreType.DMA,
                pltpu.SemaphoreType.DMA((2,)),
                pltpu.SemaphoreType.DMA((3,)),
            ],
        ),
        out_shape=[
            jax.ShapeDtypeStruct((2, 2, PROJ_ROWS, HALF), BF),
            jax.ShapeDtypeStruct((3, 4, 80, HALF), BF),
            jax.ShapeDtypeStruct((2, 4, 80, HALF), BF),
            jax.ShapeDtypeStruct((2, rows, HALF), BF),
            jax.ShapeDtypeStruct((rows, D), BF),
        ],
        **comm_params("final", 6),
    )(lens, seq_tok, dk, dv, gco, dq, gqm, gpt, gpre, dep, w5, wdep, smf, gbi, gwk, gbk, half0, piece1, mid2)


def end_kernel(
    pay, rest_ref, own_half, oth_half, ght, sum_ref, small_ref, big_ref,
    small, total_sum, near, far, out, mid, ybuf, zbuf, s, v, ns, nr, cs, cr, last, es, er, ls, hs, hr,
):
    p = Place()
    r, c = p.r, p.c
    meet(everyone(p))
    chunks = 4
    rows = PROJ_ROWS // chunks
    summed = Sum(p, far, mid, ybuf, zbuf, total_sum, rows, s, v)

    def part(ch):
        return slice(ch * rows, (ch + 1) * rows)

    def beside(n, ch):
        rr = 1 - r if n == 0 else r
        k = n * chunks + ch
        return send(pay.at[rr, 1 - c, part(ch), :], near.at[rr, part(ch), :], ns.at[k], nr.at[k], p.core)

    def cross(ch):
        return send(out.at[part(ch), :], far.at[part(ch), :], cs.at[ch], cr.at[ch], p.across)

    for ch in range(chunks):
        for n in range(2):
            beside(n, ch).start()
    back_half = send(own_half.at[2], last, es.at[0], er.at[0], p.beside)
    back_half.start()
    back = FromRows(p, rest_ref, ght, ls, hs, hr)
    for ch in range(chunks):
        beside(0, ch).wait_recv()
        both = near[1 - r, part(ch), :].astype(F32) + pay[1 - r, c, part(ch), :].astype(F32)
        out[part(ch), :] = both.astype(BF)
        cross(ch).start()
    back.start()

    def arrive(ch):
        beside(1, ch).wait_recv()
        cross(ch).wait_recv()
        both = near[r, part(ch), :].astype(F32) + pay[r, c, part(ch), :].astype(F32)
        far[part(ch), :] = (both + far[part(ch), :].astype(F32)).astype(BF)
        summed.half(ch)

    stages = [
        arrive,
        summed.quarter,
        lambda ch: summed.along(ch, summed.collect(ch)),
        summed.back,
        summed.finish_spread,
    ]
    for tick in range(chunks + len(stages) - 1):
        for n, stage in enumerate(stages):
            if 0 <= tick - n < chunks:
                stage(tick - n)
        if tick == 0:
            for ch in range(2):
                big_ref[ch, p.y] = own_half[ch]
                big_ref[ch, 1 - p.y] = oth_half[ch]
            big_ref[2, p.y] = own_half[2]
    own = total_sum.at[960:PROJ_ROWS, :]
    moves = [
        send(own, small.at[r * 2 + c], es.at[1 + n], er.at[1 + n], device)
        for n, device in enumerate((p.across, p.core, p.diagonal))
    ]
    for move in moves:
        move.start()
    small[r * 2 + c] = total_sum[960:PROJ_ROWS, :]
    sum_ref[...] = total_sum[...]
    for ch in range(chunks):
        summed.finish_sum(ch)
        cross(ch).wait_send()
        for n in range(2):
            beside(n, ch).wait_send()
    for n, (rr, cc) in enumerate(((1 - r, c), (r, 1 - c), (1 - r, 1 - c))):
        send(own, small.at[rr * 2 + cc], es.at[1 + n], er.at[1 + n], p.core).wait_recv()
    for move in moves:
        move.wait_send()
    back_half.wait()
    big_ref[2, 1 - p.y] = last[...]
    small_ref[...] = small[...]
    back.finish()


def end(pay, rest, own_half, oth_half):
    return pl.pallas_call(
        end_kernel,
        in_specs=[VMEM] * 4,
        out_specs=[HBM, VMEM, VMEM, VMEM],
        out_shape=[
            jax.ShapeDtypeStruct((2, ROWS // 2, HALF), BF),
            jax.ShapeDtypeStruct((PROJ_ROWS, HALF), BF),
            jax.ShapeDtypeStruct((4, 64, HALF), BF),
            jax.ShapeDtypeStruct((3, 2, 4, 80, HALF), BF),
        ],
        scratch_shapes=[
            pltpu.VMEM((4, 64, HALF), BF),
            pltpu.VMEM((PROJ_ROWS, HALF), BF),
            pltpu.VMEM((2, PROJ_ROWS, HALF), BF),
            pltpu.VMEM((PROJ_ROWS, HALF), BF),
            pltpu.VMEM((PROJ_ROWS, HALF), BF),
            *Sum.scratch(PROJ_ROWS // 4, 4),
            pltpu.SemaphoreType.DMA((8,)),
            pltpu.SemaphoreType.DMA((8,)),
            pltpu.SemaphoreType.DMA((4,)),
            pltpu.SemaphoreType.DMA((4,)),
            pltpu.VMEM((4, 80, HALF), BF),
            pltpu.SemaphoreType.DMA((4,)),
            pltpu.SemaphoreType.DMA((4,)),
            pltpu.SemaphoreType.DMA,
            pltpu.SemaphoreType.DMA((2,)),
            pltpu.SemaphoreType.DMA((3,)),
        ],
        **comm_params("end", 7),
    )(pay, rest, own_half, oth_half)


def outputs_kernel(
    ght0, ght1, hid, t0, t1, t2, t3, t4, big_i0, big_i1, big_o, big_d, small, perm_ref,
    hid_ref, gt_ref, gk_ref, gv_ref, gc_ref, gq_ref, gp_ref, gi_ref, go_ref, gd_ref,
    gdep_ref, gbq_ref, gbv_ref, gbc_ref, gbp_ref, gwk_ref, gbk_ref,
    gbd_ref, gg1_ref, gb1_ref, gbi_ref, gbo_ref, gg2_ref, gb2_ref,
):
    i = pl.program_id(0)
    hid_ref[...] = hid[...]

    @pl.when(lax.rem(i, 2) == 0)
    def _():
        gt_ref[...] = ght0[0].astype(F32)

    @pl.when(lax.rem(i, 2) == 1)
    def _():
        gt_ref[...] = ght1[0].astype(F32)

    for src, ref in ((t0, gk_ref), (t1, gv_ref), (t2, gc_ref), (t3, gq_ref), (t4, gp_ref), (big_o, go_ref), (big_d, gd_ref)):
        ref[...] = src[...].astype(F32)
    gi_ref[:, 0:HALF] = big_i0[...].astype(F32)
    gi_ref[:, HALF:D] = big_i1[...].astype(F32)

    @pl.when(i == 0)
    def _():
        tail = small[1].astype(F32)
        norms = small[2].astype(F32)
        depth = small[3].astype(F32)
        kernel_grad = jnp.concatenate([small[0].astype(F32), tail[0:8]], axis=0).astype(BF)
        gwk_ref[...] = nn(perm_ref[...], kernel_grad)
        bias = nt(tail[16:24, 0:72].astype(BF), perm_ref[...])
        gbk_ref[...] = bias[0:1, :].reshape(54)
        for k, ref in enumerate((gbq_ref, gbv_ref, gbc_ref, gbp_ref)):
            ref[...] = tail[8 + k : 9 + k, :].reshape(HALF)
        for k, ref in enumerate((gbo_ref, gg2_ref, gb2_ref, gbd_ref, gg1_ref, gb1_ref)):
            ref[...] = jnp.concatenate([norms[k : k + 1, :], norms[8 + k : 9 + k, :]], axis=1).reshape(D)
        gbi_ref[...] = jnp.concatenate([norms[16 + k : 17 + k, :] for k in range(8)], axis=1).reshape(FF)
        gdep_ref[:, 0:HALF] = depth[0:KW, :]
        gdep_ref[:, HALF:D] = depth[16 : 16 + KW, :]


def outputs(ght0, ght1, hid, total, big, small, perm):
    rows = 512
    at = lambda n, first: pl.BlockSpec((n, HALF), lambda i: (first + i, 0))
    blk = at(rows, 0)
    chunk = pl.BlockSpec((1, rows, HALF), lambda i: (lax.div(i, 2), 0, 0))
    shapes = [(KW, D)] + [(HALF,)] * 4 + [(54, HALF), (54,)] + [(D,)] * 3 + [(FF,)] + [(D,)] * 3
    main = [(192, HALF)] * 5 + [(HALF, D), (D, HALF), (HALF, HALF)]
    return pl.pallas_call(
        outputs_kernel,
        grid=(4,),
        in_specs=[chunk, chunk, blk]
        + [at(48, 4 * j) for j in range(5)]
        + [at(96, 0), at(96, 4), at(192, 4), at(96, 16), whole((4, 64, HALF)), whole((54, 72))],
        out_specs=[blk, blk]
        + [at(48, 0)] * 5
        + [pl.BlockSpec((96, D), lambda i: (i, 0)), at(192, 0), at(96, 0)]
        + [whole(shape) for shape in shapes],
        out_shape=[jax.ShapeDtypeStruct((LMAX, HALF), BF), jax.ShapeDtypeStruct((LMAX, HALF), F32)]
        + [jax.ShapeDtypeStruct(shape, F32) for shape in main + shapes],
        **params("outputs"),
    )(ght0, ght1, hid, total, total, total, total, total, big, big, big, big, small, perm)


def constants():
    spread = np.zeros((72, KW * HALF), np.float32)
    ones8 = np.zeros((8, HALF), np.float32)
    ones24 = np.zeros((24, HALF), np.float32)
    perm = np.zeros((72, 54), np.float32)
    for head in range(6):
        cols = slice(head * HD, (head + 1) * HD)
        ones8[head, cols] = 1
        ones24[head // 2 * 8 + head % 2, cols] = 1
        for j in range(KW):
            spread[j * 8 + head, j * HALF + head * HD : j * HALF + (head + 1) * HD] = 1
            perm[j * 8 + head, head * KW + j] = 1
    return [jnp.asarray(a, BF) for a in (spread, ones8, ones24, perm)]


def per_device(
    groups, tokens, cotangent, seq_lengths, w_query, w_key, w_value, w_convout, w_point, w_depth,
    b_query, b_value, b_convout, b_point, w_kernel, b_kernel, w_dense, b_dense, gain_one, bias_one,
    w_inter, b_inter, w_output, b_output, gain_two, bias_two,
):
    lens = seq_lengths
    spread, ones8, ones24, perm = constants()
    wdep = w_depth.T

    kd, kt, vz, q, qs, pt, kp, conv, mix, dep, hown, wk72, bk72, seq, w5, wi, wd, cot, wop = front(
        lens, tokens, (w_key.T, w_value.T, w_convout.T, w_query.T, w_point.T), w_kernel.T, b_kernel, perm,
        wdep, b_value, b_convout, b_query, b_point, spread,
        w_inter[0], w_dense.reshape(2, 192, HALF), w_output[0], cotangent,
    )
    ctx, lse, wo = attend(lens, qs, kd, vz, w_output[0], wop)
    vectors = (b_dense, gain_one, bias_one, b_output, gain_two, bias_two)
    hid, gpre, gctx, gcv, delta, payf, smf, gbi = ffn(
        lens, ctx, mix, hown, cot, wd.reshape(D, D), wi, wo, vectors, b_inter, ones24
    )
    gqm, gpt, gco, gwk, gbk, dq, dk, dv, half0, piece1, mid2, hid = back(
        lens, gcv, conv, kp, q, pt, wk72, spread, ones8, qs, gctx, kd, vz, kt, lse, delta, payf, hid
    )
    pay5, own_half, oth_half, ght0, rest = final(
        lens, seq, dk, dv, gco, dq, gqm, gpt, gpre, dep, w5, wdep, smf, gbi, gwk, gbk, half0, piece1, mid2
    )
    ght1, total, small, big = end(pay5, rest, own_half, oth_half)
    big = big.reshape(FFN_ROWS, HALF)
    if groups > 8:
        total, big, small = lax.psum(tuple(x.astype(F32) * 0.125 for x in (total, big, small)), "dp")
        total, big, small = total.astype(BF), big.astype(BF), small.astype(BF)
    (
        hidden_out, gt, gk, gv, gc, gq, gp, gi, go, gd, gdep, gbq, gbv, gbc, gbp, gwk, gbk, gbd, gg1, gb1, gbi, gbo, gg2, gb2,
    ) = outputs(ght0, ght1, hid.reshape(LMAX, HALF), total, big, small, perm.T)
    return (
        hidden_out, gt, gq.T, gk.T, gv.T, gc.T, gp.T, gdep.T, gbq, gbv, gbc, gbp, gwk.T, gbk, gd, gbd, gg1, gb1,
        gi[None], gbi, go[None], gbo, gg2, gb2,
    )


def solution(mesh):
    act = P(("dp", "col"), "row")
    rep = P()
    proj = P("row", "col")
    in_specs = (
        act, act, P("dp"), proj, proj, proj, proj, proj, rep, rep, rep, rep, rep, rep, rep, P("col", "row"),
        rep, rep, rep, P("row", None, "col"), rep, P("row", "col", None), rep, rep, rep,
    )
    out_specs = (
        act, act, proj, proj, proj, proj, proj, rep, rep, rep, rep, rep, rep, rep, P("col", "row"),
        rep, rep, rep, P("row", None, "col"), rep, P("row", "col", None), rep, rep, rep,
    )
    return jax.shard_map(
        functools.partial(per_device, mesh.shape["dp"]), mesh=mesh, in_specs=in_specs, out_specs=out_specs, check_vma=False)
```

```python
import functools

import jax
import jax.numpy as jnp
import numpy as np
from jax import lax
from jax.experimental import pallas as pl
from jax.experimental.pallas import tpu as pltpu
from jax.sharding import PartitionSpec as P

D = 768
HALF = 384
HD = 64
KW = 9
FF = 3072
GW = 1536
LMAX = 2048
ROWS = 1024
EPS = 1e-12
LOG2E = 1.4426950408889634
LN2 = 0.6931471805599453
BF = jnp.bfloat16
F32 = jnp.float32
VMEM_BYTES = 63 * 1024 * 1024
PAD = 16
FFN_ROWS = 1920
FFN_CHUNK = 640
PROJ_ROWS = 640
MESH = pl.DeviceIdType.MESH
HBM = pl.BlockSpec(memory_space=pl.ANY)
VMEM = pl.BlockSpec(memory_space=pltpu.VMEM)


def nn(a, b):
    return lax.dot_general(a, b, (((1,), (0,)), ((), ())), preferred_element_type=F32)


def nt(a, b):
    return lax.dot_general(a, b, (((1,), (1,)), ((), ())), preferred_element_type=F32)


def col_sum(x):
    return jnp.sum(x, axis=0, keepdims=True)


def row_ids(start, rows):
    return start + lax.broadcasted_iota(jnp.int32, (rows, 1), 0)


def whole(shape):
    return pl.BlockSpec(shape, lambda *_: (0,) * len(shape))


def once(shape):
    return pl.BlockSpec(shape, lambda *_: (0,) * len(shape), pipeline_mode=pl.Buffered(1))


def half_index():
    return lax.axis_index("col")


def length(lens):
    return lens[lax.axis_index("row")]


def line(ref):
    return ref[...].astype(F32).reshape(1, ref.shape[0])


def put_tiles(buf, value, first=0):
    for t in range(value.shape[1] // 128):
        buf[t, first : first + value.shape[0], :] = value[:, t * 128 : (t + 1) * 128]


def params(name):
    return dict(
        name=name,
        compiler_params=pltpu.CompilerParams(vmem_limit_bytes=VMEM_BYTES),
    )


def lanes(k, width=HALF):
    return pl.ds(pl.multiple_of(k * width, 128), width)


def rows_at(start, count, step=16):
    return pl.ds(pl.multiple_of(start, step), count)


def send(src, dst, send_sem, recv_sem, device):
    return pltpu.make_async_remote_copy(
        src_ref=src, dst_ref=dst, send_sem=send_sem, recv_sem=recv_sem, device_id=device, device_id_type=MESH
    )


class Place:
    def __init__(self):
        self.d = lax.axis_index("dp")
        self.r = lax.axis_index("row")
        self.c = lax.axis_index("col")
        self.k = lax.rem(self.d, 8)
        self.base = self.d - self.k
        self.y = lax.rem(self.k, 2)
        self.z = lax.div(self.k, 2)
        self.beside = {"dp": self.base + self.z * 2 + 1 - self.y}
        self.across = {"row": 1 - self.r}
        self.core = {"col": 1 - self.c}
        self.diagonal = {"row": 1 - self.r, "col": 1 - self.c}

    def eight(self, offset):
        other = lax.rem(self.k + offset, 8)
        return other, {"dp": self.base + other}

    def four(self, offset):
        other = lax.rem(self.z + offset, 4)
        return other, {"dp": self.base + other * 2 + self.y}


def meet(devices):
    barrier = pltpu.get_barrier_semaphore()
    for device in devices:
        pl.semaphore_signal(barrier, inc=1, device_id=device, device_id_type=MESH)
    pl.semaphore_wait(barrier, len(devices))


def comm_params(name, number):
    return dict(
        name=name,
        compiler_params=pltpu.CompilerParams(
            vmem_limit_bytes=VMEM_BYTES, collective_id=number, has_side_effects=True
        ),
    )


class Gather:
    def __init__(self, place, own, full, part, block, step, send_sem, recv_sem, first):
        self.p, self.own, self.full, self.part, self.block, self.h = place, own, full, part, block, step
        self.s, self.v, self.f = send_sem, recv_sem, first

    def _move(self, src, dst, n, device):
        return send(src, dst, self.s.at[self.f + n], self.v.at[self.f + n], device)

    def _cross(self, r):
        p = self.p
        at = (p.y * 4 + p.z) * self.h
        return self._move(self.part(self.own, at, self.h), self.block(self.full, r, p.c, at, self.h), 0, p.across)

    def _near(self, c):
        p = self.p
        return self._move(self.own, self.block(self.full, p.r, c, 0, 8 * self.h), 1, p.core)

    def _pass(self, offset, z):
        p = self.p
        here = self.block(self.full, 1 - p.r, p.c, (p.y * 4 + z) * self.h, self.h)
        return self._move(here, here, 1 + offset, p.four(offset)[1])

    def _turn(self, y):
        p = self.p
        here = self.block(self.full, 1 - p.r, p.c, y * 4 * self.h, 4 * self.h)
        return self._move(here, here, 5, p.beside)

    def _last(self, c):
        p = self.p
        here = self.block(self.full, 1 - p.r, c, 0, 8 * self.h)
        return self._move(here, here, 6, p.core)

    def start(self):
        self._cross(self.p.r).start()
        self._near(self.p.c).start()

    def relay(self):
        p = self.p
        self._cross(1 - p.r).wait_recv()
        for offset in (1, 2, 3):
            self._pass(offset, p.z).start()

    def turn(self):
        p = self.p
        for offset in (1, 2, 3):
            self._pass(offset, lax.rem(p.z + 4 - offset, 4)).wait_recv()
        self._turn(p.y).start()

    def share(self):
        p = self.p
        self._turn(1 - p.y).wait_recv()
        self._last(p.c).start()

    def finish(self):
        p = self.p
        self._last(1 - p.c).wait_recv()
        self._near(1 - p.c).wait_recv()
        self._cross(p.r).wait_send()
        self._near(p.c).wait_send()
        for offset in (1, 2, 3):
            self._pass(offset, p.z).wait_send()
        self._turn(p.y).wait_send()
        self._last(p.c).wait_send()


def middle_part(ref, first, rows):
    return ref.at[:, rows_at(first, rows, 8), :]


def middle_block(ref, r, c, first, rows):
    return ref.at[:, rows_at(c * 192 + first, rows, 8), lanes(r)]


def rows_part(ref, first, rows):
    return ref.at[rows_at(first, rows), :]


def inter_block(ref, r, c, first, rows):
    return ref.at[r, rows_at(first, rows), lanes(c, 768)]


def output_block(ref, r, c, first, rows):
    return ref.at[r, rows_at(c * 768 + first, rows), :]


class ToRows:
    def __init__(self, place, src, dst, stage, local_sem, send_sem, recv_sem):
        self.p, self.src, self.dst, self.stage = place, src, dst, stage
        self.l, self.s, self.v = local_sem, send_sem, recv_sem

    def _cross(self, q, k):
        half = self.src.at[q * ROWS : (q + 1) * ROWS, :]
        return send(half, self.dst.at[:, lanes(k)], self.s.at[q], self.v.at[0], {"row": 1 - self.p.r, "col": q})

    def _near(self):
        p = self.p
        half = self.src.at[rows_at((1 - p.c) * ROWS, ROWS), :]
        return send(half, self.dst.at[:, lanes(p.r)], self.s.at[2], self.v.at[1], p.core)

    def _load(self):
        return pltpu.make_async_copy(self.src.at[rows_at(self.p.c * ROWS, ROWS), :], self.stage, self.l.at[0])

    def _store(self):
        return pltpu.make_async_copy(self.stage, self.dst.at[:, lanes(self.p.r)], self.l.at[1])

    def start(self):
        p = self.p

        @pl.when(p.r != p.c)
        def _():
            self._cross(0, p.r).start()
            self._cross(1, p.r).start()

        @pl.when(p.r == p.c)
        def _():
            self._near().start()
            self._load().start()

    def store(self):
        @pl.when(self.p.r == self.p.c)
        def _():
            self._load().wait()
            self._store().start()

    def finish(self):
        p = self.p
        self._cross(0, 1 - p.r).wait_recv()

        @pl.when(p.r != p.c)
        def _():
            self._cross(0, p.r).wait_send()
            self._cross(1, p.r).wait_send()
            self._near().wait_recv()

        @pl.when(p.r == p.c)
        def _():
            self._near().wait_send()
            self._store().wait()


class FromRows:
    def __init__(self, place, src, dst, local_sem, send_sem, recv_sem):
        self.p, self.src, self.dst = place, src, dst
        self.l, self.s, self.v = local_sem, send_sem, recv_sem

    def _cross(self, q):
        p = self.p
        place = self.dst.at[q]
        return send(self.src.at[:, lanes(1 - p.r)], place, self.s.at[0], self.v.at[q], {"row": 1 - p.r, "col": p.r})

    def _near(self, q):
        p = self.p
        place = self.dst.at[q]
        return send(self.src.at[:, lanes(p.r)], place, self.s.at[1], self.v.at[2], p.core)

    def _local(self):
        p = self.p
        place = self.dst.at[p.c]
        return pltpu.make_async_copy(self.src.at[:, lanes(p.r)], place, self.l)

    def start(self):
        p = self.p
        self._cross(p.c).start()

        @pl.when(p.r != p.c)
        def _():
            self._near(p.c).start()

        @pl.when(p.r == p.c)
        def _():
            self._local().start()

    def finish(self):
        p = self.p
        self._cross(p.c).wait_send()

        @pl.when(p.r != p.c)
        def _():
            self._near(p.c).wait_send()
            self._cross(0).wait_recv()
            self._cross(1).wait_recv()

        @pl.when(p.r == p.c)
        def _():
            self._near(1 - p.c).wait_recv()
            self._local().wait()


class Sum:
    def __init__(self, place, far, mid, ybuf, zbuf, total, rows, s, v, first=0):
        self.p, self.far, self.mid, self.ybuf, self.zbuf, self.total = place, far, mid, ybuf, zbuf, total
        self.rows, self.s, self.v, self.first = rows, s, v, first

    def _sems(self, ch, n):
        i = self.first + ch * 8 + n
        return self.s.at[i], self.v.at[i]

    def _beside(self):
        return self.p.beside

    def _halves(self, ch, y):
        return rows_at(ch * self.rows + y * (self.rows // 2), self.rows // 2)

    def _piece(self, ch, z):
        return rows_at(ch * self.rows + self.p.y * (self.rows // 2) + z * (self.rows // 8), self.rows // 8)

    def _half(self, ch):
        return send(self.far.at[self._halves(ch, 1 - self.p.y), :], self.ybuf.at[ch], *self._sems(ch, 0), self._beside())

    def _quarter(self, ch, offset):
        other, device = self.p.four(offset)
        src = self.mid.at[ch, rows_at(other * (self.rows // 8), self.rows // 8), :]
        return send(src, self.zbuf.at[ch, offset - 1], *self._sems(ch, offset), device)

    def _along(self, ch, offset, z):
        _, device = self.p.four(offset)
        here = self.total.at[self._piece(ch, z), :]
        return send(here, here, *self._sems(ch, 3 + offset), device)

    def _back(self, ch, y):
        here = self.total.at[self._halves(ch, y), :]
        return send(here, here, *self._sems(ch, 7), self._beside())

    def half(self, ch):
        self._half(ch).start()

    def quarter(self, ch):
        self._half(ch).wait_recv()
        both = self.far[self._halves(ch, self.p.y), :].astype(F32) + self.ybuf[ch].astype(F32)
        self.mid[ch] = both.astype(BF)
        for offset in (1, 2, 3):
            self._quarter(ch, offset).start()

    def collect(self, ch):
        both = self.mid[ch, rows_at(self.p.z * (self.rows // 8), self.rows // 8), :].astype(F32)
        for offset in (1, 2, 3):
            self._quarter(ch, offset).wait_recv()
            both = both + self.zbuf[ch, offset - 1].astype(F32)
        return both.astype(BF)

    def along(self, ch, piece):
        self.total[self._piece(ch, self.p.z), :] = piece
        for offset in (1, 2, 3):
            self._along(ch, offset, self.p.z).start()

    def back(self, ch):
        for offset in (1, 2, 3):
            self._along(ch, offset, lax.rem(self.p.z + 4 - offset, 4)).wait_recv()
        self._back(ch, self.p.y).start()

    def finish_sum(self, ch):
        self._half(ch).wait_send()
        for offset in (1, 2, 3):
            self._quarter(ch, offset).wait_send()

    def finish_spread(self, ch):
        self._back(ch, 1 - self.p.y).wait_recv()
        for offset in (1, 2, 3):
            self._along(ch, offset, self.p.z).wait_send()
        self._back(ch, self.p.y).wait_send()

    @staticmethod
    def scratch(rows, chunks):
        return [
            pltpu.VMEM((chunks, rows // 2, HALF), BF),
            pltpu.VMEM((chunks, rows // 2, HALF), BF),
            pltpu.VMEM((chunks, 3, rows // 8, HALF), BF),
            pltpu.SemaphoreType.DMA((8 * chunks,)),
            pltpu.SemaphoreType.DMA((8 * chunks,)),
        ]


class Groups:
    def __init__(self, place, s, v):
        self.p, self.s, self.v = place, s, v

    def half(self, n, mine, ybuf):
        return send(mine.at[1 - self.p.y], ybuf, self.s.at[n], self.v.at[n], self.p.beside)

    def quarter(self, n, mid, zbuf, offset):
        other, device = self.p.four(offset)
        n = n + offset - 1
        return send(mid.at[other], zbuf.at[offset - 1], self.s.at[n], self.v.at[n], device)

    def cross(self, n, both, xbuf):
        return send(both.at[1 - self.p.r], xbuf, self.s.at[n], self.v.at[n], self.p.across)

    def along(self, n, half, offset, z):
        n = n + offset - 1
        return send(half.at[z], half.at[z], self.s.at[n], self.v.at[n], self.p.four(offset)[1])

    def back(self, n, half, other):
        return send(half, other, self.s.at[n], self.v.at[n], self.p.beside)

    def start_quarters(self, n, mid, zbuf):
        for offset in (1, 2, 3):
            self.quarter(n, mid, zbuf, offset).start()

    def collect(self, n, mid, zbuf, both):
        total = mid[self.p.z].astype(F32)
        for offset in (1, 2, 3):
            self.quarter(n, mid, zbuf, offset).wait_recv()
            total = total + zbuf[offset - 1].astype(F32)
        both[...] = total.astype(BF)

    def start_along(self, n, half, piece):
        half[self.p.z] = piece
        for offset in (1, 2, 3):
            self.along(n, half, offset, self.p.z).start()

    def await_along(self, n, half):
        for offset in (1, 2, 3):
            self.along(n, half, offset, lax.rem(self.p.z + 4 - offset, 4)).wait_recv()

    def sent(self, n, ref, kind):
        for offset in (1, 2, 3):
            kind(n, *ref, offset).wait_send()


def everyone(p):
    return [p.across, p.core, p.diagonal, p.beside] + [p.four(o)[1] for o in (1, 2, 3)]


def front_kernel(
    lens, tok_ref, wk_own, wv_own, wc_own, wq_own, wp_own, kern_ref, kb_ref, perm_ref,
    wdep_ref, bv_ref, bc_ref, bq_ref, bp_ref, spread_ref, wi_own, wd_own, wo_own, cot_own,
    kd_ref, kt_ref, vz_ref, q_ref, qs_ref, pt_ref, kp_ref, conv_ref, mix_ref, dep_ref, h_ref, wk_ref, bk_ref,
    seq_out, w5_out, wi_ref, wd_ref, cot_ref, wo_ref,
    own, seq_ref, w_ref, stage, first_key, hbuf, cbuf, lsem, ts, tr, gs, gr, cs, cr,
):
    i = pl.program_id(0)
    p = Place()
    r, c = p.r, p.c
    n = lens[r]
    proj = Gather(p, own, w_ref, middle_part, middle_block, 24, gs, gr, 0)
    inter = Gather(p, wi_own, wi_ref, rows_part, inter_block, 48, gs, gr, 7)
    dense = Gather(p, wd_own, wd_ref, middle_part, middle_block, 24, gs, gr, 14)
    cot_rows = ToRows(p, cot_own, cot_ref, stage, lsem, cs, cr)
    output = Gather(p, wo_own, wo_ref, rows_part, output_block, 96, gs, gr, 21)
    keep_output = pltpu.make_async_copy(wo_own, output_block(wo_ref, r, c, 0, D), lsem.at[7])
    keep_inter = pltpu.make_async_copy(wi_own, inter_block(wi_ref, r, c, 0, HALF), lsem.at[2])
    keep_dense = pltpu.make_async_copy(wd_own, middle_block(wd_ref, r, c, 0, 192), lsem.at[3])
    keep_own = pltpu.make_async_copy(tok_ref, seq_ref.at[PAD : PAD + LMAX, lanes(r)], lsem.at[4])
    keep_seq = pltpu.make_async_copy(seq_ref, seq_out, lsem.at[5])
    keep_w = pltpu.make_async_copy(w_ref, w5_out, lsem.at[6])

    def chunk(m, k):
        return seq_ref.at[PAD + m * 512 : PAD + (m + 1) * 512, lanes(k)]

    def cross(m, k):
        return send(tok_ref.at[m * 512 : (m + 1) * 512, :], chunk(m, k), ts.at[m], tr.at[m], {"row": 1 - r, "col": m // 2})

    def near(k):
        return send(tok_ref, seq_ref.at[PAD : PAD + LMAX, lanes(k)], ts.at[4], tr.at[4], p.core)

    def forward(m):
        return send(chunk(m, 1 - r), chunk(m, 1 - r), ts.at[5 + m], tr.at[5 + m], p.core)

    @pl.when(i == 0)
    def _():
        for j, ref in enumerate((wk_own, wv_own, wc_own, wq_own, wp_own)):
            own[j] = ref[...]
        seq_ref[0:PAD, :] = jnp.zeros((PAD, D), BF)
        seq_ref[PAD + LMAX :, :] = jnp.zeros((PAD, D), BF)
        meet(everyone(p))
        proj.start()
        inter._cross(r).start()
        dense._cross(r).start()
        output._cross(r).start()

        @pl.when(r != c)
        def _():
            for m in (0, 2, 1, 3):
                cross(m, r).start()

        @pl.when(r == c)
        def _():
            near(r).start()
            keep_own.start()

        cot_rows.start()
        inter._near(c).start()
        dense._near(c).start()
        output._near(c).start()
        keep_inter.start()
        keep_dense.start()
        keep_output.start()
        middle_block(w_ref, r, c, 0, 192)[...] = own[...]
        wk_ref[...] = nn(perm_ref[...], kern_ref[...]).astype(BF)
        bk_ref[...] = nt(perm_ref[...], jnp.broadcast_to(line(kb_ref), (128, 54)).astype(BF))
        proj.relay()
        inter.relay()
        dense.relay()
        output.relay()
        proj.turn()
        for q in range(2):

            @pl.when(c == q)
            def _():
                for m in (2 * q, 2 * q + 1):
                    cross(m, 1 - r).wait_recv()
                    forward(m).start()

        proj.share()
        for q in range(2):

            @pl.when(c == q)
            def _():
                for m in (2 - 2 * q, 3 - 2 * q):
                    forward(m).wait_recv()
                for m in (2 * q, 2 * q + 1):
                    forward(m).wait_send()

        @pl.when(r != c)
        def _():
            for m in range(4):
                cross(m, r).wait_send()
            near(r).wait_recv()

        @pl.when(r == c)
        def _():
            near(r).wait_send()
            keep_own.wait()

        proj.finish()
        keep_seq.start()
        keep_w.start()

    @pl.when(i == 1)
    def _():
        inter.turn()
        dense.turn()
        cot_rows.store()

    @pl.when(i == 2)
    def _():
        output.turn()

    @pl.when(i == 3)
    def _():
        inter.share()
        dense.share()

    krows = kd_ref.shape[0]
    keep_key = row_ids(i * krows, krows) < n
    tok = seq_ref[rows_at(PAD + i * krows, krows), :]
    h = jnp.where(keep_key, tok.astype(F32), 0.0).astype(BF)
    k = nt(h, w_ref[0])
    v = nt(h, w_ref[1]) + line(bv_ref)

    @pl.when(i == 0)
    def _():
        first_key[...] = k[0:8]

    kd_ref[...] = jnp.where(keep_key, k, first_key[0:1]).astype(BF)
    kt_ref[...] = k.T.astype(BF)
    vz_ref[...] = jnp.where(keep_key, v, 0.0).astype(BF)

    rows = q_ref.shape[0]
    wide = rows + 32
    base = pl.multiple_of(i * rows, 16)
    start = pl.multiple_of(p.c * ROWS + i * rows, 16)
    ids = row_ids(start - 16, wide)
    keep = (ids >= 0) & (ids < n)
    hw = jnp.where(keep, seq_ref[pl.ds(start, wide), :].astype(F32), 0.0)
    put_tiles(hbuf, hw)
    wdep = wdep_ref[...].astype(F32)
    for t in range(D // 128):
        cols = slice(t * 128, (t + 1) * 128)

        def strip(s, carry):
            r0 = pl.multiple_of(s * 64, 64)
            depth = jnp.zeros((64, 128), F32)
            for j in range(KW):
                depth = depth + hbuf[t, pl.ds(r0 + 12 + j, 64), :] * wdep[j : j + 1, cols]
            dep_ref[pl.ds(r0, 64), cols] = depth.astype(BF)
            return carry

        lax.fori_loop(0, rows // 64, strip, 0)
    depth_low = dep_ref[...]
    hl = hw.astype(BF)
    h_ref[...] = hl[16 : 16 + rows]
    conv = jnp.where(keep, nt(hl, w_ref[2]) + line(bc_ref), 0.0)
    put_tiles(cbuf, conv)
    conv_ref[pl.ds(base, wide), :] = conv.astype(BF)
    q = nt(hl[16 : 16 + rows], w_ref[3]) + line(bq_ref)
    q_low = q.astype(BF)
    q_ref[...] = q_low
    qs_ref[...] = (q * (0.125 * LOG2E)).astype(BF)
    pt = nt(depth_low, w_ref[4]) + line(bp_ref)
    pt_ref[...] = pt.astype(BF)
    mixer = (pt * q_low.astype(F32)).astype(BF)
    logits = (nt(wk_ref[...], mixer) + bk_ref[:, 0:1]).reshape(KW, 8, rows)
    peak = jnp.max(logits, axis=0, keepdims=True)
    raised = jnp.exp(logits - peak)
    kp = (raised / jnp.sum(raised, axis=0, keepdims=True)).reshape(KW * 8, rows)
    kp_ref[...] = kp
    kpt = kp.T.astype(BF)
    for t in range(HALF // 128):
        mix = jnp.zeros((rows, 128), F32)
        for j in range(KW):
            wide_probs = nn(kpt, spread_ref[:, j * HALF + t * 128 : j * HALF + (t + 1) * 128])
            mix = mix + wide_probs * cbuf[t, 12 + j : 12 + j + rows, :]
        mix_ref[:, t * 128 : (t + 1) * 128] = mix.astype(BF)

    @pl.when(i == pl.num_programs(0) - 1)
    def _():
        inter.finish()
        dense.finish()
        cot_rows.finish()
        output.share()
        output.finish()
        keep_output.wait()
        keep_inter.wait()
        keep_dense.wait()
        keep_seq.wait()
        keep_w.wait()


def front(lens, tokens, weights, w_kernel, b_kernel, perm, wdep, bv, bc, bq, bp, spread, w_inter, w_dense, w_output, cotangent):
    rows = 256
    keys = 512
    blk = pl.BlockSpec((rows, HALF), lambda i, lens: (i, 0))
    full = pl.BlockSpec((rows, D), lambda i, lens: (i, 0))
    half = jax.ShapeDtypeStruct((ROWS, HALF), BF)
    return pl.pallas_call(
        front_kernel,
        grid_spec=pltpu.PrefetchScalarGridSpec(
            num_scalar_prefetch=1,
            grid=(ROWS // rows,),
            in_specs=[HBM]
            + [once((192, HALF))] * 5
            + [once((54, HALF)), whole((54,)), once((72, 54)), once((KW, D))]
            + [whole((HALF,))] * 4
            + [once((72, KW * HALF)), once((HALF, D)), once((2, 192, HALF)), once((D, HALF)), HBM],
            out_specs=[
                pl.BlockSpec((keys, HALF), lambda i, lens: (i, 0)),
                pl.BlockSpec((HALF, keys), lambda i, lens: (0, i)),
                pl.BlockSpec((keys, HALF), lambda i, lens: (i, 0)),
                blk,
                blk,
                blk,
                pl.BlockSpec((72, rows), lambda i, lens: (0, i)),
                whole((ROWS + 32, HALF)),
                blk,
                full,
                full,
                whole((72, HALF)),
                whole((72, 128)),
            ]
            + [HBM] * 6,
            scratch_shapes=[
                pltpu.VMEM((5, 192, HALF), BF),
                pltpu.VMEM((LMAX + 2 * PAD, D), BF),
                pltpu.VMEM((5, HALF, D), BF),
                pltpu.VMEM((ROWS, HALF), BF),
                pltpu.VMEM((8, HALF), F32),
                pltpu.VMEM((D // 128, rows + 32, 128), F32),
                pltpu.VMEM((HALF // 128, rows + 32, 128), F32),
                pltpu.SemaphoreType.DMA((8,)),
                pltpu.SemaphoreType.DMA((9,)),
                pltpu.SemaphoreType.DMA((9,)),
                pltpu.SemaphoreType.DMA((28,)),
                pltpu.SemaphoreType.DMA((28,)),
                pltpu.SemaphoreType.DMA((3,)),
                pltpu.SemaphoreType.DMA((2,)),
            ],
        ),
        out_shape=[
            jax.ShapeDtypeStruct((LMAX, HALF), BF),
            jax.ShapeDtypeStruct((HALF, LMAX), BF),
            jax.ShapeDtypeStruct((LMAX, HALF), BF),
            half,
            half,
            half,
            jax.ShapeDtypeStruct((72, ROWS), F32),
            jax.ShapeDtypeStruct((ROWS + 32, HALF), BF),
            half,
            jax.ShapeDtypeStruct((ROWS, D), BF),
            jax.ShapeDtypeStruct((ROWS, D), BF),
            jax.ShapeDtypeStruct((72, HALF), BF),
            jax.ShapeDtypeStruct((72, 128), F32),
            jax.ShapeDtypeStruct((LMAX + 2 * PAD, D), BF),
            jax.ShapeDtypeStruct((5, HALF, D), BF),
            jax.ShapeDtypeStruct((2, HALF, GW), BF),
            jax.ShapeDtypeStruct((2, HALF, D), BF),
            jax.ShapeDtypeStruct((ROWS, D), BF),
            jax.ShapeDtypeStruct((2, GW, HALF), BF),
        ],
        **comm_params("front", 2),
    )(
        lens, tokens, *weights, w_kernel, b_kernel, perm, wdep, bv, bc, bq, bp, spread, w_inter, w_dense, w_output, cotangent
    )


def attend_kernel(lens, q_ref, k_ref, v_ref, ctx_ref, lse_ref):
    k = k_ref[...]
    ones = jnp.where(row_ids(0, LMAX) < length(lens), 1.0, 0.0)
    ve = jnp.concatenate([v_ref[...], jnp.broadcast_to(ones, (LMAX, 128)).astype(BF)], axis=1)
    rows = 256
    lane = lax.broadcasted_iota(jnp.int32, (rows, 128), 1)
    for u in range(ROWS // rows):
        part = slice(u * rows, (u + 1) * rows)
        outs = []
        for hh in range(2):
            q = jnp.where((lane < HD) == (hh == 0), q_ref[part, :], jnp.zeros((), BF))
            s = nt(q, k)
            peak = jnp.max(s, axis=1, keepdims=True)
            prob = jnp.exp2(s - peak).astype(BF)
            o = nn(prob, ve)
            outs.append(o[:, :128] / o[:, 128:])
            lse_ref[0, hh : hh + 1, part] = (peak + jnp.log2(o[:, 128:129])).T
        ctx_ref[part, :] = jnp.where(lane < HD, outs[0], outs[1]).astype(BF)


def attend(lens, qs, kd, vz):
    pair = lambda rows: pl.BlockSpec((rows, 128), lambda p, lens: (0, p))
    return pl.pallas_call(
        attend_kernel,
        grid_spec=pltpu.PrefetchScalarGridSpec(
            num_scalar_prefetch=1,
            grid=(3,),
            in_specs=[pair(ROWS), pair(LMAX), pair(LMAX)],
            out_specs=[pair(ROWS), pl.BlockSpec((1, 8, ROWS), lambda p, lens: (p, 0, 0))],
        ),
        out_shape=[
            jax.ShapeDtypeStruct((ROWS, HALF), BF),
            jax.ShapeDtypeStruct((3, 8, ROWS), F32),
        ],
        **params("attend"),
    )(lens, qs, kd, vz)


def back_kernel(
    lens, gcv_ref, conv_ref, kp_ref, q_ref, pt_ref, wk_ref, spread_ref, ones_ref,
    qs_ref, do_ref, k_ref, v_ref, kt_ref, lse_ref, del_ref, pay_all, pay_ref, hid_ref,
    seq_ref, wc_ref, wp_ref, gpre_ref, dep_ref, wdep_ref, smf_ref, gbi_ref,
    gqm_ref, dq_ref, dk_ref, dv_ref, ghm_ref, edge_ref, half_ref, piece_ref, both_ref, mid_ref, out_ref,
    acc, wbuf, tbuf, dka, dva, near, mine, ybuf, mid, zbuf, both, xbuf, half,
    gpad, dbuf, hwin, sbuf, agc, agp, gwk, gbk, sm, gdp, pcp, near_cp, mine_cp, ybuf_cp,
    ns, nr, s, v_sem, ls, hs, hr,
):
    step = pl.program_id(0)
    place = Place()
    n = lens[place.r]
    groups = Groups(place, s, v_sem)
    hidden = FromRows(place, hid_ref, out_ref, ls, hs, hr)

    def near_copy(k):
        rr = 1 - place.r if k % 2 == 0 else place.r
        src, dst = (pay_all, near) if k < 2 else (pcp, near_cp)
        return send(src.at[rr, 1 - place.c], dst.at[rr], ns.at[k], nr.at[k], place.core)

    @pl.when(step == 0)
    def _():
        meet(everyone(place))
        near_copy(0).start()
        near_copy(1).start()
        hidden.start()
        for ref in (acc, tbuf, gwk, gbk, agc, agp, sm, gdp):
            ref[...] = jnp.zeros_like(ref)
        gpad[0:32, :] = jnp.zeros((32, HALF), BF)
        gpad[32 + ROWS :, :] = jnp.zeros((32, HALF), BF)

    @pl.when(step == 2)
    def _():
        near_copy(0).wait()
        near_copy(1).wait()
        for ch in range(3):
            for rr in range(2):
                total = near[rr, ch].astype(F32) + pay_ref[rr, 0, ch].astype(F32)
                mine[ch, :, :, rr] = total.astype(BF)
            groups.half(ch, mine.at[ch], ybuf.at[ch]).start()

    def settle(ch):
        groups.half(ch, mine.at[ch], ybuf.at[ch]).wait_recv()
        mid[ch] = (mine[ch, place.y].astype(F32) + ybuf[ch].astype(F32)).astype(BF)

    def merge(ch):
        groups.cross(13 + ch, both.at[ch], xbuf.at[ch]).wait_recv()
        return (both[ch, place.r].astype(F32) + xbuf[ch].astype(F32)).astype(BF)

    def quarters(ch):
        return 4 + 3 * ch, mid.at[ch], zbuf.at[ch]

    @pl.when(step == 6)
    def _():
        settle(0)
        groups.start_quarters(*quarters(0))
        near_copy(2).start()
        near_copy(3).start()

    @pl.when(step == 7)
    def _():
        near_copy(2).wait()
        near_copy(3).wait()
        for rr in range(2):
            total = near_cp[rr].astype(F32) + pcp[rr, place.c].astype(F32)
            mine_cp[:, :, rr] = total.astype(BF)
        groups.half(3, mine_cp, ybuf_cp).start()

    @pl.when(step == 8)
    def _():
        settle(1)
        groups.start_quarters(*quarters(1))
        groups.collect(*quarters(0), both.at[0])
        groups.cross(13, both.at[0], xbuf.at[0]).start()

    @pl.when(step == 9)
    def _():
        groups.start_along(15, half, merge(0))
        settle(2)
        groups.start_quarters(*quarters(2))

    @pl.when(step == 10)
    def _():
        groups.collect(*quarters(1), both.at[1])
        groups.cross(14, both.at[1], xbuf.at[1]).start()

    @pl.when(step == 11)
    def _():
        piece_ref[...] = merge(1)
        groups.half(3, mine_cp, ybuf_cp).wait_recv()
        mid_ref[...] = (mine_cp[place.y].astype(F32) + ybuf_cp[...].astype(F32)).astype(BF)

    @pl.when(step < 4)
    def _():
        rows = gcv_ref.shape[0]
        wide = rows + 32
        put_tiles(wbuf, conv_ref[pl.ds(pl.multiple_of(step * rows, 16), wide), :].astype(F32))
        kp = kp_ref[...]
        kpt = kp.T.astype(BF)
        gkps = [None] * KW
        there = pl.ds(pl.multiple_of(place.c * ROWS + step * rows, 16), wide)
        for t in range(HALF // 128):
            cols = slice(t * 128, (t + 1) * 128)
            gcv = gcv_ref[:, cols].astype(F32)
            total = jnp.zeros((wide, 128), F32)
            for j in range(KW):
                prod = (gcv * wbuf[t, 12 + j : 12 + j + rows, :]).astype(BF)
                part = nt(ones_ref[:, cols], prod)
                gkps[j] = part if t == 0 else gkps[j] + part
                tbuf[j % 3, 24 : 24 + rows, :] = nn(kpt, spread_ref[:, j * HALF + t * 128 : j * HALF + (t + 1) * 128]) * gcv
                total = total + tbuf[j % 3, 12 - j : 12 - j + wide, :]
            acc[there, cols] += total
        gkp = jnp.concatenate(gkps, axis=0).reshape(KW, 8, rows)
        kp3 = kp.reshape(KW, 8, rows)
        inner = jnp.sum(kp3 * gkp, axis=0, keepdims=True)
        gl = (kp3 * (gkp - inner)).reshape(KW * 8, rows)
        glt = gl.T.astype(BF)
        gbk[0:1, 0:72] += col_sum(glt.astype(F32))
        q = q_ref[...].astype(F32)
        pt = pt_ref[...].astype(F32)
        gwk[...] += nn(gl.astype(BF), (pt * q).astype(BF))
        gmix = nn(glt, wk_ref[...])
        gqm_ref[...] = (gmix * pt).astype(BF)
        gpad[rows_at(32 + step * rows, rows), :] = (gmix * q).astype(BF)

    def conv_grads(first, rows):
        keep = row_ids(first, rows) < n
        gco = jnp.where(keep, acc[rows_at(16 + first, rows), :], 0.0).astype(BF)
        tok = seq_ref[rows_at(PAD + first, rows), :]
        h = jnp.where(keep, tok.astype(F32), 0.0).astype(BF)
        agc[...] += nn(gco.T, h)
        sm[2:3, :] += col_sum(gco.astype(F32))
        return nn(gco, wc_ref[0])

    @pl.when(step == 4)
    def _():
        wdep = wdep_ref[...].astype(F32)
        at = pl.multiple_of((1 - place.c) * (ROWS + 16), 16)
        sbuf[...] = nn(gpad[pl.ds(at, 48), :], wp_ref[0])
        total = conv_grads(pl.multiple_of(ROWS - 16 * place.c, 16), 16)
        for j in range(KW):
            total = total + sbuf[20 - j : 36 - j, :] * wdep[j : j + 1, :]
        edge_ref[...] = total

    @pl.when((step == 4) | (step == 5))
    def _():
        m = step - 4
        rows = gpre_ref.shape[0]
        wide = rows + 32
        first = pl.multiple_of(place.c * ROWS + m * rows, 16)
        wdep = wdep_ref[...].astype(F32)
        win = gpad[rows_at(m * rows + 16, wide), :]
        gpt = win[16 : 16 + rows]
        sm[3:4, :] += col_sum(gpt.astype(F32))
        agp[...] += nn(gpt.T, dep_ref[...])
        put_tiles(dbuf, nn(win, wp_ref[0]))
        ids = row_ids(first - 16, wide)
        inside = (ids >= 0) & (ids < n)
        put_tiles(hwin, jnp.where(inside, seq_ref[pl.ds(first, wide), :].astype(F32), 0.0))
        ghm_ref[...] = (conv_grads(first, rows) + gpre_ref[...].astype(F32)).astype(BF)
        for t in range(D // 128):
            cols = slice(t * 128, (t + 1) * 128)

            def strip(k, sums):
                r0 = pl.multiple_of(k * 64, 64)
                gdep = dbuf[t, pl.ds(r0 + 16, 64), :]
                total = ghm_ref[pl.ds(r0, 64), cols].astype(F32)
                new = []
                for j in range(KW):
                    prod = gdep * hwin[t, pl.ds(r0 + 12 + j, 64), :]
                    new.append(sums[j] + jnp.sum(prod.reshape(8, 8, 128), axis=0))
                    total = total + dbuf[t, pl.ds(r0 + 20 - j, 64), :] * wdep[j : j + 1, cols]
                ghm_ref[pl.ds(r0, 64), cols] = total.astype(BF)
                return tuple(new)

            sums = lax.fori_loop(0, rows // 64, strip, (jnp.zeros((8, 128), F32),) * KW)
            for j in range(KW):
                gdp[j : j + 1, cols] += col_sum(sums[j])

    @pl.when(step == 5)
    def _():
        def put(r, c, first, value):
            pcp[r, c, first // 256, first // 64 % 4] = value.astype(BF)

        for r in range(2):
            for c in range(2):
                for k in range(3):
                    rows = slice(c * 192 + k * 64, c * 192 + (k + 1) * 64)
                    put(r, c, k * 64, agc[rows, r * HALF : (r + 1) * HALF])
                    put(r, c, 192 + k * 64, agp[rows, r * HALF : (r + 1) * HALF])
                put(r, c, 448, jnp.zeros((64, HALF), F32))
        zeros = lambda k: jnp.zeros((k, HALF), F32)
        put(0, 0, 384, gwk[0:64, :])
        bias = jnp.concatenate([gbk[...], jnp.zeros((8, 256), F32)], axis=1)
        put(0, 1, 384, jnp.concatenate([gwk[64:72, :], sm[...], bias, zeros(40)], axis=0))
        inter = jnp.concatenate([gbi_ref[:, k * HALF : (k + 1) * HALF] for k in range(8)], axis=0)
        put(1, 0, 384, jnp.concatenate([smf_ref[:, 0:HALF], smf_ref[:, HALF:D], inter, zeros(40)], axis=0))
        put(1, 1, 384, jnp.concatenate([gdp[:, 0:HALF], gdp[:, HALF:D], zeros(32)], axis=0))

    @pl.when(step >= 6)
    def _():
        i = lax.rem(step, 2)
        k = k_ref[...]
        v = v_ref[...]
        rows = qs_ref.shape[0]
        lane = lax.broadcasted_iota(jnp.int32, (rows, 128), 1)
        dk = dv = None
        for hh in range(2):
            head = (lane < HD) == (hh == 0)
            q = jnp.where(head, qs_ref[...], jnp.zeros((), BF))
            do = jnp.where(head, do_ref[...], jnp.zeros((), BF))
            p = jnp.exp2(nt(k, q) - lse_ref[0, hh : hh + 1, :])
            ds = (p * (nt(v, do) - del_ref[0, hh : hh + 1, :])).astype(BF)
            dv_one = nn(p.astype(BF), do)
            dk_one = nn(ds, q)
            dv = dv_one if dv is None else dv + dv_one
            dk = dk_one if dk is None else dk + dk_one
            dq_ref[hh * HD : (hh + 1) * HD, :] = (nn(kt_ref[hh * HD : (hh + 1) * HD, :], ds) * 0.125).astype(BF)

        @pl.when(i == 0)
        def _():
            dka[...] = dk
            dva[...] = dv

        @pl.when(i == 1)
        def _():
            keep = row_ids(0, LMAX) < n
            dk_ref[...] = jnp.where(keep, (dka[...] + dk) * LN2, 0.0).astype(BF)
            dv_ref[...] = jnp.where(keep, dva[...] + dv, 0.0).astype(BF)

    @pl.when(step == 11)
    def _():
        groups.collect(*quarters(2), both_ref)
        groups.await_along(15, half)
        half_ref[...] = half[...]
        for ch in range(3):
            groups.half(ch, mine.at[ch], ybuf.at[ch]).wait_send()
            for offset in (1, 2, 3):
                groups.quarter(*quarters(ch), offset).wait_send()
        groups.half(3, mine_cp, ybuf_cp).wait_send()
        for ch in range(2):
            groups.cross(13 + ch, both.at[ch], xbuf.at[ch]).wait_send()
        for offset in (1, 2, 3):
            groups.along(15, half, offset, place.z).wait_send()
        hidden.finish()


def back(
    lens, gcv, conv, kp, q, pt, wk72, spread, ones8, qs, do, kd, vz, kt, lse, delta, pay, hid,
    seq, w5, gpre, dep, wdep, smf, gbi,
):
    crows = 256
    rows = 512
    early = lambda s: jnp.minimum(s, 3)
    between = lambda s: jnp.minimum(jnp.maximum(s - 4, 0), 1)
    late = lambda s: jnp.maximum(s - 6, 0)
    which = lambda s: lax.div(late(s), 2)
    part = lambda s: lax.rem(late(s), 2)
    cblk = pl.BlockSpec((crows, HALF), lambda s, lens: (early(s), 0))
    mine = pl.BlockSpec((rows, 128), lambda s, lens: (part(s), which(s)))
    pair = pl.BlockSpec((LMAX, 128), lambda s, lens: (0, which(s)))
    stats = pl.BlockSpec((1, 8, rows), lambda s, lens: (which(s), 0, part(s)))
    full = pl.BlockSpec((rows, D), lambda s, lens: (between(s), 0))
    weight = lambda j: pl.BlockSpec((1, HALF, D), lambda s, lens: (j, 0, 0), pipeline_mode=pl.Buffered(1))
    block = (3, 2, 4, 80, HALF)
    pay = pay.reshape((2, 2) + block)
    mine_pay = pl.BlockSpec(
        (2, 1) + block, lambda s, lens: (0, half_index(), 0, 0, 0, 0, 0), pipeline_mode=pl.Buffered(1)
    )
    return pl.pallas_call(
        back_kernel,
        grid_spec=pltpu.PrefetchScalarGridSpec(
            num_scalar_prefetch=1,
            grid=(12,),
            in_specs=[
                cblk,
                once((ROWS + 32, HALF)),
                pl.BlockSpec((72, crows), lambda s, lens: (0, early(s))),
                cblk,
                cblk,
                once((72, HALF)),
                once((72, KW * HALF)),
                once((8, HALF)),
                mine,
                mine,
                pair,
                pair,
                pl.BlockSpec((128, LMAX), lambda s, lens: (which(s), 0)),
                stats,
                stats,
                HBM,
                mine_pay,
                once((ROWS, D)),
                once((LMAX + 2 * PAD, D)),
                weight(2),
                weight(4),
                full,
                full,
                once((KW, D)),
                once((8, D)),
                once((1, FF)),
            ],
            out_specs=[
                cblk,
                pl.BlockSpec((128, rows), lambda s, lens: (which(s), part(s))),
                pair,
                pair,
                full,
                once((16, D)),
                once((4, 80, HALF)),
                once((80, HALF)),
                once((2, 80, HALF)),
                once((4, 2, 64, HALF)),
                HBM,
            ],
            scratch_shapes=[
                pltpu.VMEM((LMAX + 32, HALF), F32),
                pltpu.VMEM((HALF // 128, crows + 32, 128), F32),
                pltpu.VMEM((3, crows + 48, 128), F32),
                pltpu.VMEM((LMAX, 128), F32),
                pltpu.VMEM((LMAX, 128), F32),
                pltpu.VMEM((2,) + block, BF),
                pltpu.VMEM((3, 2, 4, 2, 80, HALF), BF),
                pltpu.VMEM((3, 4, 2, 80, HALF), BF),
                pltpu.VMEM((3, 4, 2, 80, HALF), BF),
                pltpu.VMEM((3, 3, 2, 80, HALF), BF),
                pltpu.VMEM((2, 2, 80, HALF), BF),
                pltpu.VMEM((2, 80, HALF), BF),
                pltpu.VMEM((4, 80, HALF), BF),
                pltpu.VMEM((ROWS + 64, HALF), BF),
                pltpu.VMEM((D // 128, rows + 32, 128), F32),
                pltpu.VMEM((D // 128, rows + 32, 128), F32),
                pltpu.VMEM((48, D), F32),
                pltpu.VMEM((HALF, D), F32),
                pltpu.VMEM((HALF, D), F32),
                pltpu.VMEM((72, HALF), F32),
                pltpu.VMEM((8, 128), F32),
                pltpu.VMEM((8, HALF), F32),
                pltpu.VMEM((16, D), F32),
                pltpu.VMEM((2, 2, 2, 4, 64, HALF), BF),
                pltpu.VMEM((2, 2, 4, 64, HALF), BF),
                pltpu.VMEM((2, 4, 2, 64, HALF), BF),
                pltpu.VMEM((4, 2, 64, HALF), BF),
                pltpu.SemaphoreType.DMA((4,)),
                pltpu.SemaphoreType.DMA((4,)),
                pltpu.SemaphoreType.DMA((18,)),
                pltpu.SemaphoreType.DMA((18,)),
                pltpu.SemaphoreType.DMA,
                pltpu.SemaphoreType.DMA((2,)),
                pltpu.SemaphoreType.DMA((3,)),
            ],
        ),
        out_shape=[
            jax.ShapeDtypeStruct((ROWS, HALF), BF),
            jax.ShapeDtypeStruct((HALF, ROWS), BF),
            jax.ShapeDtypeStruct((LMAX, HALF), BF),
            jax.ShapeDtypeStruct((LMAX, HALF), BF),
            jax.ShapeDtypeStruct((ROWS, D), BF),
            jax.ShapeDtypeStruct((16, D), F32),
            jax.ShapeDtypeStruct((4, 80, HALF), BF),
            jax.ShapeDtypeStruct((80, HALF), BF),
            jax.ShapeDtypeStruct((2, 80, HALF), BF),
            jax.ShapeDtypeStruct((4, 2, 64, HALF), BF),
            jax.ShapeDtypeStruct((2, ROWS, HALF), BF),
        ],
        **comm_params("back", 4),
    )(
        lens, gcv, conv, kp, q, pt, wk72, spread, ones8, qs, do, kd, vz, kt, lse, delta, pay, pay, hid,
        seq, w5, w5, gpre, dep, wdep, smf, gbi,
    )


def norm_parts(x):
    xc = x - jnp.mean(x, axis=1, keepdims=True)
    inv = lax.rsqrt(jnp.mean(xc * xc, axis=1, keepdims=True) + EPS)
    return xc * inv, inv


def norm_back(up, normal, inv, gain):
    e = up * gain
    return inv * (e - jnp.mean(e, axis=1, keepdims=True) - normal * jnp.mean(e * normal, axis=1, keepdims=True))


def ffn_kernel(
    lens, ctx_ref, mix_ref, tok_ref, cot_ref, wd_ref, wi_ref, wo_ref, v0, v1, v2, v3, v4, v5, bi_ref, ones_ref,
    hid_ref, gpre_ref, gctx_ref, gcv_ref, del_ref, pay_ref, sm_ref, gbi_ref,
    act_s, gp_s, awd, awi, awo,
):
    i = pl.program_id(0)
    rows = ctx_ref.shape[0]
    keep = row_ids(half_index() * ROWS + i * rows, rows) < length(lens)

    @pl.when(i == 0)
    def _():
        awd[...] = jnp.zeros_like(awd)
        awi[...] = jnp.zeros_like(awi)
        awo[...] = jnp.zeros_like(awo)
        sm_ref[...] = jnp.zeros_like(sm_ref)
        gbi_ref[...] = jnp.zeros_like(gbi_ref)

    vectors = [line(ref) for ref in (v0, v1, v2, v3, v4, v5)]
    vec = lambda k: vectors[k]
    inter_bias = line(bi_ref)
    h = tok_ref[...].astype(F32)
    ctx = ctx_ref[...]
    mixed = jnp.concatenate([ctx, mix_ref[...]], axis=1)
    n1, inv1 = norm_parts(nn(mixed, wd_ref[...]) + vec(0) + h)
    f1 = n1 * vec(1) + vec(2)
    fl = f1.astype(BF)
    chunk = 512
    outs = []
    for g in range(2):
        fg = fl[:, g * HALF : (g + 1) * HALF]
        for ch in range(GW // chunk):
            cols = slice(ch * chunk, (ch + 1) * chunk)
            put = slice(g * GW + ch * chunk, g * GW + (ch + 1) * chunk)
            x = nn(fg, wi_ref[g, :, cols]) + inter_bias[:, put]
            phi = 0.5 + 0.5 * lax.erf(x * 0.7071067811865476)
            act_s[:, put] = (x * phi).astype(BF)
            gp_s[:, put] = phi + x * jnp.exp2(x * x * (-0.5 * LOG2E)) * 0.3989422804014327
        outs.append(nn(act_s[:, g * GW : (g + 1) * GW], wo_ref[g]))
    n2, inv2 = norm_parts(jnp.concatenate(outs, axis=1) + vec(3) + f1)
    hid_ref[...] = (n2 * vec(4) + vec(5)).astype(BF)
    u = jnp.where(keep, cot_ref[...].astype(F32), 0.0)
    gp2 = norm_back(u, n2, inv2, vec(4))
    go = gp2.astype(BF)
    got = go.T
    flt = fl.T
    gfs = []
    for g in range(2):
        sel = slice(g * HALF, (g + 1) * HALF)
        gf = gp2[:, sel]
        for ch in range(GW // chunk):
            cols = slice(ch * chunk, (ch + 1) * chunk)
            put = slice(g * GW + ch * chunk, g * GW + (ch + 1) * chunk)
            gi = (gp_s[:, put] * nt(go[:, sel], wo_ref[g, cols, :])).astype(BF)
            gbi_ref[0:1, put] += col_sum(gi.astype(F32))
            awo[g, :, cols] += nn(got[sel], act_s[:, put])
            awi[g, :, cols] += nn(flt[sel], gi)
            gf = gf + nt(gi, wi_ref[g, :, cols])
        gfs.append(gf)
    gf = jnp.concatenate(gfs, axis=1)
    gpre = norm_back(gf, n1, inv1, vec(1))
    gd = gpre.astype(BF)
    gpre_ref[...] = gd
    sm_ref[0:1, :] += col_sum(go.astype(F32))
    sm_ref[1:2, :] += col_sum(u * n2)
    sm_ref[2:3, :] += col_sum(u)
    sm_ref[3:4, :] += col_sum(gd.astype(F32))
    sm_ref[4:5, :] += col_sum(gf * n1)
    sm_ref[5:6, :] += col_sum(gf)
    awd[...] += nn(mixed.T, gd)
    gm = nt(gd, wd_ref[...])
    gctx = gm[:, :HALF].astype(BF)
    gctx_ref[...] = gctx
    gcv_ref[...] = gm[:, HALF:].astype(BF)
    prod = (gctx.astype(F32) * ctx.astype(F32)).astype(BF)
    del_ref[...] = nt(ones_ref[...], prod).reshape(3, 8, rows)

    @pl.when(i == pl.num_programs(0) - 1)
    def _():
        for r in range(2):
            for c in range(2):
                pay_ref[r, c, 0:HALF, :] = awi[r, :, c * D : c * D + HALF].astype(BF)
                pay_ref[r, c, HALF:D, :] = awi[r, :, c * D + HALF : (c + 1) * D].astype(BF)
                pay_ref[r, c, D : 2 * D, :] = awo[r, :, c * D : (c + 1) * D].T.astype(BF)
                for part in range(2):
                    piece = awd[part * HALF + c * 192 : part * HALF + (c + 1) * 192, r * HALF : (r + 1) * HALF]
                    pay_ref[r, c, 2 * D + part * 192 : 2 * D + (part + 1) * 192, :] = piece.astype(BF)


def ffn(lens, ctx, mix, tok, cot, wd, wi, wo, vectors, bi, ones24):
    rows = 256
    blk = lambda w: pl.BlockSpec((rows, w), lambda i, lens: (i, 0))
    return pl.pallas_call(
        ffn_kernel,
        grid_spec=pltpu.PrefetchScalarGridSpec(
            num_scalar_prefetch=1,
            grid=(ROWS // rows,),
            in_specs=[
                blk(HALF),
                blk(HALF),
                blk(D),
                blk(D),
                whole((D, D)),
                whole((2, HALF, GW)),
                whole((2, GW, HALF)),
                *[whole((D,))] * 6,
                whole((FF,)),
                whole((24, HALF)),
            ],
            out_specs=[
                blk(D),
                blk(D),
                blk(HALF),
                blk(HALF),
                pl.BlockSpec((3, 8, rows), lambda i, lens: (0, 0, i)),
                whole((2, 2, FFN_ROWS, HALF)),
                whole((8, D)),
                whole((1, FF)),
            ],
            scratch_shapes=[
                pltpu.VMEM((rows, FF), BF),
                pltpu.VMEM((rows, FF), F32),
                pltpu.VMEM((D, D), F32),
                pltpu.VMEM((2, HALF, GW), F32),
                pltpu.VMEM((2, HALF, GW), F32),
            ],
        ),
        out_shape=[
            jax.ShapeDtypeStruct((ROWS, D), BF),
            jax.ShapeDtypeStruct((ROWS, D), BF),
            jax.ShapeDtypeStruct((ROWS, HALF), BF),
            jax.ShapeDtypeStruct((ROWS, HALF), BF),
            jax.ShapeDtypeStruct((3, 8, ROWS), F32),
            jax.ShapeDtypeStruct((2, 2, FFN_ROWS, HALF), BF),
            jax.ShapeDtypeStruct((8, D), F32),
            jax.ShapeDtypeStruct((1, FF), F32),
        ],
        **params("ffn"),
    )(lens, ctx, mix, tok, cot, wd, wi, wo, *vectors, bi, ones24)


def tail_kernel(
    lens, seq_ref, dk_ref, dv_ref, dq_ref, gqm_ref, ghm_ref, edge_ref, w_ref, half0, piece1, both2, mid3,
    big_ref, cp_ref, sum_ref, small_ref, ght_ref,
    agw, accb, sm, tsend, trecv, gho, halves, other, zbuf, both, xbuf, xbuf_cp, half_cp, last_cp,
    pay, small, total_sum, near, far, out, mid, ybuf, zsum, s, v, ns, nr, cs, cr, gs, gr, own, es, er, ls, hs, hr,
):
    step = pl.program_id(0)
    i = lax.rem(step, 4)
    p = Place()
    r, c = p.r, p.c
    rows = dk_ref.shape[0]
    b = lax.rem((1 - c) * 2 + i, 4)
    n = lens[r]
    groups = Groups(p, gs, gr)
    chunks = 5
    crows = PROJ_ROWS // chunks
    summed = Sum(p, far, mid, ybuf, zsum, total_sum, crows, s, v)
    places = [FromRows(p, gho.at[k], ght_ref.at[k], ls.at[k], hs.at[k], hr.at[k]) for k in range(2)]

    def theirs(k):
        return send(tsend.at[k], trecv.at[k], es.at[k], er.at[k], p.core)

    def part(ch):
        return slice(ch * crows, (ch + 1) * crows)

    def beside(k, ch):
        rr = 1 - r if k == 0 else r
        at = k * chunks + ch
        return send(pay.at[rr, 1 - c, part(ch), :], near.at[rr, part(ch), :], ns.at[at], nr.at[at], p.core)

    def cross(ch):
        return send(out.at[part(ch), :], far.at[part(ch), :], cs.at[ch], cr.at[ch], p.across)

    def arrive(ch):
        beside(1, ch).wait_recv()
        cross(ch).wait_recv()
        total = near[r, part(ch), :].astype(F32) + pay[r, c, part(ch), :].astype(F32)
        far[part(ch), :] = (total + far[part(ch), :].astype(F32)).astype(BF)
        summed.half(ch)

    stages = [
        arrive,
        summed.quarter,
        lambda ch: summed.along(ch, summed.collect(ch)),
        summed.back,
        summed.finish_spread,
    ]

    def tick(t):
        for k, stage in enumerate(stages):
            if 0 <= t - k < chunks:
                stage(t - k)

    @pl.when(step == 0)
    def _():
        meet(everyone(p))
        groups.cross(3, both2, xbuf).start()
        groups.start_quarters(0, mid3, zbuf)
        groups.start_along(5, halves.at[0], piece1[...])
        groups.back(14, half0, other.at[0]).start()
        agw[...] = jnp.zeros_like(agw)
        sm[...] = jnp.zeros_like(sm)

    @pl.when(step == 2)
    def _():
        groups.cross(3, both2, xbuf).wait_recv()
        groups.start_along(8, halves.at[1], (both2[r].astype(F32) + xbuf[...].astype(F32)).astype(BF))

    @pl.when(step == 4)
    def _():
        for ch in range(chunks):
            beside(0, ch).wait_recv()
            total = near[1 - r, part(ch), :].astype(F32) + pay[1 - r, c, part(ch), :].astype(F32)
            out[part(ch), :] = total.astype(BF)
            cross(ch).start()

    @pl.when(step == 5)
    def _():
        groups.collect(0, mid3, zbuf, both)
        groups.cross(4, both, xbuf_cp).start()
        groups.await_along(5, halves.at[0])
        groups.back(15, halves.at[0], other.at[1]).start()

    @pl.when(step == 6)
    def _():
        groups.cross(4, both, xbuf_cp).wait_recv()
        groups.start_along(11, half_cp, (both[r].astype(F32) + xbuf_cp[...].astype(F32)).astype(BF))
        tick(0)

    @pl.when(step == 7)
    def _():
        groups.await_along(8, halves.at[1])
        groups.back(16, halves.at[1], other.at[2]).start()
        tick(1)

    keep = row_ids(b * rows, rows) < n

    def query_grad():
        return (dq_ref[...].astype(F32) + gqm_ref[...].astype(F32).T).astype(BF)

    @pl.when(step < 4)
    def _():
        tok = seq_ref[rows_at(PAD + b * rows, rows), :]
        h = jnp.where(keep, tok.astype(F32), 0.0).astype(BF)
        agw[0] += nn(dk_ref[...].T, h)
        agw[1] += nn(dv_ref[...].T, h)
        sm[1:2, :] += col_sum(dv_ref[...].astype(F32))

        @pl.when(step >= 2)
        def _():
            gqt = query_grad()
            sm[0:1, :] += col_sum(gqt.T.astype(F32))
            agw[2] += nn(gqt, h)

    @pl.when(step == 3)
    def _():
        for rr in range(2):
            for cc in range(2):
                for j in range(3):
                    piece = agw[j, cc * 192 : (cc + 1) * 192, rr * HALF : (rr + 1) * HALF]
                    pay[rr, cc, j * 192 : (j + 1) * 192, :] = piece.astype(BF)
                pay[rr, cc, 576:, :] = jnp.zeros((64, HALF), BF)
        pay[0, 0, 576:, :] = jnp.concatenate([sm[...], jnp.zeros((56, HALF), F32)], axis=0).astype(BF)
        for ch in range(chunks):
            for k in range(2):
                beside(k, ch).start()

    @pl.when(step >= 4)
    def _():
        accb[...] = nn(dk_ref[...], w_ref[0]) + nn(dv_ref[...], w_ref[1])

        @pl.when(step >= 6)
        def _():
            accb[...] += nn(query_grad().T, w_ref[3]) + ghm_ref[...].astype(F32)

    for k in range(2):

        @pl.when((step == 4 + k) & (c == k))
        def _():
            at = slice(0, 16) if k == 0 else slice(rows - 16, rows)
            accb[at, :] += edge_ref[...]

        @pl.when(step == 4 + k)
        def _():
            tsend[k] = jnp.where(keep, accb[...], 0.0).astype(BF)
            theirs(k).start()

        @pl.when(step == 6 + k)
        def _():
            theirs(k).wait_recv()
            gho[k] = jnp.where(keep, accb[...] + trecv[k].astype(F32), 0.0).astype(BF)
            places[k].start()

    @pl.when(step == 7)
    def _():
        tick(2)
        groups.await_along(11, half_cp)
        groups.back(17, half_cp, last_cp).start()
        tick(3)
        groups.back(14, half0, other.at[0]).wait_recv()
        groups.back(15, halves.at[0], other.at[1]).wait_recv()
        big_ref[0, p.y] = half0[...]
        big_ref[0, 1 - p.y] = other[0]
        big_ref[1, p.y] = halves[0]
        big_ref[1, 1 - p.y] = other[1]
        tick(4)
        groups.back(16, halves.at[1], other.at[2]).wait_recv()
        big_ref[2, p.y] = halves[1]
        big_ref[2, 1 - p.y] = other[2]
        tick(5)
        groups.back(17, half_cp, last_cp).wait_recv()
        cp_ref[p.y] = half_cp[...]
        cp_ref[1 - p.y] = last_cp[...]
        own[0] = cp_ref[1, 2]
        for t in range(6, chunks + len(stages) - 1):
            tick(t)
        own[1] = total_sum[576:PROJ_ROWS, :]
        mine = small.at[r * 2 + c]
        moves = [
            send(own, mine, es.at[2 + k], er.at[2 + k], device)
            for k, device in enumerate((p.across, p.core, p.diagonal))
        ]
        for move in moves:
            move.start()
        small[r * 2 + c] = own[...]
        sum_ref[...] = total_sum[...]
        for ch in range(chunks):
            summed.finish_sum(ch)
            cross(ch).wait_send()
            for k in range(2):
                beside(k, ch).wait_send()
        groups.back(14, half0, other.at[0]).wait_send()
        groups.back(15, halves.at[0], other.at[1]).wait_send()
        groups.back(16, halves.at[1], other.at[2]).wait_send()
        groups.back(17, half_cp, last_cp).wait_send()
        for offset in (1, 2, 3):
            groups.quarter(0, mid3, zbuf, offset).wait_send()
            groups.along(5, halves.at[0], offset, p.z).wait_send()
            groups.along(8, halves.at[1], offset, p.z).wait_send()
            groups.along(11, half_cp, offset, p.z).wait_send()
        groups.cross(3, both2, xbuf).wait_send()
        groups.cross(4, both, xbuf_cp).wait_send()
        theirs(0).wait_send()
        theirs(1).wait_send()
        for k, (rr, cc) in enumerate(((1 - r, c), (r, 1 - c), (1 - r, 1 - c))):
            send(own, small.at[rr * 2 + cc], es.at[2 + k], er.at[2 + k], p.core).wait_recv()
        for move in moves:
            move.wait_send()
        small_ref[...] = small[...]
        places[0].finish()
        places[1].finish()


def tail(lens, seq_tok, dk, dv, dq, gqm, ghm, edge, w5, half0, piece1, both2, mid3):
    rows = 512
    mine = lambda s: jnp.maximum(lax.rem(s, 4) - 2, 0)
    seq = pl.BlockSpec((rows, HALF), lambda s, lens: (lax.rem((1 - half_index()) * 2 + s, 4), 0))
    own = lambda w: pl.BlockSpec((rows, w), lambda s, lens: (mine(s), 0))
    crows = PROJ_ROWS // 5
    return pl.pallas_call(
        tail_kernel,
        grid_spec=pltpu.PrefetchScalarGridSpec(
            num_scalar_prefetch=1,
            grid=(8,),
            in_specs=[
                once((LMAX + 2 * PAD, D)),
                seq,
                seq,
                pl.BlockSpec((HALF, rows), lambda s, lens: (0, mine(s))),
                own(HALF),
                own(D),
                once((16, D)),
                once((5, HALF, D)),
                once((4, 80, HALF)),
                once((80, HALF)),
                once((2, 80, HALF)),
                once((4, 2, 64, HALF)),
            ],
            out_specs=[
                once((3, 2, 4, 80, HALF)),
                once((2, 4, 64, HALF)),
                once((PROJ_ROWS, HALF)),
                once((4, 2, 64, HALF)),
                HBM,
            ],
            scratch_shapes=[
                pltpu.VMEM((3, HALF, D), F32),
                pltpu.VMEM((rows, D), F32),
                pltpu.VMEM((8, HALF), F32),
                pltpu.VMEM((2, rows, D), BF),
                pltpu.VMEM((2, rows, D), BF),
                pltpu.VMEM((2, rows, D), BF),
                pltpu.VMEM((2, 4, 80, HALF), BF),
                pltpu.VMEM((3, 4, 80, HALF), BF),
                pltpu.VMEM((3, 2, 64, HALF), BF),
                pltpu.VMEM((2, 64, HALF), BF),
                pltpu.VMEM((80, HALF), BF),
                pltpu.VMEM((64, HALF), BF),
                pltpu.VMEM((4, 64, HALF), BF),
                pltpu.VMEM((4, 64, HALF), BF),
                pltpu.VMEM((2, 2, PROJ_ROWS, HALF), BF),
                pltpu.VMEM((4, 2, 64, HALF), BF),
                pltpu.VMEM((PROJ_ROWS, HALF), BF),
                pltpu.VMEM((2, PROJ_ROWS, HALF), BF),
                pltpu.VMEM((PROJ_ROWS, HALF), BF),
                pltpu.VMEM((PROJ_ROWS, HALF), BF),
                *Sum.scratch(crows, 5),
                pltpu.SemaphoreType.DMA((10,)),
                pltpu.SemaphoreType.DMA((10,)),
                pltpu.SemaphoreType.DMA((5,)),
                pltpu.SemaphoreType.DMA((5,)),
                pltpu.SemaphoreType.DMA((18,)),
                pltpu.SemaphoreType.DMA((18,)),
                pltpu.VMEM((2, 64, HALF), BF),
                pltpu.SemaphoreType.DMA((5,)),
                pltpu.SemaphoreType.DMA((5,)),
                pltpu.SemaphoreType.DMA((2,)),
                pltpu.SemaphoreType.DMA((2, 2)),
                pltpu.SemaphoreType.DMA((2, 3)),
            ],
        ),
        out_shape=[
            jax.ShapeDtypeStruct((3, 2, 4, 80, HALF), BF),
            jax.ShapeDtypeStruct((2, 4, 64, HALF), BF),
            jax.ShapeDtypeStruct((PROJ_ROWS, HALF), BF),
            jax.ShapeDtypeStruct((4, 2, 64, HALF), BF),
            jax.ShapeDtypeStruct((2, 2, rows, HALF), BF),
        ],
        **comm_params("tail", 6),
    )(lens, seq_tok, dk, dv, dq, gqm, ghm, edge, w5, half0, piece1, both2, mid3)


def outputs_kernel(
    ght, hid, t0, t1, t2, t3, t4, big_i0, big_i1, big_o, big_d, small, perm_ref,
    hid_ref, gt_ref, gk_ref, gv_ref, gc_ref, gq_ref, gp_ref, gi_ref, go_ref, gd_ref,
    gdep_ref, gbq_ref, gbv_ref, gbc_ref, gbp_ref, gwk_ref, gbk_ref,
    gbd_ref, gg1_ref, gb1_ref, gbi_ref, gbo_ref, gg2_ref, gb2_ref,
):
    i = pl.program_id(0)
    hid_ref[...] = hid[...]
    gt_ref[...] = ght[0, 0].astype(F32)

    for src, ref in ((t0, gk_ref), (t1, gv_ref), (t2, gq_ref), (t3, gc_ref), (t4, gp_ref), (big_o, go_ref), (big_d, gd_ref)):
        ref[...] = src[...].astype(F32)
    gi_ref[:, 0:HALF] = big_i0[...].astype(F32)
    gi_ref[:, HALF:D] = big_i1[...].astype(F32)

    @pl.when(i == 0)
    def _():
        tail = small[1, 0].astype(F32)
        norms = small[2, 0].astype(F32)
        depth = small[3, 0].astype(F32)
        late = small[0, 1].astype(F32)
        kernel_grad = jnp.concatenate([small[0, 0].astype(F32), tail[0:8]], axis=0).astype(BF)
        gwk_ref[...] = nn(perm_ref[...], kernel_grad)
        bias = nt(tail[16:24, 0:72].astype(BF), perm_ref[...])
        gbk_ref[...] = bias[0:1, :].reshape(54)
        for k, ref in enumerate((gbq_ref, gbv_ref)):
            ref[...] = late[k : k + 1, :].reshape(HALF)
        for k, ref in enumerate((gbc_ref, gbp_ref)):
            ref[...] = tail[10 + k : 11 + k, :].reshape(HALF)
        for k, ref in enumerate((gbo_ref, gg2_ref, gb2_ref, gbd_ref, gg1_ref, gb1_ref)):
            ref[...] = jnp.concatenate([norms[k : k + 1, :], norms[8 + k : 9 + k, :]], axis=1).reshape(D)
        gbi_ref[...] = jnp.concatenate([norms[16 + k : 17 + k, :] for k in range(8)], axis=1).reshape(FF)
        gdep_ref[:, 0:HALF] = depth[0:KW, :]
        gdep_ref[:, HALF:D] = depth[16 : 16 + KW, :]


def outputs(ght, hid, total, cp, big, small, perm):
    rows = 512
    at = lambda n, first: pl.BlockSpec((n, HALF), lambda i: (first + i, 0))
    blk = at(rows, 0)
    chunk = pl.BlockSpec((1, 1, rows, HALF), lambda i: (lax.rem(i, 2), lax.div(i, 2), 0, 0))
    shapes = [(KW, D)] + [(HALF,)] * 4 + [(54, HALF), (54,)] + [(D,)] * 3 + [(FF,)] + [(D,)] * 3
    main = [(192, HALF)] * 5 + [(HALF, D), (D, HALF), (HALF, HALF)]
    return pl.pallas_call(
        outputs_kernel,
        grid=(4,),
        in_specs=[chunk, blk]
        + [at(48, 4 * j) for j in (0, 1, 2, 0, 1)]
        + [at(96, 0), at(96, 4), at(192, 4), at(96, 16), whole((4, 2, 64, HALF)), whole((54, 72))],
        out_specs=[blk, blk]
        + [at(48, 0)] * 5
        + [pl.BlockSpec((96, D), lambda i: (i, 0)), at(192, 0), at(96, 0)]
        + [whole(shape) for shape in shapes],
        out_shape=[jax.ShapeDtypeStruct((LMAX, HALF), BF), jax.ShapeDtypeStruct((LMAX, HALF), F32)]
        + [jax.ShapeDtypeStruct(shape, F32) for shape in main + shapes],
        **params("outputs"),
    )(ght, hid, total, total, total, cp, cp, big, big, big, big, small, perm)


def constants():
    spread = np.zeros((72, KW * HALF), np.float32)
    ones8 = np.zeros((8, HALF), np.float32)
    ones24 = np.zeros((24, HALF), np.float32)
    perm = np.zeros((72, 54), np.float32)
    for head in range(6):
        cols = slice(head * HD, (head + 1) * HD)
        ones8[head, cols] = 1
        ones24[head // 2 * 8 + head % 2, cols] = 1
        for j in range(KW):
            spread[j * 8 + head, j * HALF + head * HD : j * HALF + (head + 1) * HD] = 1
            perm[j * 8 + head, head * KW + j] = 1
    return [jnp.asarray(a, BF) for a in (spread, ones8, ones24, perm)]


def per_device(
    groups, tokens, cotangent, seq_lengths, w_query, w_key, w_value, w_convout, w_point, w_depth,
    b_query, b_value, b_convout, b_point, w_kernel, b_kernel, w_dense, b_dense, gain_one, bias_one,
    w_inter, b_inter, w_output, b_output, gain_two, bias_two,
):
    lens = seq_lengths
    spread, ones8, ones24, perm = constants()
    wdep = w_depth.T

    kd, kt, vz, q, qs, pt, kp, conv, mix, dep, hown, wk72, bk72, seq, w5, wi, wd, cot, wo = front(
        lens, tokens, (w_key.T, w_value.T, w_convout.T, w_query.T, w_point.T), w_kernel.T, b_kernel, perm,
        wdep, b_value, b_convout, b_query, b_point, spread,
        w_inter[0], w_dense.reshape(2, 192, HALF), w_output[0], cotangent,
    )
    ctx, lse = attend(lens, qs, kd, vz)
    vectors = (b_dense, gain_one, bias_one, b_output, gain_two, bias_two)
    hid, gpre, gctx, gcv, delta, payf, smf, gbi = ffn(
        lens, ctx, mix, hown, cot, wd.reshape(D, D), wi, wo, vectors, b_inter, ones24
    )
    gqm, dq, dk, dv, ghm, edge, half0, piece1, both2, mid3, hid = back(
        lens, gcv, conv, kp, q, pt, wk72, spread, ones8, qs, gctx, kd, vz, kt, lse, delta, payf, hid,
        seq, w5, gpre, dep, wdep, smf, gbi,
    )
    big, cp, total, small, ght = tail(lens, seq, dk, dv, dq, gqm, ghm, edge, w5, half0, piece1, both2, mid3)
    big = big.reshape(FFN_ROWS, HALF)
    cp = cp.reshape(512, HALF)
    if groups > 8:
        sums = lax.psum(tuple(x.astype(F32) * 0.125 for x in (total, cp, big, small)), "dp")
        total, cp, big, small = (x.astype(BF) for x in sums)
    (
        hidden_out, gt, gk, gv, gc, gq, gp, gi, go, gd, gdep, gbq, gbv, gbc, gbp, gwk, gbk, gbd, gg1, gb1, gbi, gbo, gg2, gb2,
    ) = outputs(ght, hid.reshape(LMAX, HALF), total, cp, big, small, perm.T)
    return (
        hidden_out, gt, gq.T, gk.T, gv.T, gc.T, gp.T, gdep.T, gbq, gbv, gbc, gbp, gwk.T, gbk, gd, gbd, gg1, gb1,
        gi[None], gbi, go[None], gbo, gg2, gb2,
    )


def solution(mesh):
    act = P(("dp", "col"), "row")
    rep = P()
    proj = P("row", "col")
    in_specs = (
        act, act, P("dp"), proj, proj, proj, proj, proj, rep, rep, rep, rep, rep, rep, rep, P("col", "row"),
        rep, rep, rep, P("row", None, "col"), rep, P("row", "col", None), rep, rep, rep,
    )
    out_specs = (
        act, act, proj, proj, proj, proj, proj, rep, rep, rep, rep, rep, rep, rep, P("col", "row"),
        rep, rep, rep, P("row", None, "col"), rep, P("row", "col", None), rep, rep, rep,
    )
    return jax.shard_map(
        functools.partial(per_device, mesh.shape["dp"]), mesh=mesh, in_specs=in_specs, out_specs=out_specs, check_vma=False)
```

```python
import functools

import jax
import jax.numpy as jnp
import numpy as np
from jax import lax
from jax.experimental import pallas as pl
from jax.experimental.pallas import tpu as pltpu
from jax.sharding import PartitionSpec as P

D = 768
HALF = 384
HD = 64
KW = 9
FF = 3072
GW = 1536
LMAX = 2048
ROWS = 1024
EPS = 1e-12
LOG2E = 1.4426950408889634
LN2 = 0.6931471805599453
BF = jnp.bfloat16
F32 = jnp.float32
VMEM_BYTES = 63 * 1024 * 1024
PAD = 16
FFN_ROWS = 1920
FFN_CHUNK = 640
PROJ_ROWS = 640
MESH = pl.DeviceIdType.MESH
HBM = pl.BlockSpec(memory_space=pl.ANY)
VMEM = pl.BlockSpec(memory_space=pltpu.VMEM)


def nn(a, b):
    return lax.dot_general(a, b, (((1,), (0,)), ((), ())), preferred_element_type=F32)


def nt(a, b):
    return lax.dot_general(a, b, (((1,), (1,)), ((), ())), preferred_element_type=F32)


def col_sum(x):
    return jnp.sum(x, axis=0, keepdims=True)


def row_ids(start, rows):
    return start + lax.broadcasted_iota(jnp.int32, (rows, 1), 0)


def whole(shape):
    return pl.BlockSpec(shape, lambda *_: (0,) * len(shape))


def once(shape):
    return pl.BlockSpec(shape, lambda *_: (0,) * len(shape), pipeline_mode=pl.Buffered(1))


def half_index():
    return lax.axis_index("col")


def length(lens):
    return lens[lax.axis_index("row")]


def line(ref):
    return ref[...].astype(F32).reshape(1, ref.shape[0])


def clear(ref, step=32):
    def body(k, carry):
        ref[pl.ds(pl.multiple_of(k * step, step), step), :] = jnp.zeros((step, ref.shape[1]), ref.dtype)
        return carry

    lax.fori_loop(0, ref.shape[0] // step, body, 0)


def put_tiles(buf, value, first=0):
    for t in range(value.shape[1] // 128):
        buf[t, first : first + value.shape[0], :] = value[:, t * 128 : (t + 1) * 128]


def params(name):
    return dict(
        name=name,
        compiler_params=pltpu.CompilerParams(vmem_limit_bytes=VMEM_BYTES),
    )


def lanes(k, width=HALF):
    return pl.ds(pl.multiple_of(k * width, 128), width)


def rows_at(start, count, step=16):
    return pl.ds(pl.multiple_of(start, step), count)


def send(src, dst, send_sem, recv_sem, device):
    return pltpu.make_async_remote_copy(
        src_ref=src, dst_ref=dst, send_sem=send_sem, recv_sem=recv_sem, device_id=device, device_id_type=MESH
    )


class Place:
    def __init__(self):
        self.d = lax.axis_index("dp")
        self.r = lax.axis_index("row")
        self.c = lax.axis_index("col")
        self.k = lax.rem(self.d, 8)
        self.base = self.d - self.k
        self.y = lax.rem(self.k, 2)
        self.z = lax.div(self.k, 2)
        self.beside = {"dp": self.base + self.z * 2 + 1 - self.y}
        self.across = {"row": 1 - self.r}
        self.core = {"col": 1 - self.c}
        self.diagonal = {"row": 1 - self.r, "col": 1 - self.c}

    def eight(self, offset):
        other = lax.rem(self.k + offset, 8)
        return other, {"dp": self.base + other}

    def four(self, offset):
        other = lax.rem(self.z + offset, 4)
        return other, {"dp": self.base + other * 2 + self.y}


def meet(devices):
    barrier = pltpu.get_barrier_semaphore()
    for device in devices:
        pl.semaphore_signal(barrier, inc=1, device_id=device, device_id_type=MESH)
    pl.semaphore_wait(barrier, len(devices))


def comm_params(name, number):
    return dict(
        name=name,
        compiler_params=pltpu.CompilerParams(
            vmem_limit_bytes=VMEM_BYTES, collective_id=number, has_side_effects=True
        ),
    )


class Gather:
    def __init__(self, place, own, full, part, block, step, send_sem, recv_sem, first):
        self.p, self.own, self.full, self.part, self.block, self.h = place, own, full, part, block, step
        self.s, self.v, self.f = send_sem, recv_sem, first

    def _move(self, src, dst, n, device):
        return send(src, dst, self.s.at[self.f + n], self.v.at[self.f + n], device)

    def _cross(self, r):
        p = self.p
        at = (p.y * 4 + p.z) * self.h
        return self._move(self.part(self.own, at, self.h), self.block(self.full, r, p.c, at, self.h), 0, p.across)

    def _near(self, c):
        p = self.p
        return self._move(self.own, self.block(self.full, p.r, c, 0, 8 * self.h), 1, p.core)

    def _pass(self, offset, z):
        p = self.p
        here = self.block(self.full, 1 - p.r, p.c, (p.y * 4 + z) * self.h, self.h)
        return self._move(here, here, 1 + offset, p.four(offset)[1])

    def _turn(self, y):
        p = self.p
        here = self.block(self.full, 1 - p.r, p.c, y * 4 * self.h, 4 * self.h)
        return self._move(here, here, 5, p.beside)

    def _last(self, c):
        p = self.p
        here = self.block(self.full, 1 - p.r, c, 0, 8 * self.h)
        return self._move(here, here, 6, p.core)

    def start(self):
        self._cross(self.p.r).start()
        self._near(self.p.c).start()

    def relay(self):
        p = self.p
        self._cross(1 - p.r).wait_recv()
        for offset in (1, 2, 3):
            self._pass(offset, p.z).start()

    def turn(self):
        p = self.p
        for offset in (1, 2, 3):
            self._pass(offset, lax.rem(p.z + 4 - offset, 4)).wait_recv()
        self._turn(p.y).start()

    def share(self):
        p = self.p
        self._turn(1 - p.y).wait_recv()
        self._last(p.c).start()

    def finish(self):
        p = self.p
        self._last(1 - p.c).wait_recv()
        self._near(1 - p.c).wait_recv()
        self._cross(p.r).wait_send()
        self._near(p.c).wait_send()
        for offset in (1, 2, 3):
            self._pass(offset, p.z).wait_send()
        self._turn(p.y).wait_send()
        self._last(p.c).wait_send()


def middle_part(ref, first, rows):
    return ref.at[:, rows_at(first, rows, 8), :]


def middle_block(ref, r, c, first, rows):
    return ref.at[:, rows_at(c * 192 + first, rows, 8), lanes(r)]


def rows_part(ref, first, rows):
    return ref.at[rows_at(first, rows), :]


def inter_block(ref, r, c, first, rows):
    return ref.at[r, rows_at(first, rows), lanes(c, 768)]


def output_block(ref, r, c, first, rows):
    return ref.at[r, rows_at(c * 768 + first, rows), :]


class ToRows:
    def __init__(self, place, src, dst, stage, local_sem, send_sem, recv_sem):
        self.p, self.src, self.dst, self.stage = place, src, dst, stage
        self.l, self.s, self.v = local_sem, send_sem, recv_sem

    def _cross(self, q, k):
        half = self.src.at[q * ROWS : (q + 1) * ROWS, :]
        return send(half, self.dst.at[:, lanes(k)], self.s.at[q], self.v.at[0], {"row": 1 - self.p.r, "col": q})

    def _near(self):
        p = self.p
        half = self.src.at[rows_at((1 - p.c) * ROWS, ROWS), :]
        return send(half, self.dst.at[:, lanes(p.r)], self.s.at[2], self.v.at[1], p.core)

    def _load(self):
        return pltpu.make_async_copy(self.src.at[rows_at(self.p.c * ROWS, ROWS), :], self.stage, self.l.at[0])

    def _store(self):
        return pltpu.make_async_copy(self.stage, self.dst.at[:, lanes(self.p.r)], self.l.at[1])

    def start(self):
        p = self.p

        @pl.when(p.r != p.c)
        def _():
            self._cross(0, p.r).start()
            self._cross(1, p.r).start()

        @pl.when(p.r == p.c)
        def _():
            self._near().start()
            self._load().start()

    def store(self):
        @pl.when(self.p.r == self.p.c)
        def _():
            self._load().wait()
            self._store().start()

    def finish(self):
        p = self.p
        self._cross(0, 1 - p.r).wait_recv()

        @pl.when(p.r != p.c)
        def _():
            self._cross(0, p.r).wait_send()
            self._cross(1, p.r).wait_send()
            self._near().wait_recv()

        @pl.when(p.r == p.c)
        def _():
            self._near().wait_send()
            self._store().wait()


class FromRows:
    def __init__(self, place, src, dst, local_sem, send_sem, recv_sem):
        self.p, self.src, self.dst = place, src, dst
        self.l, self.s, self.v = local_sem, send_sem, recv_sem

    def _cross(self, q):
        p = self.p
        place = self.dst.at[q]
        return send(self.src.at[:, lanes(1 - p.r)], place, self.s.at[0], self.v.at[q], {"row": 1 - p.r, "col": p.r})

    def _near(self, q):
        p = self.p
        place = self.dst.at[q]
        return send(self.src.at[:, lanes(p.r)], place, self.s.at[1], self.v.at[2], p.core)

    def _local(self):
        p = self.p
        place = self.dst.at[p.c]
        return pltpu.make_async_copy(self.src.at[:, lanes(p.r)], place, self.l)

    def start(self):
        p = self.p
        self._cross(p.c).start()

        @pl.when(p.r != p.c)
        def _():
            self._near(p.c).start()

        @pl.when(p.r == p.c)
        def _():
            self._local().start()

    def finish(self):
        p = self.p
        self._cross(p.c).wait_send()

        @pl.when(p.r != p.c)
        def _():
            self._near(p.c).wait_send()
            self._cross(0).wait_recv()
            self._cross(1).wait_recv()

        @pl.when(p.r == p.c)
        def _():
            self._near(1 - p.c).wait_recv()
            self._local().wait()


class Sum:
    def __init__(self, place, far, mid, ybuf, zbuf, total, rows, s, v, first=0):
        self.p, self.far, self.mid, self.ybuf, self.zbuf, self.total = place, far, mid, ybuf, zbuf, total
        self.rows, self.s, self.v, self.first = rows, s, v, first

    def _sems(self, ch, n):
        i = self.first + ch * 8 + n
        return self.s.at[i], self.v.at[i]

    def _beside(self):
        return self.p.beside

    def _halves(self, ch, y):
        return rows_at(ch * self.rows + y * (self.rows // 2), self.rows // 2)

    def _piece(self, ch, z):
        return rows_at(ch * self.rows + self.p.y * (self.rows // 2) + z * (self.rows // 8), self.rows // 8)

    def _half(self, ch):
        return send(self.far.at[self._halves(ch, 1 - self.p.y), :], self.ybuf.at[ch], *self._sems(ch, 0), self._beside())

    def _quarter(self, ch, offset):
        other, device = self.p.four(offset)
        src = self.mid.at[ch, rows_at(other * (self.rows // 8), self.rows // 8), :]
        return send(src, self.zbuf.at[ch, offset - 1], *self._sems(ch, offset), device)

    def _along(self, ch, offset, z):
        _, device = self.p.four(offset)
        here = self.total.at[self._piece(ch, z), :]
        return send(here, here, *self._sems(ch, 3 + offset), device)

    def _back(self, ch, y):
        here = self.total.at[self._halves(ch, y), :]
        return send(here, here, *self._sems(ch, 7), self._beside())

    def half(self, ch):
        self._half(ch).start()

    def quarter(self, ch):
        self._half(ch).wait_recv()
        both = self.far[self._halves(ch, self.p.y), :].astype(F32) + self.ybuf[ch].astype(F32)
        self.mid[ch] = both.astype(BF)
        for offset in (1, 2, 3):
            self._quarter(ch, offset).start()

    def collect(self, ch):
        both = self.mid[ch, rows_at(self.p.z * (self.rows // 8), self.rows // 8), :].astype(F32)
        for offset in (1, 2, 3):
            self._quarter(ch, offset).wait_recv()
            both = both + self.zbuf[ch, offset - 1].astype(F32)
        return both.astype(BF)

    def along(self, ch, piece):
        self.total[self._piece(ch, self.p.z), :] = piece
        for offset in (1, 2, 3):
            self._along(ch, offset, self.p.z).start()

    def back(self, ch):
        for offset in (1, 2, 3):
            self._along(ch, offset, lax.rem(self.p.z + 4 - offset, 4)).wait_recv()
        self._back(ch, self.p.y).start()

    def finish_sum(self, ch):
        self._half(ch).wait_send()
        for offset in (1, 2, 3):
            self._quarter(ch, offset).wait_send()

    def finish_spread(self, ch):
        self._back(ch, 1 - self.p.y).wait_recv()
        for offset in (1, 2, 3):
            self._along(ch, offset, self.p.z).wait_send()
        self._back(ch, self.p.y).wait_send()

    @staticmethod
    def scratch(rows, chunks):
        return [
            pltpu.VMEM((chunks, rows // 2, HALF), BF),
            pltpu.VMEM((chunks, rows // 2, HALF), BF),
            pltpu.VMEM((chunks, 3, rows // 8, HALF), BF),
            pltpu.SemaphoreType.DMA((8 * chunks,)),
            pltpu.SemaphoreType.DMA((8 * chunks,)),
        ]


class Groups:
    def __init__(self, place, s, v):
        self.p, self.s, self.v = place, s, v

    def half(self, n, mine, ybuf):
        return send(mine.at[1 - self.p.y], ybuf, self.s.at[n], self.v.at[n], self.p.beside)

    def quarter(self, n, mid, zbuf, offset):
        other, device = self.p.four(offset)
        n = n + offset - 1
        return send(mid.at[other], zbuf.at[offset - 1], self.s.at[n], self.v.at[n], device)

    def cross(self, n, both, xbuf):
        return send(both.at[1 - self.p.r], xbuf, self.s.at[n], self.v.at[n], self.p.across)

    def along(self, n, half, offset, z):
        n = n + offset - 1
        return send(half.at[z], half.at[z], self.s.at[n], self.v.at[n], self.p.four(offset)[1])

    def back(self, n, half, other):
        return send(half, other, self.s.at[n], self.v.at[n], self.p.beside)

    def start_quarters(self, n, mid, zbuf):
        for offset in (1, 2, 3):
            self.quarter(n, mid, zbuf, offset).start()

    def collect(self, n, mid, zbuf, both):
        total = mid[self.p.z].astype(F32)
        for offset in (1, 2, 3):
            self.quarter(n, mid, zbuf, offset).wait_recv()
            total = total + zbuf[offset - 1].astype(F32)
        both[...] = total.astype(BF)

    def start_along(self, n, half, piece):
        half[self.p.z] = piece
        for offset in (1, 2, 3):
            self.along(n, half, offset, self.p.z).start()

    def await_along(self, n, half):
        for offset in (1, 2, 3):
            self.along(n, half, offset, lax.rem(self.p.z + 4 - offset, 4)).wait_recv()

    def sent(self, n, ref, kind):
        for offset in (1, 2, 3):
            kind(n, *ref, offset).wait_send()


def everyone(p):
    return [p.across, p.core, p.diagonal, p.beside] + [p.four(o)[1] for o in (1, 2, 3)]


def front_kernel(
    lens, tok_ref, wk_own, wv_own, wc_own, wq_own, wp_own, kern_ref, kb_ref, perm_ref,
    wdep_ref, bv_ref, bc_ref, bq_ref, bp_ref, wi_own, wd_own, wo_own, cot_own,
    kd_ref, kt_ref, vz_ref, q_ref, qs_ref, pt_ref, kp_ref, conv_ref, mix_ref, dep_ref, h_ref, wk_ref, bk_ref, spread_ref,
    seq_out, w5_out, wi_ref, wd_ref, cot_ref, wo_ref,
    own, seq_ref, w_ref, stage, first_key, hbuf, cbuf, lsem, ts, tr, gs, gr, cs, cr,
):
    i = pl.program_id(0)
    p = Place()
    r, c = p.r, p.c
    n = lens[r]
    proj = Gather(p, own, w_ref, middle_part, middle_block, 24, gs, gr, 0)
    inter = Gather(p, wi_own, wi_ref, rows_part, inter_block, 48, gs, gr, 7)
    dense = Gather(p, wd_own, wd_ref, middle_part, middle_block, 24, gs, gr, 14)
    cot_rows = ToRows(p, cot_own, cot_ref, stage, lsem, cs, cr)
    output = Gather(p, wo_own, wo_ref, rows_part, output_block, 96, gs, gr, 21)
    keep_output = pltpu.make_async_copy(wo_own, output_block(wo_ref, r, c, 0, D), lsem.at[7])
    keep_inter = pltpu.make_async_copy(wi_own, inter_block(wi_ref, r, c, 0, HALF), lsem.at[2])
    keep_dense = pltpu.make_async_copy(wd_own, middle_block(wd_ref, r, c, 0, 192), lsem.at[3])
    keep_own = pltpu.make_async_copy(tok_ref, seq_ref.at[PAD : PAD + LMAX, lanes(r)], lsem.at[4])
    keep_seq = pltpu.make_async_copy(seq_ref, seq_out, lsem.at[5])
    keep_w = pltpu.make_async_copy(w_ref, w5_out, lsem.at[6])

    def chunk(m, k):
        return seq_ref.at[PAD + m * 512 : PAD + (m + 1) * 512, lanes(k)]

    def cross(m, k):
        return send(tok_ref.at[m * 512 : (m + 1) * 512, :], chunk(m, k), ts.at[m], tr.at[m], {"row": 1 - r, "col": m // 2})

    def near(k):
        return send(tok_ref, seq_ref.at[PAD : PAD + LMAX, lanes(k)], ts.at[4], tr.at[4], p.core)

    def forward(m):
        return send(chunk(m, 1 - r), chunk(m, 1 - r), ts.at[5 + m], tr.at[5 + m], p.core)

    @pl.when(i == 0)
    def _():
        for j, ref in enumerate((wk_own, wv_own, wc_own, wq_own, wp_own)):
            own[j] = ref[...]
        seq_ref[0:PAD, :] = jnp.zeros((PAD, D), BF)
        seq_ref[PAD + LMAX :, :] = jnp.zeros((PAD, D), BF)
        meet(everyone(p))
        proj.start()
        inter._cross(r).start()
        dense._cross(r).start()
        output._cross(r).start()

        @pl.when(r != c)
        def _():
            for m in (0, 2, 1, 3):
                cross(m, r).start()

        @pl.when(r == c)
        def _():
            near(r).start()
            keep_own.start()

        cot_rows.start()
        inter._near(c).start()
        dense._near(c).start()
        output._near(c).start()
        keep_inter.start()
        keep_dense.start()
        keep_output.start()
        middle_block(w_ref, r, c, 0, 192)[...] = own[...]
        wk_ref[...] = nn(perm_ref[...], kern_ref[...]).astype(BF)
        bk_ref[...] = nt(perm_ref[...], jnp.broadcast_to(line(kb_ref), (128, 54)).astype(BF))
        row = lax.broadcasted_iota(jnp.int32, spread_ref.shape, 0)
        col = lax.broadcasted_iota(jnp.int32, spread_ref.shape, 1)
        head = row & 7
        hit = (head < 6) & ((col >> 6) == (row >> 3) * 6 + head)
        spread_ref[...] = jnp.where(hit, 1.0, 0.0).astype(BF)
        proj.relay()
        inter.relay()
        dense.relay()
        output.relay()
        proj.turn()
        for q in range(2):

            @pl.when(c == q)
            def _():
                for m in (2 * q, 2 * q + 1):
                    cross(m, 1 - r).wait_recv()
                    forward(m).start()

        proj.share()
        for q in range(2):

            @pl.when(c == q)
            def _():
                for m in (2 - 2 * q, 3 - 2 * q):
                    forward(m).wait_recv()
                for m in (2 * q, 2 * q + 1):
                    forward(m).wait_send()

        @pl.when(r != c)
        def _():
            for m in range(4):
                cross(m, r).wait_send()
            near(r).wait_recv()

        @pl.when(r == c)
        def _():
            near(r).wait_send()
            keep_own.wait()

        proj.finish()
        inter.turn()
        dense.turn()
        keep_seq.start()
        keep_w.start()

    @pl.when(i == 1)
    def _():
        output.turn()
        cot_rows.store()

    @pl.when(i == 2)
    def _():
        inter.share()
        dense.share()

    @pl.when(i == 3)
    def _():
        output.share()

    krows = kd_ref.shape[0]
    keep_key = row_ids(i * krows, krows) < n
    tok = seq_ref[rows_at(PAD + i * krows, krows), :]
    h = jnp.where(keep_key, tok.astype(F32), 0.0).astype(BF)
    k = nt(h, w_ref[0])
    v = nt(h, w_ref[1]) + line(bv_ref)

    @pl.when(i == 0)
    def _():
        first_key[...] = k[0:8]

    kd_ref[...] = jnp.where(keep_key, k, first_key[0:1]).astype(BF)
    kt_ref[...] = k.T.astype(BF)
    vz_ref[...] = jnp.where(keep_key, v, 0.0).astype(BF)

    rows = q_ref.shape[0]
    wide = rows + 32
    base = pl.multiple_of(i * rows, 16)
    start = pl.multiple_of(p.c * ROWS + i * rows, 16)
    ids = row_ids(start - 16, wide)
    keep = (ids >= 0) & (ids < n)
    hw = jnp.where(keep, seq_ref[pl.ds(start, wide), :].astype(F32), 0.0)
    put_tiles(hbuf, hw)
    wdep = wdep_ref[...].astype(F32)
    for t in range(D // 128):
        cols = slice(t * 128, (t + 1) * 128)

        def strip(s, carry):
            r0 = pl.multiple_of(s * 64, 64)
            depth = jnp.zeros((64, 128), F32)
            for j in range(KW):
                depth = depth + hbuf[t, pl.ds(r0 + 12 + j, 64), :] * wdep[j : j + 1, cols]
            dep_ref[pl.ds(r0, 64), cols] = depth.astype(BF)
            return carry

        lax.fori_loop(0, rows // 64, strip, 0)
    depth_low = dep_ref[...]
    hl = hw.astype(BF)
    h_ref[...] = hl[16 : 16 + rows]
    conv = jnp.where(keep, nt(hl, w_ref[2]) + line(bc_ref), 0.0)
    put_tiles(cbuf, conv)
    conv_ref[pl.ds(base, wide), :] = conv.astype(BF)
    q = nt(hl[16 : 16 + rows], w_ref[3]) + line(bq_ref)
    q_low = q.astype(BF)
    q_ref[...] = q_low
    qs_ref[...] = (q * (0.125 * LOG2E)).astype(BF)
    pt = nt(depth_low, w_ref[4]) + line(bp_ref)
    pt_ref[...] = pt.astype(BF)
    mixer = (pt * q_low.astype(F32)).astype(BF)
    logits = (nt(wk_ref[...], mixer) + bk_ref[:, 0:1]).reshape(KW, 8, rows)
    peak = jnp.max(logits, axis=0, keepdims=True)
    raised = jnp.exp(logits - peak)
    kp = (raised / jnp.sum(raised, axis=0, keepdims=True)).reshape(KW * 8, rows)
    kp_ref[...] = kp
    kpt = kp.T.astype(BF)
    for t in range(HALF // 128):
        mix = jnp.zeros((rows, 128), F32)
        for j in range(KW):
            wide_probs = nn(kpt, spread_ref[:, j * HALF + t * 128 : j * HALF + (t + 1) * 128])
            mix = mix + wide_probs * cbuf[t, 12 + j : 12 + j + rows, :]
        mix_ref[:, t * 128 : (t + 1) * 128] = mix.astype(BF)

    @pl.when(i == pl.num_programs(0) - 1)
    def _():
        inter.finish()
        dense.finish()
        cot_rows.finish()
        output.finish()
        keep_output.wait()
        keep_inter.wait()
        keep_dense.wait()
        keep_seq.wait()
        keep_w.wait()


def front(lens, tokens, weights, w_kernel, b_kernel, perm, wdep, bv, bc, bq, bp, w_inter, w_dense, w_output, cotangent):
    rows = 256
    keys = 512
    blk = pl.BlockSpec((rows, HALF), lambda i, lens: (i, 0))
    full = pl.BlockSpec((rows, D), lambda i, lens: (i, 0))
    half = jax.ShapeDtypeStruct((ROWS, HALF), BF)
    return pl.pallas_call(
        front_kernel,
        grid_spec=pltpu.PrefetchScalarGridSpec(
            num_scalar_prefetch=1,
            grid=(ROWS // rows,),
            in_specs=[HBM]
            + [once((192, HALF))] * 5
            + [once((54, HALF)), whole((54,)), once((72, 54)), once((KW, D))]
            + [whole((HALF,))] * 4
            + [once((HALF, D)), once((2, 192, HALF)), once((D, HALF)), HBM],
            out_specs=[
                pl.BlockSpec((keys, HALF), lambda i, lens: (i, 0)),
                pl.BlockSpec((HALF, keys), lambda i, lens: (0, i)),
                pl.BlockSpec((keys, HALF), lambda i, lens: (i, 0)),
                blk,
                blk,
                blk,
                pl.BlockSpec((72, rows), lambda i, lens: (0, i)),
                whole((ROWS + 32, HALF)),
                blk,
                full,
                full,
                whole((72, HALF)),
                whole((72, 128)),
                once((72, KW * HALF)),
            ]
            + [HBM] * 6,
            scratch_shapes=[
                pltpu.VMEM((5, 192, HALF), BF),
                pltpu.VMEM((LMAX + 2 * PAD, D), BF),
                pltpu.VMEM((5, HALF, D), BF),
                pltpu.VMEM((ROWS, HALF), BF),
                pltpu.VMEM((8, HALF), F32),
                pltpu.VMEM((D // 128, rows + 32, 128), F32),
                pltpu.VMEM((HALF // 128, rows + 32, 128), F32),
                pltpu.SemaphoreType.DMA((8,)),
                pltpu.SemaphoreType.DMA((9,)),
                pltpu.SemaphoreType.DMA((9,)),
                pltpu.SemaphoreType.DMA((28,)),
                pltpu.SemaphoreType.DMA((28,)),
                pltpu.SemaphoreType.DMA((3,)),
                pltpu.SemaphoreType.DMA((2,)),
            ],
        ),
        out_shape=[
            jax.ShapeDtypeStruct((LMAX, HALF), BF),
            jax.ShapeDtypeStruct((HALF, LMAX), BF),
            jax.ShapeDtypeStruct((LMAX, HALF), BF),
            half,
            half,
            half,
            jax.ShapeDtypeStruct((72, ROWS), F32),
            jax.ShapeDtypeStruct((ROWS + 32, HALF), BF),
            half,
            jax.ShapeDtypeStruct((ROWS, D), BF),
            jax.ShapeDtypeStruct((ROWS, D), BF),
            jax.ShapeDtypeStruct((72, HALF), BF),
            jax.ShapeDtypeStruct((72, 128), F32),
            jax.ShapeDtypeStruct((72, KW * HALF), BF),
            jax.ShapeDtypeStruct((LMAX + 2 * PAD, D), BF),
            jax.ShapeDtypeStruct((5, HALF, D), BF),
            jax.ShapeDtypeStruct((2, HALF, GW), BF),
            jax.ShapeDtypeStruct((2, HALF, D), BF),
            jax.ShapeDtypeStruct((ROWS, D), BF),
            jax.ShapeDtypeStruct((2, GW, HALF), BF),
        ],
        **comm_params("front", 2),
    )(
        lens, tokens, *weights, w_kernel, b_kernel, perm, wdep, bv, bc, bq, bp, w_inter, w_dense, w_output, cotangent
    )


def attend_kernel(lens, q_ref, k_ref, v_ref, ctx_ref, lse_ref):
    k = k_ref[...]
    ones = jnp.where(row_ids(0, LMAX) < length(lens), 1.0, 0.0)
    ve = jnp.concatenate([v_ref[...], jnp.broadcast_to(ones, (LMAX, 128)).astype(BF)], axis=1)
    rows = 256
    lane = lax.broadcasted_iota(jnp.int32, (rows, 128), 1)
    for u in range(ROWS // rows):
        part = slice(u * rows, (u + 1) * rows)
        outs = []
        for hh in range(2):
            q = jnp.where((lane < HD) == (hh == 0), q_ref[part, :], jnp.zeros((), BF))
            s = nt(q, k)
            peak = jnp.max(s, axis=1, keepdims=True)
            prob = jnp.exp2(s - peak).astype(BF)
            o = nn(prob, ve)
            outs.append(o[:, :128] / o[:, 128:])
            lse_ref[0, hh : hh + 1, part] = (peak + jnp.log2(o[:, 128:129])).T
        ctx_ref[part, :] = jnp.where(lane < HD, outs[0], outs[1]).astype(BF)


def attend(lens, qs, kd, vz):
    pair = lambda rows: pl.BlockSpec((rows, 128), lambda p, lens: (0, p))
    return pl.pallas_call(
        attend_kernel,
        grid_spec=pltpu.PrefetchScalarGridSpec(
            num_scalar_prefetch=1,
            grid=(3,),
            in_specs=[pair(ROWS), pair(LMAX), pair(LMAX)],
            out_specs=[pair(ROWS), pl.BlockSpec((1, 8, ROWS), lambda p, lens: (p, 0, 0))],
        ),
        out_shape=[
            jax.ShapeDtypeStruct((ROWS, HALF), BF),
            jax.ShapeDtypeStruct((3, 8, ROWS), F32),
        ],
        **params("attend"),
    )(lens, qs, kd, vz)


def back_kernel(
    lens, gcv_ref, conv_ref, kp_ref, q_ref, pt_ref, wk_ref, spread_ref, ones_ref,
    qs_ref, do_ref, k_ref, v_ref, kt_ref, lse_ref, del_ref, pay_all, pay_ref, hid_ref,
    seq_ref, wc_ref, wp_ref, gpre_ref, dep_ref, wdep_ref, smf_ref, gbi_ref,
    gqm_ref, dq_ref, dk_ref, dv_ref, ghm_ref, edge_ref, half_ref, piece_ref, piece_cp_ref, out_ref,
    acc, wbuf, tbuf, dka, dva, near, mine, ybuf, mid, zbuf, both, xbuf, half,
    gpad, dbuf, hwin, sbuf, agc, agp, gwk, gbk, sm, gdp, pcp, near_cp,
    out2, far2, y2, mid2, z2, out_cp, far_cp, y_cp, mid_cp, z_cp,
    ns, nr, s, v_sem, ls, hs, hr,
):
    step = pl.program_id(0)
    place = Place()
    n = lens[place.r]
    groups = Groups(place, s, v_sem)
    hidden = FromRows(place, hid_ref, out_ref, ls, hs, hr)

    def near_copy(k):
        rr = 1 - place.r if k % 2 == 0 else place.r
        src, dst = (pay_all, near) if k < 2 else (pcp, near_cp)
        return send(src.at[rr, 1 - place.c], dst.at[rr], ns.at[k], nr.at[k], place.core)

    def over(k, src, dst):
        return send(src, dst, s.at[k], v_sem.at[k], place.across)

    @pl.when(step == 0)
    def _():
        meet(everyone(place))
        near_copy(0).start()
        near_copy(1).start()
        hidden.start()
        for ref in (acc, agc, agp):
            clear(ref)
        for ref in (tbuf, gwk, gbk, sm, gdp):
            ref[...] = jnp.zeros_like(ref)
        gpad[0:32, :] = jnp.zeros((32, HALF), BF)
        gpad[32 + ROWS :, :] = jnp.zeros((32, HALF), BF)

    @pl.when(step == 2)
    def _():
        near_copy(0).wait()
        near_copy(1).wait()
        there = 1 - place.r
        out2[...] = (near[there, 2].astype(F32) + pay_ref[there, 0, 2].astype(F32)).astype(BF)
        over(18, out2, far2).start()
        for ch in range(2):
            for rr in range(2):
                total = near[rr, ch].astype(F32) + pay_ref[rr, 0, ch].astype(F32)
                mine[ch, :, :, rr] = total.astype(BF)
            groups.half(ch, mine.at[ch], ybuf.at[ch]).start()

    def settle(ch):
        groups.half(ch, mine.at[ch], ybuf.at[ch]).wait_recv()
        mid[ch] = (mine[ch, place.y].astype(F32) + ybuf[ch].astype(F32)).astype(BF)

    def merge(ch):
        groups.cross(16 + ch, both.at[ch], xbuf.at[ch]).wait_recv()
        return (both[ch, place.r].astype(F32) + xbuf[ch].astype(F32)).astype(BF)

    def quarters(ch):
        if ch < 2:
            return 4 + 3 * ch, mid.at[ch], zbuf.at[ch]
        return (10, mid2, z2) if ch == 2 else (13, mid_cp, z_cp)

    @pl.when(step == 6)
    def _():
        settle(0)
        groups.start_quarters(*quarters(0))
        near_copy(2).start()
        near_copy(3).start()

    @pl.when(step == 7)
    def _():
        near_copy(2).wait()
        near_copy(3).wait()
        there = 1 - place.r
        out_cp[...] = (near_cp[there].astype(F32) + pcp[there, place.c].astype(F32)).astype(BF)
        over(19, out_cp, far_cp).start()

    @pl.when(step == 8)
    def _():
        settle(1)
        groups.start_quarters(*quarters(1))
        groups.collect(*quarters(0), both.at[0])
        groups.cross(16, both.at[0], xbuf.at[0]).start()
        over(18, out2, far2).wait_recv()
        here = near[place.r, 2].astype(F32) + pay_ref[place.r, 0, 2].astype(F32)
        far2[...] = (here + far2[...].astype(F32)).astype(BF)
        groups.half(2, far2, y2).start()

    @pl.when(step == 9)
    def _():
        groups.start_along(20, half, merge(0))
        over(19, out_cp, far_cp).wait_recv()
        here = near_cp[place.r].astype(F32) + pcp[place.r, place.c].astype(F32)
        far_cp[...] = (here + far_cp[...].astype(F32)).astype(BF)
        groups.half(3, far_cp, y_cp).start()

    @pl.when(step == 10)
    def _():
        groups.collect(*quarters(1), both.at[1])
        groups.cross(17, both.at[1], xbuf.at[1]).start()
        groups.half(2, far2, y2).wait_recv()
        mid2[...] = (far2[place.y].astype(F32) + y2[...].astype(F32)).astype(BF)
        groups.start_quarters(*quarters(2))

    @pl.when(step == 11)
    def _():
        piece_ref[0] = merge(1)
        groups.half(3, far_cp, y_cp).wait_recv()
        mid_cp[...] = (far_cp[place.y].astype(F32) + y_cp[...].astype(F32)).astype(BF)
        groups.start_quarters(*quarters(3))

    @pl.when(step < 4)
    def _():
        rows = gcv_ref.shape[0]
        wide = rows + 32
        put_tiles(wbuf, conv_ref[pl.ds(pl.multiple_of(step * rows, 16), wide), :].astype(F32))
        kp = kp_ref[...]
        kpt = kp.T.astype(BF)
        gkps = [None] * KW
        there = pl.ds(pl.multiple_of(place.c * ROWS + step * rows, 16), wide)
        for t in range(HALF // 128):
            cols = slice(t * 128, (t + 1) * 128)
            gcv = gcv_ref[:, cols].astype(F32)
            total = jnp.zeros((wide, 128), F32)
            for j in range(KW):
                prod = (gcv * wbuf[t, 12 + j : 12 + j + rows, :]).astype(BF)
                part = nt(ones_ref[:, cols], prod)
                gkps[j] = part if t == 0 else gkps[j] + part
                tbuf[j % 3, 24 : 24 + rows, :] = nn(kpt, spread_ref[:, j * HALF + t * 128 : j * HALF + (t + 1) * 128]) * gcv
                total = total + tbuf[j % 3, 12 - j : 12 - j + wide, :]
            acc[there, cols] += total
        gkp = jnp.concatenate(gkps, axis=0).reshape(KW, 8, rows)
        kp3 = kp.reshape(KW, 8, rows)
        inner = jnp.sum(kp3 * gkp, axis=0, keepdims=True)
        gl = (kp3 * (gkp - inner)).reshape(KW * 8, rows)
        glt = gl.T.astype(BF)
        gbk[0:1, 0:72] += col_sum(glt.astype(F32))
        q = q_ref[...].astype(F32)
        pt = pt_ref[...].astype(F32)
        gwk[...] += nn(gl.astype(BF), (pt * q).astype(BF))
        gmix = nn(glt, wk_ref[...])
        gqm_ref[...] = (gmix * pt).astype(BF)
        gpad[rows_at(32 + step * rows, rows), :] = (gmix * q).astype(BF)

    def conv_grads(first, rows):
        keep = row_ids(first, rows) < n
        gco = jnp.where(keep, acc[rows_at(16 + first, rows), :], 0.0).astype(BF)
        tok = seq_ref[rows_at(PAD + first, rows), :]
        h = jnp.where(keep, tok.astype(F32), 0.0).astype(BF)
        agc[...] += nn(gco.T, h)
        sm[2:3, :] += col_sum(gco.astype(F32))
        return nn(gco, wc_ref[0])

    @pl.when(step == 4)
    def _():
        wdep = wdep_ref[...].astype(F32)
        at = pl.multiple_of((1 - place.c) * (ROWS + 16), 16)
        sbuf[...] = nn(gpad[pl.ds(at, 48), :], wp_ref[0])
        total = conv_grads(pl.multiple_of(ROWS - 16 * place.c, 16), 16)
        for j in range(KW):
            total = total + sbuf[20 - j : 36 - j, :] * wdep[j : j + 1, :]
        edge_ref[...] = total

    @pl.when((step == 4) | (step == 5))
    def _():
        m = step - 4
        rows = gpre_ref.shape[0]
        wide = rows + 32
        first = pl.multiple_of(place.c * ROWS + m * rows, 16)
        wdep = wdep_ref[...].astype(F32)
        win = gpad[rows_at(m * rows + 16, wide), :]
        gpt = win[16 : 16 + rows]
        sm[3:4, :] += col_sum(gpt.astype(F32))
        agp[...] += nn(gpt.T, dep_ref[...])
        put_tiles(dbuf, nn(win, wp_ref[0]))
        ids = row_ids(first - 16, wide)
        inside = (ids >= 0) & (ids < n)
        put_tiles(hwin, jnp.where(inside, seq_ref[pl.ds(first, wide), :].astype(F32), 0.0))
        ghm_ref[...] = (conv_grads(first, rows) + gpre_ref[...].astype(F32)).astype(BF)
        for t in range(D // 128):
            cols = slice(t * 128, (t + 1) * 128)

            def strip(k, sums):
                r0 = pl.multiple_of(k * 64, 64)
                gdep = dbuf[t, pl.ds(r0 + 16, 64), :]
                total = ghm_ref[pl.ds(r0, 64), cols].astype(F32)
                new = []
                for j in range(KW):
                    prod = gdep * hwin[t, pl.ds(r0 + 12 + j, 64), :]
                    new.append(sums[j] + jnp.sum(prod.reshape(8, 8, 128), axis=0))
                    total = total + dbuf[t, pl.ds(r0 + 20 - j, 64), :] * wdep[j : j + 1, cols]
                ghm_ref[pl.ds(r0, 64), cols] = total.astype(BF)
                return tuple(new)

            sums = lax.fori_loop(0, rows // 64, strip, (jnp.zeros((8, 128), F32),) * KW)
            for j in range(KW):
                gdp[j : j + 1, cols] += col_sum(sums[j])

    @pl.when(step == 5)
    def _():
        def put(r, c, first, value):
            pcp[r, c, first // 256, first // 64 % 4] = value.astype(BF)

        for r in range(2):
            for c in range(2):
                for k in range(3):
                    rows = slice(c * 192 + k * 64, c * 192 + (k + 1) * 64)
                    put(r, c, k * 64, agc[rows, r * HALF : (r + 1) * HALF])
                    put(r, c, 192 + k * 64, agp[rows, r * HALF : (r + 1) * HALF])
                put(r, c, 448, jnp.zeros((64, HALF), F32))
        zeros = lambda k: jnp.zeros((k, HALF), F32)
        put(0, 0, 384, gwk[0:64, :])
        bias = jnp.concatenate([gbk[...], jnp.zeros((8, 256), F32)], axis=1)
        put(0, 1, 384, jnp.concatenate([gwk[64:72, :], sm[...], bias, zeros(40)], axis=0))
        inter = jnp.concatenate([gbi_ref[:, k * HALF : (k + 1) * HALF] for k in range(8)], axis=0)
        put(1, 0, 384, jnp.concatenate([smf_ref[:, 0:HALF], smf_ref[:, HALF:D], inter, zeros(40)], axis=0))
        put(1, 1, 384, jnp.concatenate([gdp[:, 0:HALF], gdp[:, HALF:D], zeros(32)], axis=0))

    @pl.when(step >= 6)
    def _():
        i = lax.rem(step, 2)
        k = k_ref[...]
        v = v_ref[...]
        rows = qs_ref.shape[0]
        lane = lax.broadcasted_iota(jnp.int32, (rows, 128), 1)
        dk = dv = None
        for hh in range(2):
            head = (lane < HD) == (hh == 0)
            q = jnp.where(head, qs_ref[...], jnp.zeros((), BF))
            do = jnp.where(head, do_ref[...], jnp.zeros((), BF))
            p = jnp.exp2(nt(k, q) - lse_ref[0, hh : hh + 1, :])
            ds = (p * (nt(v, do) - del_ref[0, hh : hh + 1, :])).astype(BF)
            dv_one = nn(p.astype(BF), do)
            dk_one = nn(ds, q)
            dv = dv_one if dv is None else dv + dv_one
            dk = dk_one if dk is None else dk + dk_one
            dq_ref[hh * HD : (hh + 1) * HD, :] = (nn(kt_ref[hh * HD : (hh + 1) * HD, :], ds) * 0.125).astype(BF)

        @pl.when(i == 0)
        def _():
            dka[...] = dk
            dva[...] = dv

        @pl.when(i == 1)
        def _():
            keep = row_ids(0, LMAX) < n
            dk_ref[...] = jnp.where(keep, (dka[...] + dk) * LN2, 0.0).astype(BF)
            dv_ref[...] = jnp.where(keep, dva[...] + dv, 0.0).astype(BF)

    @pl.when(step == 11)
    def _():
        groups.collect(*quarters(2), piece_ref.at[1])
        groups.collect(*quarters(3), piece_cp_ref)
        groups.await_along(20, half)
        half_ref[...] = half[...]
        for ch in range(2):
            groups.half(ch, mine.at[ch], ybuf.at[ch]).wait_send()
            groups.cross(16 + ch, both.at[ch], xbuf.at[ch]).wait_send()
        groups.half(2, far2, y2).wait_send()
        groups.half(3, far_cp, y_cp).wait_send()
        over(18, out2, far2).wait_send()
        over(19, out_cp, far_cp).wait_send()
        for offset in (1, 2, 3):
            for ch in range(4):
                groups.quarter(*quarters(ch), offset).wait_send()
            groups.along(20, half, offset, place.z).wait_send()
        hidden.finish()


def back(
    lens, gcv, conv, kp, q, pt, wk72, spread, ones8, qs, do, kd, vz, kt, lse, delta, pay, hid,
    seq, w5, gpre, dep, wdep, smf, gbi,
):
    crows = 256
    rows = 512
    early = lambda s: jnp.minimum(s, 3)
    between = lambda s: jnp.minimum(jnp.maximum(s - 4, 0), 1)
    late = lambda s: jnp.maximum(s - 6, 0)
    which = lambda s: lax.div(late(s), 2)
    part = lambda s: lax.rem(late(s), 2)
    cblk = pl.BlockSpec((crows, HALF), lambda s, lens: (early(s), 0))
    mine = pl.BlockSpec((rows, 128), lambda s, lens: (part(s), which(s)))
    pair = pl.BlockSpec((LMAX, 128), lambda s, lens: (0, which(s)))
    stats = pl.BlockSpec((1, 8, rows), lambda s, lens: (which(s), 0, part(s)))
    full = pl.BlockSpec((rows, D), lambda s, lens: (between(s), 0))
    weight = lambda j: pl.BlockSpec((1, HALF, D), lambda s, lens: (j, 0, 0), pipeline_mode=pl.Buffered(1))
    block = (3, 2, 4, 80, HALF)
    pay = pay.reshape((2, 2) + block)
    mine_pay = pl.BlockSpec(
        (2, 1) + block, lambda s, lens: (0, half_index(), 0, 0, 0, 0, 0), pipeline_mode=pl.Buffered(1)
    )
    return pl.pallas_call(
        back_kernel,
        grid_spec=pltpu.PrefetchScalarGridSpec(
            num_scalar_prefetch=1,
            grid=(12,),
            in_specs=[
                cblk,
                once((ROWS + 32, HALF)),
                pl.BlockSpec((72, crows), lambda s, lens: (0, early(s))),
                cblk,
                cblk,
                once((72, HALF)),
                once((72, KW * HALF)),
                once((8, HALF)),
                mine,
                mine,
                pair,
                pair,
                pl.BlockSpec((128, LMAX), lambda s, lens: (which(s), 0)),
                stats,
                stats,
                HBM,
                mine_pay,
                once((ROWS, D)),
                once((LMAX + 2 * PAD, D)),
                weight(2),
                weight(4),
                full,
                full,
                once((KW, D)),
                once((8, D)),
                once((1, FF)),
            ],
            out_specs=[
                cblk,
                pl.BlockSpec((128, rows), lambda s, lens: (which(s), part(s))),
                pair,
                pair,
                full,
                once((16, D)),
                once((4, 80, HALF)),
                once((2, 80, HALF)),
                once((64, HALF)),
                HBM,
            ],
            scratch_shapes=[
                pltpu.VMEM((LMAX + 32, HALF), F32),
                pltpu.VMEM((HALF // 128, crows + 32, 128), F32),
                pltpu.VMEM((3, crows + 48, 128), F32),
                pltpu.VMEM((LMAX, 128), F32),
                pltpu.VMEM((LMAX, 128), F32),
                pltpu.VMEM((2,) + block, BF),
                pltpu.VMEM((2, 2, 4, 2, 80, HALF), BF),
                pltpu.VMEM((2, 4, 2, 80, HALF), BF),
                pltpu.VMEM((2, 4, 2, 80, HALF), BF),
                pltpu.VMEM((2, 3, 2, 80, HALF), BF),
                pltpu.VMEM((2, 2, 80, HALF), BF),
                pltpu.VMEM((2, 80, HALF), BF),
                pltpu.VMEM((4, 80, HALF), BF),
                pltpu.VMEM((ROWS + 64, HALF), BF),
                pltpu.VMEM((D // 128, rows + 32, 128), F32),
                pltpu.VMEM((D // 128, rows + 32, 128), F32),
                pltpu.VMEM((48, D), F32),
                pltpu.VMEM((HALF, D), F32),
                pltpu.VMEM((HALF, D), F32),
                pltpu.VMEM((72, HALF), F32),
                pltpu.VMEM((8, 128), F32),
                pltpu.VMEM((8, HALF), F32),
                pltpu.VMEM((16, D), F32),
                pltpu.VMEM((2, 2, 2, 4, 64, HALF), BF),
                pltpu.VMEM((2, 2, 4, 64, HALF), BF),
                pltpu.VMEM((2, 4, 80, HALF), BF),
                pltpu.VMEM((2, 4, 80, HALF), BF),
                pltpu.VMEM((4, 80, HALF), BF),
                pltpu.VMEM((4, 80, HALF), BF),
                pltpu.VMEM((3, 80, HALF), BF),
                pltpu.VMEM((2, 4, 64, HALF), BF),
                pltpu.VMEM((2, 4, 64, HALF), BF),
                pltpu.VMEM((4, 64, HALF), BF),
                pltpu.VMEM((4, 64, HALF), BF),
                pltpu.VMEM((3, 64, HALF), BF),
                pltpu.SemaphoreType.DMA((4,)),
                pltpu.SemaphoreType.DMA((4,)),
                pltpu.SemaphoreType.DMA((23,)),
                pltpu.SemaphoreType.DMA((23,)),
                pltpu.SemaphoreType.DMA,
                pltpu.SemaphoreType.DMA((2,)),
                pltpu.SemaphoreType.DMA((3,)),
            ],
        ),
        out_shape=[
            jax.ShapeDtypeStruct((ROWS, HALF), BF),
            jax.ShapeDtypeStruct((HALF, ROWS), BF),
            jax.ShapeDtypeStruct((LMAX, HALF), BF),
            jax.ShapeDtypeStruct((LMAX, HALF), BF),
            jax.ShapeDtypeStruct((ROWS, D), BF),
            jax.ShapeDtypeStruct((16, D), F32),
            jax.ShapeDtypeStruct((4, 80, HALF), BF),
            jax.ShapeDtypeStruct((2, 80, HALF), BF),
            jax.ShapeDtypeStruct((64, HALF), BF),
            jax.ShapeDtypeStruct((2, ROWS, HALF), BF),
        ],
        **comm_params("back", 4),
    )(
        lens, gcv, conv, kp, q, pt, wk72, spread, ones8, qs, do, kd, vz, kt, lse, delta, pay, pay, hid,
        seq, w5, w5, gpre, dep, wdep, smf, gbi,
    )


def norm_parts(x):
    xc = x - jnp.mean(x, axis=1, keepdims=True)
    inv = lax.rsqrt(jnp.mean(xc * xc, axis=1, keepdims=True) + EPS)
    return xc * inv, inv


def norm_back(up, normal, inv, gain):
    e = up * gain
    return inv * (e - jnp.mean(e, axis=1, keepdims=True) - normal * jnp.mean(e * normal, axis=1, keepdims=True))


def ffn_kernel(
    lens, ctx_ref, mix_ref, tok_ref, cot_ref, wd_ref, wi_ref, wo_ref, v0, v1, v2, v3, v4, v5, bi_ref, ones_ref,
    hid_ref, gpre_ref, gctx_ref, gcv_ref, del_ref, pay_ref, sm_ref, gbi_ref,
    act_s, gp_s, awd, awi, awo,
):
    i = pl.program_id(0)
    rows = ctx_ref.shape[0]
    keep = row_ids(half_index() * ROWS + i * rows, rows) < length(lens)

    @pl.when(i == 0)
    def _():
        clear(awd)
        for g in range(2):
            clear(awi.at[g])
            clear(awo.at[g])
        sm_ref[...] = jnp.zeros_like(sm_ref)
        gbi_ref[...] = jnp.zeros_like(gbi_ref)

    vectors = [line(ref) for ref in (v0, v1, v2, v3, v4, v5)]
    vec = lambda k: vectors[k]
    inter_bias = line(bi_ref)
    h = tok_ref[...].astype(F32)
    ctx = ctx_ref[...]
    mixed = jnp.concatenate([ctx, mix_ref[...]], axis=1)
    n1, inv1 = norm_parts(nn(mixed, wd_ref[...]) + vec(0) + h)
    f1 = n1 * vec(1) + vec(2)
    fl = f1.astype(BF)
    chunk = 512
    outs = []
    for g in range(2):
        fg = fl[:, g * HALF : (g + 1) * HALF]
        for ch in range(GW // chunk):
            cols = slice(ch * chunk, (ch + 1) * chunk)
            put = slice(g * GW + ch * chunk, g * GW + (ch + 1) * chunk)
            x = nn(fg, wi_ref[g, :, cols]) + inter_bias[:, put]
            phi = 0.5 + 0.5 * lax.erf(x * 0.7071067811865476)
            act_s[:, put] = (x * phi).astype(BF)
            gp_s[:, put] = phi + x * jnp.exp2(x * x * (-0.5 * LOG2E)) * 0.3989422804014327
        outs.append(nn(act_s[:, g * GW : (g + 1) * GW], wo_ref[g]))
    n2, inv2 = norm_parts(jnp.concatenate(outs, axis=1) + vec(3) + f1)
    hid_ref[...] = (n2 * vec(4) + vec(5)).astype(BF)
    u = jnp.where(keep, cot_ref[...].astype(F32), 0.0)
    gp2 = norm_back(u, n2, inv2, vec(4))
    go = gp2.astype(BF)
    got = go.T
    flt = fl.T
    gfs = []
    for g in range(2):
        sel = slice(g * HALF, (g + 1) * HALF)
        gf = gp2[:, sel]
        for ch in range(GW // chunk):
            cols = slice(ch * chunk, (ch + 1) * chunk)
            put = slice(g * GW + ch * chunk, g * GW + (ch + 1) * chunk)
            gi = (gp_s[:, put] * nt(go[:, sel], wo_ref[g, cols, :])).astype(BF)
            gbi_ref[0:1, put] += col_sum(gi.astype(F32))
            awo[g, :, cols] += nn(got[sel], act_s[:, put])
            awi[g, :, cols] += nn(flt[sel], gi)
            gf = gf + nt(gi, wi_ref[g, :, cols])
        gfs.append(gf)
    gf = jnp.concatenate(gfs, axis=1)
    gpre = norm_back(gf, n1, inv1, vec(1))
    gd = gpre.astype(BF)
    gpre_ref[...] = gd
    sm_ref[0:1, :] += col_sum(go.astype(F32))
    sm_ref[1:2, :] += col_sum(u * n2)
    sm_ref[2:3, :] += col_sum(u)
    sm_ref[3:4, :] += col_sum(gd.astype(F32))
    sm_ref[4:5, :] += col_sum(gf * n1)
    sm_ref[5:6, :] += col_sum(gf)
    awd[...] += nn(mixed.T, gd)
    gm = nt(gd, wd_ref[...])
    gctx = gm[:, :HALF].astype(BF)
    gctx_ref[...] = gctx
    gcv_ref[...] = gm[:, HALF:].astype(BF)
    prod = (gctx.astype(F32) * ctx.astype(F32)).astype(BF)
    del_ref[...] = nt(ones_ref[...], prod).reshape(3, 8, rows)

    @pl.when(i == pl.num_programs(0) - 1)
    def _():
        for r in range(2):
            for c in range(2):
                pay_ref[r, c, 0:HALF, :] = awi[r, :, c * D : c * D + HALF].astype(BF)
                pay_ref[r, c, HALF:D, :] = awi[r, :, c * D + HALF : (c + 1) * D].astype(BF)
                pay_ref[r, c, D : 2 * D, :] = awo[r, :, c * D : (c + 1) * D].T.astype(BF)
                for part in range(2):
                    piece = awd[part * HALF + c * 192 : part * HALF + (c + 1) * 192, r * HALF : (r + 1) * HALF]
                    pay_ref[r, c, 2 * D + part * 192 : 2 * D + (part + 1) * 192, :] = piece.astype(BF)


def ffn(lens, ctx, mix, tok, cot, wd, wi, wo, vectors, bi, ones24):
    rows = 256
    blk = lambda w: pl.BlockSpec((rows, w), lambda i, lens: (i, 0))
    return pl.pallas_call(
        ffn_kernel,
        grid_spec=pltpu.PrefetchScalarGridSpec(
            num_scalar_prefetch=1,
            grid=(ROWS // rows,),
            in_specs=[
                blk(HALF),
                blk(HALF),
                blk(D),
                blk(D),
                whole((D, D)),
                whole((2, HALF, GW)),
                whole((2, GW, HALF)),
                *[whole((D,))] * 6,
                whole((FF,)),
                whole((24, HALF)),
            ],
            out_specs=[
                blk(D),
                blk(D),
                blk(HALF),
                blk(HALF),
                pl.BlockSpec((3, 8, rows), lambda i, lens: (0, 0, i)),
                whole((2, 2, FFN_ROWS, HALF)),
                whole((8, D)),
                whole((1, FF)),
            ],
            scratch_shapes=[
                pltpu.VMEM((rows, FF), BF),
                pltpu.VMEM((rows, FF), F32),
                pltpu.VMEM((D, D), F32),
                pltpu.VMEM((2, HALF, GW), F32),
                pltpu.VMEM((2, HALF, GW), F32),
            ],
        ),
        out_shape=[
            jax.ShapeDtypeStruct((ROWS, D), BF),
            jax.ShapeDtypeStruct((ROWS, D), BF),
            jax.ShapeDtypeStruct((ROWS, HALF), BF),
            jax.ShapeDtypeStruct((ROWS, HALF), BF),
            jax.ShapeDtypeStruct((3, 8, ROWS), F32),
            jax.ShapeDtypeStruct((2, 2, FFN_ROWS, HALF), BF),
            jax.ShapeDtypeStruct((8, D), F32),
            jax.ShapeDtypeStruct((1, FF), F32),
        ],
        **params("ffn"),
    )(lens, ctx, mix, tok, cot, wd, wi, wo, *vectors, bi, ones24)


def tail_kernel(
    lens, seq_ref, dk_ref, dv_ref, dq_ref, gqm_ref, ghm_ref, edge_ref, w_ref, half0, pieces, piece_cp,
    big_ref, cp_ref, sum_ref, small_ref, ght_ref,
    agw, accb, sm, tsend, trecv, gho, halves, other, half_cp, last_cp,
    pay, small, total_sum, near, far, out, mid, ybuf, zsum, s, v, ns, nr, cs, cr, gs, gr, own, es, er, ls, hs, hr,
):
    step = pl.program_id(0)
    i = lax.rem(step, 4)
    p = Place()
    r, c = p.r, p.c
    rows = dk_ref.shape[0]
    b = lax.rem((1 - c) * 2 + i, 4)
    n = lens[r]
    groups = Groups(p, gs, gr)
    chunks = 5
    crows = PROJ_ROWS // chunks
    summed = Sum(p, far, mid, ybuf, zsum, total_sum, crows, s, v)
    places = [FromRows(p, gho.at[k], ght_ref.at[k], ls.at[k], hs.at[k], hr.at[k]) for k in range(2)]

    def theirs(k):
        return send(tsend.at[k], trecv.at[k], es.at[k], er.at[k], p.core)

    def part(ch):
        return slice(ch * crows, (ch + 1) * crows)

    def beside(k, ch):
        rr = 1 - r if k == 0 else r
        at = k * chunks + ch
        return send(pay.at[rr, 1 - c, part(ch), :], near.at[rr, part(ch), :], ns.at[at], nr.at[at], p.core)

    def cross(ch):
        return send(out.at[part(ch), :], far.at[part(ch), :], cs.at[ch], cr.at[ch], p.across)

    def arrive(ch):
        beside(1, ch).wait_recv()
        cross(ch).wait_recv()
        total = near[r, part(ch), :].astype(F32) + pay[r, c, part(ch), :].astype(F32)
        far[part(ch), :] = (total + far[part(ch), :].astype(F32)).astype(BF)
        summed.half(ch)

    stages = [
        arrive,
        summed.quarter,
        lambda ch: summed.along(ch, summed.collect(ch)),
        summed.back,
        summed.finish_spread,
    ]

    def tick(t):
        for k, stage in enumerate(stages):
            if 0 <= t - k < chunks:
                stage(t - k)

    halfs = [half0, halves.at[0], halves.at[1], half_cp]
    others = [other.at[0], other.at[1], other.at[2], last_cp]

    def back(k, z):
        return groups.back(9 + 4 * k + z, halfs[k].at[z], others[k].at[z])

    @pl.when(step == 0)
    def _():
        meet(everyone(p))
        groups.start_along(0, halves.at[0], pieces[0])
        groups.start_along(3, halves.at[1], pieces[1])
        groups.start_along(6, half_cp, piece_cp[...])
        for z in range(4):
            back(0, z).start()
        for j in range(3):
            clear(agw.at[j])
        sm[...] = jnp.zeros_like(sm)

    @pl.when(step == 4)
    def _():
        for ch in range(chunks):
            beside(0, ch).wait_recv()
            total = near[1 - r, part(ch), :].astype(F32) + pay[1 - r, c, part(ch), :].astype(F32)
            out[part(ch), :] = total.astype(BF)
            cross(ch).start()

    @pl.when(step == 5)
    def _():
        groups.await_along(0, halves.at[0])
        back(1, 0).start()
        back(1, 1).start()

    @pl.when(step == 6)
    def _():
        tick(0)
        back(1, 2).start()
        back(1, 3).start()

    @pl.when(step == 7)
    def _():
        tick(1)

    keep = row_ids(b * rows, rows) < n

    def query_grad():
        return (dq_ref[...].astype(F32) + gqm_ref[...].astype(F32).T).astype(BF)

    @pl.when(step < 4)
    def _():
        tok = seq_ref[rows_at(PAD + b * rows, rows), :]
        h = jnp.where(keep, tok.astype(F32), 0.0).astype(BF)
        agw[0] += nn(dk_ref[...].T, h)
        agw[1] += nn(dv_ref[...].T, h)
        sm[1:2, :] += col_sum(dv_ref[...].astype(F32))

        @pl.when(step >= 2)
        def _():
            gqt = query_grad()
            sm[0:1, :] += col_sum(gqt.T.astype(F32))
            agw[2] += nn(gqt, h)

    @pl.when(step == 3)
    def _():
        for rr in range(2):
            for cc in range(2):
                for j in range(3):
                    piece = agw[j, cc * 192 : (cc + 1) * 192, rr * HALF : (rr + 1) * HALF]
                    pay[rr, cc, j * 192 : (j + 1) * 192, :] = piece.astype(BF)
                pay[rr, cc, 576:, :] = jnp.zeros((64, HALF), BF)
        pay[0, 0, 576:, :] = jnp.concatenate([sm[...], jnp.zeros((56, HALF), F32)], axis=0).astype(BF)
        for ch in range(chunks):
            for k in range(2):
                beside(k, ch).start()

    @pl.when(step >= 4)
    def _():
        accb[...] = nn(dk_ref[...], w_ref[0]) + nn(dv_ref[...], w_ref[1])

        @pl.when(step >= 6)
        def _():
            accb[...] += nn(query_grad().T, w_ref[3]) + ghm_ref[...].astype(F32)

    for k in range(2):

        @pl.when((step == 4 + k) & (c == k))
        def _():
            at = slice(0, 16) if k == 0 else slice(rows - 16, rows)
            accb[at, :] += edge_ref[...]

        @pl.when(step == 4 + k)
        def _():
            tsend[k] = jnp.where(keep, accb[...], 0.0).astype(BF)
            theirs(k).start()

        @pl.when(step == 6 + k)
        def _():
            theirs(k).wait_recv()
            gho[k] = jnp.where(keep, accb[...] + trecv[k].astype(F32), 0.0).astype(BF)
            places[k].start()

    @pl.when(step == 7)
    def _():
        tick(2)
        groups.await_along(3, halves.at[1])
        back(2, 0).start()
        back(2, 1).start()
        tick(3)
        back(2, 2).start()
        back(2, 3).start()
        tick(4)
        groups.await_along(6, half_cp)
        back(3, 0).start()
        back(3, 1).start()
        tick(5)
        back(3, 2).start()
        back(3, 3).start()
        tick(6)
        for ch in range(2):
            for z in range(4):
                back(ch, z).wait_recv()
        big_ref[0, p.y] = half0[...]
        big_ref[0, 1 - p.y] = other[0]
        big_ref[1, p.y] = halves[0]
        big_ref[1, 1 - p.y] = other[1]
        tick(7)
        for z in range(4):
            back(3, z).wait_recv()
        cp_ref[p.y] = half_cp[...]
        cp_ref[1 - p.y] = last_cp[...]
        own[0] = cp_ref[1, 2]
        tick(8)
        own[1] = total_sum[576:PROJ_ROWS, :]
        mine = small.at[r * 2 + c]
        moves = [
            send(own, mine, es.at[2 + k], er.at[2 + k], device)
            for k, device in enumerate((p.across, p.core, p.diagonal))
        ]
        for move in moves:
            move.start()
        small[r * 2 + c] = own[...]
        sum_ref[...] = total_sum[...]
        for z in range(4):
            back(2, z).wait_recv()
        big_ref[2, p.y] = halves[1]
        big_ref[2, 1 - p.y] = other[2]
        for ch in range(chunks):
            summed.finish_sum(ch)
            cross(ch).wait_send()
            for k in range(2):
                beside(k, ch).wait_send()
        for k in range(4):
            for z in range(4):
                back(k, z).wait_send()
        for offset in (1, 2, 3):
            groups.along(0, halves.at[0], offset, p.z).wait_send()
            groups.along(3, halves.at[1], offset, p.z).wait_send()
            groups.along(6, half_cp, offset, p.z).wait_send()
        theirs(0).wait_send()
        theirs(1).wait_send()
        for k, (rr, cc) in enumerate(((1 - r, c), (r, 1 - c), (1 - r, 1 - c))):
            send(own, small.at[rr * 2 + cc], es.at[2 + k], er.at[2 + k], p.core).wait_recv()
        for move in moves:
            move.wait_send()
        small_ref[...] = small[...]
        places[0].finish()
        places[1].finish()


def tail(lens, seq_tok, dk, dv, dq, gqm, ghm, edge, w5, half0, pieces, piece_cp):
    rows = 512
    mine = lambda s: jnp.maximum(lax.rem(s, 4) - 2, 0)
    seq = pl.BlockSpec((rows, HALF), lambda s, lens: (lax.rem((1 - half_index()) * 2 + s, 4), 0))
    own = lambda w: pl.BlockSpec((rows, w), lambda s, lens: (mine(s), 0))
    crows = PROJ_ROWS // 5
    return pl.pallas_call(
        tail_kernel,
        grid_spec=pltpu.PrefetchScalarGridSpec(
            num_scalar_prefetch=1,
            grid=(8,),
            in_specs=[
                once((LMAX + 2 * PAD, D)),
                seq,
                seq,
                pl.BlockSpec((HALF, rows), lambda s, lens: (0, mine(s))),
                own(HALF),
                own(D),
                once((16, D)),
                once((5, HALF, D)),
                once((4, 80, HALF)),
                once((2, 80, HALF)),
                once((64, HALF)),
            ],
            out_specs=[
                once((3, 2, 4, 80, HALF)),
                once((2, 4, 64, HALF)),
                once((PROJ_ROWS, HALF)),
                once((4, 2, 64, HALF)),
                HBM,
            ],
            scratch_shapes=[
                pltpu.VMEM((3, HALF, D), F32),
                pltpu.VMEM((rows, D), F32),
                pltpu.VMEM((8, HALF), F32),
                pltpu.VMEM((2, rows, D), BF),
                pltpu.VMEM((2, rows, D), BF),
                pltpu.VMEM((2, rows, D), BF),
                pltpu.VMEM((2, 4, 80, HALF), BF),
                pltpu.VMEM((3, 4, 80, HALF), BF),
                pltpu.VMEM((4, 64, HALF), BF),
                pltpu.VMEM((4, 64, HALF), BF),
                pltpu.VMEM((2, 2, PROJ_ROWS, HALF), BF),
                pltpu.VMEM((4, 2, 64, HALF), BF),
                pltpu.VMEM((PROJ_ROWS, HALF), BF),
                pltpu.VMEM((2, PROJ_ROWS, HALF), BF),
                pltpu.VMEM((PROJ_ROWS, HALF), BF),
                pltpu.VMEM((PROJ_ROWS, HALF), BF),
                *Sum.scratch(crows, 5),
                pltpu.SemaphoreType.DMA((10,)),
                pltpu.SemaphoreType.DMA((10,)),
                pltpu.SemaphoreType.DMA((5,)),
                pltpu.SemaphoreType.DMA((5,)),
                pltpu.SemaphoreType.DMA((25,)),
                pltpu.SemaphoreType.DMA((25,)),
                pltpu.VMEM((2, 64, HALF), BF),
                pltpu.SemaphoreType.DMA((5,)),
                pltpu.SemaphoreType.DMA((5,)),
                pltpu.SemaphoreType.DMA((2,)),
                pltpu.SemaphoreType.DMA((2, 2)),
                pltpu.SemaphoreType.DMA((2, 3)),
            ],
        ),
        out_shape=[
            jax.ShapeDtypeStruct((3, 2, 4, 80, HALF), BF),
            jax.ShapeDtypeStruct((2, 4, 64, HALF), BF),
            jax.ShapeDtypeStruct((PROJ_ROWS, HALF), BF),
            jax.ShapeDtypeStruct((4, 2, 64, HALF), BF),
            jax.ShapeDtypeStruct((2, 2, rows, HALF), BF),
        ],
        **comm_params("tail", 6),
    )(lens, seq_tok, dk, dv, dq, gqm, ghm, edge, w5, half0, pieces, piece_cp)


def outputs_kernel(
    ght, hid, t0, t1, t2, t3, t4, big_i0, big_i1, big_o, big_d, small, perm_ref,
    hid_ref, gt_ref, gk_ref, gv_ref, gc_ref, gq_ref, gp_ref, gi_ref, go_ref, gd_ref,
    gdep_ref, gbq_ref, gbv_ref, gbc_ref, gbp_ref, gwk_ref, gbk_ref,
    gbd_ref, gg1_ref, gb1_ref, gbi_ref, gbo_ref, gg2_ref, gb2_ref,
):
    i = pl.program_id(0)
    hid_ref[...] = hid[...]
    gt_ref[...] = ght[0, 0].astype(F32)

    for src, ref in ((t0, gk_ref), (t1, gv_ref), (t2, gq_ref), (t3, gc_ref), (t4, gp_ref), (big_o, go_ref), (big_d, gd_ref)):
        ref[...] = src[...].astype(F32)
    gi_ref[:, 0:HALF] = big_i0[...].astype(F32)
    gi_ref[:, HALF:D] = big_i1[...].astype(F32)

    @pl.when(i == 0)
    def _():
        tail = small[1, 0].astype(F32)
        norms = small[2, 0].astype(F32)
        depth = small[3, 0].astype(F32)
        late = small[0, 1].astype(F32)
        kernel_grad = jnp.concatenate([small[0, 0].astype(F32), tail[0:8]], axis=0).astype(BF)
        gwk_ref[...] = nn(perm_ref[...], kernel_grad)
        bias = nt(tail[16:24, 0:72].astype(BF), perm_ref[...])
        gbk_ref[...] = bias[0:1, :].reshape(54)
        for k, ref in enumerate((gbq_ref, gbv_ref)):
            ref[...] = late[k : k + 1, :].reshape(HALF)
        for k, ref in enumerate((gbc_ref, gbp_ref)):
            ref[...] = tail[10 + k : 11 + k, :].reshape(HALF)
        for k, ref in enumerate((gbo_ref, gg2_ref, gb2_ref, gbd_ref, gg1_ref, gb1_ref)):
            ref[...] = jnp.concatenate([norms[k : k + 1, :], norms[8 + k : 9 + k, :]], axis=1).reshape(D)
        gbi_ref[...] = jnp.concatenate([norms[16 + k : 17 + k, :] for k in range(8)], axis=1).reshape(FF)
        gdep_ref[:, 0:HALF] = depth[0:KW, :]
        gdep_ref[:, HALF:D] = depth[16 : 16 + KW, :]


def outputs(ght, hid, total, cp, big, small, perm):
    rows = 512
    at = lambda n, first: pl.BlockSpec((n, HALF), lambda i: (first + i, 0))
    blk = at(rows, 0)
    chunk = pl.BlockSpec((1, 1, rows, HALF), lambda i: (lax.rem(i, 2), lax.div(i, 2), 0, 0))
    shapes = [(KW, D)] + [(HALF,)] * 4 + [(54, HALF), (54,)] + [(D,)] * 3 + [(FF,)] + [(D,)] * 3
    main = [(192, HALF)] * 5 + [(HALF, D), (D, HALF), (HALF, HALF)]
    return pl.pallas_call(
        outputs_kernel,
        grid=(4,),
        in_specs=[chunk, blk]
        + [at(48, 4 * j) for j in (0, 1, 2, 0, 1)]
        + [at(96, 0), at(96, 4), at(192, 4), at(96, 16), whole((4, 2, 64, HALF)), whole((54, 72))],
        out_specs=[blk, blk]
        + [at(48, 0)] * 5
        + [pl.BlockSpec((96, D), lambda i: (i, 0)), at(192, 0), at(96, 0)]
        + [whole(shape) for shape in shapes],
        out_shape=[jax.ShapeDtypeStruct((LMAX, HALF), BF), jax.ShapeDtypeStruct((LMAX, HALF), F32)]
        + [jax.ShapeDtypeStruct(shape, F32) for shape in main + shapes],
        **params("outputs"),
    )(ght, hid, total, total, total, cp, cp, big, big, big, big, small, perm)


def constants():
    ones8 = np.zeros((8, HALF), np.float32)
    ones24 = np.zeros((24, HALF), np.float32)
    perm = np.zeros((72, 54), np.float32)
    for head in range(6):
        cols = slice(head * HD, (head + 1) * HD)
        ones8[head, cols] = 1
        ones24[head // 2 * 8 + head % 2, cols] = 1
        for j in range(KW):
            perm[j * 8 + head, head * KW + j] = 1
    return [jnp.asarray(a, BF) for a in (ones8, ones24, perm)]


def per_device(
    groups, tokens, cotangent, seq_lengths, w_query, w_key, w_value, w_convout, w_point, w_depth,
    b_query, b_value, b_convout, b_point, w_kernel, b_kernel, w_dense, b_dense, gain_one, bias_one,
    w_inter, b_inter, w_output, b_output, gain_two, bias_two,
):
    lens = seq_lengths
    ones8, ones24, perm = constants()
    wdep = w_depth.T

    kd, kt, vz, q, qs, pt, kp, conv, mix, dep, hown, wk72, bk72, spread, seq, w5, wi, wd, cot, wo = front(
        lens, tokens, (w_key.T, w_value.T, w_convout.T, w_query.T, w_point.T), w_kernel.T, b_kernel, perm,
        wdep, b_value, b_convout, b_query, b_point,
        w_inter[0], w_dense.reshape(2, 192, HALF), w_output[0], cotangent,
    )
    ctx, lse = attend(lens, qs, kd, vz)
    vectors = (b_dense, gain_one, bias_one, b_output, gain_two, bias_two)
    hid, gpre, gctx, gcv, delta, payf, smf, gbi = ffn(
        lens, ctx, mix, hown, cot, wd.reshape(D, D), wi, wo, vectors, b_inter, ones24
    )
    gqm, dq, dk, dv, ghm, edge, half0, pieces, piece_cp, hid = back(
        lens, gcv, conv, kp, q, pt, wk72, spread, ones8, qs, gctx, kd, vz, kt, lse, delta, payf, hid,
        seq, w5, gpre, dep, wdep, smf, gbi,
    )
    big, cp, total, small, ght = tail(lens, seq, dk, dv, dq, gqm, ghm, edge, w5, half0, pieces, piece_cp)
    big = big.reshape(FFN_ROWS, HALF)
    cp = cp.reshape(512, HALF)
    if groups > 8:
        sums = lax.psum(tuple(x.astype(F32) * 0.125 for x in (total, cp, big, small)), "dp")
        total, cp, big, small = (x.astype(BF) for x in sums)
    (
        hidden_out, gt, gk, gv, gc, gq, gp, gi, go, gd, gdep, gbq, gbv, gbc, gbp, gwk, gbk, gbd, gg1, gb1, gbi, gbo, gg2, gb2,
    ) = outputs(ght, hid.reshape(LMAX, HALF), total, cp, big, small, perm.T)
    return (
        hidden_out, gt, gq.T, gk.T, gv.T, gc.T, gp.T, gdep.T, gbq, gbv, gbc, gbp, gwk.T, gbk, gd, gbd, gg1, gb1,
        gi[None], gbi, go[None], gbo, gg2, gb2,
    )


def solution(mesh):
    act = P(("dp", "col"), "row")
    rep = P()
    proj = P("row", "col")
    in_specs = (
        act, act, P("dp"), proj, proj, proj, proj, proj, rep, rep, rep, rep, rep, rep, rep, P("col", "row"),
        rep, rep, rep, P("row", None, "col"), rep, P("row", "col", None), rep, rep, rep,
    )
    out_specs = (
        act, act, proj, proj, proj, proj, proj, rep, rep, rep, rep, rep, rep, rep, P("col", "row"),
        rep, rep, rep, P("row", None, "col"), rep, P("row", "col", None), rep, rep, rep,
    )
    return jax.shard_map(
        functools.partial(per_device, mesh.shape["dp"]), mesh=mesh, in_specs=in_specs, out_specs=out_specs, check_vma=False)
```

```python
import functools

import jax
import jax.numpy as jnp
import numpy as np
from jax import lax
from jax.experimental import pallas as pl
from jax.experimental.pallas import tpu as pltpu
from jax.sharding import PartitionSpec as P

D = 768
HALF = 384
HD = 64
KW = 9
FF = 3072
GW = 1536
LMAX = 2048
ROWS = 1024
EPS = 1e-12
LOG2E = 1.4426950408889634
LN2 = 0.6931471805599453
BF = jnp.bfloat16
F32 = jnp.float32
VMEM_BYTES = 63 * 1024 * 1024
PAD = 16
FFN_ROWS = 1920
FFN_CHUNK = 640
PROJ_ROWS = 640
MESH = pl.DeviceIdType.MESH
HBM = pl.BlockSpec(memory_space=pl.ANY)
VMEM = pl.BlockSpec(memory_space=pltpu.VMEM)


def nn(a, b):
    return lax.dot_general(a, b, (((1,), (0,)), ((), ())), preferred_element_type=F32)


def nt(a, b):
    return lax.dot_general(a, b, (((1,), (1,)), ((), ())), preferred_element_type=F32)


def col_sum(x):
    return jnp.sum(x, axis=0, keepdims=True)


def row_ids(start, rows):
    return start + lax.broadcasted_iota(jnp.int32, (rows, 1), 0)


def whole(shape):
    return pl.BlockSpec(shape, lambda *_: (0,) * len(shape))


def once(shape):
    return pl.BlockSpec(shape, lambda *_: (0,) * len(shape), pipeline_mode=pl.Buffered(1))


def half_index():
    return lax.axis_index("col")


def length(lens):
    return lens[lax.axis_index("row")]


def line(ref):
    return ref[...].astype(F32).reshape(1, ref.shape[0])


def clear(ref, step=32):
    def body(k, carry):
        ref[pl.ds(pl.multiple_of(k * step, step), step), :] = jnp.zeros((step, ref.shape[1]), ref.dtype)
        return carry

    lax.fori_loop(0, ref.shape[0] // step, body, 0)


def put_tiles(buf, value, first=0):
    for t in range(value.shape[1] // 128):
        buf[t, first : first + value.shape[0], :] = value[:, t * 128 : (t + 1) * 128]


def params(name):
    return dict(
        name=name,
        compiler_params=pltpu.CompilerParams(vmem_limit_bytes=VMEM_BYTES),
    )


def lanes(k, width=HALF):
    return pl.ds(pl.multiple_of(k * width, 128), width)


def rows_at(start, count, step=16):
    return pl.ds(pl.multiple_of(start, step), count)


def send(src, dst, send_sem, recv_sem, device):
    return pltpu.make_async_remote_copy(
        src_ref=src, dst_ref=dst, send_sem=send_sem, recv_sem=recv_sem, device_id=device, device_id_type=MESH
    )


class Place:
    def __init__(self):
        self.d = lax.axis_index("dp")
        self.r = lax.axis_index("row")
        self.c = lax.axis_index("col")
        self.k = lax.rem(self.d, 8)
        self.base = self.d - self.k
        self.y = lax.rem(self.k, 2)
        self.z = lax.div(self.k, 2)
        self.beside = {"dp": self.base + self.z * 2 + 1 - self.y}
        self.across = {"row": 1 - self.r}
        self.core = {"col": 1 - self.c}
        self.diagonal = {"row": 1 - self.r, "col": 1 - self.c}

    def eight(self, offset):
        other = lax.rem(self.k + offset, 8)
        return other, {"dp": self.base + other}

    def four(self, offset):
        other = lax.rem(self.z + offset, 4)
        return other, {"dp": self.base + other * 2 + self.y}


def meet(devices):
    barrier = pltpu.get_barrier_semaphore()
    for device in devices:
        pl.semaphore_signal(barrier, inc=1, device_id=device, device_id_type=MESH)
    pl.semaphore_wait(barrier, len(devices))


def comm_params(name, number):
    return dict(
        name=name,
        compiler_params=pltpu.CompilerParams(
            vmem_limit_bytes=VMEM_BYTES, collective_id=number, has_side_effects=True
        ),
    )


class Gather:
    def __init__(self, place, own, full, part, block, step, send_sem, recv_sem, first):
        self.p, self.own, self.full, self.part, self.block, self.h = place, own, full, part, block, step
        self.s, self.v, self.f = send_sem, recv_sem, first

    def _move(self, src, dst, n, device):
        return send(src, dst, self.s.at[self.f + n], self.v.at[self.f + n], device)

    def _cross(self, r):
        p = self.p
        at = (p.y * 4 + p.z) * self.h
        return self._move(self.part(self.own, at, self.h), self.block(self.full, r, p.c, at, self.h), 0, p.across)

    def _near(self, c):
        p = self.p
        return self._move(self.own, self.block(self.full, p.r, c, 0, 8 * self.h), 1, p.core)

    def _pass(self, offset, z):
        p = self.p
        here = self.block(self.full, 1 - p.r, p.c, (p.y * 4 + z) * self.h, self.h)
        return self._move(here, here, 1 + offset, p.four(offset)[1])

    def _turn(self, y):
        p = self.p
        here = self.block(self.full, 1 - p.r, p.c, y * 4 * self.h, 4 * self.h)
        return self._move(here, here, 5, p.beside)

    def _last(self, c):
        p = self.p
        here = self.block(self.full, 1 - p.r, c, 0, 8 * self.h)
        return self._move(here, here, 6, p.core)

    def start(self):
        self._cross(self.p.r).start()
        self._near(self.p.c).start()

    def relay(self):
        p = self.p
        self._cross(1 - p.r).wait_recv()
        for offset in (1, 2, 3):
            self._pass(offset, p.z).start()

    def turn(self):
        p = self.p
        for offset in (1, 2, 3):
            self._pass(offset, lax.rem(p.z + 4 - offset, 4)).wait_recv()
        self._turn(p.y).start()

    def share(self):
        p = self.p
        self._turn(1 - p.y).wait_recv()
        self._last(p.c).start()

    def finish(self):
        p = self.p
        self._last(1 - p.c).wait_recv()
        self._near(1 - p.c).wait_recv()
        self._cross(p.r).wait_send()
        self._near(p.c).wait_send()
        for offset in (1, 2, 3):
            self._pass(offset, p.z).wait_send()
        self._turn(p.y).wait_send()
        self._last(p.c).wait_send()


def middle_part(ref, first, rows):
    return ref.at[:, rows_at(first, rows, 8), :]


def middle_block(ref, r, c, first, rows):
    return ref.at[:, rows_at(c * 192 + first, rows, 8), lanes(r)]


def rows_part(ref, first, rows):
    return ref.at[rows_at(first, rows), :]


def inter_block(ref, r, c, first, rows):
    return ref.at[r, rows_at(first, rows), lanes(c, 768)]


def output_block(ref, r, c, first, rows):
    return ref.at[r, rows_at(c * 768 + first, rows), :]


class ToRows:
    def __init__(self, place, src, dst, stage, local_sem, send_sem, recv_sem):
        self.p, self.src, self.dst, self.stage = place, src, dst, stage
        self.l, self.s, self.v = local_sem, send_sem, recv_sem

    def _cross(self, q, k):
        half = self.src.at[q * ROWS : (q + 1) * ROWS, :]
        return send(half, self.dst.at[:, lanes(k)], self.s.at[q], self.v.at[0], {"row": 1 - self.p.r, "col": q})

    def _near(self):
        p = self.p
        half = self.src.at[rows_at((1 - p.c) * ROWS, ROWS), :]
        return send(half, self.dst.at[:, lanes(p.r)], self.s.at[2], self.v.at[1], p.core)

    def _load(self):
        return pltpu.make_async_copy(self.src.at[rows_at(self.p.c * ROWS, ROWS), :], self.stage, self.l.at[0])

    def _store(self):
        return pltpu.make_async_copy(self.stage, self.dst.at[:, lanes(self.p.r)], self.l.at[1])

    def start(self):
        p = self.p

        @pl.when(p.r != p.c)
        def _():
            self._cross(0, p.r).start()
            self._cross(1, p.r).start()

        @pl.when(p.r == p.c)
        def _():
            self._near().start()
            self._load().start()

    def store(self):
        @pl.when(self.p.r == self.p.c)
        def _():
            self._load().wait()
            self._store().start()

    def finish(self):
        p = self.p
        self._cross(0, 1 - p.r).wait_recv()

        @pl.when(p.r != p.c)
        def _():
            self._cross(0, p.r).wait_send()
            self._cross(1, p.r).wait_send()
            self._near().wait_recv()

        @pl.when(p.r == p.c)
        def _():
            self._near().wait_send()
            self._store().wait()


class FromRows:
    def __init__(self, place, src, dst, local_sem, send_sem, recv_sem):
        self.p, self.src, self.dst = place, src, dst
        self.l, self.s, self.v = local_sem, send_sem, recv_sem

    def _cross(self, q):
        p = self.p
        place = self.dst.at[q]
        return send(self.src.at[:, lanes(1 - p.r)], place, self.s.at[0], self.v.at[q], {"row": 1 - p.r, "col": p.r})

    def _near(self, q):
        p = self.p
        place = self.dst.at[q]
        return send(self.src.at[:, lanes(p.r)], place, self.s.at[1], self.v.at[2], p.core)

    def _local(self):
        p = self.p
        place = self.dst.at[p.c]
        return pltpu.make_async_copy(self.src.at[:, lanes(p.r)], place, self.l)

    def start(self):
        p = self.p
        self._cross(p.c).start()

        @pl.when(p.r != p.c)
        def _():
            self._near(p.c).start()

        @pl.when(p.r == p.c)
        def _():
            self._local().start()

    def finish(self):
        p = self.p
        self._cross(p.c).wait_send()

        @pl.when(p.r != p.c)
        def _():
            self._near(p.c).wait_send()
            self._cross(0).wait_recv()
            self._cross(1).wait_recv()

        @pl.when(p.r == p.c)
        def _():
            self._near(1 - p.c).wait_recv()
            self._local().wait()


class Sum:
    def __init__(self, place, far, mid, ybuf, zbuf, total, rows, s, v, first=0):
        self.p, self.far, self.mid, self.ybuf, self.zbuf, self.total = place, far, mid, ybuf, zbuf, total
        self.rows, self.s, self.v, self.first = rows, s, v, first

    def _sems(self, ch, n):
        i = self.first + ch * 8 + n
        return self.s.at[i], self.v.at[i]

    def _beside(self):
        return self.p.beside

    def _halves(self, ch, y):
        return rows_at(ch * self.rows + y * (self.rows // 2), self.rows // 2)

    def _piece(self, ch, z):
        return rows_at(ch * self.rows + self.p.y * (self.rows // 2) + z * (self.rows // 8), self.rows // 8)

    def _half(self, ch):
        return send(self.far.at[self._halves(ch, 1 - self.p.y), :], self.ybuf.at[ch], *self._sems(ch, 0), self._beside())

    def _quarter(self, ch, offset):
        other, device = self.p.four(offset)
        src = self.mid.at[ch, rows_at(other * (self.rows // 8), self.rows // 8), :]
        return send(src, self.zbuf.at[ch, offset - 1], *self._sems(ch, offset), device)

    def _along(self, ch, offset, z):
        _, device = self.p.four(offset)
        here = self.total.at[self._piece(ch, z), :]
        return send(here, here, *self._sems(ch, 3 + offset), device)

    def _back(self, ch, y):
        here = self.total.at[self._halves(ch, y), :]
        return send(here, here, *self._sems(ch, 7), self._beside())

    def half(self, ch):
        self._half(ch).start()

    def quarter(self, ch):
        self._half(ch).wait_recv()
        both = self.far[self._halves(ch, self.p.y), :].astype(F32) + self.ybuf[ch].astype(F32)
        self.mid[ch] = both.astype(BF)
        for offset in (1, 2, 3):
            self._quarter(ch, offset).start()

    def collect(self, ch):
        both = self.mid[ch, rows_at(self.p.z * (self.rows // 8), self.rows // 8), :].astype(F32)
        for offset in (1, 2, 3):
            self._quarter(ch, offset).wait_recv()
            both = both + self.zbuf[ch, offset - 1].astype(F32)
        return both.astype(BF)

    def along(self, ch, piece):
        self.total[self._piece(ch, self.p.z), :] = piece
        for offset in (1, 2, 3):
            self._along(ch, offset, self.p.z).start()

    def back(self, ch):
        for offset in (1, 2, 3):
            self._along(ch, offset, lax.rem(self.p.z + 4 - offset, 4)).wait_recv()
        self._back(ch, self.p.y).start()

    def finish_sum(self, ch):
        self._half(ch).wait_send()
        for offset in (1, 2, 3):
            self._quarter(ch, offset).wait_send()

    def finish_spread(self, ch):
        self._back(ch, 1 - self.p.y).wait_recv()
        for offset in (1, 2, 3):
            self._along(ch, offset, self.p.z).wait_send()
        self._back(ch, self.p.y).wait_send()

    @staticmethod
    def scratch(rows, chunks):
        return [
            pltpu.VMEM((chunks, rows // 2, HALF), BF),
            pltpu.VMEM((chunks, rows // 2, HALF), BF),
            pltpu.VMEM((chunks, 3, rows // 8, HALF), BF),
            pltpu.SemaphoreType.DMA((8 * chunks,)),
            pltpu.SemaphoreType.DMA((8 * chunks,)),
        ]


class Groups:
    def __init__(self, place, s, v):
        self.p, self.s, self.v = place, s, v

    def half(self, n, mine, ybuf):
        return send(mine.at[1 - self.p.y], ybuf, self.s.at[n], self.v.at[n], self.p.beside)

    def quarter(self, n, mid, zbuf, offset):
        other, device = self.p.four(offset)
        n = n + offset - 1
        return send(mid.at[other], zbuf.at[offset - 1], self.s.at[n], self.v.at[n], device)

    def cross(self, n, both, xbuf):
        return send(both.at[1 - self.p.r], xbuf, self.s.at[n], self.v.at[n], self.p.across)

    def along(self, n, half, offset, z):
        n = n + offset - 1
        return send(half.at[z], half.at[z], self.s.at[n], self.v.at[n], self.p.four(offset)[1])

    def back(self, n, half, other):
        return send(half, other, self.s.at[n], self.v.at[n], self.p.beside)

    def start_quarters(self, n, mid, zbuf):
        for offset in (1, 2, 3):
            self.quarter(n, mid, zbuf, offset).start()

    def collect(self, n, mid, zbuf, both):
        total = mid[self.p.z].astype(F32)
        for offset in (1, 2, 3):
            self.quarter(n, mid, zbuf, offset).wait_recv()
            total = total + zbuf[offset - 1].astype(F32)
        both[...] = total.astype(BF)

    def start_along(self, n, half, piece):
        half[self.p.z] = piece
        for offset in (1, 2, 3):
            self.along(n, half, offset, self.p.z).start()

    def await_along(self, n, half):
        for offset in (1, 2, 3):
            self.along(n, half, offset, lax.rem(self.p.z + 4 - offset, 4)).wait_recv()

    def sent(self, n, ref, kind):
        for offset in (1, 2, 3):
            kind(n, *ref, offset).wait_send()


def everyone(p):
    return [p.across, p.core, p.diagonal, p.beside] + [p.four(o)[1] for o in (1, 2, 3)]


def front_kernel(
    lens, tok_ref, wk_own, wv_own, wc_own, wq_own, wp_own, kern_ref, kb_ref, perm_ref,
    wdep_ref, bv_ref, bc_ref, bq_ref, bp_ref, wi_own, wd_own, wo_own, cot_own,
    kd_ref, kt_ref, vz_ref, q_ref, qs_ref, pt_ref, kp_ref, conv_ref, mix_ref, dep_ref, h_ref, wk_ref, bk_ref, spread_ref,
    ctx_ref, lse_ref, seq_out, w5_out, wi_ref, wd_ref, cot_ref, wo_ref,
    own, seq_ref, w_ref, stage, first_key, hbuf, cbuf, lsem, ts, tr, gs, gr, cs, cr,
):
    i = pl.program_id(0)
    p = Place()
    r, c = p.r, p.c
    n = lens[r]
    proj = Gather(p, own, w_ref, middle_part, middle_block, 24, gs, gr, 0)
    inter = Gather(p, wi_own, wi_ref, rows_part, inter_block, 48, gs, gr, 7)
    dense = Gather(p, wd_own, wd_ref, middle_part, middle_block, 24, gs, gr, 14)
    cot_rows = ToRows(p, cot_own, cot_ref, stage, lsem, cs, cr)
    output = Gather(p, wo_own, wo_ref, rows_part, output_block, 96, gs, gr, 21)
    keep_output = pltpu.make_async_copy(wo_own, output_block(wo_ref, r, c, 0, D), lsem.at[7])
    keep_inter = pltpu.make_async_copy(wi_own, inter_block(wi_ref, r, c, 0, HALF), lsem.at[2])
    keep_dense = pltpu.make_async_copy(wd_own, middle_block(wd_ref, r, c, 0, 192), lsem.at[3])
    keep_own = pltpu.make_async_copy(tok_ref, seq_ref.at[PAD : PAD + LMAX, lanes(r)], lsem.at[4])
    keep_seq = pltpu.make_async_copy(seq_ref, seq_out, lsem.at[5])
    keep_w = pltpu.make_async_copy(w_ref, w5_out, lsem.at[6])

    def chunk(m, k):
        return seq_ref.at[PAD + m * 512 : PAD + (m + 1) * 512, lanes(k)]

    def cross(m, k):
        return send(tok_ref.at[m * 512 : (m + 1) * 512, :], chunk(m, k), ts.at[m], tr.at[m], {"row": 1 - r, "col": m // 2})

    def near(k):
        return send(tok_ref, seq_ref.at[PAD : PAD + LMAX, lanes(k)], ts.at[4], tr.at[4], p.core)

    def forward(m):
        return send(chunk(m, 1 - r), chunk(m, 1 - r), ts.at[5 + m], tr.at[5 + m], p.core)

    @pl.when(i == 0)
    def _():
        for j, ref in enumerate((wk_own, wv_own, wc_own, wq_own, wp_own)):
            own[j] = ref[...]
        seq_ref[0:PAD, :] = jnp.zeros((PAD, D), BF)
        seq_ref[PAD + LMAX :, :] = jnp.zeros((PAD, D), BF)
        meet(everyone(p))
        proj.start()
        inter._cross(r).start()
        dense._cross(r).start()
        output._cross(r).start()

        @pl.when(r != c)
        def _():
            for m in (0, 2, 1, 3):
                cross(m, r).start()

        @pl.when(r == c)
        def _():
            near(r).start()
            keep_own.start()

        cot_rows.start()
        inter._near(c).start()
        dense._near(c).start()
        output._near(c).start()
        keep_inter.start()
        keep_dense.start()
        keep_output.start()
        middle_block(w_ref, r, c, 0, 192)[...] = own[...]
        wk_ref[...] = nn(perm_ref[...], kern_ref[...]).astype(BF)
        bk_ref[...] = nt(perm_ref[...], jnp.broadcast_to(line(kb_ref), (128, 54)).astype(BF))
        row = lax.broadcasted_iota(jnp.int32, spread_ref.shape, 0)
        col = lax.broadcasted_iota(jnp.int32, spread_ref.shape, 1)
        head = row & 7
        hit = (head < 6) & ((col >> 6) == (row >> 3) * 6 + head)
        spread_ref[...] = jnp.where(hit, 1.0, 0.0).astype(BF)
        proj.relay()
        proj.turn()
        inter.relay()
        dense.relay()
        output.relay()
        for q in range(2):

            @pl.when(c == q)
            def _():
                for m in (2 * q, 2 * q + 1):
                    cross(m, 1 - r).wait_recv()
                    forward(m).start()

        proj.share()
        for q in range(2):

            @pl.when(c == q)
            def _():
                for m in (2 - 2 * q, 3 - 2 * q):
                    forward(m).wait_recv()
                for m in (2 * q, 2 * q + 1):
                    forward(m).wait_send()

        @pl.when(r != c)
        def _():
            for m in range(4):
                cross(m, r).wait_send()
            near(r).wait_recv()

        @pl.when(r == c)
        def _():
            near(r).wait_send()
            keep_own.wait()

        proj.finish()
        keep_seq.start()
        keep_w.start()

    @pl.when(i == 1)
    def _():
        inter.turn()
        dense.turn()
        cot_rows.store()

    @pl.when(i == 2)
    def _():
        output.turn()

    @pl.when(i == 4)
    def _():
        inter.share()
        dense.share()

    @pl.when(i == 5)
    def _():
        output.share()

    @pl.when(i < 4)
    def _():
        krows = LMAX // 4
        keep_key = row_ids(i * krows, krows) < n
        tok = seq_ref[rows_at(PAD + i * krows, krows), :]
        h = jnp.where(keep_key, tok.astype(F32), 0.0).astype(BF)
        k = nt(h, w_ref[0])
        v = nt(h, w_ref[1]) + line(bv_ref)

        @pl.when(i == 0)
        def _():
            first_key[...] = k[0:8]

        kd_ref[rows_at(i * krows, krows), :] = jnp.where(keep_key, k, first_key[0:1]).astype(BF)
        kt_ref[...] = k.T.astype(BF)
        vz_ref[rows_at(i * krows, krows), :] = jnp.where(keep_key, v, 0.0).astype(BF)

        rows = q_ref.shape[0]
        wide = rows + 32
        base = pl.multiple_of(i * rows, 16)
        start = pl.multiple_of(c * ROWS + i * rows, 16)
        ids = row_ids(start - 16, wide)
        keep = (ids >= 0) & (ids < n)
        hw = jnp.where(keep, seq_ref[pl.ds(start, wide), :].astype(F32), 0.0)
        put_tiles(hbuf, hw)
        wdep = wdep_ref[...].astype(F32)
        for t in range(D // 128):
            cols = slice(t * 128, (t + 1) * 128)

            def strip(s, carry):
                r0 = pl.multiple_of(s * 64, 64)
                depth = jnp.zeros((64, 128), F32)
                for j in range(KW):
                    depth = depth + hbuf[t, pl.ds(r0 + 12 + j, 64), :] * wdep[j : j + 1, cols]
                dep_ref[pl.ds(r0, 64), cols] = depth.astype(BF)
                return carry

            lax.fori_loop(0, rows // 64, strip, 0)
        depth_low = dep_ref[...]
        hl = hw.astype(BF)
        h_ref[...] = hl[16 : 16 + rows]
        conv = jnp.where(keep, nt(hl, w_ref[2]) + line(bc_ref), 0.0)
        put_tiles(cbuf, conv)
        conv_ref[pl.ds(base, wide), :] = conv.astype(BF)
        q = nt(hl[16 : 16 + rows], w_ref[3]) + line(bq_ref)
        q_low = q.astype(BF)
        q_ref[...] = q_low
        qs_ref[pl.ds(base, rows), :] = (q * (0.125 * LOG2E)).astype(BF)
        pt = nt(depth_low, w_ref[4]) + line(bp_ref)
        pt_ref[...] = pt.astype(BF)
        mixer = (pt * q_low.astype(F32)).astype(BF)
        logits = (nt(wk_ref[...], mixer) + bk_ref[:, 0:1]).reshape(KW, 8, rows)
        peak = jnp.max(logits, axis=0, keepdims=True)
        raised = jnp.exp(logits - peak)
        kp = (raised / jnp.sum(raised, axis=0, keepdims=True)).reshape(KW * 8, rows)
        kp_ref[...] = kp
        kpt = kp.T.astype(BF)
        for t in range(HALF // 128):
            mix = jnp.zeros((rows, 128), F32)
            for j in range(KW):
                wide_probs = nn(kpt, spread_ref[:, j * HALF + t * 128 : j * HALF + (t + 1) * 128])
                mix = mix + wide_probs * cbuf[t, 12 + j : 12 + j + rows, :]
            mix_ref[:, t * 128 : (t + 1) * 128] = mix.astype(BF)

    @pl.when(i >= 4)
    def _():
        cols = lanes(i - 4, 128)
        k = kd_ref[:, cols]
        ones = jnp.where(row_ids(0, LMAX) < n, 1.0, 0.0)
        ve = jnp.concatenate([vz_ref[:, cols], jnp.broadcast_to(ones, (LMAX, 128)).astype(BF)], axis=1)
        rows = 256
        lane = lax.broadcasted_iota(jnp.int32, (rows, 128), 1)
        for u in range(ROWS // rows):
            part = slice(u * rows, (u + 1) * rows)
            outs = []
            for hh in range(2):
                q = jnp.where((lane < HD) == (hh == 0), qs_ref[part, cols], jnp.zeros((), BF))
                s = nt(q, k)
                peak = jnp.max(s, axis=1, keepdims=True)
                prob = jnp.exp2(s - peak).astype(BF)
                o = nn(prob, ve)
                outs.append(o[:, :128] / o[:, 128:])
                lse_ref[0, hh : hh + 1, part] = (peak + jnp.log2(o[:, 128:129])).T
            ctx_ref[part, :] = jnp.where(lane < HD, outs[0], outs[1]).astype(BF)

    @pl.when(i == pl.num_programs(0) - 1)
    def _():
        inter.finish()
        dense.finish()
        output.finish()
        cot_rows.finish()
        keep_inter.wait()
        keep_dense.wait()
        keep_output.wait()
        keep_seq.wait()
        keep_w.wait()


def front(lens, tokens, weights, w_kernel, b_kernel, perm, wdep, bv, bc, bq, bp, w_inter, w_dense, w_output, cotangent):
    rows = 256
    early = lambda i: jnp.minimum(i, 3)
    late = lambda i: jnp.maximum(i - 4, 0)
    blk = pl.BlockSpec((rows, HALF), lambda i, lens: (early(i), 0))
    full = pl.BlockSpec((rows, D), lambda i, lens: (early(i), 0))
    half = jax.ShapeDtypeStruct((ROWS, HALF), BF)
    return pl.pallas_call(
        front_kernel,
        grid_spec=pltpu.PrefetchScalarGridSpec(
            num_scalar_prefetch=1,
            grid=(7,),
            in_specs=[HBM]
            + [once((192, HALF))] * 5
            + [once((54, HALF)), whole((54,)), once((72, 54)), once((KW, D))]
            + [whole((HALF,))] * 4
            + [once((HALF, D)), once((2, 192, HALF)), once((D, HALF)), HBM],
            out_specs=[
                once((LMAX, HALF)),
                pl.BlockSpec((HALF, LMAX // 4), lambda i, lens: (0, early(i))),
                once((LMAX, HALF)),
                blk,
                once((ROWS, HALF)),
                blk,
                pl.BlockSpec((72, rows), lambda i, lens: (0, early(i))),
                once((ROWS + 32, HALF)),
                blk,
                full,
                full,
                whole((72, HALF)),
                whole((72, 128)),
                once((72, KW * HALF)),
                pl.BlockSpec((ROWS, 128), lambda i, lens: (0, late(i))),
                pl.BlockSpec((1, 8, ROWS), lambda i, lens: (late(i), 0, 0)),
            ]
            + [HBM] * 6,
            scratch_shapes=[
                pltpu.VMEM((5, 192, HALF), BF),
                pltpu.VMEM((LMAX + 2 * PAD, D), BF),
                pltpu.VMEM((5, HALF, D), BF),
                pltpu.VMEM((ROWS, HALF), BF),
                pltpu.VMEM((8, HALF), F32),
                pltpu.VMEM((D // 128, rows + 32, 128), F32),
                pltpu.VMEM((HALF // 128, rows + 32, 128), F32),
                pltpu.SemaphoreType.DMA((8,)),
                pltpu.SemaphoreType.DMA((9,)),
                pltpu.SemaphoreType.DMA((9,)),
                pltpu.SemaphoreType.DMA((28,)),
                pltpu.SemaphoreType.DMA((28,)),
                pltpu.SemaphoreType.DMA((3,)),
                pltpu.SemaphoreType.DMA((2,)),
            ],
        ),
        out_shape=[
            jax.ShapeDtypeStruct((LMAX, HALF), BF),
            jax.ShapeDtypeStruct((HALF, LMAX), BF),
            jax.ShapeDtypeStruct((LMAX, HALF), BF),
            half,
            half,
            half,
            jax.ShapeDtypeStruct((72, ROWS), F32),
            jax.ShapeDtypeStruct((ROWS + 32, HALF), BF),
            half,
            jax.ShapeDtypeStruct((ROWS, D), BF),
            jax.ShapeDtypeStruct((ROWS, D), BF),
            jax.ShapeDtypeStruct((72, HALF), BF),
            jax.ShapeDtypeStruct((72, 128), F32),
            jax.ShapeDtypeStruct((72, KW * HALF), BF),
            half,
            jax.ShapeDtypeStruct((3, 8, ROWS), F32),
            jax.ShapeDtypeStruct((LMAX + 2 * PAD, D), BF),
            jax.ShapeDtypeStruct((5, HALF, D), BF),
            jax.ShapeDtypeStruct((2, HALF, GW), BF),
            jax.ShapeDtypeStruct((2, HALF, D), BF),
            jax.ShapeDtypeStruct((ROWS, D), BF),
            jax.ShapeDtypeStruct((2, GW, HALF), BF),
        ],
        **comm_params("front", 2),
    )(
        lens, tokens, *weights, w_kernel, b_kernel, perm, wdep, bv, bc, bq, bp, w_inter, w_dense, w_output, cotangent
    )


def back_kernel(
    lens, gcv_ref, conv_ref, kp_ref, q_ref, pt_ref, wk_ref, spread_ref, ones_ref,
    qs_ref, do_ref, k_ref, v_ref, kt_ref, lse_ref, del_ref, pay_all, pay_ref, hid_ref,
    seq_ref, wc_ref, wp_ref, gpre_ref, dep_ref, wdep_ref, smf_ref, gbi_ref,
    gqm_ref, dq_ref, dk_ref, dv_ref, ghm_ref, edge_ref, half_ref, piece_ref, piece_cp_ref, out_ref,
    acc, wbuf, tbuf, dka, dva, near, mine, ybuf, mid, zbuf, both, xbuf, half,
    gpad, dbuf, hwin, sbuf, agc, agp, gwk, gbk, sm, gdp, pcp, near_cp,
    out2, far2, y2, mid2, z2, out_cp, far_cp, y_cp, mid_cp, z_cp,
    ns, nr, s, v_sem, ls, hs, hr,
):
    step = pl.program_id(0)
    place = Place()
    n = lens[place.r]
    groups = Groups(place, s, v_sem)
    hidden = FromRows(place, hid_ref, out_ref, ls, hs, hr)

    def near_copy(k):
        rr = 1 - place.r if k % 2 == 0 else place.r
        src, dst = (pay_all, near) if k < 2 else (pcp, near_cp)
        return send(src.at[rr, 1 - place.c], dst.at[rr], ns.at[k], nr.at[k], place.core)

    def over(k, src, dst):
        return send(src, dst, s.at[k], v_sem.at[k], place.across)

    @pl.when(step == 0)
    def _():
        meet(everyone(place))
        near_copy(0).start()
        near_copy(1).start()
        hidden.start()
        for ref in (acc, agc, agp):
            clear(ref)
        for ref in (tbuf, gwk, gbk, sm, gdp):
            ref[...] = jnp.zeros_like(ref)
        gpad[0:32, :] = jnp.zeros((32, HALF), BF)
        gpad[32 + ROWS :, :] = jnp.zeros((32, HALF), BF)

    @pl.when(step == 2)
    def _():
        near_copy(0).wait()
        near_copy(1).wait()
        there = 1 - place.r
        out2[...] = (near[there, 2].astype(F32) + pay_ref[there, 0, 2].astype(F32)).astype(BF)
        over(18, out2, far2).start()
        for ch in range(2):
            for rr in range(2):
                total = near[rr, ch].astype(F32) + pay_ref[rr, 0, ch].astype(F32)
                mine[ch, :, :, rr] = total.astype(BF)
            groups.half(ch, mine.at[ch], ybuf.at[ch]).start()

    def settle(ch):
        groups.half(ch, mine.at[ch], ybuf.at[ch]).wait_recv()
        mid[ch] = (mine[ch, place.y].astype(F32) + ybuf[ch].astype(F32)).astype(BF)

    def merge(ch):
        groups.cross(16 + ch, both.at[ch], xbuf.at[ch]).wait_recv()
        return (both[ch, place.r].astype(F32) + xbuf[ch].astype(F32)).astype(BF)

    def quarters(ch):
        if ch < 2:
            return 4 + 3 * ch, mid.at[ch], zbuf.at[ch]
        return (10, mid2, z2) if ch == 2 else (13, mid_cp, z_cp)

    @pl.when(step == 6)
    def _():
        settle(0)
        groups.start_quarters(*quarters(0))
        near_copy(2).start()
        near_copy(3).start()

    @pl.when(step == 7)
    def _():
        near_copy(2).wait()
        near_copy(3).wait()
        there = 1 - place.r
        out_cp[...] = (near_cp[there].astype(F32) + pcp[there, place.c].astype(F32)).astype(BF)
        over(19, out_cp, far_cp).start()

    @pl.when(step == 8)
    def _():
        settle(1)
        groups.start_quarters(*quarters(1))
        groups.collect(*quarters(0), both.at[0])
        groups.cross(16, both.at[0], xbuf.at[0]).start()
        over(18, out2, far2).wait_recv()
        here = near[place.r, 2].astype(F32) + pay_ref[place.r, 0, 2].astype(F32)
        far2[...] = (here + far2[...].astype(F32)).astype(BF)
        groups.half(2, far2, y2).start()

    @pl.when(step == 9)
    def _():
        groups.start_along(20, half, merge(0))
        over(19, out_cp, far_cp).wait_recv()
        here = near_cp[place.r].astype(F32) + pcp[place.r, place.c].astype(F32)
        far_cp[...] = (here + far_cp[...].astype(F32)).astype(BF)
        groups.half(3, far_cp, y_cp).start()

    @pl.when(step == 10)
    def _():
        groups.collect(*quarters(1), both.at[1])
        groups.cross(17, both.at[1], xbuf.at[1]).start()
        groups.half(2, far2, y2).wait_recv()
        mid2[...] = (far2[place.y].astype(F32) + y2[...].astype(F32)).astype(BF)
        groups.start_quarters(*quarters(2))

    @pl.when(step == 11)
    def _():
        piece_ref[0] = merge(1)
        groups.half(3, far_cp, y_cp).wait_recv()
        mid_cp[...] = (far_cp[place.y].astype(F32) + y_cp[...].astype(F32)).astype(BF)
        groups.start_quarters(*quarters(3))

    @pl.when(step < 4)
    def _():
        rows = gcv_ref.shape[0]
        wide = rows + 32
        put_tiles(wbuf, conv_ref[pl.ds(pl.multiple_of(step * rows, 16), wide), :].astype(F32))
        kp = kp_ref[...]
        kpt = kp.T.astype(BF)
        gkps = [None] * KW
        there = pl.ds(pl.multiple_of(place.c * ROWS + step * rows, 16), wide)
        for t in range(HALF // 128):
            cols = slice(t * 128, (t + 1) * 128)
            gcv = gcv_ref[:, cols].astype(F32)
            total = jnp.zeros((wide, 128), F32)
            for j in range(KW):
                prod = (gcv * wbuf[t, 12 + j : 12 + j + rows, :]).astype(BF)
                part = nt(ones_ref[:, cols], prod)
                gkps[j] = part if t == 0 else gkps[j] + part
                tbuf[j % 3, 24 : 24 + rows, :] = nn(kpt, spread_ref[:, j * HALF + t * 128 : j * HALF + (t + 1) * 128]) * gcv
                total = total + tbuf[j % 3, 12 - j : 12 - j + wide, :]
            acc[there, cols] += total
        gkp = jnp.concatenate(gkps, axis=0).reshape(KW, 8, rows)
        kp3 = kp.reshape(KW, 8, rows)
        inner = jnp.sum(kp3 * gkp, axis=0, keepdims=True)
        gl = (kp3 * (gkp - inner)).reshape(KW * 8, rows)
        glt = gl.T.astype(BF)
        gbk[0:1, 0:72] += col_sum(glt.astype(F32))
        q = q_ref[...].astype(F32)
        pt = pt_ref[...].astype(F32)
        gwk[...] += nn(gl.astype(BF), (pt * q).astype(BF))
        gmix = nn(glt, wk_ref[...])
        gqm_ref[...] = (gmix * pt).astype(BF)
        gpad[rows_at(32 + step * rows, rows), :] = (gmix * q).astype(BF)

    def conv_grads(first, rows):
        keep = row_ids(first, rows) < n
        gco = jnp.where(keep, acc[rows_at(16 + first, rows), :], 0.0).astype(BF)
        tok = seq_ref[rows_at(PAD + first, rows), :]
        h = jnp.where(keep, tok.astype(F32), 0.0).astype(BF)
        agc[...] += nn(gco.T, h)
        sm[2:3, :] += col_sum(gco.astype(F32))
        return nn(gco, wc_ref[0])

    @pl.when(step == 4)
    def _():
        wdep = wdep_ref[...].astype(F32)
        at = pl.multiple_of((1 - place.c) * (ROWS + 16), 16)
        sbuf[...] = nn(gpad[pl.ds(at, 48), :], wp_ref[0])
        total = conv_grads(pl.multiple_of(ROWS - 16 * place.c, 16), 16)
        for j in range(KW):
            total = total + sbuf[20 - j : 36 - j, :] * wdep[j : j + 1, :]
        edge_ref[...] = total

    @pl.when((step == 4) | (step == 5))
    def _():
        m = step - 4
        rows = gpre_ref.shape[0]
        wide = rows + 32
        first = pl.multiple_of(place.c * ROWS + m * rows, 16)
        wdep = wdep_ref[...].astype(F32)
        win = gpad[rows_at(m * rows + 16, wide), :]
        gpt = win[16 : 16 + rows]
        sm[3:4, :] += col_sum(gpt.astype(F32))
        agp[...] += nn(gpt.T, dep_ref[...])
        put_tiles(dbuf, nn(win, wp_ref[0]))
        ids = row_ids(first - 16, wide)
        inside = (ids >= 0) & (ids < n)
        put_tiles(hwin, jnp.where(inside, seq_ref[pl.ds(first, wide), :].astype(F32), 0.0))
        ghm_ref[...] = (conv_grads(first, rows) + gpre_ref[...].astype(F32)).astype(BF)
        for t in range(D // 128):
            cols = slice(t * 128, (t + 1) * 128)

            def strip(k, sums):
                r0 = pl.multiple_of(k * 64, 64)
                gdep = dbuf[t, pl.ds(r0 + 16, 64), :]
                total = ghm_ref[pl.ds(r0, 64), cols].astype(F32)
                new = []
                for j in range(KW):
                    prod = gdep * hwin[t, pl.ds(r0 + 12 + j, 64), :]
                    new.append(sums[j] + jnp.sum(prod.reshape(8, 8, 128), axis=0))
                    total = total + dbuf[t, pl.ds(r0 + 20 - j, 64), :] * wdep[j : j + 1, cols]
                ghm_ref[pl.ds(r0, 64), cols] = total.astype(BF)
                return tuple(new)

            sums = lax.fori_loop(0, rows // 64, strip, (jnp.zeros((8, 128), F32),) * KW)
            for j in range(KW):
                gdp[j : j + 1, cols] += col_sum(sums[j])

    @pl.when(step == 5)
    def _():
        def put(r, c, first, value):
            pcp[r, c, first // 256, first // 64 % 4] = value.astype(BF)

        zeros = lambda k: jnp.zeros((k, HALF), F32)
        bias = jnp.concatenate([gbk[0:1, :], jnp.zeros((1, 256), F32)], axis=1)
        mixed = [sm[2:4, :], bias, gdp[8:9, 0:HALF], gdp[8:9, HALF:D], zeros(3)]
        inter = [gbi_ref[:, k * HALF : (k + 1) * HALF] for k in range(8)]
        norms = [smf_ref[:, 0:HALF], smf_ref[:, HALF:D]]
        depth = [gdp[0:8, 0:HALF], gdp[0:8, HALF:D], zeros(8)]
        little = jnp.concatenate([gwk[...]] + mixed + norms + inter + depth, axis=0)
        for r in range(2):
            for c in range(2):
                for k in range(3):
                    rows = slice(c * 192 + k * 64, c * 192 + (k + 1) * 64)
                    put(r, c, k * 64, agc[rows, r * HALF : (r + 1) * HALF])
                    put(r, c, 192 + k * 64, agp[rows, r * HALF : (r + 1) * HALF])
                put(r, c, 384, little[0:64])
                put(r, c, 448, little[64:128])

    @pl.when(step >= 6)
    def _():
        i = lax.rem(step, 2)
        k = k_ref[...]
        v = v_ref[...]
        rows = qs_ref.shape[0]
        lane = lax.broadcasted_iota(jnp.int32, (rows, 128), 1)
        dk = dv = None
        for hh in range(2):
            head = (lane < HD) == (hh == 0)
            q = jnp.where(head, qs_ref[...], jnp.zeros((), BF))
            do = jnp.where(head, do_ref[...], jnp.zeros((), BF))
            p = jnp.exp2(nt(k, q) - lse_ref[0, hh : hh + 1, :])
            ds = (p * (nt(v, do) - del_ref[0, hh : hh + 1, :])).astype(BF)
            dv_one = nn(p.astype(BF), do)
            dk_one = nn(ds, q)
            dv = dv_one if dv is None else dv + dv_one
            dk = dk_one if dk is None else dk + dk_one
            dq_ref[hh * HD : (hh + 1) * HD, :] = (nn(kt_ref[hh * HD : (hh + 1) * HD, :], ds) * 0.125).astype(BF)

        @pl.when(i == 0)
        def _():
            dka[...] = dk
            dva[...] = dv

        @pl.when(i == 1)
        def _():
            keep = row_ids(0, LMAX) < n
            dk_ref[...] = jnp.where(keep, (dka[...] + dk) * LN2, 0.0).astype(BF)
            dv_ref[...] = jnp.where(keep, dva[...] + dv, 0.0).astype(BF)

    @pl.when(step == 11)
    def _():
        groups.collect(*quarters(2), piece_ref.at[1])
        groups.collect(*quarters(3), piece_cp_ref)
        groups.await_along(20, half)
        half_ref[...] = half[...]
        for ch in range(2):
            groups.half(ch, mine.at[ch], ybuf.at[ch]).wait_send()
            groups.cross(16 + ch, both.at[ch], xbuf.at[ch]).wait_send()
        groups.half(2, far2, y2).wait_send()
        groups.half(3, far_cp, y_cp).wait_send()
        over(18, out2, far2).wait_send()
        over(19, out_cp, far_cp).wait_send()
        for offset in (1, 2, 3):
            for ch in range(4):
                groups.quarter(*quarters(ch), offset).wait_send()
            groups.along(20, half, offset, place.z).wait_send()
        hidden.finish()


def back(
    lens, gcv, conv, kp, q, pt, wk72, spread, ones8, qs, do, kd, vz, kt, lse, delta, pay, hid,
    seq, w5, gpre, dep, wdep, smf, gbi,
):
    crows = 256
    rows = 512
    early = lambda s: jnp.minimum(s, 3)
    between = lambda s: jnp.minimum(jnp.maximum(s - 4, 0), 1)
    late = lambda s: jnp.maximum(s - 6, 0)
    which = lambda s: lax.div(late(s), 2)
    part = lambda s: lax.rem(late(s), 2)
    cblk = pl.BlockSpec((crows, HALF), lambda s, lens: (early(s), 0))
    mine = pl.BlockSpec((rows, 128), lambda s, lens: (part(s), which(s)))
    pair = pl.BlockSpec((LMAX, 128), lambda s, lens: (0, which(s)))
    stats = pl.BlockSpec((1, 8, rows), lambda s, lens: (which(s), 0, part(s)))
    full = pl.BlockSpec((rows, D), lambda s, lens: (between(s), 0))
    weight = lambda j: pl.BlockSpec((1, HALF, D), lambda s, lens: (j, 0, 0), pipeline_mode=pl.Buffered(1))
    block = (3, 2, 4, 80, HALF)
    pay = pay.reshape((2, 2) + block)
    mine_pay = pl.BlockSpec(
        (2, 1) + block, lambda s, lens: (0, half_index(), 0, 0, 0, 0, 0), pipeline_mode=pl.Buffered(1)
    )
    return pl.pallas_call(
        back_kernel,
        grid_spec=pltpu.PrefetchScalarGridSpec(
            num_scalar_prefetch=1,
            grid=(12,),
            in_specs=[
                cblk,
                once((ROWS + 32, HALF)),
                pl.BlockSpec((72, crows), lambda s, lens: (0, early(s))),
                cblk,
                cblk,
                once((72, HALF)),
                once((72, KW * HALF)),
                once((8, HALF)),
                mine,
                mine,
                pair,
                pair,
                pl.BlockSpec((128, LMAX), lambda s, lens: (which(s), 0)),
                stats,
                stats,
                HBM,
                mine_pay,
                once((ROWS, D)),
                once((LMAX + 2 * PAD, D)),
                weight(2),
                weight(4),
                full,
                full,
                once((KW, D)),
                once((8, D)),
                once((1, FF)),
            ],
            out_specs=[
                cblk,
                pl.BlockSpec((128, rows), lambda s, lens: (which(s), part(s))),
                pair,
                pair,
                full,
                once((16, D)),
                once((4, 80, HALF)),
                once((2, 80, HALF)),
                once((64, HALF)),
                HBM,
            ],
            scratch_shapes=[
                pltpu.VMEM((LMAX + 32, HALF), F32),
                pltpu.VMEM((HALF // 128, crows + 32, 128), F32),
                pltpu.VMEM((3, crows + 48, 128), F32),
                pltpu.VMEM((LMAX, 128), F32),
                pltpu.VMEM((LMAX, 128), F32),
                pltpu.VMEM((2,) + block, BF),
                pltpu.VMEM((2, 2, 4, 2, 80, HALF), BF),
                pltpu.VMEM((2, 4, 2, 80, HALF), BF),
                pltpu.VMEM((2, 4, 2, 80, HALF), BF),
                pltpu.VMEM((2, 3, 2, 80, HALF), BF),
                pltpu.VMEM((2, 2, 80, HALF), BF),
                pltpu.VMEM((2, 80, HALF), BF),
                pltpu.VMEM((4, 80, HALF), BF),
                pltpu.VMEM((ROWS + 64, HALF), BF),
                pltpu.VMEM((D // 128, rows + 32, 128), F32),
                pltpu.VMEM((D // 128, rows + 32, 128), F32),
                pltpu.VMEM((48, D), F32),
                pltpu.VMEM((HALF, D), F32),
                pltpu.VMEM((HALF, D), F32),
                pltpu.VMEM((72, HALF), F32),
                pltpu.VMEM((8, 128), F32),
                pltpu.VMEM((8, HALF), F32),
                pltpu.VMEM((16, D), F32),
                pltpu.VMEM((2, 2, 2, 4, 64, HALF), BF),
                pltpu.VMEM((2, 2, 4, 64, HALF), BF),
                pltpu.VMEM((2, 4, 80, HALF), BF),
                pltpu.VMEM((2, 4, 80, HALF), BF),
                pltpu.VMEM((4, 80, HALF), BF),
                pltpu.VMEM((4, 80, HALF), BF),
                pltpu.VMEM((3, 80, HALF), BF),
                pltpu.VMEM((2, 4, 64, HALF), BF),
                pltpu.VMEM((2, 4, 64, HALF), BF),
                pltpu.VMEM((4, 64, HALF), BF),
                pltpu.VMEM((4, 64, HALF), BF),
                pltpu.VMEM((3, 64, HALF), BF),
                pltpu.SemaphoreType.DMA((4,)),
                pltpu.SemaphoreType.DMA((4,)),
                pltpu.SemaphoreType.DMA((23,)),
                pltpu.SemaphoreType.DMA((23,)),
                pltpu.SemaphoreType.DMA,
                pltpu.SemaphoreType.DMA((2,)),
                pltpu.SemaphoreType.DMA((3,)),
            ],
        ),
        out_shape=[
            jax.ShapeDtypeStruct((ROWS, HALF), BF),
            jax.ShapeDtypeStruct((HALF, ROWS), BF),
            jax.ShapeDtypeStruct((LMAX, HALF), BF),
            jax.ShapeDtypeStruct((LMAX, HALF), BF),
            jax.ShapeDtypeStruct((ROWS, D), BF),
            jax.ShapeDtypeStruct((16, D), F32),
            jax.ShapeDtypeStruct((4, 80, HALF), BF),
            jax.ShapeDtypeStruct((2, 80, HALF), BF),
            jax.ShapeDtypeStruct((64, HALF), BF),
            jax.ShapeDtypeStruct((2, ROWS, HALF), BF),
        ],
        **comm_params("back", 4),
    )(
        lens, gcv, conv, kp, q, pt, wk72, spread, ones8, qs, do, kd, vz, kt, lse, delta, pay, pay, hid,
        seq, w5, w5, gpre, dep, wdep, smf, gbi,
    )


def norm_parts(x):
    xc = x - jnp.mean(x, axis=1, keepdims=True)
    inv = lax.rsqrt(jnp.mean(xc * xc, axis=1, keepdims=True) + EPS)
    return xc * inv, inv


def norm_back(up, normal, inv, gain):
    e = up * gain
    return inv * (e - jnp.mean(e, axis=1, keepdims=True) - normal * jnp.mean(e * normal, axis=1, keepdims=True))


def ffn_kernel(
    lens, ctx_ref, mix_ref, tok_ref, cot_ref, wd_ref, wi_ref, wo_ref, v0, v1, v2, v3, v4, v5, bi_ref, ones_ref,
    hid_ref, gpre_ref, gctx_ref, gcv_ref, del_ref, pay_ref, sm_ref, gbi_ref,
    act_s, gp_s, awd, awi, awo,
):
    i = pl.program_id(0)
    rows = ctx_ref.shape[0]
    keep = row_ids(half_index() * ROWS + i * rows, rows) < length(lens)

    @pl.when(i == 0)
    def _():
        clear(awd)
        for g in range(2):
            clear(awi.at[g])
            clear(awo.at[g])
        sm_ref[...] = jnp.zeros_like(sm_ref)
        gbi_ref[...] = jnp.zeros_like(gbi_ref)

    vectors = [line(ref) for ref in (v0, v1, v2, v3, v4, v5)]
    vec = lambda k: vectors[k]
    inter_bias = line(bi_ref)
    h = tok_ref[...].astype(F32)
    ctx = ctx_ref[...]
    mixed = jnp.concatenate([ctx, mix_ref[...]], axis=1)
    n1, inv1 = norm_parts(nn(mixed, wd_ref[...]) + vec(0) + h)
    f1 = n1 * vec(1) + vec(2)
    fl = f1.astype(BF)
    chunk = 512
    outs = []
    for g in range(2):
        fg = fl[:, g * HALF : (g + 1) * HALF]
        for ch in range(GW // chunk):
            cols = slice(ch * chunk, (ch + 1) * chunk)
            put = slice(g * GW + ch * chunk, g * GW + (ch + 1) * chunk)
            x = nn(fg, wi_ref[g, :, cols]) + inter_bias[:, put]
            phi = 0.5 + 0.5 * lax.erf(x * 0.7071067811865476)
            act_s[:, put] = (x * phi).astype(BF)
            gp_s[:, put] = phi + x * jnp.exp2(x * x * (-0.5 * LOG2E)) * 0.3989422804014327
        outs.append(nn(act_s[:, g * GW : (g + 1) * GW], wo_ref[g]))
    n2, inv2 = norm_parts(jnp.concatenate(outs, axis=1) + vec(3) + f1)
    hid_ref[...] = (n2 * vec(4) + vec(5)).astype(BF)
    u = jnp.where(keep, cot_ref[...].astype(F32), 0.0)
    gp2 = norm_back(u, n2, inv2, vec(4))
    go = gp2.astype(BF)
    got = go.T
    flt = fl.T
    gfs = []
    for g in range(2):
        sel = slice(g * HALF, (g + 1) * HALF)
        gf = gp2[:, sel]
        for ch in range(GW // chunk):
            cols = slice(ch * chunk, (ch + 1) * chunk)
            put = slice(g * GW + ch * chunk, g * GW + (ch + 1) * chunk)
            gi = (gp_s[:, put] * nt(go[:, sel], wo_ref[g, cols, :])).astype(BF)
            gbi_ref[0:1, put] += col_sum(gi.astype(F32))
            awo[g, :, cols] += nn(got[sel], act_s[:, put])
            awi[g, :, cols] += nn(flt[sel], gi)
            gf = gf + nt(gi, wi_ref[g, :, cols])
        gfs.append(gf)
    gf = jnp.concatenate(gfs, axis=1)
    gpre = norm_back(gf, n1, inv1, vec(1))
    gd = gpre.astype(BF)
    gpre_ref[...] = gd
    sm_ref[0:1, :] += col_sum(go.astype(F32))
    sm_ref[1:2, :] += col_sum(u * n2)
    sm_ref[2:3, :] += col_sum(u)
    sm_ref[3:4, :] += col_sum(gd.astype(F32))
    sm_ref[4:5, :] += col_sum(gf * n1)
    sm_ref[5:6, :] += col_sum(gf)
    awd[...] += nn(mixed.T, gd)
    gm = nt(gd, wd_ref[...])
    gctx = gm[:, :HALF].astype(BF)
    gctx_ref[...] = gctx
    gcv_ref[...] = gm[:, HALF:].astype(BF)
    prod = (gctx.astype(F32) * ctx.astype(F32)).astype(BF)
    del_ref[...] = nt(ones_ref[...], prod).reshape(3, 8, rows)

    @pl.when(i == pl.num_programs(0) - 1)
    def _():
        for r in range(2):
            for c in range(2):
                pay_ref[r, c, 0:HALF, :] = awi[r, :, c * D : c * D + HALF].astype(BF)
                pay_ref[r, c, HALF:D, :] = awi[r, :, c * D + HALF : (c + 1) * D].astype(BF)
                pay_ref[r, c, D : 2 * D, :] = awo[r, :, c * D : (c + 1) * D].T.astype(BF)
                for part in range(2):
                    piece = awd[part * HALF + c * 192 : part * HALF + (c + 1) * 192, r * HALF : (r + 1) * HALF]
                    pay_ref[r, c, 2 * D + part * 192 : 2 * D + (part + 1) * 192, :] = piece.astype(BF)


def ffn(lens, ctx, mix, tok, cot, wd, wi, wo, vectors, bi, ones24):
    rows = 512
    blk = lambda w: pl.BlockSpec((rows, w), lambda i, lens: (i, 0))
    return pl.pallas_call(
        ffn_kernel,
        grid_spec=pltpu.PrefetchScalarGridSpec(
            num_scalar_prefetch=1,
            grid=(ROWS // rows,),
            in_specs=[
                blk(HALF),
                blk(HALF),
                blk(D),
                blk(D),
                once((D, D)),
                once((2, HALF, GW)),
                once((2, GW, HALF)),
                *[whole((D,))] * 6,
                whole((FF,)),
                whole((24, HALF)),
            ],
            out_specs=[
                blk(D),
                blk(D),
                blk(HALF),
                blk(HALF),
                pl.BlockSpec((3, 8, rows), lambda i, lens: (0, 0, i)),
                once((2, 2, FFN_ROWS, HALF)),
                whole((8, D)),
                whole((1, FF)),
            ],
            scratch_shapes=[
                pltpu.VMEM((rows, FF), BF),
                pltpu.VMEM((rows, FF), F32),
                pltpu.VMEM((D, D), F32),
                pltpu.VMEM((2, HALF, GW), F32),
                pltpu.VMEM((2, HALF, GW), F32),
            ],
        ),
        out_shape=[
            jax.ShapeDtypeStruct((ROWS, D), BF),
            jax.ShapeDtypeStruct((ROWS, D), BF),
            jax.ShapeDtypeStruct((ROWS, HALF), BF),
            jax.ShapeDtypeStruct((ROWS, HALF), BF),
            jax.ShapeDtypeStruct((3, 8, ROWS), F32),
            jax.ShapeDtypeStruct((2, 2, FFN_ROWS, HALF), BF),
            jax.ShapeDtypeStruct((8, D), F32),
            jax.ShapeDtypeStruct((1, FF), F32),
        ],
        **params("ffn"),
    )(lens, ctx, mix, tok, cot, wd, wi, wo, *vectors, bi, ones24)


def tail_kernel(
    lens, seq_ref, dk_ref, dv_ref, dq_ref, gqm_ref, ghm_ref, edge_ref, w_ref, half0, pieces, piece_cp,
    big_ref, cp_ref, sum_ref, ght_ref,
    agw, accb, sm, tsend, trecv, gho, halves, other, half_cp, last_cp,
    pay, total_sum, near, far, out, mid, ybuf, zsum, s, v, ns, nr, cs, cr, gs, gr, es, er, ls, hs, hr,
):
    step = pl.program_id(0)
    i = lax.rem(step, 4)
    p = Place()
    r, c = p.r, p.c
    rows = dk_ref.shape[0]
    b = lax.rem((1 - c) * 2 + i, 4)
    n = lens[r]
    groups = Groups(p, gs, gr)
    chunks = 5
    crows = PROJ_ROWS // chunks
    summed = Sum(p, far, mid, ybuf, zsum, total_sum, crows, s, v)
    places = [FromRows(p, gho.at[k], ght_ref.at[k], ls.at[k], hs.at[k], hr.at[k]) for k in range(2)]

    def theirs(k):
        return send(tsend.at[k], trecv.at[k], es.at[k], er.at[k], p.core)

    def part(ch):
        return slice(ch * crows, (ch + 1) * crows)

    def beside(k, ch):
        rr = 1 - r if k == 0 else r
        at = k * chunks + ch
        return send(pay.at[rr, 1 - c, part(ch), :], near.at[rr, part(ch), :], ns.at[at], nr.at[at], p.core)

    def cross(ch):
        return send(out.at[part(ch), :], far.at[part(ch), :], cs.at[ch], cr.at[ch], p.across)

    def arrive(ch):
        beside(1, ch).wait_recv()
        cross(ch).wait_recv()
        total = near[r, part(ch), :].astype(F32) + pay[r, c, part(ch), :].astype(F32)
        far[part(ch), :] = (total + far[part(ch), :].astype(F32)).astype(BF)
        summed.half(ch)

    stages = [
        arrive,
        summed.quarter,
        lambda ch: summed.along(ch, summed.collect(ch)),
        summed.back,
        summed.finish_spread,
    ]

    def tick(t):
        for k, stage in enumerate(stages):
            if 0 <= t - k < chunks:
                stage(t - k)

    halfs = [half0, halves.at[0], halves.at[1], half_cp]
    others = [other.at[0], other.at[1], other.at[2], last_cp]

    def back(k, z):
        return groups.back(9 + 4 * k + z, halfs[k].at[z], others[k].at[z])

    @pl.when(step == 0)
    def _():
        meet(everyone(p))
        groups.start_along(0, halves.at[0], pieces[0])
        groups.start_along(3, halves.at[1], pieces[1])
        groups.start_along(6, half_cp, piece_cp[...])
        for z in range(4):
            back(0, z).start()
        for j in range(3):
            clear(agw.at[j])
        sm[...] = jnp.zeros_like(sm)

    @pl.when(step == 4)
    def _():
        for ch in range(chunks):
            beside(0, ch).wait_recv()
            total = near[1 - r, part(ch), :].astype(F32) + pay[1 - r, c, part(ch), :].astype(F32)
            out[part(ch), :] = total.astype(BF)
            cross(ch).start()

    @pl.when(step == 5)
    def _():
        groups.await_along(0, halves.at[0])
        back(1, 0).start()
        back(1, 1).start()

    @pl.when(step == 6)
    def _():
        tick(0)
        back(1, 2).start()
        back(1, 3).start()

    @pl.when(step == 7)
    def _():
        tick(1)

    keep = row_ids(b * rows, rows) < n

    def query_grad():
        return (dq_ref[...].astype(F32) + gqm_ref[...].astype(F32).T).astype(BF)

    @pl.when(step < 4)
    def _():
        tok = seq_ref[rows_at(PAD + b * rows, rows), :]
        h = jnp.where(keep, tok.astype(F32), 0.0).astype(BF)
        agw[0] += nn(dk_ref[...].T, h)
        agw[1] += nn(dv_ref[...].T, h)
        sm[1:2, :] += col_sum(dv_ref[...].astype(F32))

        @pl.when(step >= 2)
        def _():
            gqt = query_grad()
            sm[0:1, :] += col_sum(gqt.T.astype(F32))
            agw[2] += nn(gqt, h)

    @pl.when(step == 3)
    def _():
        for rr in range(2):
            for cc in range(2):
                for j in range(3):
                    piece = agw[j, cc * 192 : (cc + 1) * 192, rr * HALF : (rr + 1) * HALF]
                    pay[rr, cc, j * 192 : (j + 1) * 192, :] = piece.astype(BF)
                pay[rr, cc, 576:, :] = jnp.concatenate([sm[...], jnp.zeros((56, HALF), F32)], axis=0).astype(BF)
        for ch in range(chunks):
            for k in range(2):
                beside(k, ch).start()

    @pl.when(step >= 4)
    def _():
        accb[...] = nn(dk_ref[...], w_ref[0]) + nn(dv_ref[...], w_ref[1])

        @pl.when(step >= 6)
        def _():
            accb[...] += nn(query_grad().T, w_ref[3]) + ghm_ref[...].astype(F32)

    for k in range(2):

        @pl.when((step == 4 + k) & (c == k))
        def _():
            at = slice(0, 16) if k == 0 else slice(rows - 16, rows)
            accb[at, :] += edge_ref[...]

        @pl.when(step == 4 + k)
        def _():
            tsend[k] = jnp.where(keep, accb[...], 0.0).astype(BF)
            theirs(k).start()

        @pl.when(step == 6 + k)
        def _():
            theirs(k).wait_recv()
            gho[k] = jnp.where(keep, accb[...] + trecv[k].astype(F32), 0.0).astype(BF)
            places[k].start()

    @pl.when(step == 7)
    def _():
        tick(2)
        groups.await_along(3, halves.at[1])
        back(2, 0).start()
        back(2, 1).start()
        tick(3)
        back(2, 2).start()
        back(2, 3).start()
        tick(4)
        groups.await_along(6, half_cp)
        back(3, 0).start()
        back(3, 1).start()
        tick(5)
        back(3, 2).start()
        back(3, 3).start()
        tick(6)
        for ch in range(2):
            for z in range(4):
                back(ch, z).wait_recv()
        big_ref[0, p.y] = half0[...]
        big_ref[0, 1 - p.y] = other[0]
        big_ref[1, p.y] = halves[0]
        big_ref[1, 1 - p.y] = other[1]
        tick(7)
        for z in range(4):
            back(3, z).wait_recv()
        cp_ref[p.y] = half_cp[...]
        cp_ref[1 - p.y] = last_cp[...]
        tick(8)
        sum_ref[...] = total_sum[...]
        for z in range(4):
            back(2, z).wait_recv()
        big_ref[2, p.y] = halves[1]
        big_ref[2, 1 - p.y] = other[2]
        for ch in range(chunks):
            summed.finish_sum(ch)
            cross(ch).wait_send()
            for k in range(2):
                beside(k, ch).wait_send()
        for k in range(4):
            for z in range(4):
                back(k, z).wait_send()
        for offset in (1, 2, 3):
            groups.along(0, halves.at[0], offset, p.z).wait_send()
            groups.along(3, halves.at[1], offset, p.z).wait_send()
            groups.along(6, half_cp, offset, p.z).wait_send()
        theirs(0).wait_send()
        theirs(1).wait_send()
        places[0].finish()
        places[1].finish()


def tail(lens, seq_tok, dk, dv, dq, gqm, ghm, edge, w5, half0, pieces, piece_cp):
    rows = 512
    mine = lambda s: jnp.maximum(lax.rem(s, 4) - 2, 0)
    seq = pl.BlockSpec((rows, HALF), lambda s, lens: (lax.rem((1 - half_index()) * 2 + s, 4), 0))
    own = lambda w: pl.BlockSpec((rows, w), lambda s, lens: (mine(s), 0))
    crows = PROJ_ROWS // 5
    return pl.pallas_call(
        tail_kernel,
        grid_spec=pltpu.PrefetchScalarGridSpec(
            num_scalar_prefetch=1,
            grid=(8,),
            in_specs=[
                once((LMAX + 2 * PAD, D)),
                seq,
                seq,
                pl.BlockSpec((HALF, rows), lambda s, lens: (0, mine(s))),
                own(HALF),
                own(D),
                once((16, D)),
                once((5, HALF, D)),
                once((4, 80, HALF)),
                once((2, 80, HALF)),
                once((64, HALF)),
            ],
            out_specs=[
                once((3, 2, 4, 80, HALF)),
                once((2, 4, 64, HALF)),
                once((PROJ_ROWS, HALF)),
                HBM,
            ],
            scratch_shapes=[
                pltpu.VMEM((3, HALF, D), F32),
                pltpu.VMEM((rows, D), F32),
                pltpu.VMEM((8, HALF), F32),
                pltpu.VMEM((2, rows, D), BF),
                pltpu.VMEM((2, rows, D), BF),
                pltpu.VMEM((2, rows, D), BF),
                pltpu.VMEM((2, 4, 80, HALF), BF),
                pltpu.VMEM((3, 4, 80, HALF), BF),
                pltpu.VMEM((4, 64, HALF), BF),
                pltpu.VMEM((4, 64, HALF), BF),
                pltpu.VMEM((2, 2, PROJ_ROWS, HALF), BF),
                pltpu.VMEM((PROJ_ROWS, HALF), BF),
                pltpu.VMEM((2, PROJ_ROWS, HALF), BF),
                pltpu.VMEM((PROJ_ROWS, HALF), BF),
                pltpu.VMEM((PROJ_ROWS, HALF), BF),
                *Sum.scratch(crows, 5),
                pltpu.SemaphoreType.DMA((10,)),
                pltpu.SemaphoreType.DMA((10,)),
                pltpu.SemaphoreType.DMA((5,)),
                pltpu.SemaphoreType.DMA((5,)),
                pltpu.SemaphoreType.DMA((25,)),
                pltpu.SemaphoreType.DMA((25,)),
                pltpu.SemaphoreType.DMA((2,)),
                pltpu.SemaphoreType.DMA((2,)),
                pltpu.SemaphoreType.DMA((2,)),
                pltpu.SemaphoreType.DMA((2, 2)),
                pltpu.SemaphoreType.DMA((2, 3)),
            ],
        ),
        out_shape=[
            jax.ShapeDtypeStruct((3, 2, 4, 80, HALF), BF),
            jax.ShapeDtypeStruct((2, 4, 64, HALF), BF),
            jax.ShapeDtypeStruct((PROJ_ROWS, HALF), BF),
            jax.ShapeDtypeStruct((2, 2, rows, HALF), BF),
        ],
        **comm_params("tail", 6),
    )(lens, seq_tok, dk, dv, dq, gqm, ghm, edge, w5, half0, pieces, piece_cp)


def outputs_kernel(
    ght, hid, t0, t1, t2, t3, t4, big_i0, big_i1, big_o, big_d, little, late_ref, perm_ref,
    hid_ref, gt_ref, gk_ref, gv_ref, gc_ref, gq_ref, gp_ref, gi_ref, go_ref, gd_ref,
    gdep_ref, gbq_ref, gbv_ref, gbc_ref, gbp_ref, gwk_ref, gbk_ref,
    gbd_ref, gg1_ref, gb1_ref, gbi_ref, gbo_ref, gg2_ref, gb2_ref,
):
    i = pl.program_id(0)
    hid_ref[...] = hid[...]
    gt_ref[...] = ght[0, 0].astype(F32)

    for src, ref in ((t0, gk_ref), (t1, gv_ref), (t2, gq_ref), (t3, gc_ref), (t4, gp_ref), (big_o, go_ref), (big_d, gd_ref)):
        ref[...] = src[...].astype(F32)
    gi_ref[:, 0:HALF] = big_i0[...].astype(F32)
    gi_ref[:, HALF:D] = big_i1[...].astype(F32)

    @pl.when(i == 0)
    def _():
        mixed = little[72:80, :].astype(F32)
        low = little[80:88, :].astype(F32)
        high = little[88:96, :].astype(F32)
        inter = little[96:104, :].astype(F32)
        late = late_ref[0:16, :].astype(F32)
        gwk_ref[...] = nn(perm_ref[...], little[0:72, :])
        bias = nt(mixed[:, 0:72].astype(BF), perm_ref[...])
        gbk_ref[...] = bias[2:3, :].reshape(54)
        for k, ref in enumerate((gbq_ref, gbv_ref)):
            ref[...] = late[k : k + 1, :].reshape(HALF)
        for k, ref in enumerate((gbc_ref, gbp_ref)):
            ref[...] = mixed[k : k + 1, :].reshape(HALF)
        for k, ref in enumerate((gbo_ref, gg2_ref, gb2_ref, gbd_ref, gg1_ref, gb1_ref)):
            ref[...] = jnp.concatenate([low[k : k + 1, :], high[k : k + 1, :]], axis=1).reshape(D)
        gbi_ref[...] = jnp.concatenate([inter[k : k + 1, :] for k in range(8)], axis=1).reshape(FF)
        gdep_ref[0:8, 0:HALF] = little[104:112, :].astype(F32)
        gdep_ref[0:8, HALF:D] = little[112:120, :].astype(F32)
        gdep_ref[8:9, 0:HALF] = mixed[3:4, :]
        gdep_ref[8:9, HALF:D] = mixed[4:5, :]


def outputs(ght, hid, total, cp, big, perm):
    rows = 512
    at = lambda n, first: pl.BlockSpec((n, HALF), lambda i: (first + i, 0))
    blk = at(rows, 0)
    chunk = pl.BlockSpec((1, 1, rows, HALF), lambda i: (lax.rem(i, 2), lax.div(i, 2), 0, 0))
    shapes = [(KW, D)] + [(HALF,)] * 4 + [(54, HALF), (54,)] + [(D,)] * 3 + [(FF,)] + [(D,)] * 3
    main = [(192, HALF)] * 5 + [(HALF, D), (D, HALF), (HALF, HALF)]
    return pl.pallas_call(
        outputs_kernel,
        grid=(4,),
        in_specs=[chunk, blk]
        + [at(48, 4 * j) for j in (0, 1, 2, 0, 1)]
        + [at(96, 0), at(96, 4), at(192, 4), at(96, 16)]
        + [pl.BlockSpec((128, HALF), lambda i: (3, 0)), pl.BlockSpec((64, HALF), lambda i: (9, 0)), whole((54, 72))],
        out_specs=[blk, blk]
        + [at(48, 0)] * 5
        + [pl.BlockSpec((96, D), lambda i: (i, 0)), at(192, 0), at(96, 0)]
        + [whole(shape) for shape in shapes],
        out_shape=[jax.ShapeDtypeStruct((LMAX, HALF), BF), jax.ShapeDtypeStruct((LMAX, HALF), F32)]
        + [jax.ShapeDtypeStruct(shape, F32) for shape in main + shapes],
        **params("outputs"),
    )(ght, hid, total, total, total, cp, cp, big, big, big, big, cp, total, perm)


def constants():
    ones8 = np.zeros((8, HALF), np.float32)
    ones24 = np.zeros((24, HALF), np.float32)
    perm = np.zeros((72, 54), np.float32)
    for head in range(6):
        cols = slice(head * HD, (head + 1) * HD)
        ones8[head, cols] = 1
        ones24[head // 2 * 8 + head % 2, cols] = 1
        for j in range(KW):
            perm[j * 8 + head, head * KW + j] = 1
    return [jnp.asarray(a, BF) for a in (ones8, ones24, perm)]


def per_device(
    groups, tokens, cotangent, seq_lengths, w_query, w_key, w_value, w_convout, w_point, w_depth,
    b_query, b_value, b_convout, b_point, w_kernel, b_kernel, w_dense, b_dense, gain_one, bias_one,
    w_inter, b_inter, w_output, b_output, gain_two, bias_two,
):
    lens = seq_lengths
    ones8, ones24, perm = constants()
    wdep = w_depth.T

    kd, kt, vz, q, qs, pt, kp, conv, mix, dep, hown, wk72, bk72, spread, ctx, lse, seq, w5, wi, wd, cot, wo = front(
        lens, tokens, (w_key.T, w_value.T, w_convout.T, w_query.T, w_point.T), w_kernel.T, b_kernel, perm,
        wdep, b_value, b_convout, b_query, b_point,
        w_inter[0], w_dense.reshape(2, 192, HALF), w_output[0], cotangent,
    )
    vectors = (b_dense, gain_one, bias_one, b_output, gain_two, bias_two)
    hid, gpre, gctx, gcv, delta, payf, smf, gbi = ffn(
        lens, ctx, mix, hown, cot, wd.reshape(D, D), wi, wo, vectors, b_inter, ones24
    )
    gqm, dq, dk, dv, ghm, edge, half0, pieces, piece_cp, hid = back(
        lens, gcv, conv, kp, q, pt, wk72, spread, ones8, qs, gctx, kd, vz, kt, lse, delta, payf, hid,
        seq, w5, gpre, dep, wdep, smf, gbi,
    )
    big, cp, total, ght = tail(lens, seq, dk, dv, dq, gqm, ghm, edge, w5, half0, pieces, piece_cp)
    big = big.reshape(FFN_ROWS, HALF)
    cp = cp.reshape(512, HALF)
    if groups > 8:
        sums = lax.psum(tuple(x.astype(F32) * 0.125 for x in (total, cp, big)), "dp")
        total, cp, big = (x.astype(BF) for x in sums)
    (
        hidden_out, gt, gk, gv, gc, gq, gp, gi, go, gd, gdep, gbq, gbv, gbc, gbp, gwk, gbk, gbd, gg1, gb1, gbi, gbo, gg2, gb2,
    ) = outputs(ght, hid.reshape(LMAX, HALF), total, cp, big, perm.T)
    return (
        hidden_out, gt, gq.T, gk.T, gv.T, gc.T, gp.T, gdep.T, gbq, gbv, gbc, gbp, gwk.T, gbk, gd, gbd, gg1, gb1,
        gi[None], gbi, go[None], gbo, gg2, gb2,
    )


def solution(mesh):
    act = P(("dp", "col"), "row")
    rep = P()
    proj = P("row", "col")
    in_specs = (
        act, act, P("dp"), proj, proj, proj, proj, proj, rep, rep, rep, rep, rep, rep, rep, P("col", "row"),
        rep, rep, rep, P("row", None, "col"), rep, P("row", "col", None), rep, rep, rep,
    )
    out_specs = (
        act, act, proj, proj, proj, proj, proj, rep, rep, rep, rep, rep, rep, rep, P("col", "row"),
        rep, rep, rep, P("row", None, "col"), rep, P("row", "col", None), rep, rep, rep,
    )
    return jax.shard_map(
        functools.partial(per_device, mesh.shape["dp"]), mesh=mesh, in_specs=in_specs, out_specs=out_specs, check_vma=False)
```

```python
import functools

import jax
import jax.numpy as jnp
import numpy as np
from jax import lax
from jax.experimental import pallas as pl
from jax.experimental.pallas import tpu as pltpu
from jax.sharding import PartitionSpec as P

D = 768
HALF = 384
HD = 64
KW = 9
FF = 3072
GW = 1536
LMAX = 2048
ROWS = 1024
EPS = 1e-12
LOG2E = 1.4426950408889634
LN2 = 0.6931471805599453
BF = jnp.bfloat16
F32 = jnp.float32
VMEM_BYTES = 63 * 1024 * 1024
PAD = 16
FFN_ROWS = 1920
FFN_CHUNK = 640
PROJ_ROWS = 640
MESH = pl.DeviceIdType.MESH
HBM = pl.BlockSpec(memory_space=pl.ANY)
VMEM = pl.BlockSpec(memory_space=pltpu.VMEM)


def nn(a, b):
    return lax.dot_general(a, b, (((1,), (0,)), ((), ())), preferred_element_type=F32)


def nt(a, b):
    return lax.dot_general(a, b, (((1,), (1,)), ((), ())), preferred_element_type=F32)


def col_sum(x):
    return jnp.sum(x, axis=0, keepdims=True)


def row_ids(start, rows):
    return start + lax.broadcasted_iota(jnp.int32, (rows, 1), 0)


def whole(shape):
    return pl.BlockSpec(shape, lambda *_: (0,) * len(shape))


def once(shape):
    return pl.BlockSpec(shape, lambda *_: (0,) * len(shape), pipeline_mode=pl.Buffered(1))


def half_index():
    return lax.axis_index("col")


def length(lens):
    return lens[lax.axis_index("row")]


def line(ref):
    return ref[...].astype(F32).reshape(1, ref.shape[0])


def spread_taps(probs, spread_ref, t):
    taps = []
    for j in range(0, KW, 2):
        count = min(2, KW - j)
        at = (t * KW + j) * 128
        both = nn(probs, spread_ref[:, at : at + count * 128])
        taps += [both[:, k * 128 : (k + 1) * 128] for k in range(count)]
    return taps


def clear(ref, step=32):
    def body(k, carry):
        ref[pl.ds(pl.multiple_of(k * step, step), step), :] = jnp.zeros((step, ref.shape[1]), ref.dtype)
        return carry

    lax.fori_loop(0, ref.shape[0] // step, body, 0)


def put_tiles(buf, value, first=0):
    for t in range(value.shape[1] // 128):
        buf[t, first : first + value.shape[0], :] = value[:, t * 128 : (t + 1) * 128]


def params(name):
    return dict(
        name=name,
        compiler_params=pltpu.CompilerParams(vmem_limit_bytes=VMEM_BYTES),
    )


def lanes(k, width=HALF):
    return pl.ds(pl.multiple_of(k * width, 128), width)


def rows_at(start, count, step=16):
    return pl.ds(pl.multiple_of(start, step), count)


def send(src, dst, send_sem, recv_sem, device):
    return pltpu.make_async_remote_copy(
        src_ref=src, dst_ref=dst, send_sem=send_sem, recv_sem=recv_sem, device_id=device, device_id_type=MESH
    )


class Place:
    def __init__(self):
        self.d = lax.axis_index("dp")
        self.r = lax.axis_index("row")
        self.c = lax.axis_index("col")
        self.k = lax.rem(self.d, 8)
        self.base = self.d - self.k
        self.y = lax.rem(self.k, 2)
        self.z = lax.div(self.k, 2)
        self.beside = {"dp": self.base + self.z * 2 + 1 - self.y}
        self.across = {"row": 1 - self.r}
        self.core = {"col": 1 - self.c}
        self.diagonal = {"row": 1 - self.r, "col": 1 - self.c}

    def eight(self, offset):
        other = lax.rem(self.k + offset, 8)
        return other, {"dp": self.base + other}

    def four(self, offset):
        other = lax.rem(self.z + offset, 4)
        return other, {"dp": self.base + other * 2 + self.y}


def meet(devices):
    barrier = pltpu.get_barrier_semaphore()
    for device in devices:
        pl.semaphore_signal(barrier, inc=1, device_id=device, device_id_type=MESH)
    pl.semaphore_wait(barrier, len(devices))


def comm_params(name, number):
    return dict(
        name=name,
        compiler_params=pltpu.CompilerParams(
            vmem_limit_bytes=VMEM_BYTES, collective_id=number, has_side_effects=True
        ),
    )


class Gather:
    def __init__(self, place, own, full, part, block, step, send_sem, recv_sem, first):
        self.p, self.own, self.full, self.part, self.block, self.h = place, own, full, part, block, step
        self.s, self.v, self.f = send_sem, recv_sem, first

    def _move(self, src, dst, n, device):
        return send(src, dst, self.s.at[self.f + n], self.v.at[self.f + n], device)

    def _cross(self, r):
        p = self.p
        at = (p.y * 4 + p.z) * self.h
        return self._move(self.part(self.own, at, self.h), self.block(self.full, r, p.c, at, self.h), 0, p.across)

    def _near(self, c):
        p = self.p
        return self._move(self.own, self.block(self.full, p.r, c, 0, 8 * self.h), 1, p.core)

    def _pass(self, offset, z):
        p = self.p
        here = self.block(self.full, 1 - p.r, p.c, (p.y * 4 + z) * self.h, self.h)
        return self._move(here, here, 1 + offset, p.four(offset)[1])

    def _turn(self, y):
        p = self.p
        here = self.block(self.full, 1 - p.r, p.c, y * 4 * self.h, 4 * self.h)
        return self._move(here, here, 5, p.beside)

    def _last(self, c):
        p = self.p
        here = self.block(self.full, 1 - p.r, c, 0, 8 * self.h)
        return self._move(here, here, 6, p.core)

    def start(self):
        self._cross(self.p.r).start()
        self._near(self.p.c).start()

    def relay(self):
        p = self.p
        self._cross(1 - p.r).wait_recv()
        for offset in (1, 2, 3):
            self._pass(offset, p.z).start()

    def turn(self):
        p = self.p
        for offset in (1, 2, 3):
            self._pass(offset, lax.rem(p.z + 4 - offset, 4)).wait_recv()
        self._turn(p.y).start()

    def share(self):
        p = self.p
        self._turn(1 - p.y).wait_recv()
        self._last(p.c).start()

    def finish(self):
        p = self.p
        self._last(1 - p.c).wait_recv()
        self._near(1 - p.c).wait_recv()
        self._cross(p.r).wait_send()
        self._near(p.c).wait_send()
        for offset in (1, 2, 3):
            self._pass(offset, p.z).wait_send()
        self._turn(p.y).wait_send()
        self._last(p.c).wait_send()


def middle_part(ref, first, rows):
    return ref.at[:, rows_at(first, rows, 8), :]


def middle_block(ref, r, c, first, rows):
    return ref.at[:, rows_at(c * 192 + first, rows, 8), lanes(r)]


def rows_part(ref, first, rows):
    return ref.at[rows_at(first, rows), :]


def inter_block(ref, r, c, first, rows):
    return ref.at[r, rows_at(first, rows), lanes(c, 768)]


def output_block(ref, r, c, first, rows):
    return ref.at[r, rows_at(c * 768 + first, rows), :]


class ToRows:
    def __init__(self, place, src, dst, stage, local_sem, send_sem, recv_sem):
        self.p, self.src, self.dst, self.stage = place, src, dst, stage
        self.l, self.s, self.v = local_sem, send_sem, recv_sem

    def _cross(self, q, k):
        half = self.src.at[q * ROWS : (q + 1) * ROWS, :]
        return send(half, self.dst.at[:, lanes(k)], self.s.at[q], self.v.at[0], {"row": 1 - self.p.r, "col": q})

    def _near(self):
        p = self.p
        half = self.src.at[rows_at((1 - p.c) * ROWS, ROWS), :]
        return send(half, self.dst.at[:, lanes(p.r)], self.s.at[2], self.v.at[1], p.core)

    def _load(self):
        return pltpu.make_async_copy(self.src.at[rows_at(self.p.c * ROWS, ROWS), :], self.stage, self.l.at[0])

    def _store(self):
        return pltpu.make_async_copy(self.stage, self.dst.at[:, lanes(self.p.r)], self.l.at[1])

    def start(self):
        p = self.p

        @pl.when(p.r != p.c)
        def _():
            self._cross(0, p.r).start()
            self._cross(1, p.r).start()

        @pl.when(p.r == p.c)
        def _():
            self._near().start()
            self._load().start()

    def store(self):
        @pl.when(self.p.r == self.p.c)
        def _():
            self._load().wait()
            self._store().start()

    def finish(self):
        p = self.p
        self._cross(0, 1 - p.r).wait_recv()

        @pl.when(p.r != p.c)
        def _():
            self._cross(0, p.r).wait_send()
            self._cross(1, p.r).wait_send()
            self._near().wait_recv()

        @pl.when(p.r == p.c)
        def _():
            self._near().wait_send()
            self._store().wait()


class FromRows:
    def __init__(self, place, src, dst, local_sem, send_sem, recv_sem):
        self.p, self.src, self.dst = place, src, dst
        self.l, self.s, self.v = local_sem, send_sem, recv_sem

    def _cross(self, q):
        p = self.p
        place = self.dst.at[q]
        return send(self.src.at[:, lanes(1 - p.r)], place, self.s.at[0], self.v.at[q], {"row": 1 - p.r, "col": p.r})

    def _near(self, q):
        p = self.p
        place = self.dst.at[q]
        return send(self.src.at[:, lanes(p.r)], place, self.s.at[1], self.v.at[2], p.core)

    def _local(self):
        p = self.p
        place = self.dst.at[p.c]
        return pltpu.make_async_copy(self.src.at[:, lanes(p.r)], place, self.l)

    def start(self):
        p = self.p
        self._cross(p.c).start()

        @pl.when(p.r != p.c)
        def _():
            self._near(p.c).start()

        @pl.when(p.r == p.c)
        def _():
            self._local().start()

    def finish(self):
        p = self.p
        self._cross(p.c).wait_send()

        @pl.when(p.r != p.c)
        def _():
            self._near(p.c).wait_send()
            self._cross(0).wait_recv()
            self._cross(1).wait_recv()

        @pl.when(p.r == p.c)
        def _():
            self._near(1 - p.c).wait_recv()
            self._local().wait()


class Sum:
    def __init__(self, place, far, mid, ybuf, zbuf, total, rows, s, v, first=0):
        self.p, self.far, self.mid, self.ybuf, self.zbuf, self.total = place, far, mid, ybuf, zbuf, total
        self.rows, self.s, self.v, self.first = rows, s, v, first

    def _sems(self, ch, n):
        i = self.first + ch * 8 + n
        return self.s.at[i], self.v.at[i]

    def _beside(self):
        return self.p.beside

    def _halves(self, ch, y):
        return rows_at(ch * self.rows + y * (self.rows // 2), self.rows // 2)

    def _piece(self, ch, z):
        return rows_at(ch * self.rows + self.p.y * (self.rows // 2) + z * (self.rows // 8), self.rows // 8)

    def _half(self, ch):
        return send(self.far.at[self._halves(ch, 1 - self.p.y), :], self.ybuf.at[ch], *self._sems(ch, 0), self._beside())

    def _quarter(self, ch, offset):
        other, device = self.p.four(offset)
        src = self.mid.at[ch, rows_at(other * (self.rows // 8), self.rows // 8), :]
        return send(src, self.zbuf.at[ch, offset - 1], *self._sems(ch, offset), device)

    def _along(self, ch, offset, z):
        _, device = self.p.four(offset)
        here = self.total.at[self._piece(ch, z), :]
        return send(here, here, *self._sems(ch, 3 + offset), device)

    def _back(self, ch, y):
        here = self.total.at[self._halves(ch, y), :]
        return send(here, here, *self._sems(ch, 7), self._beside())

    def half(self, ch):
        self._half(ch).start()

    def quarter(self, ch):
        self._half(ch).wait_recv()
        both = self.far[self._halves(ch, self.p.y), :].astype(F32) + self.ybuf[ch].astype(F32)
        self.mid[ch] = both.astype(BF)
        for offset in (1, 2, 3):
            self._quarter(ch, offset).start()

    def collect(self, ch):
        both = self.mid[ch, rows_at(self.p.z * (self.rows // 8), self.rows // 8), :].astype(F32)
        for offset in (1, 2, 3):
            self._quarter(ch, offset).wait_recv()
            both = both + self.zbuf[ch, offset - 1].astype(F32)
        return both.astype(BF)

    def along(self, ch, piece):
        self.total[self._piece(ch, self.p.z), :] = piece
        for offset in (1, 2, 3):
            self._along(ch, offset, self.p.z).start()

    def back(self, ch):
        for offset in (1, 2, 3):
            self._along(ch, offset, lax.rem(self.p.z + 4 - offset, 4)).wait_recv()
        self._back(ch, self.p.y).start()

    def finish_sum(self, ch):
        self._half(ch).wait_send()
        for offset in (1, 2, 3):
            self._quarter(ch, offset).wait_send()

    def finish_spread(self, ch):
        self._back(ch, 1 - self.p.y).wait_recv()
        for offset in (1, 2, 3):
            self._along(ch, offset, self.p.z).wait_send()
        self._back(ch, self.p.y).wait_send()

    @staticmethod
    def scratch(rows, chunks):
        return [
            pltpu.VMEM((chunks, rows // 2, HALF), BF),
            pltpu.VMEM((chunks, rows // 2, HALF), BF),
            pltpu.VMEM((chunks, 3, rows // 8, HALF), BF),
            pltpu.SemaphoreType.DMA((8 * chunks,)),
            pltpu.SemaphoreType.DMA((8 * chunks,)),
        ]


class Groups:
    def __init__(self, place, s, v):
        self.p, self.s, self.v = place, s, v

    def half(self, n, mine, ybuf):
        return send(mine.at[1 - self.p.y], ybuf, self.s.at[n], self.v.at[n], self.p.beside)

    def quarter(self, n, mid, zbuf, offset):
        other, device = self.p.four(offset)
        n = n + offset - 1
        return send(mid.at[other], zbuf.at[offset - 1], self.s.at[n], self.v.at[n], device)

    def cross(self, n, both, xbuf):
        return send(both.at[1 - self.p.r], xbuf, self.s.at[n], self.v.at[n], self.p.across)

    def along(self, n, half, offset, z):
        n = n + offset - 1
        return send(half.at[z], half.at[z], self.s.at[n], self.v.at[n], self.p.four(offset)[1])

    def back(self, n, half, other):
        return send(half, other, self.s.at[n], self.v.at[n], self.p.beside)

    def start_quarters(self, n, mid, zbuf):
        for offset in (1, 2, 3):
            self.quarter(n, mid, zbuf, offset).start()

    def collect(self, n, mid, zbuf, both):
        total = mid[self.p.z].astype(F32)
        for offset in (1, 2, 3):
            self.quarter(n, mid, zbuf, offset).wait_recv()
            total = total + zbuf[offset - 1].astype(F32)
        both[...] = total.astype(BF)

    def start_along(self, n, half, piece):
        half[self.p.z] = piece
        for offset in (1, 2, 3):
            self.along(n, half, offset, self.p.z).start()

    def await_along(self, n, half):
        for offset in (1, 2, 3):
            self.along(n, half, offset, lax.rem(self.p.z + 4 - offset, 4)).wait_recv()

    def sent(self, n, ref, kind):
        for offset in (1, 2, 3):
            kind(n, *ref, offset).wait_send()


def everyone(p):
    return [p.across, p.core, p.diagonal, p.beside] + [p.four(o)[1] for o in (1, 2, 3)]


def front_kernel(
    lens, tok_ref, wk_own, wv_own, wc_own, wq_own, wp_own, kern_ref, kb_ref, perm_ref,
    wdep_ref, bv_ref, bc_ref, bq_ref, bp_ref, wi_own, wd_own, wo_own, cot_own,
    kd_ref, kt_ref, vz_ref, q_ref, qs_ref, pt_ref, kp_ref, conv_ref, mix_ref, dep_ref, h_ref, wk_ref, bk_ref, spread_ref,
    ctx_ref, lse_ref, seq_out, w5_out, wi_ref, wd_ref, cot_ref, wo_ref,
    own, seq_ref, w_ref, stage, first_key, hbuf, cbuf, lsem, ts, tr, gs, gr, cs, cr,
):
    i = pl.program_id(0)
    p = Place()
    r, c = p.r, p.c
    n = lens[r]
    proj = Gather(p, own, w_ref, middle_part, middle_block, 24, gs, gr, 0)
    inter = Gather(p, wi_own, wi_ref, rows_part, inter_block, 48, gs, gr, 7)
    dense = Gather(p, wd_own, wd_ref, middle_part, middle_block, 24, gs, gr, 14)
    cot_rows = ToRows(p, cot_own, cot_ref, stage, lsem, cs, cr)
    output = Gather(p, wo_own, wo_ref, rows_part, output_block, 96, gs, gr, 21)
    keep_output = pltpu.make_async_copy(wo_own, output_block(wo_ref, r, c, 0, D), lsem.at[7])
    keep_inter = pltpu.make_async_copy(wi_own, inter_block(wi_ref, r, c, 0, HALF), lsem.at[2])
    keep_dense = pltpu.make_async_copy(wd_own, middle_block(wd_ref, r, c, 0, 192), lsem.at[3])
    keep_own = pltpu.make_async_copy(tok_ref, seq_ref.at[PAD : PAD + LMAX, lanes(r)], lsem.at[4])
    keep_seq = pltpu.make_async_copy(seq_ref, seq_out, lsem.at[5])
    keep_w = pltpu.make_async_copy(w_ref, w5_out, lsem.at[6])

    def chunk(m, k):
        return seq_ref.at[PAD + m * 512 : PAD + (m + 1) * 512, lanes(k)]

    def cross(m, k):
        return send(tok_ref.at[m * 512 : (m + 1) * 512, :], chunk(m, k), ts.at[m], tr.at[m], {"row": 1 - r, "col": m // 2})

    def near(k):
        return send(tok_ref, seq_ref.at[PAD : PAD + LMAX, lanes(k)], ts.at[4], tr.at[4], p.core)

    def forward(m):
        return send(chunk(m, 1 - r), chunk(m, 1 - r), ts.at[5 + m], tr.at[5 + m], p.core)

    @pl.when(i == 0)
    def _():
        for j, ref in enumerate((wk_own, wv_own, wc_own, wq_own, wp_own)):
            own[j] = ref[...]
        seq_ref[0:PAD, :] = jnp.zeros((PAD, D), BF)
        seq_ref[PAD + LMAX :, :] = jnp.zeros((PAD, D), BF)
        meet(everyone(p))
        proj.start()
        inter._cross(r).start()
        dense._cross(r).start()
        output._cross(r).start()

        @pl.when(r != c)
        def _():
            for m in (0, 2, 1, 3):
                cross(m, r).start()

        @pl.when(r == c)
        def _():
            near(r).start()
            keep_own.start()

        cot_rows.start()
        inter._near(c).start()
        dense._near(c).start()
        output._near(c).start()
        keep_inter.start()
        keep_dense.start()
        keep_output.start()
        middle_block(w_ref, r, c, 0, 192)[...] = own[...]
        wk_ref[...] = nn(perm_ref[...], kern_ref[...]).astype(BF)
        bk_ref[...] = nt(perm_ref[...], jnp.broadcast_to(line(kb_ref), (128, 54)).astype(BF))
        row = lax.broadcasted_iota(jnp.int32, (72, 128), 0)
        head = lax.broadcasted_iota(jnp.int32, (72, 128), 1) >> 6
        for t in range(HALF // 128):
            for j in range(KW):
                at = (t * KW + j) * 128
                spread_ref[:, at : at + 128] = jnp.where(row == head + (j * 8 + 2 * t), 1.0, 0.0).astype(BF)
        proj.relay()
        proj.turn()
        inter.relay()
        dense.relay()
        output.relay()
        for q in range(2):

            @pl.when(c == q)
            def _():
                for m in (2 * q, 2 * q + 1):
                    cross(m, 1 - r).wait_recv()
                    forward(m).start()

        proj.share()
        for q in range(2):

            @pl.when(c == q)
            def _():
                for m in (2 - 2 * q, 3 - 2 * q):
                    forward(m).wait_recv()
                for m in (2 * q, 2 * q + 1):
                    forward(m).wait_send()

        @pl.when(r != c)
        def _():
            for m in range(4):
                cross(m, r).wait_send()
            near(r).wait_recv()

        @pl.when(r == c)
        def _():
            near(r).wait_send()
            keep_own.wait()

        proj.finish()
        keep_seq.start()
        keep_w.start()

    @pl.when(i == 1)
    def _():
        inter.turn()
        dense.turn()
        cot_rows.store()

    @pl.when(i == 2)
    def _():
        output.turn()

    @pl.when(i == 4)
    def _():
        inter.share()
        dense.share()

    @pl.when(i == 5)
    def _():
        output.share()

    @pl.when(i < 4)
    def _():
        krows = LMAX // 4
        keep_key = row_ids(i * krows, krows) < n
        tok = seq_ref[rows_at(PAD + i * krows, krows), :]
        h = jnp.where(keep_key, tok.astype(F32), 0.0).astype(BF)
        k = nt(h, w_ref[0])
        v = nt(h, w_ref[1]) + line(bv_ref)

        @pl.when(i == 0)
        def _():
            first_key[...] = k[0:8]

        kd_ref[rows_at(i * krows, krows), :] = jnp.where(keep_key, k, first_key[0:1]).astype(BF)
        kt_ref[...] = k.T.astype(BF)
        vz_ref[rows_at(i * krows, krows), :] = jnp.where(keep_key, v, 0.0).astype(BF)

        rows = q_ref.shape[0]
        wide = rows + 32
        base = pl.multiple_of(i * rows, 16)
        start = pl.multiple_of(c * ROWS + i * rows, 16)
        ids = row_ids(start - 16, wide)
        keep = (ids >= 0) & (ids < n)
        hw = jnp.where(keep, seq_ref[pl.ds(start, wide), :].astype(F32), 0.0)
        put_tiles(hbuf, hw)
        wdep = wdep_ref[...].astype(F32)
        for t in range(D // 128):
            cols = slice(t * 128, (t + 1) * 128)
            depth = jnp.zeros((rows, 128), F32)
            for j in range(KW):
                depth = depth + hbuf[t, 12 + j : 12 + j + rows, :] * wdep[j : j + 1, cols]
            dep_ref[:, cols] = depth.astype(BF)
        depth_low = dep_ref[...]
        hl = hw.astype(BF)
        h_ref[...] = hl[16 : 16 + rows]
        conv = jnp.where(keep, nt(hl, w_ref[2]) + line(bc_ref), 0.0)
        put_tiles(cbuf, conv)
        conv_ref[pl.ds(base, wide), :] = conv.astype(BF)
        q = nt(hl[16 : 16 + rows], w_ref[3]) + line(bq_ref)
        q_low = q.astype(BF)
        q_ref[...] = q_low
        qs_ref[pl.ds(base, rows), :] = (q * (0.125 * LOG2E)).astype(BF)
        pt = nt(depth_low, w_ref[4]) + line(bp_ref)
        pt_ref[...] = pt.astype(BF)
        mixer = (pt * q_low.astype(F32)).astype(BF)
        logits = (nt(wk_ref[...], mixer) + bk_ref[:, 0:1]).reshape(KW, 8, rows)
        peak = jnp.max(logits, axis=0, keepdims=True)
        raised = jnp.exp(logits - peak)
        kp = (raised / jnp.sum(raised, axis=0, keepdims=True)).reshape(KW * 8, rows)
        kp_ref[...] = kp
        kpt = kp.T.astype(BF)
        for t in range(HALF // 128):
            mix = jnp.zeros((rows, 128), F32)
            for j, tap in enumerate(spread_taps(kpt, spread_ref, t)):
                mix = mix + tap * cbuf[t, 12 + j : 12 + j + rows, :]
            mix_ref[:, t * 128 : (t + 1) * 128] = mix.astype(BF)

    @pl.when(i >= 4)
    def _():
        cols = lanes(i - 4, 128)
        k = kd_ref[:, cols]
        ones = jnp.where(row_ids(0, LMAX) < n, 1.0, 0.0)
        ve = jnp.concatenate([vz_ref[:, cols], jnp.broadcast_to(ones, (LMAX, 128)).astype(BF)], axis=1)
        rows = 256
        lane = lax.broadcasted_iota(jnp.int32, (rows, 128), 1)
        for u in range(ROWS // rows):
            part = slice(u * rows, (u + 1) * rows)
            outs = []
            for hh in range(2):
                q = jnp.where((lane < HD) == (hh == 0), qs_ref[part, cols], jnp.zeros((), BF))
                s = nt(q, k)
                peak = jnp.max(s, axis=1, keepdims=True)
                prob = jnp.exp2(s - peak).astype(BF)
                o = nn(prob, ve)
                outs.append(o[:, :128] / o[:, 128:])
                lse_ref[0, hh : hh + 1, part] = (peak + jnp.log2(o[:, 128:129])).T
            ctx_ref[part, :] = jnp.where(lane < HD, outs[0], outs[1]).astype(BF)

    @pl.when(i == pl.num_programs(0) - 1)
    def _():
        inter.finish()
        dense.finish()
        output.finish()
        cot_rows.finish()
        keep_inter.wait()
        keep_dense.wait()
        keep_output.wait()
        keep_seq.wait()
        keep_w.wait()


def front(lens, tokens, weights, w_kernel, b_kernel, perm, wdep, bv, bc, bq, bp, w_inter, w_dense, w_output, cotangent):
    rows = 256
    early = lambda i: jnp.minimum(i, 3)
    late = lambda i: jnp.maximum(i - 4, 0)
    blk = pl.BlockSpec((rows, HALF), lambda i, lens: (early(i), 0))
    full = pl.BlockSpec((rows, D), lambda i, lens: (early(i), 0))
    half = jax.ShapeDtypeStruct((ROWS, HALF), BF)
    return pl.pallas_call(
        front_kernel,
        grid_spec=pltpu.PrefetchScalarGridSpec(
            num_scalar_prefetch=1,
            grid=(7,),
            in_specs=[HBM]
            + [once((192, HALF))] * 5
            + [once((54, HALF)), whole((54,)), once((72, 54)), once((KW, D))]
            + [whole((HALF,))] * 4
            + [once((HALF, D)), once((2, 192, HALF)), once((D, HALF)), HBM],
            out_specs=[
                once((LMAX, HALF)),
                pl.BlockSpec((HALF, LMAX // 4), lambda i, lens: (0, early(i))),
                once((LMAX, HALF)),
                blk,
                once((ROWS, HALF)),
                blk,
                pl.BlockSpec((72, rows), lambda i, lens: (0, early(i))),
                once((ROWS + 32, HALF)),
                blk,
                full,
                full,
                whole((72, HALF)),
                whole((72, 128)),
                once((72, KW * HALF)),
                pl.BlockSpec((ROWS, 128), lambda i, lens: (0, late(i))),
                pl.BlockSpec((1, 8, ROWS), lambda i, lens: (late(i), 0, 0)),
            ]
            + [HBM] * 6,
            scratch_shapes=[
                pltpu.VMEM((5, 192, HALF), BF),
                pltpu.VMEM((LMAX + 2 * PAD, D), BF),
                pltpu.VMEM((5, HALF, D), BF),
                pltpu.VMEM((ROWS, HALF), BF),
                pltpu.VMEM((8, HALF), F32),
                pltpu.VMEM((D // 128, rows + 32, 128), F32),
                pltpu.VMEM((HALF // 128, rows + 32, 128), F32),
                pltpu.SemaphoreType.DMA((8,)),
                pltpu.SemaphoreType.DMA((9,)),
                pltpu.SemaphoreType.DMA((9,)),
                pltpu.SemaphoreType.DMA((28,)),
                pltpu.SemaphoreType.DMA((28,)),
                pltpu.SemaphoreType.DMA((3,)),
                pltpu.SemaphoreType.DMA((2,)),
            ],
        ),
        out_shape=[
            jax.ShapeDtypeStruct((LMAX, HALF), BF),
            jax.ShapeDtypeStruct((HALF, LMAX), BF),
            jax.ShapeDtypeStruct((LMAX, HALF), BF),
            half,
            half,
            half,
            jax.ShapeDtypeStruct((72, ROWS), F32),
            jax.ShapeDtypeStruct((ROWS + 32, HALF), BF),
            half,
            jax.ShapeDtypeStruct((ROWS, D), BF),
            jax.ShapeDtypeStruct((ROWS, D), BF),
            jax.ShapeDtypeStruct((72, HALF), BF),
            jax.ShapeDtypeStruct((72, 128), F32),
            jax.ShapeDtypeStruct((72, KW * HALF), BF),
            half,
            jax.ShapeDtypeStruct((3, 8, ROWS), F32),
            jax.ShapeDtypeStruct((LMAX + 2 * PAD, D), BF),
            jax.ShapeDtypeStruct((5, HALF, D), BF),
            jax.ShapeDtypeStruct((2, HALF, GW), BF),
            jax.ShapeDtypeStruct((2, HALF, D), BF),
            jax.ShapeDtypeStruct((ROWS, D), BF),
            jax.ShapeDtypeStruct((2, GW, HALF), BF),
        ],
        **comm_params("front", 2),
    )(
        lens, tokens, *weights, w_kernel, b_kernel, perm, wdep, bv, bc, bq, bp, w_inter, w_dense, w_output, cotangent
    )


def back_kernel(
    lens, gcv_ref, conv_ref, kp_ref, q_ref, pt_ref, wk_ref, spread_ref, ones_ref,
    qs_ref, do_ref, k_ref, v_ref, kt_ref, lse_ref, del_ref, pay_all, pay_ref, hid_ref,
    seq_ref, wc_ref, wp_ref, gpre_ref, dep_ref, wdep_ref, smf_ref, gbi_ref,
    gqm_ref, dq_ref, dk_ref, dv_ref, ghm_ref, edge_ref, half_ref, piece_ref, piece_cp_ref, out_ref,
    acc, wbuf, tbuf, dka, dva, near, mine, ybuf, mid, zbuf, both, xbuf, half,
    gpad, dbuf, hwin, sbuf, agc, agp, gwk, gbk, sm, gdp, pcp, near_cp,
    out2, far2, y2, mid2, z2, out_cp, far_cp, y_cp, mid_cp, z_cp,
    ns, nr, s, v_sem, ls, hs, hr,
):
    step = pl.program_id(0)
    place = Place()
    n = lens[place.r]
    groups = Groups(place, s, v_sem)
    hidden = FromRows(place, hid_ref, out_ref, ls, hs, hr)

    def near_copy(k):
        rr = 1 - place.r if k % 2 == 0 else place.r
        src, dst = (pay_all, near) if k < 2 else (pcp, near_cp)
        return send(src.at[rr, 1 - place.c], dst.at[rr], ns.at[k], nr.at[k], place.core)

    def over(k, src, dst):
        return send(src, dst, s.at[k], v_sem.at[k], place.across)

    @pl.when(step == 0)
    def _():
        meet(everyone(place))
        near_copy(0).start()
        near_copy(1).start()
        hidden.start()
        for ref in (acc, agc, agp):
            clear(ref)
        for ref in (tbuf, gwk, gbk, sm, gdp):
            ref[...] = jnp.zeros_like(ref)
        gpad[0:32, :] = jnp.zeros((32, HALF), BF)
        gpad[32 + ROWS :, :] = jnp.zeros((32, HALF), BF)

    @pl.when(step == 2)
    def _():
        near_copy(0).wait()
        near_copy(1).wait()
        there = 1 - place.r
        out2[...] = (near[there, 2].astype(F32) + pay_ref[there, 0, 2].astype(F32)).astype(BF)
        over(18, out2, far2).start()
        for ch in range(2):
            for rr in range(2):
                total = near[rr, ch].astype(F32) + pay_ref[rr, 0, ch].astype(F32)
                mine[ch, :, :, rr] = total.astype(BF)
            groups.half(ch, mine.at[ch], ybuf.at[ch]).start()

    def settle(ch):
        groups.half(ch, mine.at[ch], ybuf.at[ch]).wait_recv()
        mid[ch] = (mine[ch, place.y].astype(F32) + ybuf[ch].astype(F32)).astype(BF)

    def merge(ch):
        groups.cross(16 + ch, both.at[ch], xbuf.at[ch]).wait_recv()
        return (both[ch, place.r].astype(F32) + xbuf[ch].astype(F32)).astype(BF)

    def quarters(ch):
        if ch < 2:
            return 4 + 3 * ch, mid.at[ch], zbuf.at[ch]
        return (10, mid2, z2) if ch == 2 else (13, mid_cp, z_cp)

    @pl.when(step == 6)
    def _():
        settle(0)
        groups.start_quarters(*quarters(0))
        near_copy(2).start()
        near_copy(3).start()

    @pl.when(step == 7)
    def _():
        near_copy(2).wait()
        near_copy(3).wait()
        there = 1 - place.r
        out_cp[...] = (near_cp[there].astype(F32) + pcp[there, place.c].astype(F32)).astype(BF)
        over(19, out_cp, far_cp).start()

    @pl.when(step == 8)
    def _():
        settle(1)
        groups.start_quarters(*quarters(1))
        groups.collect(*quarters(0), both.at[0])
        groups.cross(16, both.at[0], xbuf.at[0]).start()
        over(18, out2, far2).wait_recv()
        here = near[place.r, 2].astype(F32) + pay_ref[place.r, 0, 2].astype(F32)
        far2[...] = (here + far2[...].astype(F32)).astype(BF)
        groups.half(2, far2, y2).start()

    @pl.when(step == 9)
    def _():
        groups.start_along(20, half, merge(0))
        over(19, out_cp, far_cp).wait_recv()
        here = near_cp[place.r].astype(F32) + pcp[place.r, place.c].astype(F32)
        far_cp[...] = (here + far_cp[...].astype(F32)).astype(BF)
        groups.half(3, far_cp, y_cp).start()

    @pl.when(step == 10)
    def _():
        groups.collect(*quarters(1), both.at[1])
        groups.cross(17, both.at[1], xbuf.at[1]).start()
        groups.half(2, far2, y2).wait_recv()
        mid2[...] = (far2[place.y].astype(F32) + y2[...].astype(F32)).astype(BF)
        groups.start_quarters(*quarters(2))

    @pl.when(step == 11)
    def _():
        piece_ref[0] = merge(1)
        groups.half(3, far_cp, y_cp).wait_recv()
        mid_cp[...] = (far_cp[place.y].astype(F32) + y_cp[...].astype(F32)).astype(BF)
        groups.start_quarters(*quarters(3))

    @pl.when(step < 4)
    def _():
        rows = gcv_ref.shape[0]
        wide = rows + 32
        put_tiles(wbuf, conv_ref[pl.ds(pl.multiple_of(step * rows, 16), wide), :].astype(F32))
        kp = kp_ref[...]
        kpt = kp.T.astype(BF)
        gkps = [None] * KW
        there = pl.ds(pl.multiple_of(place.c * ROWS + step * rows, 16), wide)
        for t in range(HALF // 128):
            cols = slice(t * 128, (t + 1) * 128)
            gcv = gcv_ref[:, cols].astype(F32)
            total = jnp.zeros((wide, 128), F32)
            for j in range(KW):
                prod = (gcv * wbuf[t, 12 + j : 12 + j + rows, :]).astype(BF)
                part = nt(ones_ref[:, cols], prod)
                gkps[j] = part if t == 0 else gkps[j] + part
                at = (t * KW + j) * 128
                tbuf[j % 3, 24 : 24 + rows, :] = nn(kpt, spread_ref[:, at : at + 128]) * gcv
                total = total + tbuf[j % 3, 12 - j : 12 - j + wide, :]
            acc[there, cols] += total
        gkp = jnp.concatenate(gkps, axis=0).reshape(KW, 8, rows)
        kp3 = kp.reshape(KW, 8, rows)
        inner = jnp.sum(kp3 * gkp, axis=0, keepdims=True)
        gl = (kp3 * (gkp - inner)).reshape(KW * 8, rows)
        glt = gl.T.astype(BF)
        gbk[0:1, 0:72] += col_sum(glt.astype(F32))
        q = q_ref[...].astype(F32)
        pt = pt_ref[...].astype(F32)
        gwk[...] += nn(gl.astype(BF), (pt * q).astype(BF))
        gmix = nn(glt, wk_ref[...])
        gqm_ref[...] = (gmix * pt).astype(BF)
        gpad[rows_at(32 + step * rows, rows), :] = (gmix * q).astype(BF)

    def conv_grads(first, rows):
        keep = row_ids(first, rows) < n
        gco = jnp.where(keep, acc[rows_at(16 + first, rows), :], 0.0).astype(BF)
        tok = seq_ref[rows_at(PAD + first, rows), :]
        h = jnp.where(keep, tok.astype(F32), 0.0).astype(BF)
        agc[...] += nn(gco.T, h)
        sm[2:3, :] += col_sum(gco.astype(F32))
        return nn(gco, wc_ref[0])

    @pl.when(step == 4)
    def _():
        wdep = wdep_ref[...].astype(F32)
        at = pl.multiple_of((1 - place.c) * (ROWS + 16), 16)
        sbuf[...] = nn(gpad[pl.ds(at, 48), :], wp_ref[0])
        total = conv_grads(pl.multiple_of(ROWS - 16 * place.c, 16), 16)
        for j in range(KW):
            total = total + sbuf[20 - j : 36 - j, :] * wdep[j : j + 1, :]
        edge_ref[...] = total

    @pl.when((step == 4) | (step == 5))
    def _():
        m = step - 4
        rows = gpre_ref.shape[0]
        wide = rows + 32
        first = pl.multiple_of(place.c * ROWS + m * rows, 16)
        wdep = wdep_ref[...].astype(F32)
        win = gpad[rows_at(m * rows + 16, wide), :]
        gpt = win[16 : 16 + rows]
        sm[3:4, :] += col_sum(gpt.astype(F32))
        agp[...] += nn(gpt.T, dep_ref[...])
        put_tiles(dbuf, nn(win, wp_ref[0]))
        ids = row_ids(first - 16, wide)
        inside = (ids >= 0) & (ids < n)
        put_tiles(hwin, jnp.where(inside, seq_ref[pl.ds(first, wide), :].astype(F32), 0.0))
        ghm_ref[...] = (conv_grads(first, rows) + gpre_ref[...].astype(F32)).astype(BF)
        for t in range(D // 128):
            cols = slice(t * 128, (t + 1) * 128)

            def strip(k, sums):
                r0 = pl.multiple_of(k * 64, 64)
                gdep = dbuf[t, pl.ds(r0 + 16, 64), :]
                total = ghm_ref[pl.ds(r0, 64), cols].astype(F32)
                new = []
                for j in range(KW):
                    prod = gdep * hwin[t, pl.ds(r0 + 12 + j, 64), :]
                    new.append(sums[j] + jnp.sum(prod.reshape(8, 8, 128), axis=0))
                    total = total + dbuf[t, pl.ds(r0 + 20 - j, 64), :] * wdep[j : j + 1, cols]
                ghm_ref[pl.ds(r0, 64), cols] = total.astype(BF)
                return tuple(new)

            sums = lax.fori_loop(0, rows // 64, strip, (jnp.zeros((8, 128), F32),) * KW)
            for j in range(KW):
                gdp[j : j + 1, cols] += col_sum(sums[j])

    @pl.when(step == 5)
    def _():
        def put(r, c, first, value):
            pcp[r, c, first // 256, first // 64 % 4] = value.astype(BF)

        zeros = lambda k: jnp.zeros((k, HALF), F32)
        bias = jnp.concatenate([gbk[0:1, :], jnp.zeros((1, 256), F32)], axis=1)
        mixed = [sm[2:4, :], bias, gdp[8:9, 0:HALF], gdp[8:9, HALF:D], zeros(3)]
        inter = [gbi_ref[:, k * HALF : (k + 1) * HALF] for k in range(8)]
        norms = [smf_ref[:, 0:HALF], smf_ref[:, HALF:D]]
        depth = [gdp[0:8, 0:HALF], gdp[0:8, HALF:D], zeros(8)]
        little = jnp.concatenate([gwk[...]] + mixed + norms + inter + depth, axis=0)
        for r in range(2):
            for c in range(2):
                for k in range(3):
                    rows = slice(c * 192 + k * 64, c * 192 + (k + 1) * 64)
                    put(r, c, k * 64, agc[rows, r * HALF : (r + 1) * HALF])
                    put(r, c, 192 + k * 64, agp[rows, r * HALF : (r + 1) * HALF])
                put(r, c, 384, little[0:64])
                put(r, c, 448, little[64:128])

    @pl.when(step >= 6)
    def _():
        i = lax.rem(step, 2)
        k = k_ref[...]
        v = v_ref[...]
        rows = qs_ref.shape[0]
        lane = lax.broadcasted_iota(jnp.int32, (rows, 128), 1)
        dk = dv = None
        for hh in range(2):
            head = (lane < HD) == (hh == 0)
            q = jnp.where(head, qs_ref[...], jnp.zeros((), BF))
            do = jnp.where(head, do_ref[...], jnp.zeros((), BF))
            p = jnp.exp2(nt(k, q) - lse_ref[0, hh : hh + 1, :])
            ds = (p * (nt(v, do) - del_ref[0, hh : hh + 1, :])).astype(BF)
            dv_one = nn(p.astype(BF), do)
            dk_one = nn(ds, q)
            dv = dv_one if dv is None else dv + dv_one
            dk = dk_one if dk is None else dk + dk_one
            dq_ref[hh * HD : (hh + 1) * HD, :] = (nn(kt_ref[hh * HD : (hh + 1) * HD, :], ds) * 0.125).astype(BF)

        @pl.when(i == 0)
        def _():
            dka[...] = dk
            dva[...] = dv

        @pl.when(i == 1)
        def _():
            keep = row_ids(0, LMAX) < n
            dk_ref[...] = jnp.where(keep, (dka[...] + dk) * LN2, 0.0).astype(BF)
            dv_ref[...] = jnp.where(keep, dva[...] + dv, 0.0).astype(BF)

    @pl.when(step == 11)
    def _():
        groups.collect(*quarters(2), piece_ref.at[1])
        groups.collect(*quarters(3), piece_cp_ref)
        groups.await_along(20, half)
        half_ref[...] = half[...]
        for ch in range(2):
            groups.half(ch, mine.at[ch], ybuf.at[ch]).wait_send()
            groups.cross(16 + ch, both.at[ch], xbuf.at[ch]).wait_send()
        groups.half(2, far2, y2).wait_send()
        groups.half(3, far_cp, y_cp).wait_send()
        over(18, out2, far2).wait_send()
        over(19, out_cp, far_cp).wait_send()
        for offset in (1, 2, 3):
            for ch in range(4):
                groups.quarter(*quarters(ch), offset).wait_send()
            groups.along(20, half, offset, place.z).wait_send()
        hidden.finish()


def back(
    lens, gcv, conv, kp, q, pt, wk72, spread, ones8, qs, do, kd, vz, kt, lse, delta, pay, hid,
    seq, w5, gpre, dep, wdep, smf, gbi,
):
    crows = 256
    rows = 512
    early = lambda s: jnp.minimum(s, 3)
    between = lambda s: jnp.minimum(jnp.maximum(s - 4, 0), 1)
    late = lambda s: jnp.maximum(s - 6, 0)
    which = lambda s: lax.div(late(s), 2)
    part = lambda s: lax.rem(late(s), 2)
    cblk = pl.BlockSpec((crows, HALF), lambda s, lens: (early(s), 0))
    mine = pl.BlockSpec((rows, 128), lambda s, lens: (part(s), which(s)))
    pair = pl.BlockSpec((LMAX, 128), lambda s, lens: (0, which(s)))
    stats = pl.BlockSpec((1, 8, rows), lambda s, lens: (which(s), 0, part(s)))
    full = pl.BlockSpec((rows, D), lambda s, lens: (between(s), 0))
    weight = lambda j: pl.BlockSpec((1, HALF, D), lambda s, lens: (j, 0, 0), pipeline_mode=pl.Buffered(1))
    block = (3, 2, 4, 80, HALF)
    pay = pay.reshape((2, 2) + block)
    mine_pay = pl.BlockSpec(
        (2, 1) + block, lambda s, lens: (0, half_index(), 0, 0, 0, 0, 0), pipeline_mode=pl.Buffered(1)
    )
    return pl.pallas_call(
        back_kernel,
        grid_spec=pltpu.PrefetchScalarGridSpec(
            num_scalar_prefetch=1,
            grid=(12,),
            in_specs=[
                cblk,
                once((ROWS + 32, HALF)),
                pl.BlockSpec((72, crows), lambda s, lens: (0, early(s))),
                cblk,
                cblk,
                once((72, HALF)),
                once((72, KW * HALF)),
                once((8, HALF)),
                mine,
                mine,
                pair,
                pair,
                pl.BlockSpec((128, LMAX), lambda s, lens: (which(s), 0)),
                stats,
                stats,
                HBM,
                mine_pay,
                once((ROWS, D)),
                once((LMAX + 2 * PAD, D)),
                weight(2),
                weight(4),
                full,
                full,
                once((KW, D)),
                once((8, D)),
                once((1, FF)),
            ],
            out_specs=[
                cblk,
                pl.BlockSpec((128, rows), lambda s, lens: (which(s), part(s))),
                pair,
                pair,
                full,
                once((16, D)),
                once((4, 80, HALF)),
                once((2, 80, HALF)),
                once((64, HALF)),
                HBM,
            ],
            scratch_shapes=[
                pltpu.VMEM((LMAX + 32, HALF), F32),
                pltpu.VMEM((HALF // 128, crows + 32, 128), F32),
                pltpu.VMEM((3, crows + 48, 128), F32),
                pltpu.VMEM((LMAX, 128), F32),
                pltpu.VMEM((LMAX, 128), F32),
                pltpu.VMEM((2,) + block, BF),
                pltpu.VMEM((2, 2, 4, 2, 80, HALF), BF),
                pltpu.VMEM((2, 4, 2, 80, HALF), BF),
                pltpu.VMEM((2, 4, 2, 80, HALF), BF),
                pltpu.VMEM((2, 3, 2, 80, HALF), BF),
                pltpu.VMEM((2, 2, 80, HALF), BF),
                pltpu.VMEM((2, 80, HALF), BF),
                pltpu.VMEM((4, 80, HALF), BF),
                pltpu.VMEM((ROWS + 64, HALF), BF),
                pltpu.VMEM((D // 128, rows + 32, 128), F32),
                pltpu.VMEM((D // 128, rows + 32, 128), F32),
                pltpu.VMEM((48, D), F32),
                pltpu.VMEM((HALF, D), F32),
                pltpu.VMEM((HALF, D), F32),
                pltpu.VMEM((72, HALF), F32),
                pltpu.VMEM((8, 128), F32),
                pltpu.VMEM((8, HALF), F32),
                pltpu.VMEM((16, D), F32),
                pltpu.VMEM((2, 2, 2, 4, 64, HALF), BF),
                pltpu.VMEM((2, 2, 4, 64, HALF), BF),
                pltpu.VMEM((2, 4, 80, HALF), BF),
                pltpu.VMEM((2, 4, 80, HALF), BF),
                pltpu.VMEM((4, 80, HALF), BF),
                pltpu.VMEM((4, 80, HALF), BF),
                pltpu.VMEM((3, 80, HALF), BF),
                pltpu.VMEM((2, 4, 64, HALF), BF),
                pltpu.VMEM((2, 4, 64, HALF), BF),
                pltpu.VMEM((4, 64, HALF), BF),
                pltpu.VMEM((4, 64, HALF), BF),
                pltpu.VMEM((3, 64, HALF), BF),
                pltpu.SemaphoreType.DMA((4,)),
                pltpu.SemaphoreType.DMA((4,)),
                pltpu.SemaphoreType.DMA((23,)),
                pltpu.SemaphoreType.DMA((23,)),
                pltpu.SemaphoreType.DMA,
                pltpu.SemaphoreType.DMA((2,)),
                pltpu.SemaphoreType.DMA((3,)),
            ],
        ),
        out_shape=[
            jax.ShapeDtypeStruct((ROWS, HALF), BF),
            jax.ShapeDtypeStruct((HALF, ROWS), BF),
            jax.ShapeDtypeStruct((LMAX, HALF), BF),
            jax.ShapeDtypeStruct((LMAX, HALF), BF),
            jax.ShapeDtypeStruct((ROWS, D), BF),
            jax.ShapeDtypeStruct((16, D), F32),
            jax.ShapeDtypeStruct((4, 80, HALF), BF),
            jax.ShapeDtypeStruct((2, 80, HALF), BF),
            jax.ShapeDtypeStruct((64, HALF), BF),
            jax.ShapeDtypeStruct((2, ROWS, HALF), BF),
        ],
        **comm_params("back", 4),
    )(
        lens, gcv, conv, kp, q, pt, wk72, spread, ones8, qs, do, kd, vz, kt, lse, delta, pay, pay, hid,
        seq, w5, w5, gpre, dep, wdep, smf, gbi,
    )


def norm_parts(x):
    xc = x - jnp.mean(x, axis=1, keepdims=True)
    inv = lax.rsqrt(jnp.mean(xc * xc, axis=1, keepdims=True) + EPS)
    return xc * inv, inv


def norm_back(up, normal, inv, gain):
    e = up * gain
    return inv * (e - jnp.mean(e, axis=1, keepdims=True) - normal * jnp.mean(e * normal, axis=1, keepdims=True))


def ffn_kernel(
    lens, ctx_ref, mix_ref, tok_ref, cot_ref, wd_ref, wi_ref, wo_ref, v0, v1, v2, v3, v4, v5, bi_ref, ones_ref,
    hid_ref, gpre_ref, gctx_ref, gcv_ref, del_ref, pay_ref, sm_ref, gbi_ref,
    act_s, gp_s, awd, awi, awo,
):
    i = pl.program_id(0)
    rows = ctx_ref.shape[0]
    keep = row_ids(half_index() * ROWS + i * rows, rows) < length(lens)

    @pl.when(i == 0)
    def _():
        clear(awd)
        for g in range(2):
            clear(awi.at[g])
            clear(awo.at[g])
        sm_ref[...] = jnp.zeros_like(sm_ref)
        gbi_ref[...] = jnp.zeros_like(gbi_ref)

    vectors = [line(ref) for ref in (v0, v1, v2, v3, v4, v5)]
    vec = lambda k: vectors[k]
    inter_bias = line(bi_ref)
    h = tok_ref[...].astype(F32)
    ctx = ctx_ref[...]
    mixed = jnp.concatenate([ctx, mix_ref[...]], axis=1)
    n1, inv1 = norm_parts(nn(mixed, wd_ref[...]) + vec(0) + h)
    f1 = n1 * vec(1) + vec(2)
    fl = f1.astype(BF)
    chunk = 512
    outs = []
    for g in range(2):
        fg = fl[:, g * HALF : (g + 1) * HALF]
        for ch in range(GW // chunk):
            cols = slice(ch * chunk, (ch + 1) * chunk)
            put = slice(g * GW + ch * chunk, g * GW + (ch + 1) * chunk)
            x = nn(fg, wi_ref[g, :, cols]) + inter_bias[:, put]
            phi = 0.5 + 0.5 * lax.erf(x * 0.7071067811865476)
            act_s[:, put] = (x * phi).astype(BF)
            gp_s[:, put] = phi + x * jnp.exp2(x * x * (-0.5 * LOG2E)) * 0.3989422804014327
        outs.append(nn(act_s[:, g * GW : (g + 1) * GW], wo_ref[g]))
    n2, inv2 = norm_parts(jnp.concatenate(outs, axis=1) + vec(3) + f1)
    hid_ref[...] = (n2 * vec(4) + vec(5)).astype(BF)
    u = jnp.where(keep, cot_ref[...].astype(F32), 0.0)
    gp2 = norm_back(u, n2, inv2, vec(4))
    go = gp2.astype(BF)
    got = go.T
    flt = fl.T
    gfs = []
    for g in range(2):
        sel = slice(g * HALF, (g + 1) * HALF)
        gf = gp2[:, sel]
        for ch in range(GW // chunk):
            cols = slice(ch * chunk, (ch + 1) * chunk)
            put = slice(g * GW + ch * chunk, g * GW + (ch + 1) * chunk)
            gi = (gp_s[:, put] * nt(go[:, sel], wo_ref[g, cols, :])).astype(BF)
            gbi_ref[0:1, put] += col_sum(gi.astype(F32))
            awo[g, :, cols] += nn(got[sel], act_s[:, put])
            awi[g, :, cols] += nn(flt[sel], gi)
            gf = gf + nt(gi, wi_ref[g, :, cols])
        gfs.append(gf)
    gf = jnp.concatenate(gfs, axis=1)
    gpre = norm_back(gf, n1, inv1, vec(1))
    gd = gpre.astype(BF)
    gpre_ref[...] = gd
    sm_ref[0:1, :] += col_sum(go.astype(F32))
    sm_ref[1:2, :] += col_sum(u * n2)
    sm_ref[2:3, :] += col_sum(u)
    sm_ref[3:4, :] += col_sum(gd.astype(F32))
    sm_ref[4:5, :] += col_sum(gf * n1)
    sm_ref[5:6, :] += col_sum(gf)
    awd[...] += nn(mixed.T, gd)
    gm = nt(gd, wd_ref[...])
    gctx = gm[:, :HALF].astype(BF)
    gctx_ref[...] = gctx
    gcv_ref[...] = gm[:, HALF:].astype(BF)
    prod = (gctx.astype(F32) * ctx.astype(F32)).astype(BF)
    del_ref[...] = nt(ones_ref[...], prod).reshape(3, 8, rows)

    @pl.when(i == pl.num_programs(0) - 1)
    def _():
        for r in range(2):
            for c in range(2):
                pay_ref[r, c, 0:HALF, :] = awi[r, :, c * D : c * D + HALF].astype(BF)
                pay_ref[r, c, HALF:D, :] = awi[r, :, c * D + HALF : (c + 1) * D].astype(BF)
                pay_ref[r, c, D : 2 * D, :] = awo[r, :, c * D : (c + 1) * D].T.astype(BF)
                for part in range(2):
                    piece = awd[part * HALF + c * 192 : part * HALF + (c + 1) * 192, r * HALF : (r + 1) * HALF]
                    pay_ref[r, c, 2 * D + part * 192 : 2 * D + (part + 1) * 192, :] = piece.astype(BF)


def ffn(lens, ctx, mix, tok, cot, wd, wi, wo, vectors, bi, ones24):
    rows = 256
    blk = lambda w: pl.BlockSpec((rows, w), lambda i, lens: (i, 0))
    return pl.pallas_call(
        ffn_kernel,
        grid_spec=pltpu.PrefetchScalarGridSpec(
            num_scalar_prefetch=1,
            grid=(ROWS // rows,),
            in_specs=[
                blk(HALF),
                blk(HALF),
                blk(D),
                blk(D),
                once((D, D)),
                once((2, HALF, GW)),
                once((2, GW, HALF)),
                *[whole((D,))] * 6,
                whole((FF,)),
                whole((24, HALF)),
            ],
            out_specs=[
                blk(D),
                blk(D),
                blk(HALF),
                blk(HALF),
                pl.BlockSpec((3, 8, rows), lambda i, lens: (0, 0, i)),
                once((2, 2, FFN_ROWS, HALF)),
                whole((8, D)),
                whole((1, FF)),
            ],
            scratch_shapes=[
                pltpu.VMEM((rows, FF), BF),
                pltpu.VMEM((rows, FF), F32),
                pltpu.VMEM((D, D), F32),
                pltpu.VMEM((2, HALF, GW), F32),
                pltpu.VMEM((2, HALF, GW), F32),
            ],
        ),
        out_shape=[
            jax.ShapeDtypeStruct((ROWS, D), BF),
            jax.ShapeDtypeStruct((ROWS, D), BF),
            jax.ShapeDtypeStruct((ROWS, HALF), BF),
            jax.ShapeDtypeStruct((ROWS, HALF), BF),
            jax.ShapeDtypeStruct((3, 8, ROWS), F32),
            jax.ShapeDtypeStruct((2, 2, FFN_ROWS, HALF), BF),
            jax.ShapeDtypeStruct((8, D), F32),
            jax.ShapeDtypeStruct((1, FF), F32),
        ],
        **params("ffn"),
    )(lens, ctx, mix, tok, cot, wd, wi, wo, *vectors, bi, ones24)


def tail_kernel(
    lens, seq_ref, dk_ref, dv_ref, dq_ref, gqm_ref, ghm_ref, edge_ref, w_ref, half0, pieces, piece_cp,
    big_ref, cp_ref, sum_ref, ght_ref,
    agw, accb, sm, tsend, trecv, gho, halves, other, half_cp, last_cp,
    pay, total_sum, near, far, out, mid, ybuf, zsum, s, v, ns, nr, cs, cr, gs, gr, es, er, ls, hs, hr,
):
    step = pl.program_id(0)
    i = lax.rem(step, 4)
    p = Place()
    r, c = p.r, p.c
    rows = dk_ref.shape[0]
    b = lax.rem((1 - c) * 2 + i, 4)
    n = lens[r]
    groups = Groups(p, gs, gr)
    chunks = 5
    crows = PROJ_ROWS // chunks
    summed = Sum(p, far, mid, ybuf, zsum, total_sum, crows, s, v)
    places = [FromRows(p, gho.at[k], ght_ref.at[k], ls.at[k], hs.at[k], hr.at[k]) for k in range(2)]

    def theirs(k):
        return send(tsend.at[k], trecv.at[k], es.at[k], er.at[k], p.core)

    def part(ch):
        return slice(ch * crows, (ch + 1) * crows)

    def beside(k, ch):
        rr = 1 - r if k == 0 else r
        at = k * chunks + ch
        return send(pay.at[rr, 1 - c, part(ch), :], near.at[rr, part(ch), :], ns.at[at], nr.at[at], p.core)

    def cross(ch):
        return send(out.at[part(ch), :], far.at[part(ch), :], cs.at[ch], cr.at[ch], p.across)

    def arrive(ch):
        beside(1, ch).wait_recv()
        cross(ch).wait_recv()
        total = near[r, part(ch), :].astype(F32) + pay[r, c, part(ch), :].astype(F32)
        far[part(ch), :] = (total + far[part(ch), :].astype(F32)).astype(BF)
        summed.half(ch)

    stages = [
        arrive,
        summed.quarter,
        lambda ch: summed.along(ch, summed.collect(ch)),
        summed.back,
        summed.finish_spread,
    ]

    def tick(t):
        for k, stage in enumerate(stages):
            if 0 <= t - k < chunks:
                stage(t - k)

    halfs = [half0, halves.at[0], halves.at[1], half_cp]
    others = [other.at[0], other.at[1], other.at[2], last_cp]

    def back(k, z):
        return groups.back(9 + 4 * k + z, halfs[k].at[z], others[k].at[z])

    @pl.when(step == 0)
    def _():
        meet(everyone(p))
        groups.start_along(0, halves.at[0], pieces[0])
        groups.start_along(3, halves.at[1], pieces[1])
        groups.start_along(6, half_cp, piece_cp[...])
        for z in range(4):
            back(0, z).start()
        for j in range(3):
            clear(agw.at[j])
        sm[...] = jnp.zeros_like(sm)

    @pl.when(step == 4)
    def _():
        for ch in range(chunks):
            beside(0, ch).wait_recv()
            total = near[1 - r, part(ch), :].astype(F32) + pay[1 - r, c, part(ch), :].astype(F32)
            out[part(ch), :] = total.astype(BF)
            cross(ch).start()

    @pl.when(step == 5)
    def _():
        groups.await_along(0, halves.at[0])
        back(1, 0).start()
        back(1, 1).start()

    @pl.when(step == 6)
    def _():
        tick(0)
        back(1, 2).start()
        back(1, 3).start()

    @pl.when(step == 7)
    def _():
        tick(1)

    keep = row_ids(b * rows, rows) < n

    def query_grad():
        return (dq_ref[...].astype(F32) + gqm_ref[...].astype(F32).T).astype(BF)

    @pl.when(step < 4)
    def _():
        tok = seq_ref[rows_at(PAD + b * rows, rows), :]
        h = jnp.where(keep, tok.astype(F32), 0.0).astype(BF)
        agw[0] += nn(dk_ref[...].T, h)
        agw[1] += nn(dv_ref[...].T, h)
        sm[1:2, :] += col_sum(dv_ref[...].astype(F32))

        @pl.when(step >= 2)
        def _():
            gqt = query_grad()
            sm[0:1, :] += col_sum(gqt.T.astype(F32))
            agw[2] += nn(gqt, h)

    @pl.when(step == 3)
    def _():
        for rr in range(2):
            for cc in range(2):
                for j in range(3):
                    piece = agw[j, cc * 192 : (cc + 1) * 192, rr * HALF : (rr + 1) * HALF]
                    pay[rr, cc, j * 192 : (j + 1) * 192, :] = piece.astype(BF)
                pay[rr, cc, 576:, :] = jnp.concatenate([sm[...], jnp.zeros((56, HALF), F32)], axis=0).astype(BF)
        for ch in range(chunks):
            for k in range(2):
                beside(k, ch).start()

    @pl.when(step >= 4)
    def _():
        accb[...] = nn(dk_ref[...], w_ref[0]) + nn(dv_ref[...], w_ref[1])

        @pl.when(step >= 6)
        def _():
            accb[...] += nn(query_grad().T, w_ref[3]) + ghm_ref[...].astype(F32)

    for k in range(2):

        @pl.when((step == 4 + k) & (c == k))
        def _():
            at = slice(0, 16) if k == 0 else slice(rows - 16, rows)
            accb[at, :] += edge_ref[...]

        @pl.when(step == 4 + k)
        def _():
            tsend[k] = jnp.where(keep, accb[...], 0.0).astype(BF)
            theirs(k).start()

        @pl.when(step == 6 + k)
        def _():
            theirs(k).wait_recv()
            gho[k] = jnp.where(keep, accb[...] + trecv[k].astype(F32), 0.0).astype(BF)
            places[k].start()

    @pl.when(step == 7)
    def _():
        tick(2)
        groups.await_along(3, halves.at[1])
        back(2, 0).start()
        back(2, 1).start()
        tick(3)
        back(2, 2).start()
        back(2, 3).start()
        tick(4)
        groups.await_along(6, half_cp)
        back(3, 0).start()
        back(3, 1).start()
        tick(5)
        back(3, 2).start()
        back(3, 3).start()
        tick(6)
        for ch in range(2):
            for z in range(4):
                back(ch, z).wait_recv()
        big_ref[0, p.y] = half0[...]
        big_ref[0, 1 - p.y] = other[0]
        big_ref[1, p.y] = halves[0]
        big_ref[1, 1 - p.y] = other[1]
        tick(7)
        for z in range(4):
            back(3, z).wait_recv()
        cp_ref[p.y] = half_cp[...]
        cp_ref[1 - p.y] = last_cp[...]
        tick(8)
        sum_ref[...] = total_sum[...]
        for z in range(4):
            back(2, z).wait_recv()
        big_ref[2, p.y] = halves[1]
        big_ref[2, 1 - p.y] = other[2]
        for ch in range(chunks):
            summed.finish_sum(ch)
            cross(ch).wait_send()
            for k in range(2):
                beside(k, ch).wait_send()
        for k in range(4):
            for z in range(4):
                back(k, z).wait_send()
        for offset in (1, 2, 3):
            groups.along(0, halves.at[0], offset, p.z).wait_send()
            groups.along(3, halves.at[1], offset, p.z).wait_send()
            groups.along(6, half_cp, offset, p.z).wait_send()
        theirs(0).wait_send()
        theirs(1).wait_send()
        places[0].finish()
        places[1].finish()


def tail(lens, seq_tok, dk, dv, dq, gqm, ghm, edge, w5, half0, pieces, piece_cp):
    rows = 512
    mine = lambda s: jnp.maximum(lax.rem(s, 4) - 2, 0)
    seq = pl.BlockSpec((rows, HALF), lambda s, lens: (lax.rem((1 - half_index()) * 2 + s, 4), 0))
    own = lambda w: pl.BlockSpec((rows, w), lambda s, lens: (mine(s), 0))
    crows = PROJ_ROWS // 5
    return pl.pallas_call(
        tail_kernel,
        grid_spec=pltpu.PrefetchScalarGridSpec(
            num_scalar_prefetch=1,
            grid=(8,),
            in_specs=[
                once((LMAX + 2 * PAD, D)),
                seq,
                seq,
                pl.BlockSpec((HALF, rows), lambda s, lens: (0, mine(s))),
                own(HALF),
                own(D),
                once((16, D)),
                once((5, HALF, D)),
                once((4, 80, HALF)),
                once((2, 80, HALF)),
                once((64, HALF)),
            ],
            out_specs=[
                once((3, 2, 4, 80, HALF)),
                once((2, 4, 64, HALF)),
                once((PROJ_ROWS, HALF)),
                HBM,
            ],
            scratch_shapes=[
                pltpu.VMEM((3, HALF, D), F32),
                pltpu.VMEM((rows, D), F32),
                pltpu.VMEM((8, HALF), F32),
                pltpu.VMEM((2, rows, D), BF),
                pltpu.VMEM((2, rows, D), BF),
                pltpu.VMEM((2, rows, D), BF),
                pltpu.VMEM((2, 4, 80, HALF), BF),
                pltpu.VMEM((3, 4, 80, HALF), BF),
                pltpu.VMEM((4, 64, HALF), BF),
                pltpu.VMEM((4, 64, HALF), BF),
                pltpu.VMEM((2, 2, PROJ_ROWS, HALF), BF),
                pltpu.VMEM((PROJ_ROWS, HALF), BF),
                pltpu.VMEM((2, PROJ_ROWS, HALF), BF),
                pltpu.VMEM((PROJ_ROWS, HALF), BF),
                pltpu.VMEM((PROJ_ROWS, HALF), BF),
                *Sum.scratch(crows, 5),
                pltpu.SemaphoreType.DMA((10,)),
                pltpu.SemaphoreType.DMA((10,)),
                pltpu.SemaphoreType.DMA((5,)),
                pltpu.SemaphoreType.DMA((5,)),
                pltpu.SemaphoreType.DMA((25,)),
                pltpu.SemaphoreType.DMA((25,)),
                pltpu.SemaphoreType.DMA((2,)),
                pltpu.SemaphoreType.DMA((2,)),
                pltpu.SemaphoreType.DMA((2,)),
                pltpu.SemaphoreType.DMA((2, 2)),
                pltpu.SemaphoreType.DMA((2, 3)),
            ],
        ),
        out_shape=[
            jax.ShapeDtypeStruct((3, 2, 4, 80, HALF), BF),
            jax.ShapeDtypeStruct((2, 4, 64, HALF), BF),
            jax.ShapeDtypeStruct((PROJ_ROWS, HALF), BF),
            jax.ShapeDtypeStruct((2, 2, rows, HALF), BF),
        ],
        **comm_params("tail", 6),
    )(lens, seq_tok, dk, dv, dq, gqm, ghm, edge, w5, half0, pieces, piece_cp)


def outputs_kernel(
    ght, hid, t0, t1, t2, t3, t4, big_i0, big_i1, big_o, big_d, little, late_ref, perm_ref,
    hid_ref, gt_ref, gk_ref, gv_ref, gc_ref, gq_ref, gp_ref, gi_ref, go_ref, gd_ref,
    gdep_ref, gbq_ref, gbv_ref, gbc_ref, gbp_ref, gwk_ref, gbk_ref,
    gbd_ref, gg1_ref, gb1_ref, gbi_ref, gbo_ref, gg2_ref, gb2_ref,
):
    i = pl.program_id(0)
    hid_ref[...] = hid[...]
    gt_ref[...] = ght[0, 0].astype(F32)

    for src, ref in ((t0, gk_ref), (t1, gv_ref), (t2, gq_ref), (t3, gc_ref), (t4, gp_ref), (big_o, go_ref), (big_d, gd_ref)):
        ref[...] = src[...].astype(F32)
    gi_ref[:, 0:HALF] = big_i0[...].astype(F32)
    gi_ref[:, HALF:D] = big_i1[...].astype(F32)

    @pl.when(i == 0)
    def _():
        mixed = little[72:80, :].astype(F32)
        low = little[80:88, :].astype(F32)
        high = little[88:96, :].astype(F32)
        inter = little[96:104, :].astype(F32)
        late = late_ref[0:16, :].astype(F32)
        gwk_ref[...] = nn(perm_ref[...], little[0:72, :])
        bias = nt(mixed[:, 0:72].astype(BF), perm_ref[...])
        gbk_ref[...] = bias[2:3, :].reshape(54)
        for k, ref in enumerate((gbq_ref, gbv_ref)):
            ref[...] = late[k : k + 1, :].reshape(HALF)
        for k, ref in enumerate((gbc_ref, gbp_ref)):
            ref[...] = mixed[k : k + 1, :].reshape(HALF)
        for k, ref in enumerate((gbo_ref, gg2_ref, gb2_ref, gbd_ref, gg1_ref, gb1_ref)):
            ref[...] = jnp.concatenate([low[k : k + 1, :], high[k : k + 1, :]], axis=1).reshape(D)
        gbi_ref[...] = jnp.concatenate([inter[k : k + 1, :] for k in range(8)], axis=1).reshape(FF)
        gdep_ref[0:8, 0:HALF] = little[104:112, :].astype(F32)
        gdep_ref[0:8, HALF:D] = little[112:120, :].astype(F32)
        gdep_ref[8:9, 0:HALF] = mixed[3:4, :]
        gdep_ref[8:9, HALF:D] = mixed[4:5, :]


def outputs(ght, hid, total, cp, big, perm):
    rows = 512
    at = lambda n, first: pl.BlockSpec((n, HALF), lambda i: (first + i, 0))
    blk = at(rows, 0)
    chunk = pl.BlockSpec((1, 1, rows, HALF), lambda i: (lax.rem(i, 2), lax.div(i, 2), 0, 0))
    shapes = [(KW, D)] + [(HALF,)] * 4 + [(54, HALF), (54,)] + [(D,)] * 3 + [(FF,)] + [(D,)] * 3
    main = [(192, HALF)] * 5 + [(HALF, D), (D, HALF), (HALF, HALF)]
    return pl.pallas_call(
        outputs_kernel,
        grid=(4,),
        in_specs=[chunk, blk]
        + [at(48, 4 * j) for j in (0, 1, 2, 0, 1)]
        + [at(96, 0), at(96, 4), at(192, 4), at(96, 16)]
        + [pl.BlockSpec((128, HALF), lambda i: (3, 0)), pl.BlockSpec((64, HALF), lambda i: (9, 0)), whole((54, 72))],
        out_specs=[blk, blk]
        + [at(48, 0)] * 5
        + [pl.BlockSpec((96, D), lambda i: (i, 0)), at(192, 0), at(96, 0)]
        + [whole(shape) for shape in shapes],
        out_shape=[jax.ShapeDtypeStruct((LMAX, HALF), BF), jax.ShapeDtypeStruct((LMAX, HALF), F32)]
        + [jax.ShapeDtypeStruct(shape, F32) for shape in main + shapes],
        **params("outputs"),
    )(ght, hid, total, total, total, cp, cp, big, big, big, big, cp, total, perm)


def constants():
    ones8 = np.zeros((8, HALF), np.float32)
    ones24 = np.zeros((24, HALF), np.float32)
    perm = np.zeros((72, 54), np.float32)
    for head in range(6):
        cols = slice(head * HD, (head + 1) * HD)
        ones8[head, cols] = 1
        ones24[head // 2 * 8 + head % 2, cols] = 1
        for j in range(KW):
            perm[j * 8 + head, head * KW + j] = 1
    return [jnp.asarray(a, BF) for a in (ones8, ones24, perm)]


def per_device(
    groups, tokens, cotangent, seq_lengths, w_query, w_key, w_value, w_convout, w_point, w_depth,
    b_query, b_value, b_convout, b_point, w_kernel, b_kernel, w_dense, b_dense, gain_one, bias_one,
    w_inter, b_inter, w_output, b_output, gain_two, bias_two,
):
    lens = seq_lengths
    ones8, ones24, perm = constants()
    wdep = w_depth.T

    kd, kt, vz, q, qs, pt, kp, conv, mix, dep, hown, wk72, bk72, spread, ctx, lse, seq, w5, wi, wd, cot, wo = front(
        lens, tokens, (w_key.T, w_value.T, w_convout.T, w_query.T, w_point.T), w_kernel.T, b_kernel, perm,
        wdep, b_value, b_convout, b_query, b_point,
        w_inter[0], w_dense.reshape(2, 192, HALF), w_output[0], cotangent,
    )
    vectors = (b_dense, gain_one, bias_one, b_output, gain_two, bias_two)
    hid, gpre, gctx, gcv, delta, payf, smf, gbi = ffn(
        lens, ctx, mix, hown, cot, wd.reshape(D, D), wi, wo, vectors, b_inter, ones24
    )
    gqm, dq, dk, dv, ghm, edge, half0, pieces, piece_cp, hid = back(
        lens, gcv, conv, kp, q, pt, wk72, spread, ones8, qs, gctx, kd, vz, kt, lse, delta, payf, hid,
        seq, w5, gpre, dep, wdep, smf, gbi,
    )
    big, cp, total, ght = tail(lens, seq, dk, dv, dq, gqm, ghm, edge, w5, half0, pieces, piece_cp)
    big = big.reshape(FFN_ROWS, HALF)
    cp = cp.reshape(512, HALF)
    if groups > 8:
        sums = lax.psum(tuple(x.astype(F32) * 0.125 for x in (total, cp, big)), "dp")
        total, cp, big = (x.astype(BF) for x in sums)
    (
        hidden_out, gt, gk, gv, gc, gq, gp, gi, go, gd, gdep, gbq, gbv, gbc, gbp, gwk, gbk, gbd, gg1, gb1, gbi, gbo, gg2, gb2,
    ) = outputs(ght, hid.reshape(LMAX, HALF), total, cp, big, perm.T)
    return (
        hidden_out, gt, gq.T, gk.T, gv.T, gc.T, gp.T, gdep.T, gbq, gbv, gbc, gbp, gwk.T, gbk, gd, gbd, gg1, gb1,
        gi[None], gbi, go[None], gbo, gg2, gb2,
    )


def solution(mesh):
    act = P(("dp", "col"), "row")
    rep = P()
    proj = P("row", "col")
    in_specs = (
        act, act, P("dp"), proj, proj, proj, proj, proj, rep, rep, rep, rep, rep, rep, rep, P("col", "row"),
        rep, rep, rep, P("row", None, "col"), rep, P("row", "col", None), rep, rep, rep,
    )
    out_specs = (
        act, act, proj, proj, proj, proj, proj, rep, rep, rep, rep, rep, rep, rep, P("col", "row"),
        rep, rep, rep, P("row", None, "col"), rep, P("row", "col", None), rep, rep, rep,
    )
    return jax.shard_map(
        functools.partial(per_device, mesh.shape["dp"]), mesh=mesh, in_specs=in_specs, out_specs=out_specs, check_vma=False)
```

```python
import functools

import jax
import jax.numpy as jnp
import numpy as np
from jax import lax
from jax.experimental import pallas as pl
from jax.experimental.pallas import tpu as pltpu
from jax.sharding import PartitionSpec as P

D = 768
HALF = 384
HD = 64
KW = 9
FF = 3072
GW = 1536
LMAX = 2048
ROWS = 1024
EPS = 1e-12
LOG2E = 1.4426950408889634
LN2 = 0.6931471805599453
BF = jnp.bfloat16
F32 = jnp.float32
VMEM_BYTES = 63 * 1024 * 1024
PAD = 16
FFN_ROWS = 1920
FFN_CHUNK = 640
PROJ_ROWS = 640
MESH = pl.DeviceIdType.MESH
HBM = pl.BlockSpec(memory_space=pl.ANY)
VMEM = pl.BlockSpec(memory_space=pltpu.VMEM)


def nn(a, b):
    return lax.dot_general(a, b, (((1,), (0,)), ((), ())), preferred_element_type=F32)


def nt(a, b):
    return lax.dot_general(a, b, (((1,), (1,)), ((), ())), preferred_element_type=F32)


def col_sum(x):
    return jnp.sum(x, axis=0, keepdims=True)


def row_ids(start, rows):
    return start + lax.broadcasted_iota(jnp.int32, (rows, 1), 0)


def whole(shape):
    return pl.BlockSpec(shape, lambda *_: (0,) * len(shape))


def once(shape):
    return pl.BlockSpec(shape, lambda *_: (0,) * len(shape), pipeline_mode=pl.Buffered(1))


def half_index():
    return lax.axis_index("col")


def length(lens):
    return lens[lax.axis_index("row")]


def line(ref):
    return ref[...].astype(F32).reshape(1, ref.shape[0])


def spread_taps(probs, spread_ref, t):
    taps = []
    for j in range(0, KW, 2):
        count = min(2, KW - j)
        at = (t * KW + j) * 128
        both = nn(probs, spread_ref[:, at : at + count * 128])
        taps += [both[:, k * 128 : (k + 1) * 128] for k in range(count)]
    return taps


def clear(ref, step=32):
    def body(k, carry):
        ref[pl.ds(pl.multiple_of(k * step, step), step), :] = jnp.zeros((step, ref.shape[1]), ref.dtype)
        return carry

    lax.fori_loop(0, ref.shape[0] // step, body, 0)


def put_tiles(buf, value, first=0):
    for t in range(value.shape[1] // 128):
        buf[t, first : first + value.shape[0], :] = value[:, t * 128 : (t + 1) * 128]


def params(name):
    return dict(
        name=name,
        compiler_params=pltpu.CompilerParams(vmem_limit_bytes=VMEM_BYTES),
    )


def lanes(k, width=HALF):
    return pl.ds(pl.multiple_of(k * width, 128), width)


def rows_at(start, count, step=16):
    return pl.ds(pl.multiple_of(start, step), count)


def send(src, dst, send_sem, recv_sem, device):
    return pltpu.make_async_remote_copy(
        src_ref=src, dst_ref=dst, send_sem=send_sem, recv_sem=recv_sem, device_id=device, device_id_type=MESH
    )


class Place:
    def __init__(self):
        self.d = lax.axis_index("dp")
        self.r = lax.axis_index("row")
        self.c = lax.axis_index("col")
        self.k = lax.rem(self.d, 8)
        self.base = self.d - self.k
        self.y = lax.rem(self.k, 2)
        self.z = lax.div(self.k, 2)
        self.beside = {"dp": self.base + self.z * 2 + 1 - self.y}
        self.across = {"row": 1 - self.r}
        self.core = {"col": 1 - self.c}
        self.diagonal = {"row": 1 - self.r, "col": 1 - self.c}

    def eight(self, offset):
        other = lax.rem(self.k + offset, 8)
        return other, {"dp": self.base + other}

    def four(self, offset):
        other = lax.rem(self.z + offset, 4)
        return other, {"dp": self.base + other * 2 + self.y}


def meet(devices):
    barrier = pltpu.get_barrier_semaphore()
    for device in devices:
        pl.semaphore_signal(barrier, inc=1, device_id=device, device_id_type=MESH)
    pl.semaphore_wait(barrier, len(devices))


def comm_params(name, number):
    return dict(
        name=name,
        compiler_params=pltpu.CompilerParams(
            vmem_limit_bytes=VMEM_BYTES, collective_id=number, has_side_effects=True
        ),
    )


class Gather:
    def __init__(self, place, own, full, part, block, step, send_sem, recv_sem, first):
        self.p, self.own, self.full, self.part, self.block, self.h = place, own, full, part, block, step
        self.s, self.v, self.f = send_sem, recv_sem, first

    def _move(self, src, dst, n, device):
        return send(src, dst, self.s.at[self.f + n], self.v.at[self.f + n], device)

    def _cross(self, r):
        p = self.p
        at = (p.y * 4 + p.z) * self.h
        return self._move(self.part(self.own, at, self.h), self.block(self.full, r, p.c, at, self.h), 0, p.across)

    def _near(self, c):
        p = self.p
        return self._move(self.own, self.block(self.full, p.r, c, 0, 8 * self.h), 1, p.core)

    def _pass(self, offset, z):
        p = self.p
        here = self.block(self.full, 1 - p.r, p.c, (p.y * 4 + z) * self.h, self.h)
        return self._move(here, here, 1 + offset, p.four(offset)[1])

    def _turn(self, y):
        p = self.p
        here = self.block(self.full, 1 - p.r, p.c, y * 4 * self.h, 4 * self.h)
        return self._move(here, here, 5, p.beside)

    def _last(self, c):
        p = self.p
        here = self.block(self.full, 1 - p.r, c, 0, 8 * self.h)
        return self._move(here, here, 6, p.core)

    def start(self):
        self._cross(self.p.r).start()
        self._near(self.p.c).start()

    def relay(self):
        p = self.p
        self._cross(1 - p.r).wait_recv()
        for offset in (1, 2, 3):
            self._pass(offset, p.z).start()

    def turn(self):
        p = self.p
        for offset in (1, 2, 3):
            self._pass(offset, lax.rem(p.z + 4 - offset, 4)).wait_recv()
        self._turn(p.y).start()

    def share(self):
        p = self.p
        self._turn(1 - p.y).wait_recv()
        self._last(p.c).start()

    def finish(self):
        p = self.p
        self._last(1 - p.c).wait_recv()
        self._near(1 - p.c).wait_recv()
        self._cross(p.r).wait_send()
        self._near(p.c).wait_send()
        for offset in (1, 2, 3):
            self._pass(offset, p.z).wait_send()
        self._turn(p.y).wait_send()
        self._last(p.c).wait_send()


def middle_part(ref, first, rows):
    return ref.at[:, rows_at(first, rows, 8), :]


def middle_block(ref, r, c, first, rows):
    return ref.at[:, rows_at(c * 192 + first, rows, 8), lanes(r)]


def rows_part(ref, first, rows):
    return ref.at[rows_at(first, rows), :]


def inter_block(ref, r, c, first, rows):
    return ref.at[r, rows_at(first, rows), lanes(c, 768)]


def output_block(ref, r, c, first, rows):
    return ref.at[r, rows_at(c * 768 + first, rows), :]


class ToRows:
    def __init__(self, place, src, dst, stage, local_sem, send_sem, recv_sem):
        self.p, self.src, self.dst, self.stage = place, src, dst, stage
        self.l, self.s, self.v = local_sem, send_sem, recv_sem

    def _cross(self, q, k):
        half = self.src.at[q * ROWS : (q + 1) * ROWS, :]
        return send(half, self.dst.at[:, lanes(k)], self.s.at[q], self.v.at[0], {"row": 1 - self.p.r, "col": q})

    def _near(self):
        p = self.p
        half = self.src.at[rows_at((1 - p.c) * ROWS, ROWS), :]
        return send(half, self.dst.at[:, lanes(p.r)], self.s.at[2], self.v.at[1], p.core)

    def _load(self):
        return pltpu.make_async_copy(self.src.at[rows_at(self.p.c * ROWS, ROWS), :], self.stage, self.l.at[0])

    def _store(self):
        return pltpu.make_async_copy(self.stage, self.dst.at[:, lanes(self.p.r)], self.l.at[1])

    def start(self):
        p = self.p

        @pl.when(p.r != p.c)
        def _():
            self._cross(0, p.r).start()
            self._cross(1, p.r).start()

        @pl.when(p.r == p.c)
        def _():
            self._near().start()
            self._load().start()

    def store(self):
        @pl.when(self.p.r == self.p.c)
        def _():
            self._load().wait()
            self._store().start()

    def finish(self):
        p = self.p
        self._cross(0, 1 - p.r).wait_recv()

        @pl.when(p.r != p.c)
        def _():
            self._cross(0, p.r).wait_send()
            self._cross(1, p.r).wait_send()
            self._near().wait_recv()

        @pl.when(p.r == p.c)
        def _():
            self._near().wait_send()
            self._store().wait()


class FromRows:
    def __init__(self, place, src, dst, local_sem, send_sem, recv_sem):
        self.p, self.src, self.dst = place, src, dst
        self.l, self.s, self.v = local_sem, send_sem, recv_sem

    def _cross(self, q):
        p = self.p
        place = self.dst.at[q]
        return send(self.src.at[:, lanes(1 - p.r)], place, self.s.at[0], self.v.at[q], {"row": 1 - p.r, "col": p.r})

    def _near(self, q):
        p = self.p
        place = self.dst.at[q]
        return send(self.src.at[:, lanes(p.r)], place, self.s.at[1], self.v.at[2], p.core)

    def _local(self):
        p = self.p
        place = self.dst.at[p.c]
        return pltpu.make_async_copy(self.src.at[:, lanes(p.r)], place, self.l)

    def start(self):
        p = self.p
        self._cross(p.c).start()

        @pl.when(p.r != p.c)
        def _():
            self._near(p.c).start()

        @pl.when(p.r == p.c)
        def _():
            self._local().start()

    def finish(self):
        p = self.p
        self._cross(p.c).wait_send()

        @pl.when(p.r != p.c)
        def _():
            self._near(p.c).wait_send()
            self._cross(0).wait_recv()
            self._cross(1).wait_recv()

        @pl.when(p.r == p.c)
        def _():
            self._near(1 - p.c).wait_recv()
            self._local().wait()


class Sum:
    def __init__(self, place, far, mid, ybuf, zbuf, total, rows, s, v, first=0):
        self.p, self.far, self.mid, self.ybuf, self.zbuf, self.total = place, far, mid, ybuf, zbuf, total
        self.rows, self.s, self.v, self.first = rows, s, v, first

    def _sems(self, ch, n):
        i = self.first + ch * 8 + n
        return self.s.at[i], self.v.at[i]

    def _beside(self):
        return self.p.beside

    def _halves(self, ch, y):
        return rows_at(ch * self.rows + y * (self.rows // 2), self.rows // 2)

    def _piece(self, ch, z):
        return rows_at(ch * self.rows + self.p.y * (self.rows // 2) + z * (self.rows // 8), self.rows // 8)

    def _half(self, ch):
        return send(self.far.at[self._halves(ch, 1 - self.p.y), :], self.ybuf.at[ch], *self._sems(ch, 0), self._beside())

    def _quarter(self, ch, offset):
        other, device = self.p.four(offset)
        src = self.mid.at[ch, rows_at(other * (self.rows // 8), self.rows // 8), :]
        return send(src, self.zbuf.at[ch, offset - 1], *self._sems(ch, offset), device)

    def _along(self, ch, offset, z):
        _, device = self.p.four(offset)
        here = self.total.at[self._piece(ch, z), :]
        return send(here, here, *self._sems(ch, 3 + offset), device)

    def _back(self, ch, y):
        here = self.total.at[self._halves(ch, y), :]
        return send(here, here, *self._sems(ch, 7), self._beside())

    def half(self, ch):
        self._half(ch).start()

    def quarter(self, ch):
        self._half(ch).wait_recv()
        both = self.far[self._halves(ch, self.p.y), :].astype(F32) + self.ybuf[ch].astype(F32)
        self.mid[ch] = both.astype(BF)
        for offset in (1, 2, 3):
            self._quarter(ch, offset).start()

    def collect(self, ch):
        both = self.mid[ch, rows_at(self.p.z * (self.rows // 8), self.rows // 8), :].astype(F32)
        for offset in (1, 2, 3):
            self._quarter(ch, offset).wait_recv()
            both = both + self.zbuf[ch, offset - 1].astype(F32)
        return both.astype(BF)

    def along(self, ch, piece):
        self.total[self._piece(ch, self.p.z), :] = piece
        for offset in (1, 2, 3):
            self._along(ch, offset, self.p.z).start()

    def back(self, ch):
        for offset in (1, 2, 3):
            self._along(ch, offset, lax.rem(self.p.z + 4 - offset, 4)).wait_recv()
        self._back(ch, self.p.y).start()

    def finish_sum(self, ch):
        self._half(ch).wait_send()
        for offset in (1, 2, 3):
            self._quarter(ch, offset).wait_send()

    def finish_spread(self, ch):
        self._back(ch, 1 - self.p.y).wait_recv()
        for offset in (1, 2, 3):
            self._along(ch, offset, self.p.z).wait_send()
        self._back(ch, self.p.y).wait_send()

    @staticmethod
    def scratch(rows, chunks):
        return [
            pltpu.VMEM((chunks, rows // 2, HALF), BF),
            pltpu.VMEM((chunks, rows // 2, HALF), BF),
            pltpu.VMEM((chunks, 3, rows // 8, HALF), BF),
            pltpu.SemaphoreType.DMA((8 * chunks,)),
            pltpu.SemaphoreType.DMA((8 * chunks,)),
        ]


class Groups:
    def __init__(self, place, s, v):
        self.p, self.s, self.v = place, s, v

    def half(self, n, mine, ybuf):
        return send(mine.at[1 - self.p.y], ybuf, self.s.at[n], self.v.at[n], self.p.beside)

    def quarter(self, n, mid, zbuf, offset):
        other, device = self.p.four(offset)
        n = n + offset - 1
        return send(mid.at[other], zbuf.at[offset - 1], self.s.at[n], self.v.at[n], device)

    def cross(self, n, both, xbuf):
        return send(both.at[1 - self.p.r], xbuf, self.s.at[n], self.v.at[n], self.p.across)

    def along(self, n, half, offset, z):
        n = n + offset - 1
        return send(half.at[z], half.at[z], self.s.at[n], self.v.at[n], self.p.four(offset)[1])

    def back(self, n, half, other):
        return send(half, other, self.s.at[n], self.v.at[n], self.p.beside)

    def start_quarters(self, n, mid, zbuf):
        for offset in (1, 2, 3):
            self.quarter(n, mid, zbuf, offset).start()

    def collect(self, n, mid, zbuf, both):
        total = mid[self.p.z].astype(F32)
        for offset in (1, 2, 3):
            self.quarter(n, mid, zbuf, offset).wait_recv()
            total = total + zbuf[offset - 1].astype(F32)
        both[...] = total.astype(BF)

    def start_along(self, n, half, piece):
        half[self.p.z] = piece
        for offset in (1, 2, 3):
            self.along(n, half, offset, self.p.z).start()

    def await_along(self, n, half):
        for offset in (1, 2, 3):
            self.along(n, half, offset, lax.rem(self.p.z + 4 - offset, 4)).wait_recv()

    def sent(self, n, ref, kind):
        for offset in (1, 2, 3):
            kind(n, *ref, offset).wait_send()


def everyone(p):
    return [p.across, p.core, p.diagonal, p.beside] + [p.four(o)[1] for o in (1, 2, 3)]


def front_kernel(
    lens, tok_ref, wk_own, wv_own, wc_own, wq_own, wp_own, kern_ref, kb_ref, perm_ref,
    wdep_ref, bv_ref, bc_ref, bq_ref, bp_ref, wi_own, wd_own, wo_own, cot_own,
    kd_ref, kt_ref, vz_ref, q_ref, qs_ref, pt_ref, kp_ref, conv_ref, mix_ref, dep_ref, h_ref, wk_ref, bk_ref, spread_ref,
    ctx_ref, lse_ref, seq_out, w5_out, wi_ref, wd_ref, cot_ref, wo_ref,
    own, seq_ref, w_ref, stage, first_key, hbuf, cbuf, lsem, ts, tr, gs, gr, cs, cr,
):
    i = pl.program_id(0)
    p = Place()
    r, c = p.r, p.c
    n = lens[r]
    keys = Gather(p, own.at[0:2], w_ref.at[0:2], middle_part, middle_block, 24, gs, gr, 0)
    proj = Gather(p, own.at[2:5], w_ref.at[2:5], middle_part, middle_block, 24, gs, gr, 28)
    inter = Gather(p, wi_own, wi_ref, rows_part, inter_block, 48, gs, gr, 7)
    dense = Gather(p, wd_own, wd_ref, middle_part, middle_block, 24, gs, gr, 14)
    cot_rows = ToRows(p, cot_own, cot_ref, stage, lsem, cs, cr)
    output = Gather(p, wo_own, wo_ref, rows_part, output_block, 96, gs, gr, 21)
    keep_output = pltpu.make_async_copy(wo_own, output_block(wo_ref, r, c, 0, D), lsem.at[7])
    keep_inter = pltpu.make_async_copy(wi_own, inter_block(wi_ref, r, c, 0, HALF), lsem.at[2])
    keep_dense = pltpu.make_async_copy(wd_own, middle_block(wd_ref, r, c, 0, 192), lsem.at[3])
    keep_own = pltpu.make_async_copy(tok_ref, seq_ref.at[PAD : PAD + LMAX, lanes(r)], lsem.at[4])
    keep_seq = pltpu.make_async_copy(seq_ref, seq_out, lsem.at[5])
    keep_w = pltpu.make_async_copy(w_ref, w5_out, lsem.at[6])

    def chunk(m, k):
        return seq_ref.at[PAD + m * 512 : PAD + (m + 1) * 512, lanes(k)]

    def cross(m, k):
        return send(tok_ref.at[m * 512 : (m + 1) * 512, :], chunk(m, k), ts.at[m], tr.at[m], {"row": 1 - r, "col": m // 2})

    def near(k):
        return send(tok_ref, seq_ref.at[PAD : PAD + LMAX, lanes(k)], ts.at[4], tr.at[4], p.core)

    def forward(m):
        return send(chunk(m, 1 - r), chunk(m, 1 - r), ts.at[5 + m], tr.at[5 + m], p.core)

    @pl.when(i == 0)
    def _():
        for j, ref in enumerate((wk_own, wv_own, wc_own, wq_own, wp_own)):
            own[j] = ref[...]
        seq_ref[0:PAD, :] = jnp.zeros((PAD, D), BF)
        seq_ref[PAD + LMAX :, :] = jnp.zeros((PAD, D), BF)
        meet(everyone(p))
        keys.start()
        proj.start()
        inter._cross(r).start()
        dense._cross(r).start()

        @pl.when(r != c)
        def _():
            for m in (0, 2, 1, 3):
                cross(m, r).start()

        @pl.when(r == c)
        def _():
            near(r).start()
            keep_own.start()

        output._cross(r).start()
        cot_rows.start()
        inter._near(c).start()
        dense._near(c).start()
        output._near(c).start()
        keep_inter.start()
        keep_dense.start()
        keep_output.start()
        middle_block(w_ref, r, c, 0, 192)[...] = own[...]
        wk_ref[...] = nn(perm_ref[...], kern_ref[...]).astype(BF)
        bk_ref[...] = nt(perm_ref[...], jnp.broadcast_to(line(kb_ref), (128, 54)).astype(BF))
        row = lax.broadcasted_iota(jnp.int32, (72, 128), 0)
        head = lax.broadcasted_iota(jnp.int32, (72, 128), 1) >> 6
        for t in range(HALF // 128):
            for j in range(KW):
                at = (t * KW + j) * 128
                spread_ref[:, at : at + 128] = jnp.where(row == head + (j * 8 + 2 * t), 1.0, 0.0).astype(BF)
        keys.relay()
        proj.relay()
        keys.turn()
        proj.turn()
        inter.relay()
        dense.relay()

        @pl.when(r != c)
        def _():
            near(r).wait_recv()

        @pl.when(r == c)
        def _():
            keep_own.wait()

        keys.share()
        keys.finish()

        def project(k, carry):
            for at, m in enumerate((0, 2, 1, 3)):

                @pl.when((k == at) & (c == m // 2))
                def _():
                    cross(m, 1 - r).wait_recv()
                    forward(m).start()

                @pl.when((k == at) & (c != m // 2))
                def _():
                    forward(m).wait_recv()

            @pl.when(k == 2)
            def _():
                proj.share()

            krows = LMAX // 4
            first = pl.multiple_of((2 * lax.rem(k, 2) + lax.div(k, 2)) * krows, krows)
            keep_key = row_ids(first, krows) < n
            tok = seq_ref[rows_at(PAD + first, krows), :]
            h = jnp.where(keep_key, tok.astype(F32), 0.0).astype(BF)
            kf = nt(h, w_ref[0])
            v = nt(h, w_ref[1]) + line(bv_ref)

            @pl.when(k == 0)
            def _():
                first_key[...] = kf[0:8]

            kd_ref[pl.ds(first, krows), :] = jnp.where(keep_key, kf, first_key[0:1]).astype(BF)
            kt_ref[:, pl.ds(first, krows)] = kf.T.astype(BF)
            vz_ref[pl.ds(first, krows), :] = jnp.where(keep_key, v, 0.0).astype(BF)
            return carry

        lax.fori_loop(0, 4, project, 0)
        for q in range(2):

            @pl.when(c == q)
            def _():
                for m in (2 * q, 2 * q + 1):
                    forward(m).wait_send()

        @pl.when(r != c)
        def _():
            for m in range(4):
                cross(m, r).wait_send()

        @pl.when(r == c)
        def _():
            near(r).wait_send()

        proj.finish()
        output.relay()
        keep_seq.start()
        keep_w.start()

    @pl.when(i == 1)
    def _():
        inter.turn()
        dense.turn()
        cot_rows.store()

    @pl.when(i == 3)
    def _():
        output.turn()

    @pl.when(i == 4)
    def _():
        inter.share()
        dense.share()

    @pl.when(i == 6)
    def _():
        output.share()

    @pl.when(i < 4)
    def _():
        rows = q_ref.shape[0]
        wide = rows + 32
        base = pl.multiple_of(i * rows, 16)
        start = pl.multiple_of(c * ROWS + i * rows, 16)
        ids = row_ids(start - 16, wide)
        keep = (ids >= 0) & (ids < n)
        hw = jnp.where(keep, seq_ref[pl.ds(start, wide), :].astype(F32), 0.0)
        put_tiles(hbuf, hw)
        wdep = wdep_ref[...].astype(F32)
        for t in range(D // 128):
            cols = slice(t * 128, (t + 1) * 128)
            depth = jnp.zeros((rows, 128), F32)
            for j in range(KW):
                depth = depth + hbuf[t, 12 + j : 12 + j + rows, :] * wdep[j : j + 1, cols]
            dep_ref[:, cols] = depth.astype(BF)
        depth_low = dep_ref[...]
        hl = hw.astype(BF)
        h_ref[...] = hl[16 : 16 + rows]
        conv = jnp.where(keep, nt(hl, w_ref[2]) + line(bc_ref), 0.0)
        put_tiles(cbuf, conv)
        conv_ref[pl.ds(base, wide), :] = conv.astype(BF)
        q = nt(hl[16 : 16 + rows], w_ref[3]) + line(bq_ref)
        q_low = q.astype(BF)
        q_ref[...] = q_low
        qs_ref[pl.ds(base, rows), :] = (q * (0.125 * LOG2E)).astype(BF)
        pt = nt(depth_low, w_ref[4]) + line(bp_ref)
        pt_ref[...] = pt.astype(BF)
        mixer = (pt * q_low.astype(F32)).astype(BF)
        logits = (nt(wk_ref[...], mixer) + bk_ref[:, 0:1]).reshape(KW, 8, rows)
        peak = jnp.max(logits, axis=0, keepdims=True)
        raised = jnp.exp(logits - peak)
        kp = (raised / jnp.sum(raised, axis=0, keepdims=True)).reshape(KW * 8, rows)
        kp_ref[...] = kp
        kpt = kp.T.astype(BF)
        for t in range(HALF // 128):
            mix = jnp.zeros((rows, 128), F32)
            for j, tap in enumerate(spread_taps(kpt, spread_ref, t)):
                mix = mix + tap * cbuf[t, 12 + j : 12 + j + rows, :]
            mix_ref[:, t * 128 : (t + 1) * 128] = mix.astype(BF)

    @pl.when(i >= 4)
    def _():
        cols = lanes(i - 4, 128)
        k = kd_ref[:, cols]
        ones = jnp.where(row_ids(0, LMAX) < n, 1.0, 0.0)
        ve = jnp.concatenate([vz_ref[:, cols], jnp.broadcast_to(ones, (LMAX, 128)).astype(BF)], axis=1)
        rows = 256
        lane = lax.broadcasted_iota(jnp.int32, (rows, 128), 1)
        for u in range(ROWS // rows):
            part = slice(u * rows, (u + 1) * rows)
            outs = []
            for hh in range(2):
                q = jnp.where((lane < HD) == (hh == 0), qs_ref[part, cols], jnp.zeros((), BF))
                s = nt(q, k)
                peak = jnp.max(s, axis=1, keepdims=True)
                prob = jnp.exp2(s - peak).astype(BF)
                o = nn(prob, ve)
                outs.append(o[:, :128] / o[:, 128:])
                lse_ref[0, hh : hh + 1, part] = (peak + jnp.log2(o[:, 128:129])).T
            ctx_ref[part, :] = jnp.where(lane < HD, outs[0], outs[1]).astype(BF)

    @pl.when(i == pl.num_programs(0) - 1)
    def _():
        inter.finish()
        dense.finish()
        output.finish()
        cot_rows.finish()
        keep_inter.wait()
        keep_dense.wait()
        keep_output.wait()
        keep_seq.wait()
        keep_w.wait()


def front(lens, tokens, weights, w_kernel, b_kernel, perm, wdep, bv, bc, bq, bp, w_inter, w_dense, w_output, cotangent):
    rows = 256
    early = lambda i: jnp.minimum(i, 3)
    late = lambda i: jnp.maximum(i - 4, 0)
    blk = pl.BlockSpec((rows, HALF), lambda i, lens: (early(i), 0))
    full = pl.BlockSpec((rows, D), lambda i, lens: (early(i), 0))
    half = jax.ShapeDtypeStruct((ROWS, HALF), BF)
    return pl.pallas_call(
        front_kernel,
        grid_spec=pltpu.PrefetchScalarGridSpec(
            num_scalar_prefetch=1,
            grid=(7,),
            in_specs=[HBM]
            + [once((192, HALF))] * 5
            + [once((54, HALF)), whole((54,)), once((72, 54)), once((KW, D))]
            + [whole((HALF,))] * 4
            + [once((HALF, D)), once((2, 192, HALF)), once((D, HALF)), HBM],
            out_specs=[
                once((LMAX, HALF)),
                once((HALF, LMAX)),
                once((LMAX, HALF)),
                blk,
                once((ROWS, HALF)),
                blk,
                pl.BlockSpec((72, rows), lambda i, lens: (0, early(i))),
                once((ROWS + 32, HALF)),
                blk,
                full,
                full,
                whole((72, HALF)),
                whole((72, 128)),
                once((72, KW * HALF)),
                pl.BlockSpec((ROWS, 128), lambda i, lens: (0, late(i))),
                pl.BlockSpec((1, 8, ROWS), lambda i, lens: (late(i), 0, 0)),
            ]
            + [HBM] * 6,
            scratch_shapes=[
                pltpu.VMEM((5, 192, HALF), BF),
                pltpu.VMEM((LMAX + 2 * PAD, D), BF),
                pltpu.VMEM((5, HALF, D), BF),
                pltpu.VMEM((ROWS, HALF), BF),
                pltpu.VMEM((8, HALF), F32),
                pltpu.VMEM((D // 128, rows + 32, 128), F32),
                pltpu.VMEM((HALF // 128, rows + 32, 128), F32),
                pltpu.SemaphoreType.DMA((8,)),
                pltpu.SemaphoreType.DMA((9,)),
                pltpu.SemaphoreType.DMA((9,)),
                pltpu.SemaphoreType.DMA((35,)),
                pltpu.SemaphoreType.DMA((35,)),
                pltpu.SemaphoreType.DMA((3,)),
                pltpu.SemaphoreType.DMA((2,)),
            ],
        ),
        out_shape=[
            jax.ShapeDtypeStruct((LMAX, HALF), BF),
            jax.ShapeDtypeStruct((HALF, LMAX), BF),
            jax.ShapeDtypeStruct((LMAX, HALF), BF),
            half,
            half,
            half,
            jax.ShapeDtypeStruct((72, ROWS), F32),
            jax.ShapeDtypeStruct((ROWS + 32, HALF), BF),
            half,
            jax.ShapeDtypeStruct((ROWS, D), BF),
            jax.ShapeDtypeStruct((ROWS, D), BF),
            jax.ShapeDtypeStruct((72, HALF), BF),
            jax.ShapeDtypeStruct((72, 128), F32),
            jax.ShapeDtypeStruct((72, KW * HALF), BF),
            half,
            jax.ShapeDtypeStruct((3, 8, ROWS), F32),
            jax.ShapeDtypeStruct((LMAX + 2 * PAD, D), BF),
            jax.ShapeDtypeStruct((5, HALF, D), BF),
            jax.ShapeDtypeStruct((2, HALF, GW), BF),
            jax.ShapeDtypeStruct((2, HALF, D), BF),
            jax.ShapeDtypeStruct((ROWS, D), BF),
            jax.ShapeDtypeStruct((2, GW, HALF), BF),
        ],
        **comm_params("front", 2),
    )(
        lens, tokens, *weights, w_kernel, b_kernel, perm, wdep, bv, bc, bq, bp, w_inter, w_dense, w_output, cotangent
    )


def back_kernel(
    lens, gcv_ref, conv_ref, kp_ref, q_ref, pt_ref, wk_ref, spread_ref, ones_ref,
    qs_ref, do_ref, k_ref, v_ref, kt_ref, lse_ref, del_ref, pay_all, hid_ref,
    seq_hbm, wc_ref, wp_ref, gpre_ref, dep_ref, wdep_ref, smf_ref, gbi_ref,
    gqm_ref, dq_ref, dk_ref, dv_ref, ghm_ref, edge_ref, half_ref, piece_ref, piece_cp_ref, out_ref,
    acc, wbuf, tbuf, dka, dva, near, mine, ybuf, mid, zbuf, both, xbuf, half,
    gpad, dbuf, hwin, sbuf, agc, agp, gwk, gbk, sm, gdp, pcp, near_cp,
    out2, far2, y2, mid2, z2, out_cp, far_cp, y_cp, mid_cp, z_cp, pay_ref, seq_ref, loads,
    ns, nr, s, v_sem, ls, hs, hr,
):
    step = pl.program_id(0)
    place = Place()
    n = lens[place.r]
    groups = Groups(place, s, v_sem)
    hidden = FromRows(place, hid_ref, out_ref, ls, hs, hr)
    load_pay = pltpu.make_async_copy(pay_all.at[:, place.c], pay_ref, loads.at[0])
    load_seq = pltpu.make_async_copy(seq_hbm, seq_ref, loads.at[1])

    def near_copy(k):
        rr = 1 - place.r if k % 2 == 0 else place.r
        src, dst = (pay_all, near) if k < 2 else (pcp, near_cp)
        return send(src.at[rr, 1 - place.c], dst.at[rr], ns.at[k], nr.at[k], place.core)

    def over(k, src, dst):
        return send(src, dst, s.at[k], v_sem.at[k], place.across)

    @pl.when(step == 0)
    def _():
        meet(everyone(place))
        near_copy(0).start()
        near_copy(1).start()
        hidden.start()
        load_pay.start()
        load_seq.start()
        for ref in (acc, agc, agp):
            clear(ref)
        for ref in (tbuf, gwk, gbk, sm, gdp):
            ref[...] = jnp.zeros_like(ref)
        gpad[0:32, :] = jnp.zeros((32, HALF), BF)
        gpad[32 + ROWS :, :] = jnp.zeros((32, HALF), BF)

    @pl.when(step == 2)
    def _():
        near_copy(0).wait()
        near_copy(1).wait()
        load_pay.wait()
        there = 1 - place.r
        out2[...] = (near[there, 2].astype(F32) + pay_ref[there, 2].astype(F32)).astype(BF)
        over(18, out2, far2).start()
        for ch in range(2):
            for rr in range(2):
                total = near[rr, ch].astype(F32) + pay_ref[rr, ch].astype(F32)
                mine[ch, :, :, rr] = total.astype(BF)
            groups.half(ch, mine.at[ch], ybuf.at[ch]).start()

    def settle(ch):
        groups.half(ch, mine.at[ch], ybuf.at[ch]).wait_recv()
        mid[ch] = (mine[ch, place.y].astype(F32) + ybuf[ch].astype(F32)).astype(BF)

    def merge(ch):
        groups.cross(16 + ch, both.at[ch], xbuf.at[ch]).wait_recv()
        return (both[ch, place.r].astype(F32) + xbuf[ch].astype(F32)).astype(BF)

    def quarters(ch):
        if ch < 2:
            return 4 + 3 * ch, mid.at[ch], zbuf.at[ch]
        return (10, mid2, z2) if ch == 2 else (13, mid_cp, z_cp)

    @pl.when(step == 6)
    def _():
        settle(0)
        groups.start_quarters(*quarters(0))
        near_copy(2).start()
        near_copy(3).start()

    @pl.when(step == 7)
    def _():
        near_copy(2).wait()
        near_copy(3).wait()
        there = 1 - place.r
        out_cp[...] = (near_cp[there].astype(F32) + pcp[there, place.c].astype(F32)).astype(BF)
        over(19, out_cp, far_cp).start()

    @pl.when(step == 8)
    def _():
        settle(1)
        groups.start_quarters(*quarters(1))
        groups.collect(*quarters(0), both.at[0])
        groups.cross(16, both.at[0], xbuf.at[0]).start()
        over(18, out2, far2).wait_recv()
        here = near[place.r, 2].astype(F32) + pay_ref[place.r, 2].astype(F32)
        far2[...] = (here + far2[...].astype(F32)).astype(BF)
        groups.half(2, far2, y2).start()

    @pl.when(step == 9)
    def _():
        groups.start_along(20, half, merge(0))
        over(19, out_cp, far_cp).wait_recv()
        here = near_cp[place.r].astype(F32) + pcp[place.r, place.c].astype(F32)
        far_cp[...] = (here + far_cp[...].astype(F32)).astype(BF)
        groups.half(3, far_cp, y_cp).start()

    @pl.when(step == 10)
    def _():
        groups.collect(*quarters(1), both.at[1])
        groups.cross(17, both.at[1], xbuf.at[1]).start()
        groups.half(2, far2, y2).wait_recv()
        mid2[...] = (far2[place.y].astype(F32) + y2[...].astype(F32)).astype(BF)
        groups.start_quarters(*quarters(2))

    @pl.when(step == 11)
    def _():
        piece_ref[0] = merge(1)
        groups.half(3, far_cp, y_cp).wait_recv()
        mid_cp[...] = (far_cp[place.y].astype(F32) + y_cp[...].astype(F32)).astype(BF)
        groups.start_quarters(*quarters(3))

    @pl.when(step < 4)
    def _():
        rows = gcv_ref.shape[0]
        wide = rows + 32
        put_tiles(wbuf, conv_ref[pl.ds(pl.multiple_of(step * rows, 16), wide), :].astype(F32))
        kp = kp_ref[...]
        kpt = kp.T.astype(BF)
        gkps = [None] * KW
        there = pl.ds(pl.multiple_of(place.c * ROWS + step * rows, 16), wide)
        for t in range(HALF // 128):
            cols = slice(t * 128, (t + 1) * 128)
            gcv = gcv_ref[:, cols].astype(F32)
            total = jnp.zeros((wide, 128), F32)
            for j in range(KW):
                prod = (gcv * wbuf[t, 12 + j : 12 + j + rows, :]).astype(BF)
                part = nt(ones_ref[:, cols], prod)
                gkps[j] = part if t == 0 else gkps[j] + part
                at = (t * KW + j) * 128
                tbuf[j % 3, 24 : 24 + rows, :] = nn(kpt, spread_ref[:, at : at + 128]) * gcv
                total = total + tbuf[j % 3, 12 - j : 12 - j + wide, :]
            acc[there, cols] += total
        gkp = jnp.concatenate(gkps, axis=0).reshape(KW, 8, rows)
        kp3 = kp.reshape(KW, 8, rows)
        inner = jnp.sum(kp3 * gkp, axis=0, keepdims=True)
        gl = (kp3 * (gkp - inner)).reshape(KW * 8, rows)
        glt = gl.T.astype(BF)
        gbk[0:1, 0:72] += col_sum(glt.astype(F32))
        q = q_ref[...].astype(F32)
        pt = pt_ref[...].astype(F32)
        gwk[...] += nn(gl.astype(BF), (pt * q).astype(BF))
        gmix = nn(glt, wk_ref[...])
        gqm_ref[...] = (gmix * pt).astype(BF)
        gpad[rows_at(32 + step * rows, rows), :] = (gmix * q).astype(BF)

    def conv_grads(first, rows):
        keep = row_ids(first, rows) < n
        gco = jnp.where(keep, acc[rows_at(16 + first, rows), :], 0.0).astype(BF)
        tok = seq_ref[rows_at(PAD + first, rows), :]
        h = jnp.where(keep, tok.astype(F32), 0.0).astype(BF)
        agc[...] += nn(gco.T, h)
        sm[2:3, :] += col_sum(gco.astype(F32))
        return nn(gco, wc_ref[0])

    @pl.when(step == 4)
    def _():
        load_seq.wait()
        wdep = wdep_ref[...].astype(F32)
        at = pl.multiple_of((1 - place.c) * (ROWS + 16), 16)
        sbuf[...] = nn(gpad[pl.ds(at, 48), :], wp_ref[0])
        total = conv_grads(pl.multiple_of(ROWS - 16 * place.c, 16), 16)
        for j in range(KW):
            total = total + sbuf[20 - j : 36 - j, :] * wdep[j : j + 1, :]
        edge_ref[...] = total

    @pl.when((step == 4) | (step == 5))
    def _():
        m = step - 4
        rows = gpre_ref.shape[0]
        wide = rows + 32
        first = pl.multiple_of(place.c * ROWS + m * rows, 16)
        wdep = wdep_ref[...].astype(F32)
        win = gpad[rows_at(m * rows + 16, wide), :]
        gpt = win[16 : 16 + rows]
        sm[3:4, :] += col_sum(gpt.astype(F32))
        agp[...] += nn(gpt.T, dep_ref[...])
        put_tiles(dbuf, nn(win, wp_ref[0]))
        ids = row_ids(first - 16, wide)
        inside = (ids >= 0) & (ids < n)
        put_tiles(hwin, jnp.where(inside, seq_ref[pl.ds(first, wide), :].astype(F32), 0.0))
        ghm_ref[...] = (conv_grads(first, rows) + gpre_ref[...].astype(F32)).astype(BF)
        for t in range(D // 128):
            cols = slice(t * 128, (t + 1) * 128)

            def strip(k, sums):
                r0 = pl.multiple_of(k * 64, 64)
                gdep = dbuf[t, pl.ds(r0 + 16, 64), :]
                total = ghm_ref[pl.ds(r0, 64), cols].astype(F32)
                new = []
                for j in range(KW):
                    prod = gdep * hwin[t, pl.ds(r0 + 12 + j, 64), :]
                    new.append(sums[j] + jnp.sum(prod.reshape(8, 8, 128), axis=0))
                    total = total + dbuf[t, pl.ds(r0 + 20 - j, 64), :] * wdep[j : j + 1, cols]
                ghm_ref[pl.ds(r0, 64), cols] = total.astype(BF)
                return tuple(new)

            sums = lax.fori_loop(0, rows // 64, strip, (jnp.zeros((8, 128), F32),) * KW)
            for j in range(KW):
                gdp[j : j + 1, cols] += col_sum(sums[j])

    @pl.when(step == 5)
    def _():
        def put(r, c, first, value):
            pcp[r, c, first // 256, first // 64 % 4] = value.astype(BF)

        zeros = lambda k: jnp.zeros((k, HALF), F32)
        bias = jnp.concatenate([gbk[0:1, :], jnp.zeros((1, 256), F32)], axis=1)
        mixed = [sm[2:4, :], bias, gdp[8:9, 0:HALF], gdp[8:9, HALF:D], zeros(3)]
        inter = [gbi_ref[:, k * HALF : (k + 1) * HALF] for k in range(8)]
        norms = [smf_ref[:, 0:HALF], smf_ref[:, HALF:D]]
        depth = [gdp[0:8, 0:HALF], gdp[0:8, HALF:D], zeros(8)]
        little = jnp.concatenate([gwk[...]] + mixed + norms + inter + depth, axis=0)
        for r in range(2):
            for c in range(2):
                for k in range(3):
                    rows = slice(c * 192 + k * 64, c * 192 + (k + 1) * 64)
                    put(r, c, k * 64, agc[rows, r * HALF : (r + 1) * HALF])
                    put(r, c, 192 + k * 64, agp[rows, r * HALF : (r + 1) * HALF])
                put(r, c, 384, little[0:64])
                put(r, c, 448, little[64:128])

    @pl.when(step >= 6)
    def _():
        i = lax.rem(step, 2)
        k = k_ref[...]
        v = v_ref[...]
        rows = qs_ref.shape[0]
        lane = lax.broadcasted_iota(jnp.int32, (rows, 128), 1)
        dk = dv = None
        for hh in range(2):
            head = (lane < HD) == (hh == 0)
            q = jnp.where(head, qs_ref[...], jnp.zeros((), BF))
            do = jnp.where(head, do_ref[...], jnp.zeros((), BF))
            p = jnp.exp2(nt(k, q) - lse_ref[0, hh : hh + 1, :])
            ds = (p * (nt(v, do) - del_ref[0, hh : hh + 1, :])).astype(BF)
            dv_one = nn(p.astype(BF), do)
            dk_one = nn(ds, q)
            dv = dv_one if dv is None else dv + dv_one
            dk = dk_one if dk is None else dk + dk_one
            dq_ref[hh * HD : (hh + 1) * HD, :] = (nn(kt_ref[hh * HD : (hh + 1) * HD, :], ds) * 0.125).astype(BF)

        @pl.when(i == 0)
        def _():
            dka[...] = dk
            dva[...] = dv

        @pl.when(i == 1)
        def _():
            keep = row_ids(0, LMAX) < n
            dk_ref[...] = jnp.where(keep, (dka[...] + dk) * LN2, 0.0).astype(BF)
            dv_ref[...] = jnp.where(keep, dva[...] + dv, 0.0).astype(BF)

    @pl.when(step == 11)
    def _():
        groups.collect(*quarters(2), piece_ref.at[1])
        groups.collect(*quarters(3), piece_cp_ref)
        groups.await_along(20, half)
        half_ref[...] = half[...]
        for ch in range(2):
            groups.half(ch, mine.at[ch], ybuf.at[ch]).wait_send()
            groups.cross(16 + ch, both.at[ch], xbuf.at[ch]).wait_send()
        groups.half(2, far2, y2).wait_send()
        groups.half(3, far_cp, y_cp).wait_send()
        over(18, out2, far2).wait_send()
        over(19, out_cp, far_cp).wait_send()
        for offset in (1, 2, 3):
            for ch in range(4):
                groups.quarter(*quarters(ch), offset).wait_send()
            groups.along(20, half, offset, place.z).wait_send()
        hidden.finish()


def back(
    lens, gcv, conv, kp, q, pt, wk72, spread, ones8, qs, do, kd, vz, kt, lse, delta, pay, hid,
    seq, w5, gpre, dep, wdep, smf, gbi,
):
    crows = 256
    rows = 512
    early = lambda s: jnp.minimum(s, 3)
    between = lambda s: jnp.minimum(jnp.maximum(s - 4, 0), 1)
    late = lambda s: jnp.maximum(s - 6, 0)
    which = lambda s: lax.div(late(s), 2)
    part = lambda s: lax.rem(late(s), 2)
    cblk = pl.BlockSpec((crows, HALF), lambda s, lens: (early(s), 0))
    mine = pl.BlockSpec((rows, 128), lambda s, lens: (part(s), which(s)))
    pair = pl.BlockSpec((LMAX, 128), lambda s, lens: (0, which(s)))
    stats = pl.BlockSpec((1, 8, rows), lambda s, lens: (which(s), 0, part(s)))
    full = pl.BlockSpec((rows, D), lambda s, lens: (between(s), 0))
    weight = lambda j: pl.BlockSpec((1, HALF, D), lambda s, lens: (j, 0, 0), pipeline_mode=pl.Buffered(1))
    block = (3, 2, 4, 80, HALF)
    pay = pay.reshape((2, 2) + block)
    return pl.pallas_call(
        back_kernel,
        grid_spec=pltpu.PrefetchScalarGridSpec(
            num_scalar_prefetch=1,
            grid=(12,),
            in_specs=[
                cblk,
                once((ROWS + 32, HALF)),
                pl.BlockSpec((72, crows), lambda s, lens: (0, early(s))),
                cblk,
                cblk,
                once((72, HALF)),
                once((72, KW * HALF)),
                once((8, HALF)),
                mine,
                mine,
                pair,
                pair,
                pl.BlockSpec((128, LMAX), lambda s, lens: (which(s), 0)),
                stats,
                stats,
                HBM,
                once((ROWS, D)),
                HBM,
                weight(2),
                weight(4),
                full,
                full,
                once((KW, D)),
                once((8, D)),
                once((1, FF)),
            ],
            out_specs=[
                cblk,
                pl.BlockSpec((128, rows), lambda s, lens: (which(s), part(s))),
                pair,
                pair,
                full,
                once((16, D)),
                once((4, 80, HALF)),
                once((2, 80, HALF)),
                once((64, HALF)),
                HBM,
            ],
            scratch_shapes=[
                pltpu.VMEM((LMAX + 32, HALF), F32),
                pltpu.VMEM((HALF // 128, crows + 32, 128), F32),
                pltpu.VMEM((3, crows + 48, 128), F32),
                pltpu.VMEM((LMAX, 128), F32),
                pltpu.VMEM((LMAX, 128), F32),
                pltpu.VMEM((2,) + block, BF),
                pltpu.VMEM((2, 2, 4, 2, 80, HALF), BF),
                pltpu.VMEM((2, 4, 2, 80, HALF), BF),
                pltpu.VMEM((2, 4, 2, 80, HALF), BF),
                pltpu.VMEM((2, 3, 2, 80, HALF), BF),
                pltpu.VMEM((2, 2, 80, HALF), BF),
                pltpu.VMEM((2, 80, HALF), BF),
                pltpu.VMEM((4, 80, HALF), BF),
                pltpu.VMEM((ROWS + 64, HALF), BF),
                pltpu.VMEM((D // 128, rows + 32, 128), F32),
                pltpu.VMEM((D // 128, rows + 32, 128), F32),
                pltpu.VMEM((48, D), F32),
                pltpu.VMEM((HALF, D), F32),
                pltpu.VMEM((HALF, D), F32),
                pltpu.VMEM((72, HALF), F32),
                pltpu.VMEM((8, 128), F32),
                pltpu.VMEM((8, HALF), F32),
                pltpu.VMEM((16, D), F32),
                pltpu.VMEM((2, 2, 2, 4, 64, HALF), BF),
                pltpu.VMEM((2, 2, 4, 64, HALF), BF),
                pltpu.VMEM((2, 4, 80, HALF), BF),
                pltpu.VMEM((2, 4, 80, HALF), BF),
                pltpu.VMEM((4, 80, HALF), BF),
                pltpu.VMEM((4, 80, HALF), BF),
                pltpu.VMEM((3, 80, HALF), BF),
                pltpu.VMEM((2, 4, 64, HALF), BF),
                pltpu.VMEM((2, 4, 64, HALF), BF),
                pltpu.VMEM((4, 64, HALF), BF),
                pltpu.VMEM((4, 64, HALF), BF),
                pltpu.VMEM((3, 64, HALF), BF),
                pltpu.VMEM((2,) + block, BF),
                pltpu.VMEM((LMAX + 2 * PAD, D), BF),
                pltpu.SemaphoreType.DMA((2,)),
                pltpu.SemaphoreType.DMA((4,)),
                pltpu.SemaphoreType.DMA((4,)),
                pltpu.SemaphoreType.DMA((23,)),
                pltpu.SemaphoreType.DMA((23,)),
                pltpu.SemaphoreType.DMA,
                pltpu.SemaphoreType.DMA((2,)),
                pltpu.SemaphoreType.DMA((3,)),
            ],
        ),
        out_shape=[
            jax.ShapeDtypeStruct((ROWS, HALF), BF),
            jax.ShapeDtypeStruct((HALF, ROWS), BF),
            jax.ShapeDtypeStruct((LMAX, HALF), BF),
            jax.ShapeDtypeStruct((LMAX, HALF), BF),
            jax.ShapeDtypeStruct((ROWS, D), BF),
            jax.ShapeDtypeStruct((16, D), F32),
            jax.ShapeDtypeStruct((4, 80, HALF), BF),
            jax.ShapeDtypeStruct((2, 80, HALF), BF),
            jax.ShapeDtypeStruct((64, HALF), BF),
            jax.ShapeDtypeStruct((2, ROWS, HALF), BF),
        ],
        **comm_params("back", 4),
    )(
        lens, gcv, conv, kp, q, pt, wk72, spread, ones8, qs, do, kd, vz, kt, lse, delta, pay, hid,
        seq, w5, w5, gpre, dep, wdep, smf, gbi,
    )


def norm_parts(x):
    xc = x - jnp.mean(x, axis=1, keepdims=True)
    inv = lax.rsqrt(jnp.mean(xc * xc, axis=1, keepdims=True) + EPS)
    return xc * inv, inv


def norm_back(up, normal, inv, gain):
    e = up * gain
    return inv * (e - jnp.mean(e, axis=1, keepdims=True) - normal * jnp.mean(e * normal, axis=1, keepdims=True))


def ffn_kernel(
    lens, ctx_ref, mix_ref, tok_ref, cot_ref, wd_ref, wi_hbm, wo_hbm, v0, v1, v2, v3, v4, v5, bi_ref, ones_ref,
    hid_ref, gpre_ref, gctx_ref, gcv_ref, del_ref, pay_ref, sm_ref, gbi_ref,
    act_s, gp_s, awd, awi, awo, wi_ref, wo_ref, loads,
):
    i = pl.program_id(0)
    rows = ctx_ref.shape[0]
    keep = row_ids(half_index() * ROWS + i * rows, rows) < length(lens)

    load_wi = pltpu.make_async_copy(wi_hbm, wi_ref, loads.at[0])
    load_wo = pltpu.make_async_copy(wo_hbm, wo_ref, loads.at[1])

    @pl.when(i == 0)
    def _():
        load_wi.start()
        load_wo.start()
        clear(awd)
        for g in range(2):
            clear(awi.at[g])
            clear(awo.at[g])
        sm_ref[...] = jnp.zeros_like(sm_ref)
        gbi_ref[...] = jnp.zeros_like(gbi_ref)

    vectors = [line(ref) for ref in (v0, v1, v2, v3, v4, v5)]
    vec = lambda k: vectors[k]
    inter_bias = line(bi_ref)
    h = tok_ref[...].astype(F32)
    ctx = ctx_ref[...]
    mixed = jnp.concatenate([ctx, mix_ref[...]], axis=1)
    n1, inv1 = norm_parts(nn(mixed, wd_ref[...]) + vec(0) + h)
    f1 = n1 * vec(1) + vec(2)
    fl = f1.astype(BF)

    @pl.when(i == 0)
    def _():
        load_wi.wait()
        load_wo.wait()

    chunk = 512
    outs = []
    for g in range(2):
        fg = fl[:, g * HALF : (g + 1) * HALF]
        for ch in range(GW // chunk):
            cols = slice(ch * chunk, (ch + 1) * chunk)
            put = slice(g * GW + ch * chunk, g * GW + (ch + 1) * chunk)
            x = nn(fg, wi_ref[g, :, cols]) + inter_bias[:, put]
            phi = 0.5 + 0.5 * lax.erf(x * 0.7071067811865476)
            act_s[:, put] = (x * phi).astype(BF)
            gp_s[:, put] = phi + x * jnp.exp2(x * x * (-0.5 * LOG2E)) * 0.3989422804014327
        outs.append(nn(act_s[:, g * GW : (g + 1) * GW], wo_ref[g]))
    n2, inv2 = norm_parts(jnp.concatenate(outs, axis=1) + vec(3) + f1)
    hid_ref[...] = (n2 * vec(4) + vec(5)).astype(BF)
    u = jnp.where(keep, cot_ref[...].astype(F32), 0.0)
    gp2 = norm_back(u, n2, inv2, vec(4))
    go = gp2.astype(BF)
    got = go.T
    flt = fl.T
    gfs = []
    for g in range(2):
        sel = slice(g * HALF, (g + 1) * HALF)
        gf = gp2[:, sel]
        for ch in range(GW // chunk):
            cols = slice(ch * chunk, (ch + 1) * chunk)
            put = slice(g * GW + ch * chunk, g * GW + (ch + 1) * chunk)
            gi = (gp_s[:, put] * nt(go[:, sel], wo_ref[g, cols, :])).astype(BF)
            gbi_ref[0:1, put] += col_sum(gi.astype(F32))
            awo[g, :, cols] += nn(got[sel], act_s[:, put])
            awi[g, :, cols] += nn(flt[sel], gi)
            gf = gf + nt(gi, wi_ref[g, :, cols])
        gfs.append(gf)
    gf = jnp.concatenate(gfs, axis=1)
    gpre = norm_back(gf, n1, inv1, vec(1))
    gd = gpre.astype(BF)
    gpre_ref[...] = gd
    sm_ref[0:1, :] += col_sum(go.astype(F32))
    sm_ref[1:2, :] += col_sum(u * n2)
    sm_ref[2:3, :] += col_sum(u)
    sm_ref[3:4, :] += col_sum(gd.astype(F32))
    sm_ref[4:5, :] += col_sum(gf * n1)
    sm_ref[5:6, :] += col_sum(gf)
    awd[...] += nn(mixed.T, gd)
    gm = nt(gd, wd_ref[...])
    gctx = gm[:, :HALF].astype(BF)
    gctx_ref[...] = gctx
    gcv_ref[...] = gm[:, HALF:].astype(BF)
    prod = (gctx.astype(F32) * ctx.astype(F32)).astype(BF)
    del_ref[...] = nt(ones_ref[...], prod).reshape(3, 8, rows)

    @pl.when(i == pl.num_programs(0) - 1)
    def _():
        for r in range(2):
            for c in range(2):
                pay_ref[r, c, 0:HALF, :] = awi[r, :, c * D : c * D + HALF].astype(BF)
                pay_ref[r, c, HALF:D, :] = awi[r, :, c * D + HALF : (c + 1) * D].astype(BF)
                pay_ref[r, c, D : 2 * D, :] = awo[r, :, c * D : (c + 1) * D].T.astype(BF)
                for part in range(2):
                    piece = awd[part * HALF + c * 192 : part * HALF + (c + 1) * 192, r * HALF : (r + 1) * HALF]
                    pay_ref[r, c, 2 * D + part * 192 : 2 * D + (part + 1) * 192, :] = piece.astype(BF)


def ffn(lens, ctx, mix, tok, cot, wd, wi, wo, vectors, bi, ones24):
    rows = 256
    blk = lambda w: pl.BlockSpec((rows, w), lambda i, lens: (i, 0))
    return pl.pallas_call(
        ffn_kernel,
        grid_spec=pltpu.PrefetchScalarGridSpec(
            num_scalar_prefetch=1,
            grid=(ROWS // rows,),
            in_specs=[
                blk(HALF),
                blk(HALF),
                blk(D),
                blk(D),
                once((D, D)),
                HBM,
                HBM,
                *[whole((D,))] * 6,
                whole((FF,)),
                whole((24, HALF)),
            ],
            out_specs=[
                blk(D),
                blk(D),
                blk(HALF),
                blk(HALF),
                pl.BlockSpec((3, 8, rows), lambda i, lens: (0, 0, i)),
                once((2, 2, FFN_ROWS, HALF)),
                whole((8, D)),
                whole((1, FF)),
            ],
            scratch_shapes=[
                pltpu.VMEM((rows, FF), BF),
                pltpu.VMEM((rows, FF), F32),
                pltpu.VMEM((D, D), F32),
                pltpu.VMEM((2, HALF, GW), F32),
                pltpu.VMEM((2, HALF, GW), F32),
                pltpu.VMEM((2, HALF, GW), BF),
                pltpu.VMEM((2, GW, HALF), BF),
                pltpu.SemaphoreType.DMA((2,)),
            ],
        ),
        out_shape=[
            jax.ShapeDtypeStruct((ROWS, D), BF),
            jax.ShapeDtypeStruct((ROWS, D), BF),
            jax.ShapeDtypeStruct((ROWS, HALF), BF),
            jax.ShapeDtypeStruct((ROWS, HALF), BF),
            jax.ShapeDtypeStruct((3, 8, ROWS), F32),
            jax.ShapeDtypeStruct((2, 2, FFN_ROWS, HALF), BF),
            jax.ShapeDtypeStruct((8, D), F32),
            jax.ShapeDtypeStruct((1, FF), F32),
        ],
        **params("ffn"),
    )(lens, ctx, mix, tok, cot, wd, wi, wo, *vectors, bi, ones24)


def tail_kernel(
    lens, seq_hbm, dk_ref, dv_ref, dq_ref, gqm_ref, ghm_ref, edge_ref, w_hbm, half0, pieces, piece_cp,
    big_ref, cp_ref, sum_ref, ght_ref,
    agw, accb, sm, tsend, trecv, gho, halves, other, half_cp, last_cp,
    pay, total_sum, near, far, out, mid, ybuf, zsum, s, v, ns, nr, cs, cr, gs, gr, es, er, ls, hs, hr,
    toks, w_ref, loads,
):
    step = pl.program_id(0)
    i = lax.rem(step, 4)
    p = Place()
    r, c = p.r, p.c
    rows = dk_ref.shape[0]
    b = lax.rem((1 - c) * 2 + i, 4)
    n = lens[r]
    groups = Groups(p, gs, gr)
    chunks = 5
    crows = PROJ_ROWS // chunks
    summed = Sum(p, far, mid, ybuf, zsum, total_sum, crows, s, v)
    places = [FromRows(p, gho.at[k], ght_ref.at[k], ls.at[k], hs.at[k], hr.at[k]) for k in range(2)]

    def load(k):
        first = lax.rem((1 - c) * 2 + k, 4) * rows + PAD
        return pltpu.make_async_copy(seq_hbm.at[rows_at(first, rows), :], toks.at[k], loads.at[k])

    load_w = pltpu.make_async_copy(w_hbm, w_ref, loads.at[4])

    def theirs(k):
        return send(tsend.at[k], trecv.at[k], es.at[k], er.at[k], p.core)

    def part(ch):
        return slice(ch * crows, (ch + 1) * crows)

    def beside(k, ch):
        rr = 1 - r if k == 0 else r
        at = k * chunks + ch
        return send(pay.at[rr, 1 - c, part(ch), :], near.at[rr, part(ch), :], ns.at[at], nr.at[at], p.core)

    def cross(ch):
        return send(out.at[part(ch), :], far.at[part(ch), :], cs.at[ch], cr.at[ch], p.across)

    def arrive(ch):
        beside(1, ch).wait_recv()
        cross(ch).wait_recv()
        total = near[r, part(ch), :].astype(F32) + pay[r, c, part(ch), :].astype(F32)
        far[part(ch), :] = (total + far[part(ch), :].astype(F32)).astype(BF)
        summed.half(ch)

    stages = [
        arrive,
        summed.quarter,
        lambda ch: summed.along(ch, summed.collect(ch)),
        summed.back,
        summed.finish_spread,
    ]

    def tick(t):
        for k, stage in enumerate(stages):
            if 0 <= t - k < chunks:
                stage(t - k)

    halfs = [half0, halves.at[0], halves.at[1], half_cp]
    others = [other.at[0], other.at[1], other.at[2], last_cp]

    def back(k, z):
        return groups.back(9 + 4 * k + z, halfs[k].at[z], others[k].at[z])

    @pl.when(step == 0)
    def _():
        for k in range(4):
            load(k).start()
        load_w.start()
        meet(everyone(p))
        groups.start_along(0, halves.at[0], pieces[0])
        groups.start_along(3, halves.at[1], pieces[1])
        groups.start_along(6, half_cp, piece_cp[...])
        for z in range(4):
            back(0, z).start()
        for j in range(3):
            clear(agw.at[j])
        sm[...] = jnp.zeros_like(sm)

    for k in range(4):

        @pl.when(step == k)
        def _():
            load(k).wait()

    @pl.when(step == 4)
    def _():
        load_w.wait()
        for ch in range(chunks):
            beside(0, ch).wait_recv()
            total = near[1 - r, part(ch), :].astype(F32) + pay[1 - r, c, part(ch), :].astype(F32)
            out[part(ch), :] = total.astype(BF)
            cross(ch).start()

    @pl.when(step == 5)
    def _():
        groups.await_along(0, halves.at[0])
        back(1, 0).start()
        back(1, 1).start()

    @pl.when(step == 6)
    def _():
        tick(0)
        back(1, 2).start()
        back(1, 3).start()

    @pl.when(step == 7)
    def _():
        tick(1)

    keep = row_ids(b * rows, rows) < n

    def query_grad():
        return (dq_ref[...].astype(F32) + gqm_ref[...].astype(F32).T).astype(BF)

    @pl.when(step < 4)
    def _():
        h = jnp.where(keep, toks[i].astype(F32), 0.0).astype(BF)
        agw[0] += nn(dk_ref[...].T, h)
        agw[1] += nn(dv_ref[...].T, h)
        sm[1:2, :] += col_sum(dv_ref[...].astype(F32))

        @pl.when(step >= 2)
        def _():
            gqt = query_grad()
            sm[0:1, :] += col_sum(gqt.T.astype(F32))
            agw[2] += nn(gqt, h)

    @pl.when(step == 3)
    def _():
        for rr in range(2):
            for cc in range(2):
                for j in range(3):
                    piece = agw[j, cc * 192 : (cc + 1) * 192, rr * HALF : (rr + 1) * HALF]
                    pay[rr, cc, j * 192 : (j + 1) * 192, :] = piece.astype(BF)
                pay[rr, cc, 576:, :] = jnp.concatenate([sm[...], jnp.zeros((56, HALF), F32)], axis=0).astype(BF)
        for ch in range(chunks):
            for k in range(2):
                beside(k, ch).start()

    @pl.when(step >= 4)
    def _():
        accb[...] = nn(dk_ref[...], w_ref[0]) + nn(dv_ref[...], w_ref[1])

        @pl.when(step >= 6)
        def _():
            accb[...] += nn(query_grad().T, w_ref[3]) + ghm_ref[...].astype(F32)

    for k in range(2):

        @pl.when((step == 4 + k) & (c == k))
        def _():
            at = slice(0, 16) if k == 0 else slice(rows - 16, rows)
            accb[at, :] += edge_ref[...]

        @pl.when(step == 4 + k)
        def _():
            tsend[k] = jnp.where(keep, accb[...], 0.0).astype(BF)
            theirs(k).start()

        @pl.when(step == 6 + k)
        def _():
            theirs(k).wait_recv()
            gho[k] = jnp.where(keep, accb[...] + trecv[k].astype(F32), 0.0).astype(BF)
            places[k].start()

    @pl.when(step == 7)
    def _():
        tick(2)
        groups.await_along(3, halves.at[1])
        back(2, 0).start()
        back(2, 1).start()
        tick(3)
        back(2, 2).start()
        back(2, 3).start()
        tick(4)
        groups.await_along(6, half_cp)
        back(3, 0).start()
        back(3, 1).start()
        tick(5)
        back(3, 2).start()
        back(3, 3).start()
        tick(6)
        for ch in range(2):
            for z in range(4):
                back(ch, z).wait_recv()
        big_ref[0, p.y] = half0[...]
        big_ref[0, 1 - p.y] = other[0]
        big_ref[1, p.y] = halves[0]
        big_ref[1, 1 - p.y] = other[1]
        tick(7)
        for z in range(4):
            back(3, z).wait_recv()
        cp_ref[p.y] = half_cp[...]
        cp_ref[1 - p.y] = last_cp[...]
        tick(8)
        sum_ref[...] = total_sum[...]
        for z in range(4):
            back(2, z).wait_recv()
        big_ref[2, p.y] = halves[1]
        big_ref[2, 1 - p.y] = other[2]
        for ch in range(chunks):
            summed.finish_sum(ch)
            cross(ch).wait_send()
            for k in range(2):
                beside(k, ch).wait_send()
        for k in range(4):
            for z in range(4):
                back(k, z).wait_send()
        for offset in (1, 2, 3):
            groups.along(0, halves.at[0], offset, p.z).wait_send()
            groups.along(3, halves.at[1], offset, p.z).wait_send()
            groups.along(6, half_cp, offset, p.z).wait_send()
        theirs(0).wait_send()
        theirs(1).wait_send()
        places[0].finish()
        places[1].finish()


def tail(lens, seq_tok, dk, dv, dq, gqm, ghm, edge, w5, half0, pieces, piece_cp):
    rows = 512
    mine = lambda s: jnp.maximum(lax.rem(s, 4) - 2, 0)
    seq = pl.BlockSpec((rows, HALF), lambda s, lens: (lax.rem((1 - half_index()) * 2 + s, 4), 0))
    own = lambda w: pl.BlockSpec((rows, w), lambda s, lens: (mine(s), 0))
    crows = PROJ_ROWS // 5
    return pl.pallas_call(
        tail_kernel,
        grid_spec=pltpu.PrefetchScalarGridSpec(
            num_scalar_prefetch=1,
            grid=(8,),
            in_specs=[
                HBM,
                seq,
                seq,
                pl.BlockSpec((HALF, rows), lambda s, lens: (0, mine(s))),
                own(HALF),
                own(D),
                once((16, D)),
                HBM,
                once((4, 80, HALF)),
                once((2, 80, HALF)),
                once((64, HALF)),
            ],
            out_specs=[
                once((3, 2, 4, 80, HALF)),
                once((2, 4, 64, HALF)),
                once((PROJ_ROWS, HALF)),
                HBM,
            ],
            scratch_shapes=[
                pltpu.VMEM((3, HALF, D), F32),
                pltpu.VMEM((rows, D), F32),
                pltpu.VMEM((8, HALF), F32),
                pltpu.VMEM((2, rows, D), BF),
                pltpu.VMEM((2, rows, D), BF),
                pltpu.VMEM((2, rows, D), BF),
                pltpu.VMEM((2, 4, 80, HALF), BF),
                pltpu.VMEM((3, 4, 80, HALF), BF),
                pltpu.VMEM((4, 64, HALF), BF),
                pltpu.VMEM((4, 64, HALF), BF),
                pltpu.VMEM((2, 2, PROJ_ROWS, HALF), BF),
                pltpu.VMEM((PROJ_ROWS, HALF), BF),
                pltpu.VMEM((2, PROJ_ROWS, HALF), BF),
                pltpu.VMEM((PROJ_ROWS, HALF), BF),
                pltpu.VMEM((PROJ_ROWS, HALF), BF),
                *Sum.scratch(crows, 5),
                pltpu.SemaphoreType.DMA((10,)),
                pltpu.SemaphoreType.DMA((10,)),
                pltpu.SemaphoreType.DMA((5,)),
                pltpu.SemaphoreType.DMA((5,)),
                pltpu.SemaphoreType.DMA((25,)),
                pltpu.SemaphoreType.DMA((25,)),
                pltpu.SemaphoreType.DMA((2,)),
                pltpu.SemaphoreType.DMA((2,)),
                pltpu.SemaphoreType.DMA((2,)),
                pltpu.SemaphoreType.DMA((2, 2)),
                pltpu.SemaphoreType.DMA((2, 3)),
                pltpu.VMEM((4, rows, D), BF),
                pltpu.VMEM((5, HALF, D), BF),
                pltpu.SemaphoreType.DMA((5,)),
            ],
        ),
        out_shape=[
            jax.ShapeDtypeStruct((3, 2, 4, 80, HALF), BF),
            jax.ShapeDtypeStruct((2, 4, 64, HALF), BF),
            jax.ShapeDtypeStruct((PROJ_ROWS, HALF), BF),
            jax.ShapeDtypeStruct((2, 2, rows, HALF), BF),
        ],
        **comm_params("tail", 6),
    )(lens, seq_tok, dk, dv, dq, gqm, ghm, edge, w5, half0, pieces, piece_cp)


def outputs_kernel(
    ght, hid, t0, t1, t2, t3, t4, big_i0, big_i1, big_o, big_d, little, late_ref, perm_ref,
    hid_ref, gt_ref, gk_ref, gv_ref, gc_ref, gq_ref, gp_ref, gi_ref, go_ref, gd_ref,
    gdep_ref, gbq_ref, gbv_ref, gbc_ref, gbp_ref, gwk_ref, gbk_ref,
    gbd_ref, gg1_ref, gb1_ref, gbi_ref, gbo_ref, gg2_ref, gb2_ref,
):
    i = pl.program_id(0)
    hid_ref[...] = hid[...]
    gt_ref[...] = ght[0, 0].astype(F32)

    for src, ref in ((t0, gk_ref), (t1, gv_ref), (t2, gq_ref), (t3, gc_ref), (t4, gp_ref), (big_o, go_ref), (big_d, gd_ref)):
        ref[...] = src[...].astype(F32)
    gi_ref[:, 0:HALF] = big_i0[...].astype(F32)
    gi_ref[:, HALF:D] = big_i1[...].astype(F32)

    @pl.when(i == 0)
    def _():
        mixed = little[72:80, :].astype(F32)
        low = little[80:88, :].astype(F32)
        high = little[88:96, :].astype(F32)
        inter = little[96:104, :].astype(F32)
        late = late_ref[0:16, :].astype(F32)
        gwk_ref[...] = nn(perm_ref[...], little[0:72, :])
        bias = nt(mixed[:, 0:72].astype(BF), perm_ref[...])
        gbk_ref[...] = bias[2:3, :].reshape(54)
        for k, ref in enumerate((gbq_ref, gbv_ref)):
            ref[...] = late[k : k + 1, :].reshape(HALF)
        for k, ref in enumerate((gbc_ref, gbp_ref)):
            ref[...] = mixed[k : k + 1, :].reshape(HALF)
        for k, ref in enumerate((gbo_ref, gg2_ref, gb2_ref, gbd_ref, gg1_ref, gb1_ref)):
            ref[...] = jnp.concatenate([low[k : k + 1, :], high[k : k + 1, :]], axis=1).reshape(D)
        gbi_ref[...] = jnp.concatenate([inter[k : k + 1, :] for k in range(8)], axis=1).reshape(FF)
        gdep_ref[0:8, 0:HALF] = little[104:112, :].astype(F32)
        gdep_ref[0:8, HALF:D] = little[112:120, :].astype(F32)
        gdep_ref[8:9, 0:HALF] = mixed[3:4, :]
        gdep_ref[8:9, HALF:D] = mixed[4:5, :]


def outputs(ght, hid, total, cp, big, perm):
    rows = 512
    at = lambda n, first: pl.BlockSpec((n, HALF), lambda i: (first + i, 0))
    blk = at(rows, 0)
    chunk = pl.BlockSpec((1, 1, rows, HALF), lambda i: (lax.rem(i, 2), lax.div(i, 2), 0, 0))
    shapes = [(KW, D)] + [(HALF,)] * 4 + [(54, HALF), (54,)] + [(D,)] * 3 + [(FF,)] + [(D,)] * 3
    main = [(192, HALF)] * 5 + [(HALF, D), (D, HALF), (HALF, HALF)]
    return pl.pallas_call(
        outputs_kernel,
        grid=(4,),
        in_specs=[chunk, blk]
        + [at(48, 4 * j) for j in (0, 1, 2, 0, 1)]
        + [at(96, 0), at(96, 4), at(192, 4), at(96, 16)]
        + [pl.BlockSpec((128, HALF), lambda i: (3, 0)), pl.BlockSpec((64, HALF), lambda i: (9, 0)), whole((54, 72))],
        out_specs=[blk, blk]
        + [at(48, 0)] * 5
        + [pl.BlockSpec((96, D), lambda i: (i, 0)), at(192, 0), at(96, 0)]
        + [whole(shape) for shape in shapes],
        out_shape=[jax.ShapeDtypeStruct((LMAX, HALF), BF), jax.ShapeDtypeStruct((LMAX, HALF), F32)]
        + [jax.ShapeDtypeStruct(shape, F32) for shape in main + shapes],
        **params("outputs"),
    )(ght, hid, total, total, total, cp, cp, big, big, big, big, cp, total, perm)


def constants():
    ones8 = np.zeros((8, HALF), np.float32)
    ones24 = np.zeros((24, HALF), np.float32)
    perm = np.zeros((72, 54), np.float32)
    for head in range(6):
        cols = slice(head * HD, (head + 1) * HD)
        ones8[head, cols] = 1
        ones24[head // 2 * 8 + head % 2, cols] = 1
        for j in range(KW):
            perm[j * 8 + head, head * KW + j] = 1
    return [jnp.asarray(a, BF) for a in (ones8, ones24, perm)]


def per_device(
    groups, tokens, cotangent, seq_lengths, w_query, w_key, w_value, w_convout, w_point, w_depth,
    b_query, b_value, b_convout, b_point, w_kernel, b_kernel, w_dense, b_dense, gain_one, bias_one,
    w_inter, b_inter, w_output, b_output, gain_two, bias_two,
):
    lens = seq_lengths
    ones8, ones24, perm = constants()
    wdep = w_depth.T

    kd, kt, vz, q, qs, pt, kp, conv, mix, dep, hown, wk72, bk72, spread, ctx, lse, seq, w5, wi, wd, cot, wo = front(
        lens, tokens, (w_key.T, w_value.T, w_convout.T, w_query.T, w_point.T), w_kernel.T, b_kernel, perm,
        wdep, b_value, b_convout, b_query, b_point,
        w_inter[0], w_dense.reshape(2, 192, HALF), w_output[0], cotangent,
    )
    vectors = (b_dense, gain_one, bias_one, b_output, gain_two, bias_two)
    hid, gpre, gctx, gcv, delta, payf, smf, gbi = ffn(
        lens, ctx, mix, hown, cot, wd.reshape(D, D), wi, wo, vectors, b_inter, ones24
    )
    gqm, dq, dk, dv, ghm, edge, half0, pieces, piece_cp, hid = back(
        lens, gcv, conv, kp, q, pt, wk72, spread, ones8, qs, gctx, kd, vz, kt, lse, delta, payf, hid,
        seq, w5, gpre, dep, wdep, smf, gbi,
    )
    big, cp, total, ght = tail(lens, seq, dk, dv, dq, gqm, ghm, edge, w5, half0, pieces, piece_cp)
    big = big.reshape(FFN_ROWS, HALF)
    cp = cp.reshape(512, HALF)
    if groups > 8:
        sums = lax.psum(tuple(x.astype(F32) * 0.125 for x in (total, cp, big)), "dp")
        total, cp, big = (x.astype(BF) for x in sums)
    (
        hidden_out, gt, gk, gv, gc, gq, gp, gi, go, gd, gdep, gbq, gbv, gbc, gbp, gwk, gbk, gbd, gg1, gb1, gbi, gbo, gg2, gb2,
    ) = outputs(ght, hid.reshape(LMAX, HALF), total, cp, big, perm.T)
    return (
        hidden_out, gt, gq.T, gk.T, gv.T, gc.T, gp.T, gdep.T, gbq, gbv, gbc, gbp, gwk.T, gbk, gd, gbd, gg1, gb1,
        gi[None], gbi, go[None], gbo, gg2, gb2,
    )


def solution(mesh):
    act = P(("dp", "col"), "row")
    rep = P()
    proj = P("row", "col")
    in_specs = (
        act, act, P("dp"), proj, proj, proj, proj, proj, rep, rep, rep, rep, rep, rep, rep, P("col", "row"),
        rep, rep, rep, P("row", None, "col"), rep, P("row", "col", None), rep, rep, rep,
    )
    out_specs = (
        act, act, proj, proj, proj, proj, proj, rep, rep, rep, rep, rep, rep, rep, P("col", "row"),
        rep, rep, rep, P("row", None, "col"), rep, P("row", "col", None), rep, rep, rep,
    )
    return jax.shard_map(
        functools.partial(per_device, mesh.shape["dp"]), mesh=mesh, in_specs=in_specs, out_specs=out_specs, check_vma=False)
```

```python
import functools

import jax
import jax.numpy as jnp
import numpy as np
from jax import lax
from jax.experimental import pallas as pl
from jax.experimental.pallas import tpu as pltpu
from jax.sharding import PartitionSpec as P

D = 768
HALF = 384
HD = 64
KW = 9
FF = 3072
GW = 1536
LMAX = 2048
ROWS = 1024
EPS = 1e-12
LOG2E = 1.4426950408889634
LN2 = 0.6931471805599453
BF = jnp.bfloat16
F32 = jnp.float32
VMEM_BYTES = 63 * 1024 * 1024
PAD = 16
FFN_ROWS = 1920
FFN_CHUNK = 640
PROJ_ROWS = 640
MESH = pl.DeviceIdType.MESH
HBM = pl.BlockSpec(memory_space=pl.ANY)
VMEM = pl.BlockSpec(memory_space=pltpu.VMEM)


def nn(a, b):
    return lax.dot_general(a, b, (((1,), (0,)), ((), ())), preferred_element_type=F32)


def nt(a, b):
    return lax.dot_general(a, b, (((1,), (1,)), ((), ())), preferred_element_type=F32)


def col_sum(x):
    return jnp.sum(x, axis=0, keepdims=True)


def row_ids(start, rows):
    return start + lax.broadcasted_iota(jnp.int32, (rows, 1), 0)


def whole(shape):
    return pl.BlockSpec(shape, lambda *_: (0,) * len(shape))


def once(shape):
    return pl.BlockSpec(shape, lambda *_: (0,) * len(shape), pipeline_mode=pl.Buffered(1))


def half_index():
    return lax.axis_index("col")


def length(lens):
    return lens[lax.axis_index("row")]


def line(ref):
    return ref[...].astype(F32).reshape(1, ref.shape[0])


def spread_taps(probs, spread_ref, t):
    taps = []
    for j in range(0, KW, 2):
        count = min(2, KW - j)
        at = (t * KW + j) * 128
        both = nn(probs, spread_ref[:, at : at + count * 128])
        taps += [both[:, k * 128 : (k + 1) * 128] for k in range(count)]
    return taps


def clear(ref, step=32):
    def body(k, carry):
        ref[pl.ds(pl.multiple_of(k * step, step), step), :] = jnp.zeros((step, ref.shape[1]), ref.dtype)
        return carry

    lax.fori_loop(0, ref.shape[0] // step, body, 0)


def put_tiles(buf, value, first=0):
    for t in range(value.shape[1] // 128):
        buf[t, first : first + value.shape[0], :] = value[:, t * 128 : (t + 1) * 128]


def params(name):
    return dict(
        name=name,
        compiler_params=pltpu.CompilerParams(vmem_limit_bytes=VMEM_BYTES),
    )


def lanes(k, width=HALF):
    return pl.ds(pl.multiple_of(k * width, 128), width)


def rows_at(start, count, step=16):
    return pl.ds(pl.multiple_of(start, step), count)


def send(src, dst, send_sem, recv_sem, device):
    return pltpu.make_async_remote_copy(
        src_ref=src, dst_ref=dst, send_sem=send_sem, recv_sem=recv_sem, device_id=device, device_id_type=MESH
    )


class Place:
    def __init__(self):
        self.d = lax.axis_index("dp")
        self.r = lax.axis_index("row")
        self.c = lax.axis_index("col")
        self.k = lax.rem(self.d, 8)
        self.base = self.d - self.k
        self.y = lax.rem(self.k, 2)
        self.z = lax.div(self.k, 2)
        self.beside = {"dp": self.base + self.z * 2 + 1 - self.y}
        self.across = {"row": 1 - self.r}
        self.core = {"col": 1 - self.c}
        self.diagonal = {"row": 1 - self.r, "col": 1 - self.c}

    def eight(self, offset):
        other = lax.rem(self.k + offset, 8)
        return other, {"dp": self.base + other}

    def four(self, offset):
        other = lax.rem(self.z + offset, 4)
        return other, {"dp": self.base + other * 2 + self.y}


def meet(devices):
    barrier = pltpu.get_barrier_semaphore()
    for device in devices:
        pl.semaphore_signal(barrier, inc=1, device_id=device, device_id_type=MESH)
    pl.semaphore_wait(barrier, len(devices))


def comm_params(name, number):
    return dict(
        name=name,
        compiler_params=pltpu.CompilerParams(
            vmem_limit_bytes=VMEM_BYTES, collective_id=number, has_side_effects=True
        ),
    )


class Gather:
    def __init__(self, place, own, full, part, block, step, send_sem, recv_sem, first):
        self.p, self.own, self.full, self.part, self.block, self.h = place, own, full, part, block, step
        self.s, self.v, self.f = send_sem, recv_sem, first

    def _move(self, src, dst, n, device):
        return send(src, dst, self.s.at[self.f + n], self.v.at[self.f + n], device)

    def _cross(self, r):
        p = self.p
        at = (p.y * 4 + p.z) * self.h
        return self._move(self.part(self.own, at, self.h), self.block(self.full, r, p.c, at, self.h), 0, p.across)

    def _near(self, c):
        p = self.p
        return self._move(self.own, self.block(self.full, p.r, c, 0, 8 * self.h), 1, p.core)

    def _pass(self, offset, z):
        p = self.p
        here = self.block(self.full, 1 - p.r, p.c, (p.y * 4 + z) * self.h, self.h)
        return self._move(here, here, 1 + offset, p.four(offset)[1])

    def _turn(self, y):
        p = self.p
        here = self.block(self.full, 1 - p.r, p.c, y * 4 * self.h, 4 * self.h)
        return self._move(here, here, 5, p.beside)

    def _last(self, c):
        p = self.p
        here = self.block(self.full, 1 - p.r, c, 0, 8 * self.h)
        return self._move(here, here, 6, p.core)

    def start(self):
        self._cross(self.p.r).start()
        self._near(self.p.c).start()

    def relay(self):
        p = self.p
        self._cross(1 - p.r).wait_recv()
        for offset in (1, 2, 3):
            self._pass(offset, p.z).start()

    def turn(self):
        p = self.p
        for offset in (1, 2, 3):
            self._pass(offset, lax.rem(p.z + 4 - offset, 4)).wait_recv()
        self._turn(p.y).start()

    def share(self):
        p = self.p
        self._turn(1 - p.y).wait_recv()
        self._last(p.c).start()

    def finish(self):
        p = self.p
        self._last(1 - p.c).wait_recv()
        self._near(1 - p.c).wait_recv()
        self._cross(p.r).wait_send()
        self._near(p.c).wait_send()
        for offset in (1, 2, 3):
            self._pass(offset, p.z).wait_send()
        self._turn(p.y).wait_send()
        self._last(p.c).wait_send()


def middle_part(ref, first, rows):
    return ref.at[:, rows_at(first, rows, 8), :]


def middle_block(ref, r, c, first, rows):
    return ref.at[:, rows_at(c * 192 + first, rows, 8), lanes(r)]


def rows_part(ref, first, rows):
    return ref.at[rows_at(first, rows), :]


def inter_block(ref, r, c, first, rows):
    return ref.at[r, rows_at(first, rows), lanes(c, 768)]


def output_block(ref, r, c, first, rows):
    return ref.at[r, rows_at(c * 768 + first, rows), :]


class ToRows:
    def __init__(self, place, src, dst, stage, local_sem, send_sem, recv_sem):
        self.p, self.src, self.dst, self.stage = place, src, dst, stage
        self.l, self.s, self.v = local_sem, send_sem, recv_sem

    def _cross(self, q, k):
        half = self.src.at[q * ROWS : (q + 1) * ROWS, :]
        return send(half, self.dst.at[:, lanes(k)], self.s.at[q], self.v.at[0], {"row": 1 - self.p.r, "col": q})

    def _near(self):
        p = self.p
        half = self.src.at[rows_at((1 - p.c) * ROWS, ROWS), :]
        return send(half, self.dst.at[:, lanes(p.r)], self.s.at[2], self.v.at[1], p.core)

    def _load(self):
        return pltpu.make_async_copy(self.src.at[rows_at(self.p.c * ROWS, ROWS), :], self.stage, self.l.at[0])

    def _store(self):
        return pltpu.make_async_copy(self.stage, self.dst.at[:, lanes(self.p.r)], self.l.at[1])

    def start(self):
        p = self.p

        @pl.when(p.r != p.c)
        def _():
            self._cross(0, p.r).start()
            self._cross(1, p.r).start()

        @pl.when(p.r == p.c)
        def _():
            self._near().start()
            self._load().start()

    def store(self):
        @pl.when(self.p.r == self.p.c)
        def _():
            self._load().wait()
            self._store().start()

    def finish(self):
        p = self.p
        self._cross(0, 1 - p.r).wait_recv()

        @pl.when(p.r != p.c)
        def _():
            self._cross(0, p.r).wait_send()
            self._cross(1, p.r).wait_send()
            self._near().wait_recv()

        @pl.when(p.r == p.c)
        def _():
            self._near().wait_send()
            self._store().wait()


class FromRows:
    def __init__(self, place, src, dst, local_sem, send_sem, recv_sem):
        self.p, self.src, self.dst = place, src, dst
        self.l, self.s, self.v = local_sem, send_sem, recv_sem

    def _cross(self, q):
        p = self.p
        place = self.dst.at[q]
        return send(self.src.at[:, lanes(1 - p.r)], place, self.s.at[0], self.v.at[q], {"row": 1 - p.r, "col": p.r})

    def _near(self, q):
        p = self.p
        place = self.dst.at[q]
        return send(self.src.at[:, lanes(p.r)], place, self.s.at[1], self.v.at[2], p.core)

    def _local(self):
        p = self.p
        place = self.dst.at[p.c]
        return pltpu.make_async_copy(self.src.at[:, lanes(p.r)], place, self.l)

    def start(self):
        p = self.p
        self._cross(p.c).start()

        @pl.when(p.r != p.c)
        def _():
            self._near(p.c).start()

        @pl.when(p.r == p.c)
        def _():
            self._local().start()

    def finish(self):
        p = self.p
        self._cross(p.c).wait_send()

        @pl.when(p.r != p.c)
        def _():
            self._near(p.c).wait_send()
            self._cross(0).wait_recv()
            self._cross(1).wait_recv()

        @pl.when(p.r == p.c)
        def _():
            self._near(1 - p.c).wait_recv()
            self._local().wait()


class Sum:
    def __init__(self, place, far, mid, ybuf, zbuf, total, rows, s, v, first=0):
        self.p, self.far, self.mid, self.ybuf, self.zbuf, self.total = place, far, mid, ybuf, zbuf, total
        self.rows, self.s, self.v, self.first = rows, s, v, first

    def _sems(self, ch, n):
        i = self.first + ch * 8 + n
        return self.s.at[i], self.v.at[i]

    def _beside(self):
        return self.p.beside

    def _halves(self, ch, y):
        return rows_at(ch * self.rows + y * (self.rows // 2), self.rows // 2)

    def _piece(self, ch, z):
        return rows_at(ch * self.rows + self.p.y * (self.rows // 2) + z * (self.rows // 8), self.rows // 8)

    def _half(self, ch):
        return send(self.far.at[self._halves(ch, 1 - self.p.y), :], self.ybuf.at[ch], *self._sems(ch, 0), self._beside())

    def _quarter(self, ch, offset):
        other, device = self.p.four(offset)
        src = self.mid.at[ch, rows_at(other * (self.rows // 8), self.rows // 8), :]
        return send(src, self.zbuf.at[ch, offset - 1], *self._sems(ch, offset), device)

    def _along(self, ch, offset, z):
        _, device = self.p.four(offset)
        here = self.total.at[self._piece(ch, z), :]
        return send(here, here, *self._sems(ch, 3 + offset), device)

    def _back(self, ch, y):
        here = self.total.at[self._halves(ch, y), :]
        return send(here, here, *self._sems(ch, 7), self._beside())

    def half(self, ch):
        self._half(ch).start()

    def quarter(self, ch):
        self._half(ch).wait_recv()
        both = self.far[self._halves(ch, self.p.y), :].astype(F32) + self.ybuf[ch].astype(F32)
        self.mid[ch] = both.astype(BF)
        for offset in (1, 2, 3):
            self._quarter(ch, offset).start()

    def collect(self, ch):
        both = self.mid[ch, rows_at(self.p.z * (self.rows // 8), self.rows // 8), :].astype(F32)
        for offset in (1, 2, 3):
            self._quarter(ch, offset).wait_recv()
            both = both + self.zbuf[ch, offset - 1].astype(F32)
        return both.astype(BF)

    def along(self, ch, piece):
        self.total[self._piece(ch, self.p.z), :] = piece
        for offset in (1, 2, 3):
            self._along(ch, offset, self.p.z).start()

    def back(self, ch):
        for offset in (1, 2, 3):
            self._along(ch, offset, lax.rem(self.p.z + 4 - offset, 4)).wait_recv()
        self._back(ch, self.p.y).start()

    def finish_sum(self, ch):
        self._half(ch).wait_send()
        for offset in (1, 2, 3):
            self._quarter(ch, offset).wait_send()

    def finish_spread(self, ch):
        self._back(ch, 1 - self.p.y).wait_recv()
        for offset in (1, 2, 3):
            self._along(ch, offset, self.p.z).wait_send()
        self._back(ch, self.p.y).wait_send()

    @staticmethod
    def scratch(rows, chunks):
        return [
            pltpu.VMEM((chunks, rows // 2, HALF), BF),
            pltpu.VMEM((chunks, rows // 2, HALF), BF),
            pltpu.VMEM((chunks, 3, rows // 8, HALF), BF),
            pltpu.SemaphoreType.DMA((8 * chunks,)),
            pltpu.SemaphoreType.DMA((8 * chunks,)),
        ]


class Groups:
    def __init__(self, place, s, v):
        self.p, self.s, self.v = place, s, v

    def half(self, n, mine, ybuf):
        return send(mine.at[1 - self.p.y], ybuf, self.s.at[n], self.v.at[n], self.p.beside)

    def quarter(self, n, mid, zbuf, offset):
        other, device = self.p.four(offset)
        n = n + offset - 1
        return send(mid.at[other], zbuf.at[offset - 1], self.s.at[n], self.v.at[n], device)

    def cross(self, n, both, xbuf):
        return send(both.at[1 - self.p.r], xbuf, self.s.at[n], self.v.at[n], self.p.across)

    def along(self, n, half, offset, z):
        n = n + offset - 1
        return send(half.at[z], half.at[z], self.s.at[n], self.v.at[n], self.p.four(offset)[1])

    def back(self, n, half, other):
        return send(half, other, self.s.at[n], self.v.at[n], self.p.beside)

    def start_quarters(self, n, mid, zbuf):
        for offset in (1, 2, 3):
            self.quarter(n, mid, zbuf, offset).start()

    def collect(self, n, mid, zbuf, both):
        total = mid[self.p.z].astype(F32)
        for offset in (1, 2, 3):
            self.quarter(n, mid, zbuf, offset).wait_recv()
            total = total + zbuf[offset - 1].astype(F32)
        both[...] = total.astype(BF)

    def start_along(self, n, half, piece):
        half[self.p.z] = piece
        for offset in (1, 2, 3):
            self.along(n, half, offset, self.p.z).start()

    def await_along(self, n, half):
        for offset in (1, 2, 3):
            self.along(n, half, offset, lax.rem(self.p.z + 4 - offset, 4)).wait_recv()

    def sent(self, n, ref, kind):
        for offset in (1, 2, 3):
            kind(n, *ref, offset).wait_send()


def everyone(p):
    return [p.across, p.core, p.diagonal, p.beside] + [p.four(o)[1] for o in (1, 2, 3)]


def front_kernel(
    lens, tok_ref, wk_own, wv_own, wc_own, wq_own, wp_own, kern_ref, kb_ref, perm_ref,
    wdep_ref, bv_ref, bc_ref, bq_ref, bp_ref, wi_own, wd_own, wo_own, cot_own,
    kd_ref, kt_ref, vz_ref, q_ref, qs_ref, pt_ref, kp_ref, conv_ref, mix_ref, dep_ref, h_ref, wk_ref, bk_ref, spread_ref,
    ctx_ref, lse_ref, seq_out, w5_out, wi_ref, wd_ref, cot_ref, wo_ref,
    own, seq_ref, w_ref, stage, first_key, hbuf, cbuf, lsem, ts, tr, gs, gr, cs, cr,
):
    i = pl.program_id(0)
    p = Place()
    r, c = p.r, p.c
    n = lens[r]
    keys = Gather(p, own.at[0:2], w_ref.at[0:2], middle_part, middle_block, 24, gs, gr, 0)
    proj = Gather(p, own.at[2:5], w_ref.at[2:5], middle_part, middle_block, 24, gs, gr, 28)
    inter = Gather(p, wi_own, wi_ref, rows_part, inter_block, 48, gs, gr, 7)
    dense = Gather(p, wd_own, wd_ref, middle_part, middle_block, 24, gs, gr, 14)
    cot_rows = ToRows(p, cot_own, cot_ref, stage, lsem, cs, cr)
    output = Gather(p, wo_own, wo_ref, rows_part, output_block, 96, gs, gr, 21)
    keep_output = pltpu.make_async_copy(wo_own, output_block(wo_ref, r, c, 0, D), lsem.at[7])
    keep_inter = pltpu.make_async_copy(wi_own, inter_block(wi_ref, r, c, 0, HALF), lsem.at[2])
    keep_dense = pltpu.make_async_copy(wd_own, middle_block(wd_ref, r, c, 0, 192), lsem.at[3])
    keep_own = pltpu.make_async_copy(tok_ref, seq_ref.at[PAD : PAD + LMAX, lanes(r)], lsem.at[4])
    keep_seq = pltpu.make_async_copy(seq_ref, seq_out, lsem.at[5])
    keep_w = pltpu.make_async_copy(w_ref, w5_out, lsem.at[6])

    def chunk(m, k):
        return seq_ref.at[PAD + m * 512 : PAD + (m + 1) * 512, lanes(k)]

    def cross(m, k):
        return send(tok_ref.at[m * 512 : (m + 1) * 512, :], chunk(m, k), ts.at[m], tr.at[m], {"row": 1 - r, "col": m // 2})

    def near(k):
        return send(tok_ref, seq_ref.at[PAD : PAD + LMAX, lanes(k)], ts.at[4], tr.at[4], p.core)

    def forward(m):
        return send(chunk(m, 1 - r), chunk(m, 1 - r), ts.at[5 + m], tr.at[5 + m], p.core)

    @pl.when(i == 0)
    def _():
        for j, ref in enumerate((wk_own, wv_own, wc_own, wq_own, wp_own)):
            own[j] = ref[...]
        seq_ref[0:PAD, :] = jnp.zeros((PAD, D), BF)
        seq_ref[PAD + LMAX :, :] = jnp.zeros((PAD, D), BF)
        meet(everyone(p))
        keys.start()
        proj.start()
        inter._cross(r).start()
        dense._cross(r).start()

        @pl.when(r != c)
        def _():
            for m in (0, 2, 1, 3):
                cross(m, r).start()

        @pl.when(r == c)
        def _():
            near(r).start()
            keep_own.start()

        output._cross(r).start()
        cot_rows.start()
        inter._near(c).start()
        dense._near(c).start()
        output._near(c).start()
        keep_inter.start()
        keep_dense.start()
        keep_output.start()
        middle_block(w_ref, r, c, 0, 192)[...] = own[...]
        wk_ref[...] = nn(perm_ref[...], kern_ref[...]).astype(BF)
        bk_ref[...] = nt(perm_ref[...], jnp.broadcast_to(line(kb_ref), (128, 54)).astype(BF))
        row = lax.broadcasted_iota(jnp.int32, (72, 128), 0)
        head = lax.broadcasted_iota(jnp.int32, (72, 128), 1) >> 6
        for t in range(HALF // 128):
            for j in range(KW):
                at = (t * KW + j) * 128
                spread_ref[:, at : at + 128] = jnp.where(row == head + (j * 8 + 2 * t), 1.0, 0.0).astype(BF)
        keys.relay()
        proj.relay()
        keys.turn()
        proj.turn()
        inter.relay()
        dense.relay()

        @pl.when(r != c)
        def _():
            near(r).wait_recv()

        @pl.when(r == c)
        def _():
            keep_own.wait()

        keys.share()
        keys.finish()

        def project(k, carry):
            for at, m in enumerate((0, 2, 1, 3)):

                @pl.when((k == at) & (c == m // 2))
                def _():
                    cross(m, 1 - r).wait_recv()
                    forward(m).start()

                @pl.when((k == at) & (c != m // 2))
                def _():
                    forward(m).wait_recv()

            @pl.when(k == 2)
            def _():
                proj.share()

            krows = LMAX // 4
            first = pl.multiple_of((2 * lax.rem(k, 2) + lax.div(k, 2)) * krows, krows)
            keep_key = row_ids(first, krows) < n
            tok = seq_ref[rows_at(PAD + first, krows), :]
            h = jnp.where(keep_key, tok.astype(F32), 0.0).astype(BF)
            kf = nt(h, w_ref[0])
            v = nt(h, w_ref[1]) + line(bv_ref)

            @pl.when(k == 0)
            def _():
                first_key[...] = kf[0:8]

            kd_ref[pl.ds(first, krows), :] = jnp.where(keep_key, kf, first_key[0:1]).astype(BF)
            kt_ref[:, pl.ds(first, krows)] = kf.T.astype(BF)
            vz_ref[pl.ds(first, krows), :] = jnp.where(keep_key, v, 0.0).astype(BF)
            return carry

        lax.fori_loop(0, 4, project, 0)
        for q in range(2):

            @pl.when(c == q)
            def _():
                for m in (2 * q, 2 * q + 1):
                    forward(m).wait_send()

        @pl.when(r != c)
        def _():
            for m in range(4):
                cross(m, r).wait_send()

        @pl.when(r == c)
        def _():
            near(r).wait_send()

        proj.finish()
        output.relay()
        keep_seq.start()
        keep_w.start()

    @pl.when(i == 1)
    def _():
        inter.turn()
        dense.turn()
        cot_rows.store()

    @pl.when(i == 3)
    def _():
        output.turn()

    @pl.when(i == 4)
    def _():
        inter.share()
        dense.share()

    @pl.when(i == 6)
    def _():
        output.share()

    @pl.when(i < 4)
    def _():
        rows = q_ref.shape[0]
        wide = rows + 32
        base = pl.multiple_of(i * rows, 16)
        start = pl.multiple_of(c * ROWS + i * rows, 16)
        ids = row_ids(start - 16, wide)
        keep = (ids >= 0) & (ids < n)
        hw = jnp.where(keep, seq_ref[pl.ds(start, wide), :].astype(F32), 0.0)
        put_tiles(hbuf, hw)
        wdep = wdep_ref[...].astype(F32)
        for t in range(D // 128):
            cols = slice(t * 128, (t + 1) * 128)
            depth = jnp.zeros((rows, 128), F32)
            for j in range(KW):
                depth = depth + hbuf[t, 12 + j : 12 + j + rows, :] * wdep[j : j + 1, cols]
            dep_ref[:, cols] = depth.astype(BF)
        depth_low = dep_ref[...]
        hl = hw.astype(BF)
        h_ref[...] = hl[16 : 16 + rows]
        conv = jnp.where(keep, nt(hl, w_ref[2]) + line(bc_ref), 0.0)
        put_tiles(cbuf, conv)
        conv_ref[pl.ds(base, wide), :] = conv.astype(BF)
        q = nt(hl[16 : 16 + rows], w_ref[3]) + line(bq_ref)
        q_low = q.astype(BF)
        q_ref[...] = q_low
        qs_ref[pl.ds(base, rows), :] = (q * (0.125 * LOG2E)).astype(BF)
        pt = nt(depth_low, w_ref[4]) + line(bp_ref)
        pt_ref[...] = pt.astype(BF)
        mixer = (pt * q_low.astype(F32)).astype(BF)
        logits = (nt(wk_ref[...], mixer) + bk_ref[:, 0:1]).reshape(KW, 8, rows)
        peak = jnp.max(logits, axis=0, keepdims=True)
        raised = jnp.exp(logits - peak)
        kp = (raised / jnp.sum(raised, axis=0, keepdims=True)).reshape(KW * 8, rows)
        kp_ref[...] = kp
        kpt = kp.T.astype(BF)
        for t in range(HALF // 128):
            mix = jnp.zeros((rows, 128), F32)
            for j, tap in enumerate(spread_taps(kpt, spread_ref, t)):
                mix = mix + tap * cbuf[t, 12 + j : 12 + j + rows, :]
            mix_ref[:, t * 128 : (t + 1) * 128] = mix.astype(BF)

    @pl.when(i >= 4)
    def _():
        cols = lanes(i - 4, 128)
        k = kd_ref[:, cols]
        ones = jnp.where(row_ids(0, LMAX) < n, 1.0, 0.0)
        ve = jnp.concatenate([vz_ref[:, cols], jnp.broadcast_to(ones, (LMAX, 128)).astype(BF)], axis=1)
        rows = 256
        lane = lax.broadcasted_iota(jnp.int32, (rows, 128), 1)
        for u in range(ROWS // rows):
            part = slice(u * rows, (u + 1) * rows)
            outs = []
            for hh in range(2):
                q = jnp.where((lane < HD) == (hh == 0), qs_ref[part, cols], jnp.zeros((), BF))
                s = nt(q, k)
                peak = jnp.max(s, axis=1, keepdims=True)
                prob = jnp.exp2(s - peak).astype(BF)
                o = nn(prob, ve)
                outs.append(o[:, :128] / o[:, 128:])
                lse_ref[0, hh : hh + 1, part] = (peak + jnp.log2(o[:, 128:129])).T
            ctx_ref[part, :] = jnp.where(lane < HD, outs[0], outs[1]).astype(BF)

    @pl.when(i == pl.num_programs(0) - 1)
    def _():
        inter.finish()
        dense.finish()
        output.finish()
        cot_rows.finish()
        keep_inter.wait()
        keep_dense.wait()
        keep_output.wait()
        keep_seq.wait()
        keep_w.wait()


def front(lens, tokens, weights, w_kernel, b_kernel, perm, wdep, bv, bc, bq, bp, w_inter, w_dense, w_output, cotangent):
    rows = 256
    early = lambda i: jnp.minimum(i, 3)
    late = lambda i: jnp.maximum(i - 4, 0)
    blk = pl.BlockSpec((rows, HALF), lambda i, lens: (early(i), 0))
    full = pl.BlockSpec((rows, D), lambda i, lens: (early(i), 0))
    half = jax.ShapeDtypeStruct((ROWS, HALF), BF)
    return pl.pallas_call(
        front_kernel,
        grid_spec=pltpu.PrefetchScalarGridSpec(
            num_scalar_prefetch=1,
            grid=(7,),
            in_specs=[HBM]
            + [once((192, HALF))] * 5
            + [once((54, HALF)), whole((54,)), once((72, 54)), once((KW, D))]
            + [whole((HALF,))] * 4
            + [once((HALF, D)), once((2, 192, HALF)), once((D, HALF)), HBM],
            out_specs=[
                once((LMAX, HALF)),
                once((HALF, LMAX)),
                once((LMAX, HALF)),
                blk,
                once((ROWS, HALF)),
                blk,
                pl.BlockSpec((72, rows), lambda i, lens: (0, early(i))),
                once((ROWS + 32, HALF)),
                blk,
                full,
                full,
                whole((72, HALF)),
                whole((72, 128)),
                once((72, KW * HALF)),
                pl.BlockSpec((ROWS, 128), lambda i, lens: (0, late(i))),
                pl.BlockSpec((1, 8, ROWS), lambda i, lens: (late(i), 0, 0)),
            ]
            + [HBM] * 6,
            scratch_shapes=[
                pltpu.VMEM((5, 192, HALF), BF),
                pltpu.VMEM((LMAX + 2 * PAD, D), BF),
                pltpu.VMEM((5, HALF, D), BF),
                pltpu.VMEM((ROWS, HALF), BF),
                pltpu.VMEM((8, HALF), F32),
                pltpu.VMEM((D // 128, rows + 32, 128), F32),
                pltpu.VMEM((HALF // 128, rows + 32, 128), F32),
                pltpu.SemaphoreType.DMA((8,)),
                pltpu.SemaphoreType.DMA((9,)),
                pltpu.SemaphoreType.DMA((9,)),
                pltpu.SemaphoreType.DMA((35,)),
                pltpu.SemaphoreType.DMA((35,)),
                pltpu.SemaphoreType.DMA((3,)),
                pltpu.SemaphoreType.DMA((2,)),
            ],
        ),
        out_shape=[
            jax.ShapeDtypeStruct((LMAX, HALF), BF),
            jax.ShapeDtypeStruct((HALF, LMAX), BF),
            jax.ShapeDtypeStruct((LMAX, HALF), BF),
            half,
            half,
            half,
            jax.ShapeDtypeStruct((72, ROWS), F32),
            jax.ShapeDtypeStruct((ROWS + 32, HALF), BF),
            half,
            jax.ShapeDtypeStruct((ROWS, D), BF),
            jax.ShapeDtypeStruct((ROWS, D), BF),
            jax.ShapeDtypeStruct((72, HALF), BF),
            jax.ShapeDtypeStruct((72, 128), F32),
            jax.ShapeDtypeStruct((72, KW * HALF), BF),
            half,
            jax.ShapeDtypeStruct((3, 8, ROWS), F32),
            jax.ShapeDtypeStruct((LMAX + 2 * PAD, D), BF),
            jax.ShapeDtypeStruct((5, HALF, D), BF),
            jax.ShapeDtypeStruct((2, HALF, GW), BF),
            jax.ShapeDtypeStruct((2, HALF, D), BF),
            jax.ShapeDtypeStruct((ROWS, D), BF),
            jax.ShapeDtypeStruct((2, GW, HALF), BF),
        ],
        **comm_params("front", 2),
    )(
        lens, tokens, *weights, w_kernel, b_kernel, perm, wdep, bv, bc, bq, bp, w_inter, w_dense, w_output, cotangent
    )


def back_kernel(
    lens, gcv_ref, conv_ref, kp_ref, q_ref, pt_ref, wk_ref, spread_ref, ones_ref,
    qs_ref, do_ref, k_ref, v_ref, kt_ref, lse_ref, del_ref, pay_all, hid_ref,
    seq_hbm, wc_ref, wp_ref, gpre_ref, dep_ref, wdep_ref, smf_ref, gbi_ref,
    gqm_ref, dq_ref, dk_ref, dv_ref, ghm_ref, edge_ref, half_ref, piece_ref, piece_cp_ref, out_ref,
    acc, wbuf, tbuf, dka, dva, near, mine, ybuf, mid, zbuf, both, xbuf, half,
    gpad, dbuf, hwin, sbuf, agc, agp, gwk, gbk, sm, gdp, pcp, near_cp,
    out2, far2, y2, mid2, z2, out_cp, far_cp, y_cp, mid_cp, z_cp, pay_ref, seq_ref, loads,
    ns, nr, s, v_sem, ls, hs, hr,
):
    step = pl.program_id(0)
    place = Place()
    n = lens[place.r]
    groups = Groups(place, s, v_sem)
    hidden = FromRows(place, hid_ref, out_ref, ls, hs, hr)
    load_pay = pltpu.make_async_copy(pay_all.at[:, place.c], pay_ref, loads.at[0])
    load_seq = pltpu.make_async_copy(seq_hbm, seq_ref, loads.at[1])

    def near_copy(k):
        rr = 1 - place.r if k % 2 == 0 else place.r
        src, dst = (pay_all, near) if k < 2 else (pcp, near_cp)
        return send(src.at[rr, 1 - place.c], dst.at[rr], ns.at[k], nr.at[k], place.core)

    def over(k, src, dst):
        return send(src, dst, s.at[k], v_sem.at[k], place.across)

    @pl.when(step == 0)
    def _():
        meet(everyone(place))
        near_copy(0).start()
        near_copy(1).start()
        hidden.start()
        load_pay.start()
        load_seq.start()
        for ref in (acc, agc, agp):
            clear(ref)
        for ref in (tbuf, gwk, gbk, sm, gdp):
            ref[...] = jnp.zeros_like(ref)
        gpad[0:32, :] = jnp.zeros((32, HALF), BF)
        gpad[32 + ROWS :, :] = jnp.zeros((32, HALF), BF)

    @pl.when(step == 2)
    def _():
        near_copy(0).wait()
        near_copy(1).wait()
        load_pay.wait()
        there = 1 - place.r
        out2[...] = (near[there, 2].astype(F32) + pay_ref[there, 2].astype(F32)).astype(BF)
        over(18, out2, far2).start()
        for ch in range(2):
            for rr in range(2):
                total = near[rr, ch].astype(F32) + pay_ref[rr, ch].astype(F32)
                mine[ch, :, :, rr] = total.astype(BF)
            groups.half(ch, mine.at[ch], ybuf.at[ch]).start()

    def settle(ch):
        groups.half(ch, mine.at[ch], ybuf.at[ch]).wait_recv()
        mid[ch] = (mine[ch, place.y].astype(F32) + ybuf[ch].astype(F32)).astype(BF)

    def merge(ch):
        groups.cross(16 + ch, both.at[ch], xbuf.at[ch]).wait_recv()
        return (both[ch, place.r].astype(F32) + xbuf[ch].astype(F32)).astype(BF)

    def quarters(ch):
        if ch < 2:
            return 4 + 3 * ch, mid.at[ch], zbuf.at[ch]
        return (10, mid2, z2) if ch == 2 else (13, mid_cp, z_cp)

    @pl.when(step == 6)
    def _():
        settle(0)
        groups.start_quarters(*quarters(0))
        near_copy(2).start()
        near_copy(3).start()

    @pl.when(step == 7)
    def _():
        near_copy(2).wait()
        near_copy(3).wait()
        there = 1 - place.r
        out_cp[...] = (near_cp[there].astype(F32) + pcp[there, place.c].astype(F32)).astype(BF)
        over(19, out_cp, far_cp).start()

    @pl.when(step == 8)
    def _():
        settle(1)
        groups.start_quarters(*quarters(1))
        groups.collect(*quarters(0), both.at[0])
        groups.cross(16, both.at[0], xbuf.at[0]).start()
        over(18, out2, far2).wait_recv()
        here = near[place.r, 2].astype(F32) + pay_ref[place.r, 2].astype(F32)
        far2[...] = (here + far2[...].astype(F32)).astype(BF)
        groups.half(2, far2, y2).start()

    @pl.when(step == 9)
    def _():
        groups.start_along(20, half, merge(0))
        over(19, out_cp, far_cp).wait_recv()
        here = near_cp[place.r].astype(F32) + pcp[place.r, place.c].astype(F32)
        far_cp[...] = (here + far_cp[...].astype(F32)).astype(BF)
        groups.half(3, far_cp, y_cp).start()

    @pl.when(step == 10)
    def _():
        groups.collect(*quarters(1), both.at[1])
        groups.cross(17, both.at[1], xbuf.at[1]).start()
        groups.half(2, far2, y2).wait_recv()
        mid2[...] = (far2[place.y].astype(F32) + y2[...].astype(F32)).astype(BF)
        groups.start_quarters(*quarters(2))

    @pl.when(step == 11)
    def _():
        piece_ref[0] = merge(1)
        groups.half(3, far_cp, y_cp).wait_recv()
        mid_cp[...] = (far_cp[place.y].astype(F32) + y_cp[...].astype(F32)).astype(BF)
        groups.start_quarters(*quarters(3))

    @pl.when(step < 4)
    def _():
        rows = gcv_ref.shape[0]
        wide = rows + 32
        put_tiles(wbuf, conv_ref[pl.ds(pl.multiple_of(step * rows, 16), wide), :].astype(F32))
        kp = kp_ref[...]
        kpt = kp.T.astype(BF)
        gkps = [None] * KW
        there = pl.ds(pl.multiple_of(place.c * ROWS + step * rows, 16), wide)
        for t in range(HALF // 128):
            cols = slice(t * 128, (t + 1) * 128)
            gcv = gcv_ref[:, cols].astype(F32)
            total = jnp.zeros((wide, 128), F32)
            for j in range(KW):
                prod = (gcv * wbuf[t, 12 + j : 12 + j + rows, :]).astype(BF)
                part = nt(ones_ref[:, cols], prod)
                gkps[j] = part if t == 0 else gkps[j] + part
                at = (t * KW + j) * 128
                tbuf[j % 3, 24 : 24 + rows, :] = nn(kpt, spread_ref[:, at : at + 128]) * gcv
                total = total + tbuf[j % 3, 12 - j : 12 - j + wide, :]
            acc[there, cols] += total
        gkp = jnp.concatenate(gkps, axis=0).reshape(KW, 8, rows)
        kp3 = kp.reshape(KW, 8, rows)
        inner = jnp.sum(kp3 * gkp, axis=0, keepdims=True)
        gl = (kp3 * (gkp - inner)).reshape(KW * 8, rows)
        glt = gl.T.astype(BF)
        gbk[0:1, 0:72] += col_sum(glt.astype(F32))
        q = q_ref[...].astype(F32)
        pt = pt_ref[...].astype(F32)
        gwk[...] += nn(gl.astype(BF), (pt * q).astype(BF))
        gmix = nn(glt, wk_ref[...])
        gqm_ref[...] = (gmix * pt).astype(BF)
        gpad[rows_at(32 + step * rows, rows), :] = (gmix * q).astype(BF)

    def conv_grads(first, rows):
        keep = row_ids(first, rows) < n
        gco = jnp.where(keep, acc[rows_at(16 + first, rows), :], 0.0).astype(BF)
        tok = seq_ref[rows_at(PAD + first, rows), :]
        h = jnp.where(keep, tok.astype(F32), 0.0).astype(BF)
        agc[...] += nn(gco.T, h)
        sm[2:3, :] += col_sum(gco.astype(F32))
        return nn(gco, wc_ref[0])

    @pl.when(step == 4)
    def _():
        load_seq.wait()
        wdep = wdep_ref[...].astype(F32)
        at = pl.multiple_of((1 - place.c) * (ROWS + 16), 16)
        sbuf[...] = nn(gpad[pl.ds(at, 48), :], wp_ref[0])
        total = conv_grads(pl.multiple_of(ROWS - 16 * place.c, 16), 16)
        for j in range(KW):
            total = total + sbuf[20 - j : 36 - j, :] * wdep[j : j + 1, :]
        edge_ref[...] = total

    @pl.when((step == 4) | (step == 5))
    def _():
        m = step - 4
        rows = gpre_ref.shape[0]
        wide = rows + 32
        first = pl.multiple_of(place.c * ROWS + m * rows, 16)
        wdep = wdep_ref[...].astype(F32)
        win = gpad[rows_at(m * rows + 16, wide), :]
        gpt = win[16 : 16 + rows]
        sm[3:4, :] += col_sum(gpt.astype(F32))
        agp[...] += nn(gpt.T, dep_ref[...])
        put_tiles(dbuf, nn(win, wp_ref[0]))
        ids = row_ids(first - 16, wide)
        inside = (ids >= 0) & (ids < n)
        put_tiles(hwin, jnp.where(inside, seq_ref[pl.ds(first, wide), :].astype(F32), 0.0))
        ghm_ref[...] = (conv_grads(first, rows) + gpre_ref[...].astype(F32)).astype(BF)
        for t in range(D // 128):
            cols = slice(t * 128, (t + 1) * 128)

            def strip(k, sums):
                r0 = pl.multiple_of(k * 128, 128)
                gdep = dbuf[t, pl.ds(r0 + 16, 128), :]
                total = ghm_ref[pl.ds(r0, 128), cols].astype(F32)
                new = []
                for j in range(KW):
                    prod = gdep * hwin[t, pl.ds(r0 + 12 + j, 128), :]
                    new.append(sums[j] + jnp.sum(prod.reshape(16, 8, 128), axis=0))
                    total = total + dbuf[t, pl.ds(r0 + 20 - j, 128), :] * wdep[j : j + 1, cols]
                ghm_ref[pl.ds(r0, 128), cols] = total.astype(BF)
                return tuple(new)

            sums = lax.fori_loop(0, rows // 128, strip, (jnp.zeros((8, 128), F32),) * KW)
            for j in range(KW):
                gdp[j : j + 1, cols] += col_sum(sums[j])

    @pl.when(step == 5)
    def _():
        def put(r, c, first, value):
            pcp[r, c, first // 256, first // 64 % 4] = value.astype(BF)

        zeros = lambda k: jnp.zeros((k, HALF), F32)
        bias = jnp.concatenate([gbk[0:1, :], jnp.zeros((1, 256), F32)], axis=1)
        mixed = [sm[2:4, :], bias, gdp[8:9, 0:HALF], gdp[8:9, HALF:D], zeros(3)]
        inter = [gbi_ref[:, k * HALF : (k + 1) * HALF] for k in range(8)]
        norms = [smf_ref[:, 0:HALF], smf_ref[:, HALF:D]]
        depth = [gdp[0:8, 0:HALF], gdp[0:8, HALF:D], zeros(8)]
        little = jnp.concatenate([gwk[...]] + mixed + norms + inter + depth, axis=0)
        for r in range(2):
            for c in range(2):
                for k in range(3):
                    rows = slice(c * 192 + k * 64, c * 192 + (k + 1) * 64)
                    put(r, c, k * 64, agc[rows, r * HALF : (r + 1) * HALF])
                    put(r, c, 192 + k * 64, agp[rows, r * HALF : (r + 1) * HALF])
                put(r, c, 384, little[0:64])
                put(r, c, 448, little[64:128])

    @pl.when(step >= 6)
    def _():
        i = lax.rem(step, 2)
        k = k_ref[...]
        v = v_ref[...]
        rows = qs_ref.shape[0]
        lane = lax.broadcasted_iota(jnp.int32, (rows, 128), 1)
        dk = dv = None
        for hh in range(2):
            head = (lane < HD) == (hh == 0)
            q = jnp.where(head, qs_ref[...], jnp.zeros((), BF))
            do = jnp.where(head, do_ref[...], jnp.zeros((), BF))
            p = jnp.exp2(nt(k, q) - lse_ref[0, hh : hh + 1, :])
            ds = (p * (nt(v, do) - del_ref[0, hh : hh + 1, :])).astype(BF)
            dv_one = nn(p.astype(BF), do)
            dk_one = nn(ds, q)
            dv = dv_one if dv is None else dv + dv_one
            dk = dk_one if dk is None else dk + dk_one
            dq_ref[hh * HD : (hh + 1) * HD, :] = (nn(kt_ref[hh * HD : (hh + 1) * HD, :], ds) * 0.125).astype(BF)

        @pl.when(i == 0)
        def _():
            dka[...] = dk
            dva[...] = dv

        @pl.when(i == 1)
        def _():
            keep = row_ids(0, LMAX) < n
            dk_ref[...] = jnp.where(keep, (dka[...] + dk) * LN2, 0.0).astype(BF)
            dv_ref[...] = jnp.where(keep, dva[...] + dv, 0.0).astype(BF)

    @pl.when(step == 11)
    def _():
        groups.collect(*quarters(2), piece_ref.at[1])
        groups.collect(*quarters(3), piece_cp_ref)
        groups.await_along(20, half)
        half_ref[...] = half[...]
        for ch in range(2):
            groups.half(ch, mine.at[ch], ybuf.at[ch]).wait_send()
            groups.cross(16 + ch, both.at[ch], xbuf.at[ch]).wait_send()
        groups.half(2, far2, y2).wait_send()
        groups.half(3, far_cp, y_cp).wait_send()
        over(18, out2, far2).wait_send()
        over(19, out_cp, far_cp).wait_send()
        for offset in (1, 2, 3):
            for ch in range(4):
                groups.quarter(*quarters(ch), offset).wait_send()
            groups.along(20, half, offset, place.z).wait_send()
        hidden.finish()


def back(
    lens, gcv, conv, kp, q, pt, wk72, spread, ones8, qs, do, kd, vz, kt, lse, delta, pay, hid,
    seq, w5, gpre, dep, wdep, smf, gbi,
):
    crows = 256
    rows = 512
    early = lambda s: jnp.minimum(s, 3)
    between = lambda s: jnp.minimum(jnp.maximum(s - 4, 0), 1)
    late = lambda s: jnp.maximum(s - 6, 0)
    which = lambda s: lax.div(late(s), 2)
    part = lambda s: lax.rem(late(s), 2)
    cblk = pl.BlockSpec((crows, HALF), lambda s, lens: (early(s), 0))
    mine = pl.BlockSpec((rows, 128), lambda s, lens: (part(s), which(s)))
    pair = pl.BlockSpec((LMAX, 128), lambda s, lens: (0, which(s)))
    stats = pl.BlockSpec((1, 8, rows), lambda s, lens: (which(s), 0, part(s)))
    full = pl.BlockSpec((rows, D), lambda s, lens: (between(s), 0))
    weight = lambda j: pl.BlockSpec((1, HALF, D), lambda s, lens: (j, 0, 0), pipeline_mode=pl.Buffered(1))
    block = (3, 2, 4, 80, HALF)
    pay = pay.reshape((2, 2) + block)
    return pl.pallas_call(
        back_kernel,
        grid_spec=pltpu.PrefetchScalarGridSpec(
            num_scalar_prefetch=1,
            grid=(12,),
            in_specs=[
                cblk,
                once((ROWS + 32, HALF)),
                pl.BlockSpec((72, crows), lambda s, lens: (0, early(s))),
                cblk,
                cblk,
                once((72, HALF)),
                once((72, KW * HALF)),
                once((8, HALF)),
                mine,
                mine,
                pair,
                pair,
                pl.BlockSpec((128, LMAX), lambda s, lens: (which(s), 0)),
                stats,
                stats,
                HBM,
                once((ROWS, D)),
                HBM,
                weight(2),
                weight(4),
                full,
                full,
                once((KW, D)),
                once((8, D)),
                once((1, FF)),
            ],
            out_specs=[
                cblk,
                pl.BlockSpec((128, rows), lambda s, lens: (which(s), part(s))),
                pair,
                pair,
                full,
                once((16, D)),
                once((4, 80, HALF)),
                once((2, 80, HALF)),
                once((64, HALF)),
                HBM,
            ],
            scratch_shapes=[
                pltpu.VMEM((LMAX + 32, HALF), F32),
                pltpu.VMEM((HALF // 128, crows + 32, 128), F32),
                pltpu.VMEM((3, crows + 48, 128), F32),
                pltpu.VMEM((LMAX, 128), F32),
                pltpu.VMEM((LMAX, 128), F32),
                pltpu.VMEM((2,) + block, BF),
                pltpu.VMEM((2, 2, 4, 2, 80, HALF), BF),
                pltpu.VMEM((2, 4, 2, 80, HALF), BF),
                pltpu.VMEM((2, 4, 2, 80, HALF), BF),
                pltpu.VMEM((2, 3, 2, 80, HALF), BF),
                pltpu.VMEM((2, 2, 80, HALF), BF),
                pltpu.VMEM((2, 80, HALF), BF),
                pltpu.VMEM((4, 80, HALF), BF),
                pltpu.VMEM((ROWS + 64, HALF), BF),
                pltpu.VMEM((D // 128, rows + 32, 128), F32),
                pltpu.VMEM((D // 128, rows + 32, 128), F32),
                pltpu.VMEM((48, D), F32),
                pltpu.VMEM((HALF, D), F32),
                pltpu.VMEM((HALF, D), F32),
                pltpu.VMEM((72, HALF), F32),
                pltpu.VMEM((8, 128), F32),
                pltpu.VMEM((8, HALF), F32),
                pltpu.VMEM((16, D), F32),
                pltpu.VMEM((2, 2, 2, 4, 64, HALF), BF),
                pltpu.VMEM((2, 2, 4, 64, HALF), BF),
                pltpu.VMEM((2, 4, 80, HALF), BF),
                pltpu.VMEM((2, 4, 80, HALF), BF),
                pltpu.VMEM((4, 80, HALF), BF),
                pltpu.VMEM((4, 80, HALF), BF),
                pltpu.VMEM((3, 80, HALF), BF),
                pltpu.VMEM((2, 4, 64, HALF), BF),
                pltpu.VMEM((2, 4, 64, HALF), BF),
                pltpu.VMEM((4, 64, HALF), BF),
                pltpu.VMEM((4, 64, HALF), BF),
                pltpu.VMEM((3, 64, HALF), BF),
                pltpu.VMEM((2,) + block, BF),
                pltpu.VMEM((LMAX + 2 * PAD, D), BF),
                pltpu.SemaphoreType.DMA((2,)),
                pltpu.SemaphoreType.DMA((4,)),
                pltpu.SemaphoreType.DMA((4,)),
                pltpu.SemaphoreType.DMA((23,)),
                pltpu.SemaphoreType.DMA((23,)),
                pltpu.SemaphoreType.DMA,
                pltpu.SemaphoreType.DMA((2,)),
                pltpu.SemaphoreType.DMA((3,)),
            ],
        ),
        out_shape=[
            jax.ShapeDtypeStruct((ROWS, HALF), BF),
            jax.ShapeDtypeStruct((HALF, ROWS), BF),
            jax.ShapeDtypeStruct((LMAX, HALF), BF),
            jax.ShapeDtypeStruct((LMAX, HALF), BF),
            jax.ShapeDtypeStruct((ROWS, D), BF),
            jax.ShapeDtypeStruct((16, D), F32),
            jax.ShapeDtypeStruct((4, 80, HALF), BF),
            jax.ShapeDtypeStruct((2, 80, HALF), BF),
            jax.ShapeDtypeStruct((64, HALF), BF),
            jax.ShapeDtypeStruct((2, ROWS, HALF), BF),
        ],
        **comm_params("back", 4),
    )(
        lens, gcv, conv, kp, q, pt, wk72, spread, ones8, qs, do, kd, vz, kt, lse, delta, pay, hid,
        seq, w5, w5, gpre, dep, wdep, smf, gbi,
    )


def norm_parts(x):
    xc = x - jnp.mean(x, axis=1, keepdims=True)
    inv = lax.rsqrt(jnp.mean(xc * xc, axis=1, keepdims=True) + EPS)
    return xc * inv, inv


def norm_back(up, normal, inv, gain):
    e = up * gain
    return inv * (e - jnp.mean(e, axis=1, keepdims=True) - normal * jnp.mean(e * normal, axis=1, keepdims=True))


def ffn_kernel(
    lens, ctx_ref, mix_ref, tok_ref, cot_ref, wd_ref, wi_hbm, wo_hbm, v0, v1, v2, v3, v4, v5, bi_ref, ones_ref,
    hid_ref, gpre_ref, gctx_ref, gcv_ref, del_ref, pay_ref, sm_ref, gbi_ref,
    act_s, gp_s, awd, awi, awo, wi_ref, wo_ref, loads,
):
    i = pl.program_id(0)
    rows = ctx_ref.shape[0]
    keep = row_ids(half_index() * ROWS + i * rows, rows) < length(lens)

    load_wi = pltpu.make_async_copy(wi_hbm, wi_ref, loads.at[0])
    load_wo = pltpu.make_async_copy(wo_hbm, wo_ref, loads.at[1])

    @pl.when(i == 0)
    def _():
        load_wi.start()
        load_wo.start()
        clear(awd)
        for g in range(2):
            clear(awi.at[g])
            clear(awo.at[g])
        sm_ref[...] = jnp.zeros_like(sm_ref)
        gbi_ref[...] = jnp.zeros_like(gbi_ref)

    vectors = [line(ref) for ref in (v0, v1, v2, v3, v4, v5)]
    vec = lambda k: vectors[k]
    inter_bias = line(bi_ref)
    h = tok_ref[...].astype(F32)
    ctx = ctx_ref[...]
    mixed = jnp.concatenate([ctx, mix_ref[...]], axis=1)
    n1, inv1 = norm_parts(nn(mixed, wd_ref[...]) + vec(0) + h)
    f1 = n1 * vec(1) + vec(2)
    fl = f1.astype(BF)

    @pl.when(i == 0)
    def _():
        load_wi.wait()
        load_wo.wait()

    chunk = 512
    outs = []
    for g in range(2):
        fg = fl[:, g * HALF : (g + 1) * HALF]
        for ch in range(GW // chunk):
            cols = slice(ch * chunk, (ch + 1) * chunk)
            put = slice(g * GW + ch * chunk, g * GW + (ch + 1) * chunk)
            x = nn(fg, wi_ref[g, :, cols]) + inter_bias[:, put]
            phi = 0.5 + 0.5 * lax.erf(x * 0.7071067811865476)
            act_s[:, put] = (x * phi).astype(BF)
            gp_s[:, put] = phi + x * jnp.exp2(x * x * (-0.5 * LOG2E)) * 0.3989422804014327
        outs.append(nn(act_s[:, g * GW : (g + 1) * GW], wo_ref[g]))
    n2, inv2 = norm_parts(jnp.concatenate(outs, axis=1) + vec(3) + f1)
    hid_ref[...] = (n2 * vec(4) + vec(5)).astype(BF)
    u = jnp.where(keep, cot_ref[...].astype(F32), 0.0)
    gp2 = norm_back(u, n2, inv2, vec(4))
    go = gp2.astype(BF)
    got = go.T
    flt = fl.T
    gfs = []
    for g in range(2):
        sel = slice(g * HALF, (g + 1) * HALF)
        gf = gp2[:, sel]
        for ch in range(GW // chunk):
            cols = slice(ch * chunk, (ch + 1) * chunk)
            put = slice(g * GW + ch * chunk, g * GW + (ch + 1) * chunk)
            gi = (gp_s[:, put] * nt(go[:, sel], wo_ref[g, cols, :])).astype(BF)
            gbi_ref[0:1, put] += col_sum(gi.astype(F32))
            awo[g, :, cols] += nn(got[sel], act_s[:, put])
            awi[g, :, cols] += nn(flt[sel], gi)
            gf = gf + nt(gi, wi_ref[g, :, cols])
        gfs.append(gf)
    gf = jnp.concatenate(gfs, axis=1)
    gpre = norm_back(gf, n1, inv1, vec(1))
    gd = gpre.astype(BF)
    gpre_ref[...] = gd
    sm_ref[0:1, :] += col_sum(go.astype(F32))
    sm_ref[1:2, :] += col_sum(u * n2)
    sm_ref[2:3, :] += col_sum(u)
    sm_ref[3:4, :] += col_sum(gd.astype(F32))
    sm_ref[4:5, :] += col_sum(gf * n1)
    sm_ref[5:6, :] += col_sum(gf)
    awd[...] += nn(mixed.T, gd)
    gm = nt(gd, wd_ref[...])
    gctx = gm[:, :HALF].astype(BF)
    gctx_ref[...] = gctx
    gcv_ref[...] = gm[:, HALF:].astype(BF)
    prod = (gctx.astype(F32) * ctx.astype(F32)).astype(BF)
    del_ref[...] = nt(ones_ref[...], prod).reshape(3, 8, rows)

    @pl.when(i == pl.num_programs(0) - 1)
    def _():
        for r in range(2):
            for c in range(2):
                pay_ref[r, c, 0:HALF, :] = awi[r, :, c * D : c * D + HALF].astype(BF)
                pay_ref[r, c, HALF:D, :] = awi[r, :, c * D + HALF : (c + 1) * D].astype(BF)
                pay_ref[r, c, D : 2 * D, :] = awo[r, :, c * D : (c + 1) * D].T.astype(BF)
                for part in range(2):
                    piece = awd[part * HALF + c * 192 : part * HALF + (c + 1) * 192, r * HALF : (r + 1) * HALF]
                    pay_ref[r, c, 2 * D + part * 192 : 2 * D + (part + 1) * 192, :] = piece.astype(BF)


def ffn(lens, ctx, mix, tok, cot, wd, wi, wo, vectors, bi, ones24):
    rows = 256
    blk = lambda w: pl.BlockSpec((rows, w), lambda i, lens: (i, 0))
    return pl.pallas_call(
        ffn_kernel,
        grid_spec=pltpu.PrefetchScalarGridSpec(
            num_scalar_prefetch=1,
            grid=(ROWS // rows,),
            in_specs=[
                blk(HALF),
                blk(HALF),
                blk(D),
                blk(D),
                once((D, D)),
                HBM,
                HBM,
                *[whole((D,))] * 6,
                whole((FF,)),
                whole((24, HALF)),
            ],
            out_specs=[
                blk(D),
                blk(D),
                blk(HALF),
                blk(HALF),
                pl.BlockSpec((3, 8, rows), lambda i, lens: (0, 0, i)),
                once((2, 2, FFN_ROWS, HALF)),
                whole((8, D)),
                whole((1, FF)),
            ],
            scratch_shapes=[
                pltpu.VMEM((rows, FF), BF),
                pltpu.VMEM((rows, FF), F32),
                pltpu.VMEM((D, D), F32),
                pltpu.VMEM((2, HALF, GW), F32),
                pltpu.VMEM((2, HALF, GW), F32),
                pltpu.VMEM((2, HALF, GW), BF),
                pltpu.VMEM((2, GW, HALF), BF),
                pltpu.SemaphoreType.DMA((2,)),
            ],
        ),
        out_shape=[
            jax.ShapeDtypeStruct((ROWS, D), BF),
            jax.ShapeDtypeStruct((ROWS, D), BF),
            jax.ShapeDtypeStruct((ROWS, HALF), BF),
            jax.ShapeDtypeStruct((ROWS, HALF), BF),
            jax.ShapeDtypeStruct((3, 8, ROWS), F32),
            jax.ShapeDtypeStruct((2, 2, FFN_ROWS, HALF), BF),
            jax.ShapeDtypeStruct((8, D), F32),
            jax.ShapeDtypeStruct((1, FF), F32),
        ],
        **params("ffn"),
    )(lens, ctx, mix, tok, cot, wd, wi, wo, *vectors, bi, ones24)


def tail_kernel(
    lens, seq_hbm, dk_ref, dv_ref, dq_ref, gqm_ref, ghm_ref, edge_ref, w_hbm, half0, pieces, piece_cp,
    big_ref, cp_ref, sum_ref, ght_ref,
    agw, accb, sm, tsend, trecv, gho, halves, other, half_cp, last_cp,
    pay, total_sum, near, far, out, mid, ybuf, zsum, s, v, ns, nr, cs, cr, gs, gr, es, er, ls, hs, hr,
    toks, w_ref, loads,
):
    step = pl.program_id(0)
    i = lax.rem(step, 4)
    p = Place()
    r, c = p.r, p.c
    rows = dk_ref.shape[0]
    b = lax.rem((1 - c) * 2 + i, 4)
    n = lens[r]
    groups = Groups(p, gs, gr)
    chunks = 5
    crows = PROJ_ROWS // chunks
    summed = Sum(p, far, mid, ybuf, zsum, total_sum, crows, s, v)
    places = [FromRows(p, gho.at[k], ght_ref.at[k], ls.at[k], hs.at[k], hr.at[k]) for k in range(2)]

    def load(k):
        first = lax.rem((1 - c) * 2 + k, 4) * rows + PAD
        return pltpu.make_async_copy(seq_hbm.at[rows_at(first, rows), :], toks.at[k], loads.at[k])

    load_w = pltpu.make_async_copy(w_hbm, w_ref, loads.at[4])

    def theirs(k):
        return send(tsend.at[k], trecv.at[k], es.at[k], er.at[k], p.core)

    def part(ch):
        return slice(ch * crows, (ch + 1) * crows)

    def beside(k, ch):
        rr = 1 - r if k == 0 else r
        at = k * chunks + ch
        return send(pay.at[rr, 1 - c, part(ch), :], near.at[rr, part(ch), :], ns.at[at], nr.at[at], p.core)

    def cross(ch):
        return send(out.at[part(ch), :], far.at[part(ch), :], cs.at[ch], cr.at[ch], p.across)

    def arrive(ch):
        beside(1, ch).wait_recv()
        cross(ch).wait_recv()
        total = near[r, part(ch), :].astype(F32) + pay[r, c, part(ch), :].astype(F32)
        far[part(ch), :] = (total + far[part(ch), :].astype(F32)).astype(BF)
        summed.half(ch)

    stages = [
        arrive,
        summed.quarter,
        lambda ch: summed.along(ch, summed.collect(ch)),
        summed.back,
        summed.finish_spread,
    ]

    def tick(t):
        for k, stage in enumerate(stages):
            if 0 <= t - k < chunks:
                stage(t - k)

    halfs = [half0, halves.at[0], halves.at[1], half_cp]
    others = [other.at[0], other.at[1], other.at[2], last_cp]

    def back(k, z):
        return groups.back(9 + 4 * k + z, halfs[k].at[z], others[k].at[z])

    @pl.when(step == 0)
    def _():
        for k in range(4):
            load(k).start()
        load_w.start()
        meet(everyone(p))
        groups.start_along(0, halves.at[0], pieces[0])
        groups.start_along(3, halves.at[1], pieces[1])
        groups.start_along(6, half_cp, piece_cp[...])
        for z in range(4):
            back(0, z).start()
        for j in range(3):
            clear(agw.at[j])
        sm[...] = jnp.zeros_like(sm)

    for k in range(4):

        @pl.when(step == k)
        def _():
            load(k).wait()

    @pl.when(step == 4)
    def _():
        load_w.wait()
        for ch in range(chunks):
            beside(0, ch).wait_recv()
            total = near[1 - r, part(ch), :].astype(F32) + pay[1 - r, c, part(ch), :].astype(F32)
            out[part(ch), :] = total.astype(BF)
            cross(ch).start()

    @pl.when(step == 5)
    def _():
        groups.await_along(0, halves.at[0])
        back(1, 0).start()
        back(1, 1).start()

    @pl.when(step == 6)
    def _():
        tick(0)
        back(1, 2).start()
        back(1, 3).start()

    @pl.when(step == 7)
    def _():
        tick(1)

    keep = row_ids(b * rows, rows) < n

    def query_grad():
        return (dq_ref[...].astype(F32) + gqm_ref[...].astype(F32).T).astype(BF)

    @pl.when(step < 4)
    def _():
        h = jnp.where(keep, toks[i].astype(F32), 0.0).astype(BF)
        agw[0] += nn(dk_ref[...].T, h)
        agw[1] += nn(dv_ref[...].T, h)
        sm[1:2, :] += col_sum(dv_ref[...].astype(F32))

        @pl.when(step >= 2)
        def _():
            gqt = query_grad()
            sm[0:1, :] += col_sum(gqt.T.astype(F32))
            agw[2] += nn(gqt, h)

    @pl.when(step == 3)
    def _():
        for rr in range(2):
            for cc in range(2):
                for j in range(3):
                    piece = agw[j, cc * 192 : (cc + 1) * 192, rr * HALF : (rr + 1) * HALF]
                    pay[rr, cc, j * 192 : (j + 1) * 192, :] = piece.astype(BF)
                pay[rr, cc, 576:, :] = jnp.concatenate([sm[...], jnp.zeros((56, HALF), F32)], axis=0).astype(BF)
        for ch in range(chunks):
            for k in range(2):
                beside(k, ch).start()

    @pl.when(step >= 4)
    def _():
        accb[...] = nn(dk_ref[...], w_ref[0]) + nn(dv_ref[...], w_ref[1])

        @pl.when(step >= 6)
        def _():
            accb[...] += nn(query_grad().T, w_ref[3]) + ghm_ref[...].astype(F32)

    for k in range(2):

        @pl.when((step == 4 + k) & (c == k))
        def _():
            at = slice(0, 16) if k == 0 else slice(rows - 16, rows)
            accb[at, :] += edge_ref[...]

        @pl.when(step == 4 + k)
        def _():
            tsend[k] = jnp.where(keep, accb[...], 0.0).astype(BF)
            theirs(k).start()

        @pl.when(step == 6 + k)
        def _():
            theirs(k).wait_recv()
            gho[k] = jnp.where(keep, accb[...] + trecv[k].astype(F32), 0.0).astype(BF)
            places[k].start()

    @pl.when(step == 7)
    def _():
        tick(2)
        groups.await_along(3, halves.at[1])
        back(2, 0).start()
        back(2, 1).start()
        tick(3)
        back(2, 2).start()
        back(2, 3).start()
        tick(4)
        groups.await_along(6, half_cp)
        back(3, 0).start()
        back(3, 1).start()
        tick(5)
        back(3, 2).start()
        back(3, 3).start()
        tick(6)
        for ch in range(2):
            for z in range(4):
                back(ch, z).wait_recv()
        big_ref[0, p.y] = half0[...]
        big_ref[0, 1 - p.y] = other[0]
        big_ref[1, p.y] = halves[0]
        big_ref[1, 1 - p.y] = other[1]
        tick(7)
        for z in range(4):
            back(3, z).wait_recv()
        cp_ref[p.y] = half_cp[...]
        cp_ref[1 - p.y] = last_cp[...]
        tick(8)
        sum_ref[...] = total_sum[...]
        for z in range(4):
            back(2, z).wait_recv()
        big_ref[2, p.y] = halves[1]
        big_ref[2, 1 - p.y] = other[2]
        for ch in range(chunks):
            summed.finish_sum(ch)
            cross(ch).wait_send()
            for k in range(2):
                beside(k, ch).wait_send()
        for k in range(4):
            for z in range(4):
                back(k, z).wait_send()
        for offset in (1, 2, 3):
            groups.along(0, halves.at[0], offset, p.z).wait_send()
            groups.along(3, halves.at[1], offset, p.z).wait_send()
            groups.along(6, half_cp, offset, p.z).wait_send()
        theirs(0).wait_send()
        theirs(1).wait_send()
        places[0].finish()
        places[1].finish()


def tail(lens, seq_tok, dk, dv, dq, gqm, ghm, edge, w5, half0, pieces, piece_cp):
    rows = 512
    mine = lambda s: jnp.maximum(lax.rem(s, 4) - 2, 0)
    seq = pl.BlockSpec((rows, HALF), lambda s, lens: (lax.rem((1 - half_index()) * 2 + s, 4), 0))
    own = lambda w: pl.BlockSpec((rows, w), lambda s, lens: (mine(s), 0))
    crows = PROJ_ROWS // 5
    return pl.pallas_call(
        tail_kernel,
        grid_spec=pltpu.PrefetchScalarGridSpec(
            num_scalar_prefetch=1,
            grid=(8,),
            in_specs=[
                HBM,
                seq,
                seq,
                pl.BlockSpec((HALF, rows), lambda s, lens: (0, mine(s))),
                own(HALF),
                own(D),
                once((16, D)),
                HBM,
                once((4, 80, HALF)),
                once((2, 80, HALF)),
                once((64, HALF)),
            ],
            out_specs=[
                once((3, 2, 4, 80, HALF)),
                once((2, 4, 64, HALF)),
                once((PROJ_ROWS, HALF)),
                HBM,
            ],
            scratch_shapes=[
                pltpu.VMEM((3, HALF, D), F32),
                pltpu.VMEM((rows, D), F32),
                pltpu.VMEM((8, HALF), F32),
                pltpu.VMEM((2, rows, D), BF),
                pltpu.VMEM((2, rows, D), BF),
                pltpu.VMEM((2, rows, D), BF),
                pltpu.VMEM((2, 4, 80, HALF), BF),
                pltpu.VMEM((3, 4, 80, HALF), BF),
                pltpu.VMEM((4, 64, HALF), BF),
                pltpu.VMEM((4, 64, HALF), BF),
                pltpu.VMEM((2, 2, PROJ_ROWS, HALF), BF),
                pltpu.VMEM((PROJ_ROWS, HALF), BF),
                pltpu.VMEM((2, PROJ_ROWS, HALF), BF),
                pltpu.VMEM((PROJ_ROWS, HALF), BF),
                pltpu.VMEM((PROJ_ROWS, HALF), BF),
                *Sum.scratch(crows, 5),
                pltpu.SemaphoreType.DMA((10,)),
                pltpu.SemaphoreType.DMA((10,)),
                pltpu.SemaphoreType.DMA((5,)),
                pltpu.SemaphoreType.DMA((5,)),
                pltpu.SemaphoreType.DMA((25,)),
                pltpu.SemaphoreType.DMA((25,)),
                pltpu.SemaphoreType.DMA((2,)),
                pltpu.SemaphoreType.DMA((2,)),
                pltpu.SemaphoreType.DMA((2,)),
                pltpu.SemaphoreType.DMA((2, 2)),
                pltpu.SemaphoreType.DMA((2, 3)),
                pltpu.VMEM((4, rows, D), BF),
                pltpu.VMEM((5, HALF, D), BF),
                pltpu.SemaphoreType.DMA((5,)),
            ],
        ),
        out_shape=[
            jax.ShapeDtypeStruct((3, 2, 4, 80, HALF), BF),
            jax.ShapeDtypeStruct((2, 4, 64, HALF), BF),
            jax.ShapeDtypeStruct((PROJ_ROWS, HALF), BF),
            jax.ShapeDtypeStruct((2, 2, rows, HALF), BF),
        ],
        **comm_params("tail", 6),
    )(lens, seq_tok, dk, dv, dq, gqm, ghm, edge, w5, half0, pieces, piece_cp)


def outputs_kernel(
    ght, hid, t0, t1, t2, t3, t4, big_i0, big_i1, big_o, big_d, little, late_ref, perm_ref,
    hid_ref, gt_ref, gk_ref, gv_ref, gc_ref, gq_ref, gp_ref, gi_ref, go_ref, gd_ref,
    gdep_ref, gbq_ref, gbv_ref, gbc_ref, gbp_ref, gwk_ref, gbk_ref,
    gbd_ref, gg1_ref, gb1_ref, gbi_ref, gbo_ref, gg2_ref, gb2_ref,
):
    i = pl.program_id(0)
    hid_ref[...] = hid[...]
    half = gt_ref.shape[0] // 2
    gt_ref[0:half, :] = ght[0, 0].astype(F32)
    gt_ref[half:, :] = ght[1, 0].astype(F32)

    for src, ref in ((t0, gk_ref), (t1, gv_ref), (t2, gq_ref), (t3, gc_ref), (t4, gp_ref), (big_o, go_ref), (big_d, gd_ref)):
        ref[...] = src[...].astype(F32)
    gi_ref[:, 0:HALF] = big_i0[...].astype(F32)
    gi_ref[:, HALF:D] = big_i1[...].astype(F32)

    @pl.when(i == 0)
    def _():
        mixed = little[72:80, :].astype(F32)
        low = little[80:88, :].astype(F32)
        high = little[88:96, :].astype(F32)
        inter = little[96:104, :].astype(F32)
        late = late_ref[0:16, :].astype(F32)
        gwk_ref[...] = nn(perm_ref[...], little[0:72, :])
        bias = nt(mixed[:, 0:72].astype(BF), perm_ref[...])
        gbk_ref[...] = bias[2:3, :].reshape(54)
        for k, ref in enumerate((gbq_ref, gbv_ref)):
            ref[...] = late[k : k + 1, :].reshape(HALF)
        for k, ref in enumerate((gbc_ref, gbp_ref)):
            ref[...] = mixed[k : k + 1, :].reshape(HALF)
        for k, ref in enumerate((gbo_ref, gg2_ref, gb2_ref, gbd_ref, gg1_ref, gb1_ref)):
            ref[...] = jnp.concatenate([low[k : k + 1, :], high[k : k + 1, :]], axis=1).reshape(D)
        gbi_ref[...] = jnp.concatenate([inter[k : k + 1, :] for k in range(8)], axis=1).reshape(FF)
        gdep_ref[0:8, 0:HALF] = little[104:112, :].astype(F32)
        gdep_ref[0:8, HALF:D] = little[112:120, :].astype(F32)
        gdep_ref[8:9, 0:HALF] = mixed[3:4, :]
        gdep_ref[8:9, HALF:D] = mixed[4:5, :]


def outputs(ght, hid, total, cp, big, perm):
    rows = 1024
    at = lambda n, first: pl.BlockSpec((n, HALF), lambda i: (first + i, 0))
    blk = at(rows, 0)
    chunk = pl.BlockSpec((2, 1, rows // 2, HALF), lambda i: (0, i, 0, 0))
    shapes = [(KW, D)] + [(HALF,)] * 4 + [(54, HALF), (54,)] + [(D,)] * 3 + [(FF,)] + [(D,)] * 3
    main = [(192, HALF)] * 5 + [(HALF, D), (D, HALF), (HALF, HALF)]
    return pl.pallas_call(
        outputs_kernel,
        grid=(2,),
        in_specs=[chunk, blk]
        + [at(96, 2 * j) for j in (0, 1, 2, 0, 1)]
        + [at(192, 0), at(192, 2), at(384, 2), at(192, 8)]
        + [pl.BlockSpec((128, HALF), lambda i: (3, 0)), pl.BlockSpec((64, HALF), lambda i: (9, 0)), whole((54, 72))],
        out_specs=[blk, blk]
        + [at(96, 0)] * 5
        + [pl.BlockSpec((192, D), lambda i: (i, 0)), at(384, 0), at(192, 0)]
        + [whole(shape) for shape in shapes],
        out_shape=[jax.ShapeDtypeStruct((LMAX, HALF), BF), jax.ShapeDtypeStruct((LMAX, HALF), F32)]
        + [jax.ShapeDtypeStruct(shape, F32) for shape in main + shapes],
        **params("outputs"),
    )(ght, hid, total, total, total, cp, cp, big, big, big, big, cp, total, perm)


def constants():
    ones8 = np.zeros((8, HALF), np.float32)
    ones24 = np.zeros((24, HALF), np.float32)
    perm = np.zeros((72, 54), np.float32)
    for head in range(6):
        cols = slice(head * HD, (head + 1) * HD)
        ones8[head, cols] = 1
        ones24[head // 2 * 8 + head % 2, cols] = 1
        for j in range(KW):
            perm[j * 8 + head, head * KW + j] = 1
    return [jnp.asarray(a, BF) for a in (ones8, ones24, perm)]


def per_device(
    groups, tokens, cotangent, seq_lengths, w_query, w_key, w_value, w_convout, w_point, w_depth,
    b_query, b_value, b_convout, b_point, w_kernel, b_kernel, w_dense, b_dense, gain_one, bias_one,
    w_inter, b_inter, w_output, b_output, gain_two, bias_two,
):
    lens = seq_lengths
    ones8, ones24, perm = constants()
    wdep = w_depth.T

    kd, kt, vz, q, qs, pt, kp, conv, mix, dep, hown, wk72, bk72, spread, ctx, lse, seq, w5, wi, wd, cot, wo = front(
        lens, tokens, (w_key.T, w_value.T, w_convout.T, w_query.T, w_point.T), w_kernel.T, b_kernel, perm,
        wdep, b_value, b_convout, b_query, b_point,
        w_inter[0], w_dense.reshape(2, 192, HALF), w_output[0], cotangent,
    )
    vectors = (b_dense, gain_one, bias_one, b_output, gain_two, bias_two)
    hid, gpre, gctx, gcv, delta, payf, smf, gbi = ffn(
        lens, ctx, mix, hown, cot, wd.reshape(D, D), wi, wo, vectors, b_inter, ones24
    )
    gqm, dq, dk, dv, ghm, edge, half0, pieces, piece_cp, hid = back(
        lens, gcv, conv, kp, q, pt, wk72, spread, ones8, qs, gctx, kd, vz, kt, lse, delta, payf, hid,
        seq, w5, gpre, dep, wdep, smf, gbi,
    )
    big, cp, total, ght = tail(lens, seq, dk, dv, dq, gqm, ghm, edge, w5, half0, pieces, piece_cp)
    big = big.reshape(FFN_ROWS, HALF)
    cp = cp.reshape(512, HALF)
    if groups > 8:
        sums = lax.psum(tuple(x.astype(F32) * 0.125 for x in (total, cp, big)), "dp")
        total, cp, big = (x.astype(BF) for x in sums)
    (
        hidden_out, gt, gk, gv, gc, gq, gp, gi, go, gd, gdep, gbq, gbv, gbc, gbp, gwk, gbk, gbd, gg1, gb1, gbi, gbo, gg2, gb2,
    ) = outputs(ght, hid.reshape(LMAX, HALF), total, cp, big, perm.T)
    return (
        hidden_out, gt, gq.T, gk.T, gv.T, gc.T, gp.T, gdep.T, gbq, gbv, gbc, gbp, gwk.T, gbk, gd, gbd, gg1, gb1,
        gi[None], gbi, go[None], gbo, gg2, gb2,
    )


def solution(mesh):
    act = P(("dp", "col"), "row")
    rep = P()
    proj = P("row", "col")
    in_specs = (
        act, act, P("dp"), proj, proj, proj, proj, proj, rep, rep, rep, rep, rep, rep, rep, P("col", "row"),
        rep, rep, rep, P("row", None, "col"), rep, P("row", "col", None), rep, rep, rep,
    )
    out_specs = (
        act, act, proj, proj, proj, proj, proj, rep, rep, rep, rep, rep, rep, rep, P("col", "row"),
        rep, rep, rep, P("row", None, "col"), rep, P("row", "col", None), rep, rep, rep,
    )
    return jax.shard_map(
        functools.partial(per_device, mesh.shape["dp"]), mesh=mesh, in_specs=in_specs, out_specs=out_specs, check_vma=False)
```
